32 devices in a mesh: parts: 4 (over x, core), ctx: 2 (over y), fsdp: 4 (over z).
Axes of the slice: x: 2, y: 2, z: 4, core: 2. Of those that a mesh axis runs over, the one named last changes fastest.
Arguments:
- decoder_in: bfloat16 [16, 2048, 768], P(('parts', 'fsdp'), 'ctx'), may hold values from -10 to 10
- encoder_out: bfloat16 [16, 2048, 768], P(('parts', 'fsdp'), 'ctx'), may hold values from -6 to 6
- segment_ids: int32 [16, 2048], P(('parts', 'fsdp')), may hold values from 0 to 1, never falling along the last dimension, each value on 1 to 1365 neighbouring positions
- block_order: int32 [16, 4], P(('parts', 'fsdp')), may hold values from 0 to 3, each once within a row
- prompt_len: int32 [16], P(('parts', 'fsdp')), may hold values from 512 to 2048
- self_query: bfloat16 [768, 768], P('fsdp'), may hold values from -0.21875 to 0.21875
- self_key: bfloat16 [768, 768], P('fsdp'), may hold values from -0.21875 to 0.21875
- self_value: bfloat16 [768, 768], P('fsdp'), may hold values from -0.21875 to 0.21875
- self_output: bfloat16 [768, 768], P('fsdp'), may hold values from -3.5 to 3.5
- cross_query: bfloat16 [768, 768], P('fsdp'), may hold values from -0.21875 to 0.21875
- cross_key: bfloat16 [768, 768], P('fsdp'), may hold values from -0.21875 to 0.21875
- cross_value: bfloat16 [768, 768], P('fsdp'), may hold values from -0.21875 to 0.21875
- cross_output: bfloat16 [768, 768], P('fsdp'), may hold values from -6 to 6
- gate_in: bfloat16 [768, 2048], P('fsdp'), may hold values from -0.21875 to 0.21875
- up_in: bfloat16 [768, 2048], P('fsdp'), may hold values from -0.21875 to 0.21875
- down_out: bfloat16 [2048, 768], P('fsdp'), may hold values from -0.125 to 0.125
- norm_self: bfloat16 [768], P('fsdp'), may hold values from 0.5 to 1.5
- norm_cross: bfloat16 [768], P('fsdp'), may hold values from 0.5 to 1.5
- norm_mlp: bfloat16 [768], P('fsdp'), may hold values from 0.5 to 1.5
- cotangent: bfloat16 [16, 2048, 768], P(('parts', 'fsdp'), 'ctx'), may hold values from -6 to 6
Outputs:
- layer_out: bfloat16 [16, 2048, 768], P(('parts', 'fsdp'), 'ctx')
- decoder_grad: float32 [16, 2048, 768], P(('parts', 'fsdp'), 'ctx')
- encoder_grad: float32 [16, 2048, 768], P(('parts', 'fsdp'), 'ctx')
- self_query_grad: float32 [768, 768], P('fsdp')
- self_key_grad: float32 [768, 768], P('fsdp')
- self_value_grad: float32 [768, 768], P('fsdp')
- self_output_grad: float32 [768, 768], P('fsdp')
- cross_query_grad: float32 [768, 768], P('fsdp')
- cross_key_grad: float32 [768, 768], P('fsdp')
- cross_value_grad: float32 [768, 768], P('fsdp')
- cross_output_grad: float32 [768, 768], P('fsdp')
- gate_in_grad: float32 [768, 2048], P('fsdp')
- up_in_grad: float32 [768, 2048], P('fsdp')
- down_out_grad: float32 [2048, 768], P('fsdp')
- norm_self_grad: float32 [768], P('fsdp')
- norm_cross_grad: float32 [768], P('fsdp')
- norm_mlp_grad: float32 [768], P('fsdp')
- rms_values: float32 [4], replicated
The draws below stay inside these ranges and needn't reach their ends.
All inputs are finite; a program needn't handle non-finite values.
Results may differ from the reference program's by a relative error of at most 0.04.
Values may be sent and summed in bfloat16 or wider, within the bound.
No kernel may reach another device: no remote copies, remote signals or barrier semaphores. Data moves between devices by JAX's collectives and lax.ppermute only.
A program may use at most 320 MiB of HBM per device.

```python
import math
import jax
import jax.numpy as jnp
import numpy as np
from jax import lax

D = 768
HEADS = 12
HEAD_DIM = 64
FF = 2048
ENC_LEN = 2048
GROUPS = 16
DEC = 2048
BLK = 512
CONT = 2
MOSTLEN = 1365
N_CTX = 2


def draw_decoder_in(key, part):
    base = jax.random.normal(key, (GROUPS, DEC, D), jnp.float32)
    place = (jnp.arange(GROUPS, dtype=jnp.float32)[:, None] * DEC + jnp.arange(DEC, dtype=jnp.float32)[None, :]) / (GROUPS * DEC)
    scale = jnp.sqrt(1.0 + 2.0 * place)
    common = jax.random.normal(jax.random.fold_in(key, 3), (GROUPS, 1, D), jnp.float32)
    reach = 3.0 * (CONT / DEC) ** 0.5
    strength = jax.random.uniform(jax.random.fold_in(key, 5), (GROUPS, 1, 1), jnp.float32, 0.0, reach)
    mixed = (base + strength * common) * scale[:, :, None]
    return jnp.clip(mixed, -10.0, 10.0).astype(jnp.bfloat16)


def with_ends(array, own_key, low, high):
    shape = array.shape
    index_at = [jax.random.randint(jax.random.fold_in(own_key, axis), (), 0, shape[axis]) for axis in range(len(shape))]
    array = array.at[tuple(index_at)].set(low)
    longest = shape.index(max(shape))
    index_at[longest] = (index_at[longest] + 1) % shape[longest]
    return array.at[tuple(index_at)].set(high)


def block_levels(own_key, extent, shards, smallest, high):
    level, own = 1.0, jax.random.fold_in(own_key, 6)
    for position, parts in shards:
        steps = jnp.exp(jax.random.uniform(jax.random.fold_in(own, position), (parts,), jnp.float32, smallest / len(shards), high / len(shards)))
        level = level * jnp.repeat(steps, extent[position] // parts).reshape([-1 if axis == position else 1 for axis in range(len(extent))])
    return level


def length_profile(count, total, limit, slope):
    portions = [(1 << 20) // math.isqrt(grade ** slope) + 1 for grade in range(2, count + 1)]
    spare, given = total - limit - (count - 1), [1] * (count - 1)
    while spare > 0:
        movable = [i for i in range(count - 1) if given[i] < limit]
        whole, left = sum([portions[i] for i in movable]), spare
        for i in movable:
            addition = min(limit - given[i], max(1, left * portions[i] // whole), spare)
            given[i] = given[i] + addition
            spare = spare - addition
    return np.array([limit] + given)


def ragged(rng, count, total, most, slope):
    if count == 2:
        one = jax.random.randint(rng, (), max(1, total - most), min(most, total - 1) + 1)
        return jnp.stack([one, total - one])
    sizes = jnp.asarray(length_profile(count, total, most, slope), jnp.int32)
    twos = (count - 1) // 2
    donor, sink = sizes[1:1 + 2 * twos:2], sizes[2:2 + 2 * twos:2]
    room = jnp.minimum(donor - 1, most - sink)
    shifted = jax.random.randint(jax.random.fold_in(rng, 1), (twos,), 0, 1 << 20) % (room + 1)
    sizes = sizes.at[1:1 + 2 * twos:2].set(donor - shifted).at[2:2 + 2 * twos:2].set(sink + shifted)
    return sizes[jax.random.permutation(jax.random.fold_in(rng, 2), count)]


def noise(own_key, extent, width, most, cuts=(), kind=jnp.bfloat16):
    values = width * jax.random.normal(own_key, extent, jnp.float32)
    if cuts:
        values = values * block_levels(own_key, extent, cuts, -0.22, 0.18)
    return jnp.clip(values, -most, most).astype(kind)


def setup_inputs(seed: int = 0) -> dict:
    key_list = jax.random.split(jax.random.key(seed), 21)
    decoder_in = draw_decoder_in(jax.random.fold_in(key_list[20], 71), 0)
    encoder_out = noise(key_list[1], (GROUPS, ENC_LEN, D), 1.0, 6.0, ((0, 16), (1, 2)))
    segment_ids = jax.vmap(lambda own: jnp.searchsorted(jnp.cumsum(ragged(own, CONT, DEC, MOSTLEN, 1)), jnp.arange(DEC), side="right"))(jax.random.split(key_list[2], GROUPS)).reshape((GROUPS, DEC)).astype(jnp.int32)
    block_order = jax.vmap(lambda own: jax.random.permutation(own, 2 * N_CTX))(jax.random.split(key_list[3], GROUPS)).reshape((GROUPS, 2 * N_CTX)).astype(jnp.int32)
    prompt_len = with_ends(jax.random.randint(key_list[4], (GROUPS,), ENC_LEN // 4, ENC_LEN + 1), jax.random.fold_in(key_list[4], 1), ENC_LEN // 4, ENC_LEN).astype(jnp.int32)
    self_query = noise(key_list[5], (D, D), D ** -0.5, 0.21875, ((0, 4),))
    self_key = noise(key_list[6], (D, D), D ** -0.5, 0.21875, ((0, 4),))
    self_value = noise(key_list[7], (D, D), D ** -0.5, 0.21875, ((0, 4),))
    self_output = noise(key_list[8], (D, D), (max(D * 8 // DEC, 1)) ** -0.5, 3.5, ((0, 4),))
    cross_query = noise(key_list[9], (D, D), D ** -0.5, 0.21875, ((0, 4),))
    cross_key = noise(key_list[10], (D, D), D ** -0.5, 0.21875, ((0, 4),))
    cross_value = noise(key_list[11], (D, D), D ** -0.5, 0.21875, ((0, 4),))
    cross_output = noise(key_list[12], (D, D), (max(D * 4 // ENC_LEN, 1)) ** -0.5, 6.0, ((0, 4),))
    gate_in = noise(key_list[13], (D, FF), D ** -0.5, 0.21875, ((0, 4),))
    up_in = noise(key_list[14], (D, FF), D ** -0.5, 0.21875, ((0, 4),))
    down_out = noise(key_list[15], (FF, D), FF ** -0.5, 0.125, ((0, 4),))
    norm_self = jnp.clip(1.0 + 0.1 * jax.random.normal(key_list[16], (D,), jnp.float32), 0.5, 1.5).astype(jnp.bfloat16)
    norm_cross = jnp.clip(1.0 + 0.1 * jax.random.normal(key_list[17], (D,), jnp.float32), 0.5, 1.5).astype(jnp.bfloat16)
    norm_mlp = jnp.clip(1.0 + 0.1 * jax.random.normal(key_list[18], (D,), jnp.float32), 0.5, 1.5).astype(jnp.bfloat16)
    cotangent = noise(key_list[19], (GROUPS, DEC, D), 1.0, 6.0, ((0, 16), (1, 2)))
    return dict(decoder_in=decoder_in, encoder_out=encoder_out, segment_ids=segment_ids, block_order=block_order, prompt_len=prompt_len, self_query=self_query, self_key=self_key, self_value=self_value, self_output=self_output, cross_query=cross_query, cross_key=cross_key, cross_value=cross_value, cross_output=cross_output, gate_in=gate_in, up_in=up_in, down_out=down_out, norm_self=norm_self, norm_cross=norm_cross, norm_mlp=norm_mlp, cotangent=cotangent)


@jax.custom_vjp
def low(v):
    return lax.optimization_barrier(v.astype(jnp.bfloat16)).astype(jnp.float32)

@jax.custom_vjp
def low_back(v):
    return v

def low_keep(v):
    return (low(v), None)

def low_pass(kept, grad):
    return (grad,)

def back_keep(v):
    return (v, None)

def back_low(kept, grad):
    return (low(grad),)
low.defvjp(low_keep, low_pass)
low_back.defvjp(back_keep, back_low)
HIGH = lax.Precision.HIGHEST
NEG = -1e+30
EPS = 1e-06
SCALE = 0.125

def matmul(left, right):
    return jnp.dot(left, right, precision=HIGH, preferred_element_type=jnp.float32)

def normed(value, gain):
    return value * lax.rsqrt(lax.optimization_barrier(jnp.mean(value * value, axis=-1, keepdims=True)) + EPS) * gain

def attend(query, keys, values, allowed):
    rows = query.shape[0]
    q_heads = query.reshape(rows, HEADS, HEAD_DIM)
    k_heads = keys.reshape(keys.shape[0], HEADS, HEAD_DIM)
    v_heads = values.reshape(values.shape[0], HEADS, HEAD_DIM)
    scores = jnp.einsum('qhd,khd->hqk', q_heads, k_heads, precision=HIGH) * SCALE
    scores = low_back(scores)
    scores = jnp.where(allowed[None], scores, NEG)
    probs = jax.nn.softmax(scores, axis=-1)
    mixed = jnp.einsum('hqk,khd->qhd', low(probs), v_heads, precision=HIGH)
    return low(low_back(mixed.reshape(rows, D)))

def by_blocks(function, *arrays):
    rows = arrays[0].shape[0]
    block = math.gcd(512, rows)
    shaped = tuple((item.reshape((rows // block, block) + item.shape[1:]) for item in arrays))
    result = lax.map(jax.checkpoint(function), shaped)
    return result.reshape((rows,) + result.shape[2:])

def group_forward(inputs, encoder, weights, pos_rows, seg_rows, valid):
    w_query, w_key, w_value, w_out, c_query, c_key, c_value, c_out, w_gate, w_up, w_down, g_self, g_cross, g_mlp = weights
    n_self = low(normed(inputs, g_self))
    query = low(low_back(matmul(n_self, w_query)))
    keys = low(low_back(matmul(n_self, w_key)))
    values = low(low_back(matmul(n_self, w_value)))

    def self_block(items):
        q_part, pos_part, seg_part = items
        allowed = (pos_rows[None, :] <= pos_part[:, None]) & (seg_rows[None, :] == seg_part[:, None])
        return attend(q_part, keys, values, allowed)
    mixed = by_blocks(self_block, query, pos_rows, seg_rows)
    branch_self = low_back(matmul(mixed, w_out))
    after_self = inputs + branch_self
    n_cross = low(normed(after_self, g_cross))
    cross_q = low(low_back(matmul(n_cross, c_query)))
    cross_k = low(low_back(matmul(encoder, c_key)))
    cross_v = low(low_back(matmul(encoder, c_value)))
    enc_allowed = jnp.arange(ENC_LEN, dtype=jnp.int32) < valid

    def cross_block(items):
        q_part = items[0]
        allowed = jnp.broadcast_to(enc_allowed[None, :], (q_part.shape[0], ENC_LEN))
        return attend(q_part, cross_k, cross_v, allowed)
    cross_mixed = by_blocks(cross_block, cross_q)
    branch_cross = low_back(matmul(cross_mixed, c_out))
    after_cross = after_self + branch_cross
    n_mlp = low(normed(after_cross, g_mlp))
    gate = low_back(matmul(n_mlp, w_gate))
    upward = low_back(matmul(n_mlp, w_up))
    hidden = low(jax.nn.gelu(gate, approximate=True) * upward)
    branch_mlp = low_back(matmul(hidden, w_down))
    result = after_cross + branch_mlp
    stats = jnp.stack([jnp.sum(inputs * inputs), jnp.sum(branch_self * branch_self), jnp.sum(branch_cross * branch_cross), jnp.sum(result * result)])
    return (result, stats)

def reference(decoder_in, encoder_out, segment_ids, block_order, prompt_len, self_query, self_key, self_value, self_output, cross_query, cross_key, cross_value, cross_output, gate_in, up_in, down_out, norm_self, norm_cross, norm_mlp, cotangent):
    weights = tuple((item.astype(jnp.float32) for item in (self_query, self_key, self_value, self_output, cross_query, cross_key, cross_value, cross_output, gate_in, up_in, down_out, norm_self, norm_cross, norm_mlp)))
    rows = jnp.arange(DEC, dtype=jnp.int32)

    def one_group(totals, items):
        inputs, encoder, segs, order, valid, grad_top = items
        pos_rows = (order[rows // BLK] * BLK + rows % BLK).astype(jnp.int32)
        seg_rows = segs[pos_rows]

        def forward(inputs_f, encoder_f, *params):
            return group_forward(inputs_f, encoder_f, params, pos_rows, seg_rows, valid)
        result, back, stats = jax.vjp(forward, inputs.astype(jnp.float32), encoder.astype(jnp.float32), *weights, has_aux=True)
        grads = back(grad_top.astype(jnp.float32))
        new_grads = tuple((total + grad for total, grad in zip(totals[0], grads[2:])))
        return ((new_grads, totals[1] + stats), (result.astype(jnp.bfloat16), grads[0], grads[1]))
    init = (tuple((jnp.zeros_like(item) for item in weights)), jnp.zeros((4,), jnp.float32))
    (wgrads, sums), (layer_out, decoder_grad, encoder_grad) = lax.scan(one_group, init, (decoder_in, encoder_out, segment_ids, block_order, prompt_len, cotangent))
    rms_values = jnp.sqrt(sums / (GROUPS * DEC * D))
    return (layer_out, decoder_grad, encoder_grad, wgrads[0], wgrads[1], wgrads[2], wgrads[3], wgrads[4], wgrads[5], wgrads[6], wgrads[7], wgrads[8], wgrads[9], wgrads[10], wgrads[11], wgrads[12], wgrads[13], rms_values)
```

```python
import functools
import math

import jax
import jax.numpy as jnp
from jax import lax
from jax.experimental import pallas as pl
from jax.experimental.pallas import tpu as pltpu
from jax.sharding import PartitionSpec as P

HEADS = 12
HEAD = 64
SCALE = 0.125
EPS = 1e-06
BIG = 1e30
LN2 = math.log(2.0)
QSCALE = SCALE * math.log2(math.e)
PART0 = 16
SEGS = 16
BF = jnp.bfloat16
F32 = jnp.float32
MIB = 1 << 20
ALL = ("fsdp", "parts", "ctx")


def nn(a, b):
    return lax.dot_general(a, b, (((1,), (0,)), ((), ())), preferred_element_type=F32)


def nt(a, b):
    return lax.dot_general(a, b, (((1,), (1,)), ((), ())), preferred_element_type=F32)


def tn(a, b):
    return lax.dot_general(a, b, (((0,), (0,)), ((), ())), preferred_element_type=F32)


def lanes(shape):
    return lax.broadcasted_iota(jnp.int32, shape, len(shape) - 1)


def params(mib):
    return pltpu.CompilerParams(vmem_limit_bytes=mib * MIB)


def cost(flops, moved, exps=0):
    return pl.CostEstimate(flops=int(flops), bytes_accessed=int(moved), transcendentals=int(exps))


def rms_scale(h):
    return lax.rsqrt(jnp.mean(h * h, axis=-1, keepdims=True) + EPS)


def norm_back(h, gain, dn):
    r = rms_scale(h)
    t = dn * gain
    hr = h * r
    dh = r * (t - hr * jnp.mean(t * hr, axis=-1, keepdims=True))
    return dh, jnp.sum(dn * hr, axis=0, keepdims=True)


def with_parts(base, value):
    spot = lanes(base.shape) % HEAD
    hi = value.astype(BF)
    rest = value - hi.astype(F32)
    mid = rest.astype(BF)
    low = (rest - mid.astype(F32)).astype(BF)
    return jnp.where(
        spot == PART0, hi, jnp.where(spot == PART0 + 1, mid, jnp.where(spot == PART0 + 2, low, base))
    )


def pair_of(own, other):
    left = lanes(own.shape) < HEAD
    return jnp.where(left, own, other), jnp.where(left, other, own)


def forward_block(lo, n, diag, q_ref, qa_ref, kx, vx, o_ref, lse_ref, chunk):
    q = q_ref[...]
    rows = q.shape[0]
    left = lanes(q.shape) < HEAD
    sides = pair_of(q, qa_ref[...])
    scores, tops, accs = [], [], []
    for h in range(2):
        found = []
        for c in range(0, n, chunk):
            s = nt(sides[h], kx[h, pl.ds(lo + c, chunk), :])
            if diag and c + chunk > n - rows:
                r = lax.broadcasted_iota(jnp.int32, s.shape, 0) + (n - rows - c)
                s = jnp.where(lanes(s.shape) <= r, s, -BIG)
            found.append(s)
        scores.append(found)
    for h in range(2):
        top = functools.reduce(jnp.maximum, [jnp.max(s, axis=1, keepdims=True) for s in scores[h]])
        acc = None
        for i, s in enumerate(scores[h]):
            p = jnp.exp2(s - top).astype(BF)
            term = nn(p, vx[h, pl.ds(lo + i * chunk, chunk), :])
            acc = term if acc is None else acc + term
        accs.append(acc)
        tops.append(top)
    wide = jnp.where(left, accs[0], accs[1])
    total = jnp.where(left, accs[1], accs[0])
    o_ref[...] = (wide / pltpu.roll(total, HEAD, 1)).astype(o_ref.dtype)
    lse_ref[...] = jnp.where(left, tops[1], tops[0]) + jnp.log2(total)


def forward_prep(k_ref, v_ref, ka_ref, kx, vx):
    kx[0], kx[1] = pair_of(k_ref[...], ka_ref[...])
    v = v_ref[...]
    vx[0], vx[1] = pair_of(v, jnp.ones_like(v))


def backward_prep(k_ref, v_ref, ka_ref, kx, vx, km, dk_acc, dv_acc):
    k, v = k_ref[...], v_ref[...]
    spot = lanes(v.shape) % HEAD
    neg = jnp.where((spot >= PART0) & (spot < PART0 + 3), -1.0, 0.0).astype(BF)
    kx[0], kx[1] = pair_of(k, ka_ref[...])
    vx[0], vx[1] = pair_of(v, neg)
    km[0], km[1] = pair_of(k, jnp.zeros_like(k))
    dk_acc[...] = jnp.zeros_like(dk_acc)
    dv_acc[...] = jnp.zeros_like(dv_acc)


def backward_block(
    lo, n, diag, q_ref, do_ref, o_ref, lse_ref, qa_ref, kx, vx, km, dq_ref, dk_acc, dv_acc, chunk
):
    q, do = q_ref[...], do_ref[...]
    rows = q.shape[0]
    left = lanes(q.shape) < HEAD
    product = do.astype(F32) * o_ref[...].astype(F32)
    first = jnp.sum(jnp.where(left, product, 0.0), axis=1, keepdims=True)
    second = jnp.sum(jnp.where(left, 0.0, product), axis=1, keepdims=True)
    delta = jnp.where(left, second, first)
    zero = jnp.zeros_like(q)
    qx = pair_of(q, with_parts(qa_ref[...], lse_ref[...]))
    dx = pair_of(do, with_parts(zero, delta))
    qm = pair_of(q, zero)
    dm = pair_of(do, zero)
    dq = None
    for c in range(0, n, chunk):
        at = pl.ds(lo + c, chunk)
        dk = dv = None
        for h in range(2):
            st = nt(kx[h, at, :], qx[h])
            if diag and c + chunk > n - rows:
                r = lax.broadcasted_iota(jnp.int32, st.shape, 0) + (c - (n - rows))
                st = jnp.where(r <= lanes(st.shape), st, -BIG)
            pt = jnp.exp2(st)
            dp = nt(vx[h, at, :], dx[h])
            ds = (pt * dp).astype(BF)
            tv, tk, tq = nn(pt.astype(BF), dm[h]), nn(ds, qm[h]), tn(ds, km[h, at, :])
            dv = tv if dv is None else dv + tv
            dk = tk if dk is None else dk + tk
            dq = tq if dq is None else dq + tq
        dv_acc[at, :] += dv
        dk_acc[at, :] += dk
    dq_ref[...] = (dq * SCALE).astype(dq_ref.dtype)


def cross_forward_kernel(q_ref, k_ref, v_ref, qa_ref, ka_ref, o_ref, lse_ref, kx, vx):
    @pl.when(pl.program_id(1) == 0)
    def _():
        forward_prep(k_ref, v_ref, ka_ref, kx, vx)

    keys = k_ref.shape[0]
    forward_block(0, keys, False, q_ref, qa_ref, kx, vx, o_ref, lse_ref, math.gcd(512, keys))


def cross_forward(q, kv, qa, ka):
    rows, width = q.shape
    keys = kv.shape[0]
    block = min(512, rows)
    pairs = width // 128
    row = pl.BlockSpec((block, 128), lambda h, i: (i, h))
    return pl.pallas_call(
        cross_forward_kernel,
        grid=(pairs, rows // block),
        in_specs=[
            row,
            pl.BlockSpec((keys, 128), lambda h, i: (0, h)),
            pl.BlockSpec((keys, 128), lambda h, i: (0, h + pairs)),
            pl.BlockSpec((block, 128), lambda h, i: (i, 0)),
            pl.BlockSpec((keys, 128), lambda h, i: (0, 0)),
        ],
        out_specs=[row, row],
        out_shape=[
            jax.ShapeDtypeStruct((rows, width), BF),
            jax.ShapeDtypeStruct((rows, width), F32),
        ],
        scratch_shapes=[pltpu.VMEM((2, keys, 128), BF)] * 2,
        compiler_params=params(48),
        cost_estimate=cost(16 * rows * keys * width, 8 * rows * width, rows * keys * 12),
        name="cross_forward",
    )(q, kv, kv, qa, ka)


def cross_backward_kernel(
    q_ref, k_ref, v_ref, do_ref, o_ref, lse_ref, qa_ref, ka_ref,
    dq_ref, dk_ref, dv_ref, kx, vx, km, dk_acc, dv_acc,
):
    @pl.when(pl.program_id(1) == 0)
    def _():
        backward_prep(k_ref, v_ref, ka_ref, kx, vx, km, dk_acc, dv_acc)

    keys = k_ref.shape[0]
    backward_block(
        0, keys, False, q_ref, do_ref, o_ref, lse_ref, qa_ref, kx, vx, km,
        dq_ref, dk_acc, dv_acc, math.gcd(512, keys),
    )

    @pl.when(pl.program_id(1) == pl.num_programs(1) - 1)
    def _():
        dk_ref[...] = (dk_acc[...] * LN2).astype(BF)
        dv_ref[...] = dv_acc[...].astype(BF)


def cross_backward(q, kv, do, o, lse, qa, ka):
    rows, width = q.shape
    keys = kv.shape[0]
    block = min(512, rows)
    pairs = width // 128
    row = pl.BlockSpec((block, 128), lambda h, i: (i, h))
    col = pl.BlockSpec((keys, 128), lambda h, i: (0, h))
    return pl.pallas_call(
        cross_backward_kernel,
        grid=(pairs, rows // block),
        in_specs=[
            row,
            col,
            pl.BlockSpec((keys, 128), lambda h, i: (0, h + pairs)),
            row,
            row,
            row,
            pl.BlockSpec((block, 128), lambda h, i: (i, 0)),
            pl.BlockSpec((keys, 128), lambda h, i: (0, 0)),
        ],
        out_specs=[row, col, col],
        out_shape=[
            jax.ShapeDtypeStruct((rows, width), BF),
            jax.ShapeDtypeStruct((keys, width), BF),
            jax.ShapeDtypeStruct((keys, width), BF),
        ],
        scratch_shapes=[pltpu.VMEM((2, keys, 128), BF)] * 3 + [pltpu.VMEM((keys, 128), F32)] * 2,
        compiler_params=params(48),
        cost_estimate=cost(40 * rows * keys * width, 12 * rows * width, rows * keys * 12),
        name="cross_backward",
    )(q, kv, kv, do, o, lse, qa, ka)


def counts_for(blocks, least):
    return list(range(least, min(blocks, 8) + 1))


def grain_of(block):
    return min(256, block)


def needed_blocks(segs, block):
    total = segs.shape[0]
    grain = grain_of(block)
    first = segs.reshape(total // block, block)[:, 0]
    start = jnp.sum((segs[None, :] < first[:, None]).astype(jnp.int32), axis=1)
    ends = (jnp.arange(total // block, dtype=jnp.int32) + 1) * block
    need = (ends - start // grain * grain) // grain
    return jnp.minimum(need, counts_for(total // grain, block // grain)[-1])


def self_forward_kernel(
    count_ref, slot_ref, q_ref, k_ref, v_ref, qa_ref, ka_ref, o_ref, lse_ref, kx, vx
):
    i = pl.program_id(1)
    block = q_ref.shape[0]
    grain = grain_of(block)

    @pl.when(i == 0)
    def _():
        forward_prep(k_ref, v_ref, ka_ref, kx, vx)

    for n in counts_for(k_ref.shape[0] // grain, block // grain):

        @pl.when(count_ref[i] == n)
        def _():
            lo = pl.multiple_of((i + 1) * block - n * grain, grain)
            forward_block(lo, n * grain, True, q_ref, qa_ref, kx, vx, o_ref, lse_ref, grain)


def self_specs(block, total):
    row = pl.BlockSpec((block, 128), lambda h, i, n, s: (i, h))
    col = pl.BlockSpec((total, 128), lambda h, i, n, s: (0, h))
    dealt = pl.BlockSpec((block, 128), lambda h, i, n, s: (s[i], h))
    qa = pl.BlockSpec((block, 128), lambda h, i, n, s: (i, 0))
    ka = pl.BlockSpec((total, 128), lambda h, i, n, s: (0, 0))
    return row, col, dealt, qa, ka


def self_forward(counts, slots, q, k, v, qa, ka, block):
    total, width = q.shape
    row, col, dealt, qas, kas = self_specs(block, total)
    return pl.pallas_call(
        self_forward_kernel,
        grid_spec=pltpu.PrefetchScalarGridSpec(
            num_scalar_prefetch=2,
            grid=(width // 128, total // block),
            in_specs=[row, col, col, qas, kas],
            out_specs=[dealt, row],
            scratch_shapes=[pltpu.VMEM((2, total, 128), BF)] * 2,
        ),
        out_shape=[
            jax.ShapeDtypeStruct((total, width), BF),
            jax.ShapeDtypeStruct((total, width), F32),
        ],
        compiler_params=params(48),
        cost_estimate=cost(8 * total * total * width, 8 * total * width, total * total * 3),
        name="self_forward",
    )(counts, slots, q, k, v, qa, ka)


def self_backward_kernel(
    count_ref, slot_ref, q_ref, k_ref, v_ref, do_ref, o_ref, lse_ref, qa_ref, ka_ref,
    dq_ref, dk_ref, dv_ref, kx, vx, km, dk_acc, dv_acc,
):
    i = pl.program_id(1)
    block = q_ref.shape[0]
    grain = grain_of(block)

    @pl.when(i == 0)
    def _():
        backward_prep(k_ref, v_ref, ka_ref, kx, vx, km, dk_acc, dv_acc)

    for n in counts_for(k_ref.shape[0] // grain, block // grain):

        @pl.when(count_ref[i] == n)
        def _():
            lo = pl.multiple_of((i + 1) * block - n * grain, grain)
            backward_block(
                lo, n * grain, True, q_ref, do_ref, o_ref, lse_ref, qa_ref, kx, vx, km,
                dq_ref, dk_acc, dv_acc, grain,
            )

    @pl.when(i == pl.num_programs(1) - 1)
    def _():
        dk_ref[...] = (dk_acc[...] * LN2).astype(BF)
        dv_ref[...] = dv_acc[...].astype(BF)


def self_backward(counts, slots, q, k, v, do, o, lse, qa, ka, block):
    total, width = q.shape
    row, col, dealt, qas, kas = self_specs(block, total)
    return pl.pallas_call(
        self_backward_kernel,
        grid_spec=pltpu.PrefetchScalarGridSpec(
            num_scalar_prefetch=2,
            grid=(width // 128, total // block),
            in_specs=[row, col, col, dealt, dealt, row, qas, kas],
            out_specs=[row, col, col],
            scratch_shapes=[pltpu.VMEM((2, total, 128), BF)] * 3
            + [pltpu.VMEM((total, 128), F32)] * 2,
        ),
        out_shape=[jax.ShapeDtypeStruct((total, width), BF)] * 3,
        compiler_params=params(48),
        cost_estimate=cost(20 * total * total * width, 12 * total * width, total * total * 3),
        name="self_backward",
    )(counts, slots, q, k, v, do, o, lse, qa, ka)


def qkv_kernel(order_ref, x_ref, g_ref, w_ref, n_ref, q_ref, k_ref, v_ref):
    x = x_ref[...].astype(F32)
    n = (x * rms_scale(x) * g_ref[...]).astype(BF)
    n_ref[...] = n
    width = q_ref.shape[1]
    out = nn(n, w_ref[...])
    q_ref[...] = (out[:, :width] * QSCALE).astype(BF)
    k_ref[...] = out[:, width : 2 * width].astype(BF)
    v_ref[...] = out[:, 2 * width :].astype(BF)


def qkv_forward(order, x, gain, w, block):
    total, dim = x.shape
    width = w.shape[1] // 3
    here = lambda i, o: (o[i], 0)
    whole = lambda i, o: (0, 0)
    return pl.pallas_call(
        qkv_kernel,
        grid_spec=pltpu.PrefetchScalarGridSpec(
            num_scalar_prefetch=1,
            grid=(total // block,),
            in_specs=[
                pl.BlockSpec((block, dim), lambda i, o: (i, 0)),
                pl.BlockSpec((1, dim), whole),
                pl.BlockSpec(w.shape, whole),
            ],
            out_specs=[pl.BlockSpec((block, dim), here)] + [pl.BlockSpec((block, width), here)] * 3,
        ),
        out_shape=[jax.ShapeDtypeStruct((total, dim), BF)]
        + [jax.ShapeDtypeStruct((total, width), BF)] * 3,
        compiler_params=params(48),
        cost_estimate=cost(6 * total * dim * width, 8 * total * dim),
        name="qkv_forward",
    )(order, x, gain, w)


def after_self_kernel(x_ref, o_ref, wo_ref, g_ref, wq_ref, h_ref, n_ref, q_ref, s_ref):
    x = x_ref[...].astype(F32)
    a = nn(o_ref[...], wo_ref[...])
    h = x + a
    h_ref[...] = h
    n = (h * rms_scale(h) * g_ref[...]).astype(BF)
    n_ref[...] = n
    q_ref[...] = (nn(n, wq_ref[...]) * QSCALE).astype(BF)

    @pl.when(pl.program_id(0) == 0)
    def _():
        s_ref[...] = jnp.zeros_like(s_ref)

    s_ref[0:1, :] += jnp.sum(x * x, axis=0, keepdims=True)
    s_ref[1:2, :] += jnp.sum(a * a, axis=0, keepdims=True)


def after_self(x, o, wo, gain, w2):
    rows, dim = x.shape
    block = min(256, rows)
    line = lambda i: (i, 0)
    whole = lambda i: (0, 0)
    return pl.pallas_call(
        after_self_kernel,
        grid=(rows // block,),
        in_specs=[
            pl.BlockSpec((block, dim), line),
            pl.BlockSpec((block, o.shape[1]), line),
            pl.BlockSpec(wo.shape, whole),
            pl.BlockSpec((1, dim), whole),
            pl.BlockSpec((dim, dim), lambda i: (0, 1)),
        ],
        out_specs=[
            pl.BlockSpec((block, dim), line),
            pl.BlockSpec((block, dim), line),
            pl.BlockSpec((block, dim), line),
            pl.BlockSpec((8, dim), whole),
        ],
        out_shape=[
            jax.ShapeDtypeStruct((rows, dim), F32),
            jax.ShapeDtypeStruct((rows, dim), BF),
            jax.ShapeDtypeStruct((rows, dim), BF),
            jax.ShapeDtypeStruct((8, dim), F32),
        ],
        compiler_params=params(48),
        cost_estimate=cost(4 * rows * dim * dim, 14 * rows * dim),
        name="after_self",
    )(x, o, wo, gain, w2)


GELU_C = math.sqrt(2.0 / math.pi)
GELU_A = 0.044715


def mlp_kernel(
    o_ref, h1_ref, wc_ref, g_ref, t_ref, wg_ref, wu_ref, wd_ref,
    y_ref, dh_ref, do_ref, gu_ref, gd_ref, gc_ref, s_ref,
    n_scr, h_scr, m_scr, dn_scr, hid_scr, du_scr, dw_scr,
):
    j = pl.program_id(0)
    rows = o_ref.shape[0]
    step = min(256, rows)
    spans = [pl.ds(r, step) for r in range(0, rows, step)]
    gain = g_ref[...]

    @pl.when(j == 0)
    def _():
        total = None
        for at in spans:
            c = nn(o_ref[at, :], wc_ref[...])
            h = h1_ref[at, :] + c
            h_scr[at, :] = h
            n_scr[at, :] = (h * rms_scale(h) * gain).astype(BF)
            part = jnp.sum(c * c, axis=0, keepdims=True)
            total = part if total is None else total + part
        s_ref[...] = jnp.zeros_like(s_ref)
        s_ref[0:1, :] = total
        m_scr[...] = jnp.zeros_like(m_scr)
        dn_scr[...] = jnp.zeros_like(dn_scr)

    wg, wu, wd = wg_ref[...], wu_ref[...], wd_ref[...]
    width = wg.shape[1]
    for at in spans:
        n = n_scr[at, :]
        u = nn(n, wg)
        w = nn(n, wu)
        dhid = nt(t_ref[at, :], wd)
        square = u * u
        th = jnp.tanh(GELU_C * u * (1.0 + GELU_A * square))
        half = 0.5 * (1.0 + th)
        gel = u * half
        slope = half + 0.5 * u * (1.0 - th * th) * (GELU_C * (1.0 + 3.0 * GELU_A * square))
        hid = (gel * w).astype(BF)
        du = (dhid * w * slope).astype(BF)
        dw = (dhid * gel).astype(BF)
        hid_scr[at, :] = hid
        du_scr[at, :] = du
        dw_scr[at, :] = dw
        m_scr[at, :] += nn(hid, wd)
        dn_scr[at, :] += nt(du, wg) + nt(dw, wu)
    gd_ref[...] = tn(hid_scr[...], t_ref[...]).astype(BF)
    gu_ref[:, :width] = tn(n_scr[...], du_scr[...]).astype(BF)
    gu_ref[:, width:] = tn(n_scr[...], dw_scr[...]).astype(BF)

    @pl.when(j == pl.num_programs(0) - 1)
    def _():
        total = gains = None
        for at in spans:
            h = h_scr[at, :]
            y = h + m_scr[at, :]
            y_ref[at, :] = y.astype(BF)
            dh, dg = norm_back(h, gain, dn_scr[at, :])
            dh = dh + t_ref[at, :].astype(F32)
            dh_ref[at, :] = dh
            dc = dh.astype(BF)
            n_scr[at, :] = dc
            do_ref[at, :] = nt(dc, wc_ref[...]).astype(BF)
            part = jnp.sum(y * y, axis=0, keepdims=True)
            total = part if total is None else total + part
            gains = dg if gains is None else gains + dg
        gc_ref[...] = tn(o_ref[...], n_scr[...]).astype(BF)
        s_ref[1:2, :] = total
        s_ref[2:3, :] = gains


def feed_forward(o, h1, w2, gain, cot, w3, wd):
    rows, dim = o.shape
    hidden = wd.shape[0]
    width = 512
    steps = hidden // width
    whole = lambda j: (0, 0)
    once = pl.Buffered(1)
    full = pl.BlockSpec((rows, dim), whole, pipeline_mode=once)
    return pl.pallas_call(
        mlp_kernel,
        grid=(steps,),
        in_specs=[
            full,
            full,
            pl.BlockSpec((dim, dim), lambda j: (0, 4), pipeline_mode=once),
            pl.BlockSpec((1, dim), whole),
            full,
            pl.BlockSpec((dim, width), lambda j: (0, j)),
            pl.BlockSpec((dim, width), lambda j: (0, j + steps)),
            pl.BlockSpec((width, dim), lambda j: (j, 0)),
        ],
        out_specs=[
            full,
            full,
            full,
            pl.BlockSpec((dim, 2 * width), lambda j: (0, j)),
            pl.BlockSpec((width, dim), lambda j: (j, 0)),
            pl.BlockSpec((dim, dim), whole, pipeline_mode=once),
            pl.BlockSpec((8, dim), whole),
        ],
        out_shape=[
            jax.ShapeDtypeStruct((rows, dim), BF),
            jax.ShapeDtypeStruct((rows, dim), F32),
            jax.ShapeDtypeStruct((rows, dim), BF),
            jax.ShapeDtypeStruct((dim, 2 * hidden), BF),
            jax.ShapeDtypeStruct((hidden, dim), BF),
            jax.ShapeDtypeStruct((dim, dim), BF),
            jax.ShapeDtypeStruct((8, dim), F32),
        ],
        scratch_shapes=[
            pltpu.VMEM((rows, dim), BF),
            pltpu.VMEM((rows, dim), F32),
            pltpu.VMEM((rows, dim), F32),
            pltpu.VMEM((rows, dim), F32),
            pltpu.VMEM((rows, width), BF),
            pltpu.VMEM((rows, width), BF),
            pltpu.VMEM((rows, width), BF),
        ],
        compiler_params=params(60),
        cost_estimate=cost(18 * rows * dim * hidden + 6 * rows * dim * dim, 40 * MIB, rows * hidden),
        name="feed_forward",
    )(o, h1, w2, gain, cot, w3, w3, wd)


def before_self_kernel(
    dq_ref, wq_ref, h_ref, dh_ref, g_ref, wo_ref, d1_ref, da_ref, do_ref, s_ref
):
    dn = nt(dq_ref[...], wq_ref[...])
    dh, dg = norm_back(h_ref[...], g_ref[...], dn)
    d1 = dh_ref[...] + dh
    d1_ref[...] = d1
    da = d1.astype(BF)
    da_ref[...] = da
    do_ref[...] = nt(da, wo_ref[...]).astype(BF)

    @pl.when(pl.program_id(0) == 0)
    def _():
        s_ref[...] = jnp.zeros_like(s_ref)

    s_ref[0:1, :] += dg


def before_self(dq, w2, h1, dh2, gain, wo):
    rows, dim = dq.shape
    block = min(256, rows)
    line = lambda i: (i, 0)
    whole = lambda i: (0, 0)
    row = pl.BlockSpec((block, dim), line)
    return pl.pallas_call(
        before_self_kernel,
        grid=(rows // block,),
        in_specs=[
            row,
            pl.BlockSpec((dim, dim), lambda i: (0, 1)),
            row,
            row,
            pl.BlockSpec((1, dim), whole),
            pl.BlockSpec(wo.shape, whole),
        ],
        out_specs=[
            row,
            row,
            pl.BlockSpec((block, wo.shape[0]), line),
            pl.BlockSpec((8, dim), whole),
        ],
        out_shape=[
            jax.ShapeDtypeStruct((rows, dim), F32),
            jax.ShapeDtypeStruct((rows, dim), BF),
            jax.ShapeDtypeStruct((rows, wo.shape[0]), BF),
            jax.ShapeDtypeStruct((8, dim), F32),
        ],
        compiler_params=params(48),
        cost_estimate=cost(4 * rows * dim * dim, 18 * rows * dim),
        name="before_self",
    )(dq, w2, h1, dh2, gain, wo)


def qkv_back_kernel(slot_ref, dq_ref, dk_ref, dv_ref, w_ref, n_ref, x_ref, dn_ref, g_ref, acc, s_acc):
    i = pl.program_id(0)
    d = jnp.concatenate([dq_ref[...], dk_ref[...], dv_ref[...]], axis=1)
    dn = nt(d, w_ref[...])
    dn_ref[...] = dn.astype(BF)
    x = x_ref[...].astype(F32)
    dg = jnp.sum(dn * (x * rms_scale(x)), axis=0, keepdims=True)
    term = tn(n_ref[...], d)

    @pl.when(i == 0)
    def _():
        acc[...] = term
        s_acc[...] = jnp.zeros_like(s_acc)
        s_acc[0:1, :] = dg

    @pl.when(i > 0)
    def _():
        acc[...] += term
        s_acc[0:1, :] += dg

    @pl.when(i == pl.num_programs(0) - 1)
    def _():
        width = acc.shape[1]
        g_ref[:, :width] = acc[...].astype(BF)
        g_ref[:, width:] = jnp.broadcast_to(s_acc[0:1, :], (128, s_acc.shape[1])).T.astype(BF)


def qkv_backward(slots, dq, dk, dv, w, n, x, block):
    total, width = dq.shape
    dim = n.shape[1]
    row = pl.BlockSpec((block, width), lambda i, s: (i, 0))
    dealt = pl.BlockSpec((block, dim), lambda i, s: (s[i], 0))
    whole = lambda i, s: (0, 0)
    return pl.pallas_call(
        qkv_back_kernel,
        grid_spec=pltpu.PrefetchScalarGridSpec(
            num_scalar_prefetch=1,
            grid=(total // block,),
            in_specs=[
                row,
                row,
                row,
                pl.BlockSpec(w.shape, whole),
                pl.BlockSpec((block, dim), lambda i, s: (i, 0)),
                dealt,
            ],
            out_specs=[dealt, pl.BlockSpec((dim, 3 * width + 128), whole)],
            scratch_shapes=[pltpu.VMEM((dim, 3 * width), F32), pltpu.VMEM((8, dim), F32)],
        ),
        out_shape=[
            jax.ShapeDtypeStruct((total, dim), BF),
            jax.ShapeDtypeStruct((dim, 3 * width + 128), BF),
        ],
        compiler_params=params(48),
        cost_estimate=cost(12 * total * dim * width, 10 * total * dim),
        name="qkv_backward",
    )(slots, dq, dk, dv, w, n, x)


def turned(n, k):
    return [(i, (i + k) % n) for i in range(n)]


def rows_of(array, index, count):
    size = array.shape[0] // count
    return lax.dynamic_slice_in_dim(array, index * size, size, 0)


def assemble_kernel(place_ref, near_ref, far_ref, w_ref):
    z, core = place_ref[0], place_ref[1]
    count, size = near_ref.shape[0], near_ref.shape[1]
    for d in range(count):
        base = lax.rem(z - d + count, count) * (2 * size)
        w_ref[pl.ds(pl.multiple_of(base + core * size, 16), size), :] = near_ref[d]
        w_ref[pl.ds(pl.multiple_of(base + (1 - core) * size, 16), size), :] = far_ref[d]


def gather_first(own, z, part, n_fsdp, n_parts):
    size = own.shape[0] // 2
    if n_parts % 2 or size % 16:
        return lax.all_gather(own, "fsdp", axis=0, tiled=True)
    core = part % 2
    mine = lax.dynamic_slice_in_dim(own, core * size, size, 0)
    near = jnp.stack(
        [mine] + [lax.ppermute(mine, "fsdp", turned(n_fsdp, d)) for d in range(1, n_fsdp)]
    )
    far = lax.ppermute(near, "parts", [(i, i ^ 1) for i in range(n_parts)])
    return pl.pallas_call(
        assemble_kernel,
        in_specs=[
            pl.BlockSpec(memory_space=pltpu.SMEM),
            pl.BlockSpec(memory_space=pltpu.VMEM),
            pl.BlockSpec(memory_space=pltpu.VMEM),
        ],
        out_specs=pl.BlockSpec(memory_space=pltpu.VMEM),
        out_shape=jax.ShapeDtypeStruct((n_fsdp * own.shape[0], own.shape[1]), BF),
        compiler_params=params(32),
        name="assemble",
    )(jnp.stack([z, core]).astype(jnp.int32), near, far)


def sum_everywhere(value, sizes):
    for axis, size in sizes:
        bit = 1
        while bit < size:
            value = value + lax.ppermute(value, axis, [(i, i ^ bit) for i in range(size)])
            bit *= 2
    return value


def scatter_sum(grad):
    part = lax.psum_scatter(grad, ALL, scatter_dimension=0, tiled=True)
    return lax.all_gather(part, ("parts", "ctx"), axis=0, tiled=True)


def local(
    mesh_shape,
    decoder_in,
    encoder_out,
    segment_ids,
    block_order,
    prompt_len,
    self_query,
    self_key,
    self_value,
    self_output,
    cross_query,
    cross_key,
    cross_value,
    cross_output,
    gate_in,
    up_in,
    down_out,
    norm_self,
    norm_cross,
    norm_mlp,
    cotangent,
):
    n_parts, n_ctx, n_fsdp = mesh_shape
    part, place, z = lax.axis_index("parts"), lax.axis_index("ctx"), lax.axis_index("fsdp")
    plane, n_plane = part * n_ctx + place, n_parts * n_ctx
    x_own, enc_own = decoder_in[0], encoder_out[0]
    rows, dim = x_own.shape
    segs, order = segment_ids[0], block_order[0]
    total = segs.shape[0]
    slots_total = order.shape[0]
    block = total // slots_total
    per_dev = slots_total // n_ctx
    enc_rows = enc_own.shape[0]
    keys = enc_rows * n_ctx
    hidden = down_out.shape[0] * n_fsdp
    heads_here = 2 * -(-HEADS // (2 * n_ctx))
    width = heads_here * HEAD
    padded = width * n_ctx

    ring = (place + jnp.arange(n_ctx, dtype=jnp.int32)) % n_ctx
    order_here = jnp.roll(order, -per_dev * place)
    slots = jnp.argsort(order_here).astype(jnp.int32)
    counts = needed_blocks(segs, block)

    def gather_ctx(value):
        pieces = [value] + [lax.ppermute(value, "ctx", turned(n_ctx, -k)) for k in range(1, n_ctx)]
        return jnp.concatenate(pieces, axis=0)

    x_all = gather_ctx(x_own)

    def own_heads(w):
        w = jnp.pad(w, ((0, 0), (0, padded - dim)))
        return lax.dynamic_slice_in_dim(w, place * width, width, 1)

    w1 = gather_first(
        jnp.concatenate([own_heads(self_query), own_heads(self_key), own_heads(self_value)], axis=1),
        z, part, n_fsdp, n_parts,
    )
    gains = lax.all_gather(
        jnp.stack([norm_self, norm_cross, norm_mlp], axis=1), "fsdp", axis=0, tiled=True
    ).astype(F32)
    gain_self, gain_cross, gain_mlp = (gains[:, i][None] for i in range(3))
    w2 = lax.all_gather(
        jnp.concatenate(
            [
                rows_of(w, plane, n_plane)
                for w in (self_output, cross_query, cross_key, cross_value, cross_output)
            ],
            axis=1,
        ),
        ALL, axis=0, tiled=True,
    )
    enc_all = gather_ctx(enc_own)
    w3 = lax.all_gather(
        jnp.concatenate([rows_of(gate_in, plane, n_plane), rows_of(up_in, plane, n_plane)], axis=1),
        ALL, axis=0, tiled=True,
    )
    wd = lax.all_gather(rows_of(down_out, plane, n_plane), ALL, axis=0, tiled=True)

    n1, q, k, v = qkv_forward(order_here, x_all, gain_self, w1, block)
    spot = jnp.arange(128, dtype=jnp.int32)[None, :] % HEAD
    minus = jnp.where((spot >= PART0) & (spot < PART0 + 3), -1.0, 0.0)
    seg_q = jnp.where(spot == segs[:, None], 1.0, 0.0).astype(BF)
    seg_k = jnp.where((spot < SEGS) & (spot != segs[:, None]), -BIG, minus).astype(BF)
    o1, lse1 = self_forward(counts, slots, q, k, v, seg_q, seg_k, block)
    pieces = [
        lax.ppermute(o1[i * rows : (i + 1) * rows], "ctx", turned(n_ctx, i)) if i else o1[:rows]
        for i in range(n_ctx)
    ]
    o_cat = jnp.concatenate(pieces, axis=1)
    turn = (place - jnp.arange(n_ctx, dtype=jnp.int32)) % n_ctx
    wo = jnp.pad(w2[:, :dim], ((0, padded - dim), (0, 0))).reshape(n_ctx, width, dim)
    wo = jnp.take(wo, turn, axis=0).reshape(padded, dim)
    h1, n2, q2, stat1 = after_self(x_own, o_cat, wo, gain_cross, w2)

    w_kv = w2[:, 2 * dim : 4 * dim]
    kv2 = nn(enc_all, w_kv).astype(BF)
    where_key = (ring[:, None] * enc_rows + jnp.arange(enc_rows, dtype=jnp.int32)).reshape(-1, 1)
    len_q = jnp.where(spot == 0, jnp.ones((rows, 1), F32), 0.0).astype(BF)
    len_k = jnp.where((spot == 0) & (where_key >= prompt_len[0]), -BIG, minus).astype(BF)
    o2, lse2 = cross_forward(q2, kv2, len_q, len_k)

    layer_out, dh2, do2, g_gu, g_down, g_co, stat2 = feed_forward(
        o2, h1, w2, gain_mlp, cotangent[0], w3, wd
    )
    sum_gu = scatter_sum(g_gu)
    sum_down = scatter_sum(g_down)

    dq2, dk2, dv2 = cross_backward(q2, kv2, do2, o2, lse2, len_q, len_k)
    dh1, da, do1, stat3 = before_self(dq2, w2, h1, dh2, gain_cross, wo)
    do_pieces = [
        lax.ppermute(do1[:, i * width : (i + 1) * width], "ctx", turned(n_ctx, -i))
        if i
        else do1[:, :width]
        for i in range(n_ctx)
    ]
    do_all = jnp.concatenate(do_pieces, axis=0)
    g_cq = tn(n2, dq2)
    g_wo = tn(o_cat, da).reshape(n_ctx, width, dim)
    g_wo = jnp.take(g_wo, turn, axis=0).reshape(padded, dim)[:dim]
    g_ck, g_cv = tn(enc_all, dk2), tn(enc_all, dv2)
    sum_mid = scatter_sum(
        jnp.concatenate([g.astype(BF) for g in (g_wo, g_cq, g_ck, g_cv, g_co)], axis=1)
    )
    d_enc = nt(dk2, w2[:, 2 * dim : 3 * dim]) + nt(dv2, w2[:, 3 * dim : 4 * dim])
    enc_grad = d_enc[:enc_rows]
    for i in range(1, n_ctx):
        piece = d_enc[i * enc_rows : (i + 1) * enc_rows].astype(BF)
        enc_grad = enc_grad + lax.ppermute(piece, "ctx", turned(n_ctx, i)).astype(F32)

    small = jnp.concatenate([stat1[:2], stat2[:3], stat3[:1], jnp.zeros((2, dim), F32)], axis=0)
    small = sum_everywhere(small, (("parts", n_parts), ("ctx", n_ctx), ("fsdp", n_fsdp)))
    entries = float(n_parts * n_ctx * n_fsdp * rows * dim)
    rms_values = jnp.sqrt(jnp.sum(small[:4], axis=1) / entries)
    shard = dim // n_fsdp
    grad_gmlp = lax.dynamic_slice_in_dim(small[4], z * shard, shard)
    grad_gcross = lax.dynamic_slice_in_dim(small[5], z * shard, shard)

    dq, dk, dv = self_backward(counts, slots, q, k, v, do_all, o1, lse1, seg_q, seg_k, block)
    dn1, g_qkv = qkv_backward(slots, dq, dk, dv, w1, n1, x_all, block)
    dn_own = dn1[:rows].astype(F32)
    for i in range(1, n_ctx):
        piece = lax.ppermute(dn1[i * rows : (i + 1) * rows], "ctx", turned(n_ctx, i))
        dn_own = dn_own + piece.astype(F32)
    x32 = x_own.astype(F32)
    d_in, _ = norm_back(x32, gain_self, dn_own)
    decoder_grad = dh1 + d_in
    part_qkv = lax.psum_scatter(g_qkv, ("fsdp", "parts"), scatter_dimension=0, tiled=True)
    sum_qkv = lax.all_gather(part_qkv, "parts", axis=0, tiled=True)
    every = lax.all_gather(sum_qkv, "ctx", axis=0).astype(F32)
    grads_qkv = [
        jnp.concatenate([every[c, :, i * width : (i + 1) * width] for c in range(n_ctx)], axis=1)[:, :dim]
        for i in range(3)
    ]
    grad_gself = jnp.sum(every[:, :, 3 * width], axis=0)

    mids = [sum_mid[:, i * dim : (i + 1) * dim].astype(F32) for i in range(5)]
    steps = sum_gu.reshape(sum_gu.shape[0], hidden // 512, 2, 512).astype(F32)
    grad_gate = steps[:, :, 0].reshape(-1, hidden)
    grad_up = steps[:, :, 1].reshape(-1, hidden)
    return (
        layer_out[None],
        decoder_grad[None],
        enc_grad[None],
        *grads_qkv,
        mids[0],
        mids[1],
        mids[2],
        mids[3],
        mids[4],
        grad_gate,
        grad_up,
        sum_down.astype(F32),
        grad_gself,
        grad_gcross,
        grad_gmlp,
        rms_values,
    )


def solution(mesh):
    rows3 = P(("parts", "fsdp"), "ctx", None)
    group = P(("parts", "fsdp"), None)
    matrix, vector = P("fsdp", None), P("fsdp")
    shape = tuple(mesh.shape[a] for a in ("parts", "ctx", "fsdp"))
    return jax.shard_map(
        functools.partial(local, shape),
        mesh=mesh,
        in_specs=(rows3, rows3, group, group, P(("parts", "fsdp")))
        + (matrix,) * 11
        + (vector,) * 3
        + (rows3,),
        out_specs=(rows3,) * 3 + (matrix,) * 11 + (vector,) * 3 + (P(),),
        check_vma=False,
    )
```

```python
import functools
import math

import jax
import jax.numpy as jnp
from jax import lax
from jax.experimental import pallas as pl
from jax.experimental.pallas import tpu as pltpu
from jax.sharding import PartitionSpec as P

HEADS = 12
HEAD = 64
SCALE = 0.125
EPS = 1e-06
BIG = 1e30
LN2 = math.log(2.0)
QSCALE = SCALE * math.log2(math.e)
PART0 = 16
SEGS = 16
BF = jnp.bfloat16
F32 = jnp.float32
MIB = 1 << 20
ALL = ("fsdp", "parts", "ctx")


def nn(a, b):
    return lax.dot_general(a, b, (((1,), (0,)), ((), ())), preferred_element_type=F32)


def nt(a, b):
    return lax.dot_general(a, b, (((1,), (1,)), ((), ())), preferred_element_type=F32)


def tn(a, b):
    return lax.dot_general(a, b, (((0,), (0,)), ((), ())), preferred_element_type=F32)


def lanes(shape):
    return lax.broadcasted_iota(jnp.int32, shape, len(shape) - 1)


def params(mib):
    return pltpu.CompilerParams(vmem_limit_bytes=mib * MIB)


def cost(flops, moved, exps=0):
    return pl.CostEstimate(flops=int(flops), bytes_accessed=int(moved), transcendentals=int(exps))


def rms_scale(h):
    return lax.rsqrt(jnp.mean(h * h, axis=-1, keepdims=True) + EPS)


def norm_back(h, gain, dn):
    r = rms_scale(h)
    t = dn * gain
    hr = h * r
    dh = r * (t - hr * jnp.mean(t * hr, axis=-1, keepdims=True))
    return dh, jnp.sum(dn * hr, axis=0, keepdims=True)


def with_parts(base, value):
    spot = lanes(base.shape) % HEAD
    hi = value.astype(BF)
    rest = value - hi.astype(F32)
    mid = rest.astype(BF)
    low = (rest - mid.astype(F32)).astype(BF)
    return jnp.where(
        spot == PART0, hi, jnp.where(spot == PART0 + 1, mid, jnp.where(spot == PART0 + 2, low, base))
    )


def pair_of(own, other):
    left = lanes(own.shape) < HEAD
    return jnp.where(left, own, other), jnp.where(left, other, own)


def chunks_of(n, diag, rows):
    size = rows if diag else math.gcd(512, n)
    first = n % size
    return ([(0, first)] if first else []) + [(c, size) for c in range(first, n, size)]


def forward_block(lo, n, diag, q_ref, qa_ref, kx, vx, o_ref, lse_ref):
    q = q_ref[...]
    rows = q.shape[0]
    left = lanes(q.shape) < HEAD
    sides = pair_of(q, qa_ref[...])
    pieces = chunks_of(n, diag, rows)
    scores, tops, accs = [], [], []
    for h in range(2):
        found = []
        for c, size in pieces:
            s = nt(sides[h], kx[h, pl.ds(lo + c, size), :])
            if diag and c + size == n:
                r = lax.broadcasted_iota(jnp.int32, s.shape, 0)
                s = jnp.where(lanes(s.shape) <= r, s, -BIG)
            found.append(s)
        scores.append(found)
    for h in range(2):
        top = functools.reduce(jnp.maximum, [jnp.max(s, axis=1, keepdims=True) for s in scores[h]])
        acc = None
        for s, (c, size) in zip(scores[h], pieces):
            p = jnp.exp2(s - top).astype(BF)
            term = nn(p, vx[h, pl.ds(lo + c, size), :])
            acc = term if acc is None else acc + term
        accs.append(acc)
        tops.append(top)
    wide = jnp.where(left, accs[0], accs[1])
    total = jnp.where(left, accs[1], accs[0])
    o_ref[...] = (wide / pltpu.roll(total, HEAD, 1)).astype(o_ref.dtype)
    lse_ref[...] = jnp.where(left, tops[1], tops[0]) + jnp.log2(total)


def forward_prep(k_ref, v_ref, ka_ref, kx, vx):
    kx[0], kx[1] = pair_of(k_ref[...], ka_ref[...])
    v = v_ref[...]
    vx[0], vx[1] = pair_of(v, jnp.ones_like(v))


def backward_prep(k_ref, v_ref, ka_ref, kx, vx, km, dk_acc, dv_acc):
    k, v = k_ref[...], v_ref[...]
    spot = lanes(v.shape) % HEAD
    neg = jnp.where((spot >= PART0) & (spot < PART0 + 3), -1.0, 0.0).astype(BF)
    kx[0], kx[1] = pair_of(k, ka_ref[...])
    vx[0], vx[1] = pair_of(v, neg)
    km[0], km[1] = pair_of(k, jnp.zeros_like(k))
    dk_acc[...] = jnp.zeros_like(dk_acc)
    dv_acc[...] = jnp.zeros_like(dv_acc)


def backward_block(
    lo, n, diag, q_ref, do_ref, o_ref, lse_ref, qa_ref, kx, vx, km, dq_ref, dk_acc, dv_acc
):
    q, do = q_ref[...], do_ref[...]
    rows = q.shape[0]
    left = lanes(q.shape) < HEAD
    product = do.astype(F32) * o_ref[...].astype(F32)
    first = jnp.sum(jnp.where(left, product, 0.0), axis=1, keepdims=True)
    second = jnp.sum(jnp.where(left, 0.0, product), axis=1, keepdims=True)
    delta = jnp.where(left, second, first)
    zero = jnp.zeros_like(q)
    qx = pair_of(q, with_parts(qa_ref[...], lse_ref[...]))
    dx = pair_of(do, with_parts(zero, delta))
    qm = pair_of(q, zero)
    dm = pair_of(do, zero)
    dq = None
    for c, size in chunks_of(n, diag, rows):
        at = pl.ds(lo + c, size)
        dk = dv = None
        for h in range(2):
            st = nt(kx[h, at, :], qx[h])
            if diag and c + size == n:
                r = lax.broadcasted_iota(jnp.int32, st.shape, 0)
                st = jnp.where(r <= lanes(st.shape), st, -BIG)
            pt = jnp.exp2(st)
            dp = nt(vx[h, at, :], dx[h])
            ds = (pt * dp).astype(BF)
            tv, tk, tq = nn(pt.astype(BF), dm[h]), nn(ds, qm[h]), tn(ds, km[h, at, :])
            dv = tv if dv is None else dv + tv
            dk = tk if dk is None else dk + tk
            dq = tq if dq is None else dq + tq
        dv_acc[at, :] += dv
        dk_acc[at, :] += dk
    dq_ref[...] = (dq * SCALE).astype(dq_ref.dtype)


def cross_forward_kernel(q_ref, k_ref, v_ref, qa_ref, ka_ref, o_ref, lse_ref, kx, vx):
    @pl.when(pl.program_id(1) == 0)
    def _():
        forward_prep(k_ref, v_ref, ka_ref, kx, vx)

    keys = k_ref.shape[0]
    forward_block(0, keys, False, q_ref, qa_ref, kx, vx, o_ref, lse_ref)


def cross_forward(q, kv, qa, ka):
    rows, width = q.shape
    keys = kv.shape[0]
    block = min(512, rows)
    pairs = width // 128
    row = pl.BlockSpec((block, 128), lambda h, i: (i, h))
    return pl.pallas_call(
        cross_forward_kernel,
        grid=(pairs, rows // block),
        in_specs=[
            row,
            pl.BlockSpec((keys, 128), lambda h, i: (0, h)),
            pl.BlockSpec((keys, 128), lambda h, i: (0, h + pairs)),
            pl.BlockSpec((block, 128), lambda h, i: (i, 0)),
            pl.BlockSpec((keys, 128), lambda h, i: (0, 0)),
        ],
        out_specs=[row, row],
        out_shape=[
            jax.ShapeDtypeStruct((rows, width), BF),
            jax.ShapeDtypeStruct((rows, width), F32),
        ],
        scratch_shapes=[pltpu.VMEM((2, keys, 128), BF)] * 2,
        compiler_params=params(48),
        cost_estimate=cost(16 * rows * keys * width, 8 * rows * width, rows * keys * 12),
        name="cross_forward",
    )(q, kv, kv, qa, ka)


def cross_backward_kernel(
    q_ref, k_ref, v_ref, do_ref, o_ref, lse_ref, qa_ref, ka_ref,
    dq_ref, dk_ref, dv_ref, kx, vx, km, dk_acc, dv_acc,
):
    @pl.when(pl.program_id(1) == 0)
    def _():
        backward_prep(k_ref, v_ref, ka_ref, kx, vx, km, dk_acc, dv_acc)

    keys = k_ref.shape[0]
    backward_block(
        0, keys, False, q_ref, do_ref, o_ref, lse_ref, qa_ref, kx, vx, km,
        dq_ref, dk_acc, dv_acc,
    )

    @pl.when(pl.program_id(1) == pl.num_programs(1) - 1)
    def _():
        dk_ref[...] = (dk_acc[...] * LN2).astype(BF)
        dv_ref[...] = dv_acc[...].astype(BF)


def cross_backward(q, kv, do, o, lse, qa, ka):
    rows, width = q.shape
    keys = kv.shape[0]
    block = min(512, rows)
    pairs = width // 128
    row = pl.BlockSpec((block, 128), lambda h, i: (i, h))
    col = pl.BlockSpec((keys, 128), lambda h, i: (0, h))
    return pl.pallas_call(
        cross_backward_kernel,
        grid=(pairs, rows // block),
        in_specs=[
            row,
            col,
            pl.BlockSpec((keys, 128), lambda h, i: (0, h + pairs)),
            row,
            row,
            row,
            pl.BlockSpec((block, 128), lambda h, i: (i, 0)),
            pl.BlockSpec((keys, 128), lambda h, i: (0, 0)),
        ],
        out_specs=[row, col, col],
        out_shape=[
            jax.ShapeDtypeStruct((rows, width), BF),
            jax.ShapeDtypeStruct((keys, width), BF),
            jax.ShapeDtypeStruct((keys, width), BF),
        ],
        scratch_shapes=[pltpu.VMEM((2, keys, 128), BF)] * 3 + [pltpu.VMEM((keys, 128), F32)] * 2,
        compiler_params=params(48),
        cost_estimate=cost(40 * rows * keys * width, 12 * rows * width, rows * keys * 12),
        name="cross_backward",
    )(q, kv, kv, do, o, lse, qa, ka)


def counts_for(blocks, least):
    return list(range(least, min(blocks, 8) + 1))


def grain_of(block):
    return min(256, block)


def needed_blocks(segs, block):
    total = segs.shape[0]
    grain = grain_of(block)
    first = segs.reshape(total // block, block)[:, 0]
    start = jnp.sum((segs[None, :] < first[:, None]).astype(jnp.int32), axis=1)
    ends = (jnp.arange(total // block, dtype=jnp.int32) + 1) * block
    need = (ends - start // grain * grain) // grain
    return jnp.minimum(need, counts_for(total // grain, block // grain)[-1])


def self_forward_kernel(
    count_ref, slot_ref, q_ref, k_ref, v_ref, qa_ref, ka_ref, o_ref, lse_ref, kx, vx
):
    i = pl.program_id(1)
    block = q_ref.shape[0]
    grain = grain_of(block)

    @pl.when(i == 0)
    def _():
        forward_prep(k_ref, v_ref, ka_ref, kx, vx)

    for n in counts_for(k_ref.shape[0] // grain, block // grain):

        @pl.when(count_ref[i] == n)
        def _():
            lo = pl.multiple_of((i + 1) * block - n * grain, grain)
            forward_block(lo, n * grain, True, q_ref, qa_ref, kx, vx, o_ref, lse_ref)


def self_specs(block, total):
    row = pl.BlockSpec((block, 128), lambda h, i, n, s: (i, h))
    col = pl.BlockSpec((total, 128), lambda h, i, n, s: (0, h))
    dealt = pl.BlockSpec((block, 128), lambda h, i, n, s: (s[i], h))
    qa = pl.BlockSpec((block, 128), lambda h, i, n, s: (i, 0))
    ka = pl.BlockSpec((total, 128), lambda h, i, n, s: (0, 0))
    return row, col, dealt, qa, ka


def self_forward(counts, slots, q, k, v, qa, ka, block):
    total, width = q.shape
    row, col, dealt, qas, kas = self_specs(block, total)
    return pl.pallas_call(
        self_forward_kernel,
        grid_spec=pltpu.PrefetchScalarGridSpec(
            num_scalar_prefetch=2,
            grid=(width // 128, total // block),
            in_specs=[row, col, col, qas, kas],
            out_specs=[dealt, row],
            scratch_shapes=[pltpu.VMEM((2, total, 128), BF)] * 2,
        ),
        out_shape=[
            jax.ShapeDtypeStruct((total, width), BF),
            jax.ShapeDtypeStruct((total, width), F32),
        ],
        compiler_params=params(48),
        cost_estimate=cost(8 * total * total * width, 8 * total * width, total * total * 3),
        name="self_forward",
    )(counts, slots, q, k, v, qa, ka)


def self_backward_kernel(
    count_ref, slot_ref, q_ref, k_ref, v_ref, own_ref, far_ref, o_ref, lse_ref, qa_ref, ka_ref,
    dq_ref, dk_ref, dv_ref, kx, vx, km, dk_acc, dv_acc, do_ref, *, per_dev,
):
    i = pl.program_id(1)
    block = q_ref.shape[0]
    grain = grain_of(block)
    do_ref[...] = jnp.where(slot_ref[i] < per_dev, own_ref[...], far_ref[...])

    @pl.when(i == 0)
    def _():
        backward_prep(k_ref, v_ref, ka_ref, kx, vx, km, dk_acc, dv_acc)

    for n in counts_for(k_ref.shape[0] // grain, block // grain):

        @pl.when(count_ref[i] == n)
        def _():
            lo = pl.multiple_of((i + 1) * block - n * grain, grain)
            backward_block(
                lo, n * grain, True, q_ref, do_ref, o_ref, lse_ref, qa_ref, kx, vx, km,
                dq_ref, dk_acc, dv_acc,
            )

    @pl.when(i == pl.num_programs(1) - 1)
    def _():
        dk_ref[...] = (dk_acc[...] * LN2).astype(BF)
        dv_ref[...] = dv_acc[...].astype(BF)


def self_backward(counts, slots, q, k, v, own, far, o, lse, qa, ka, block):
    total, width = q.shape
    per_dev = own.shape[0] // block
    row, col, dealt, qas, kas = self_specs(block, total)
    return pl.pallas_call(
        functools.partial(self_backward_kernel, per_dev=per_dev),
        grid_spec=pltpu.PrefetchScalarGridSpec(
            num_scalar_prefetch=2,
            grid=(width // 128, total // block),
            in_specs=[
                row,
                col,
                col,
                pl.BlockSpec((block, 128), lambda h, i, n, s: (jnp.minimum(s[i], per_dev - 1), h)),
                pl.BlockSpec((block, 128), lambda h, i, n, s: (jnp.maximum(s[i] - per_dev, 0), h)),
                dealt,
                row,
                qas,
                kas,
            ],
            out_specs=[row, col, col],
            scratch_shapes=[pltpu.VMEM((2, total, 128), BF)] * 3
            + [pltpu.VMEM((total, 128), F32)] * 2
            + [pltpu.VMEM((block, 128), BF)],
        ),
        out_shape=[jax.ShapeDtypeStruct((total, width), BF)] * 3,
        compiler_params=params(48),
        cost_estimate=cost(20 * total * total * width, 12 * total * width, total * total * 3),
        name="self_backward",
    )(counts, slots, q, k, v, own, far, o, lse, qa, ka)


def qkv_kernel(order_ref, own_ref, far_ref, g_ref, w_ref, n_ref, q_ref, k_ref, v_ref, *, per_dev):
    x = jnp.where(pl.program_id(0) < per_dev, own_ref[...], far_ref[...]).astype(F32)
    n = (x * rms_scale(x) * g_ref[...]).astype(BF)
    n_ref[...] = n
    width = q_ref.shape[1]
    out = nn(n, w_ref[...])
    q_ref[...] = (out[:, :width] * QSCALE).astype(BF)
    k_ref[...] = out[:, width : 2 * width].astype(BF)
    v_ref[...] = out[:, 2 * width :].astype(BF)


def qkv_forward(order, own, far, gain, w, block):
    dim = own.shape[1]
    total = own.shape[0] + far.shape[0]
    width = w.shape[1] // 3
    per_dev = own.shape[0] // block
    here = lambda i, o: (o[i], 0)
    whole = lambda i, o: (0, 0)
    return pl.pallas_call(
        functools.partial(qkv_kernel, per_dev=per_dev),
        grid_spec=pltpu.PrefetchScalarGridSpec(
            num_scalar_prefetch=1,
            grid=(total // block,),
            in_specs=[
                pl.BlockSpec((block, dim), lambda i, o: (jnp.minimum(i, per_dev - 1), 0)),
                pl.BlockSpec((block, dim), lambda i, o: (jnp.maximum(i - per_dev, 0), 0)),
                pl.BlockSpec((1, dim), whole),
                pl.BlockSpec(w.shape, whole),
            ],
            out_specs=[pl.BlockSpec((block, dim), here)] + [pl.BlockSpec((block, width), here)] * 3,
        ),
        out_shape=[jax.ShapeDtypeStruct((total, dim), BF)]
        + [jax.ShapeDtypeStruct((total, width), BF)] * 3,
        compiler_params=params(48),
        cost_estimate=cost(6 * total * dim * width, 8 * total * dim),
        name="qkv_forward",
    )(order, own, far, gain, w)


def enc_kv_kernel(own_ref, far_ref, w_ref, kv_ref, *, own_blocks):
    enc = jnp.where(pl.program_id(0) < own_blocks, own_ref[...], far_ref[...])
    half = w_ref.shape[1] // 2
    for c in range(2):
        at = slice(c * half, (c + 1) * half)
        kv_ref[:, at] = nn(enc, w_ref[:, at]).astype(BF)


def enc_forward(own, far, w2):
    rows, dim = own.shape
    block = min(512, rows)
    keys = rows + far.shape[0]
    ours = rows // block
    return pl.pallas_call(
        functools.partial(enc_kv_kernel, own_blocks=ours),
        grid=(keys // block,),
        in_specs=[
            pl.BlockSpec((block, dim), lambda i: (jnp.minimum(i, ours - 1), 0)),
            pl.BlockSpec((block, dim), lambda i: (jnp.maximum(i - ours, 0), 0)),
            pl.BlockSpec((dim, 2 * dim), lambda i: (0, 1)),
        ],
        out_specs=pl.BlockSpec((block, 2 * dim), lambda i: (i, 0)),
        out_shape=jax.ShapeDtypeStruct((keys, 2 * dim), BF),
        compiler_params=params(48),
        cost_estimate=cost(4 * keys * dim * dim, 8 * keys * dim),
        name="enc_forward",
    )(own, far, w2)


def after_self_kernel(turn_ref, x_ref, *refs, count):
    o_refs, w_refs = refs[:count], refs[count : 2 * count]
    g_ref, wq_ref, h_ref, n_ref, q_ref, s_ref = refs[2 * count :]
    x = x_ref[...].astype(F32)
    a = nn(o_refs[0][...], w_refs[0][...])
    for o_ref, w_ref in zip(o_refs[1:], w_refs[1:]):
        a = a + nn(o_ref[...], w_ref[...])
    h = x + a
    h_ref[...] = h
    n = (h * rms_scale(h) * g_ref[...]).astype(BF)
    n_ref[...] = n
    q_ref[...] = (nn(n, wq_ref[...]) * QSCALE).astype(BF)

    @pl.when(pl.program_id(0) == 0)
    def _():
        s_ref[...] = jnp.zeros_like(s_ref)

    s_ref[0:1, :] += jnp.sum(x * x, axis=0, keepdims=True)
    s_ref[1:2, :] += jnp.sum(a * a, axis=0, keepdims=True)


def turn_specs(count, width, dim):
    return [pl.BlockSpec((width, dim), lambda i, t, k=k: (t[k], 0)) for k in range(count)]


def after_self(turn, x, pieces, wo, gain, w2):
    rows, dim = x.shape
    count, width = len(pieces), pieces[0].shape[1]
    block = min(512, rows)
    line = lambda i, t: (i, 0)
    whole = lambda i, t: (0, 0)
    row = pl.BlockSpec((block, dim), line)
    return pl.pallas_call(
        functools.partial(after_self_kernel, count=count),
        grid_spec=pltpu.PrefetchScalarGridSpec(
            num_scalar_prefetch=1,
            grid=(rows // block,),
            in_specs=[row]
            + [pl.BlockSpec((block, width), line)] * count
            + turn_specs(count, width, dim)
            + [pl.BlockSpec((1, dim), whole), pl.BlockSpec((dim, dim), lambda i, t: (0, 1))],
            out_specs=[row, row, row, pl.BlockSpec((8, dim), whole)],
        ),
        out_shape=[
            jax.ShapeDtypeStruct((rows, dim), F32),
            jax.ShapeDtypeStruct((rows, dim), BF),
            jax.ShapeDtypeStruct((rows, dim), BF),
            jax.ShapeDtypeStruct((8, dim), F32),
        ],
        compiler_params=params(56),
        cost_estimate=cost(4 * rows * dim * dim, 14 * rows * dim),
        name="after_self",
    )(turn, x, *pieces, *([wo] * count), gain, w2)


GELU_C = math.sqrt(2.0 / math.pi)
GELU_A = 0.044715


PIECES = (4, 8, 3, 64)


def mlp_kernel(
    o_ref, h1_ref, wc_ref, g_ref, t_ref, gu_ref, wd_ref,
    y_ref, dh_ref, dc_ref, do_ref, s_ref, g_out,
    n_scr, h_scr, m_scr, dn_scr, hid_scr, du_scr, dw_scr, wg_scr, wu_scr, gu_out, d_out, sems,
):
    j = pl.program_id(0)
    last = pl.num_programs(0) - 1
    rows = o_ref.shape[0]
    step = min(256, rows)
    spans = [pl.ds(r, step) for r in range(0, rows, step)]
    gain = g_ref[...]
    n_fsdp, n_two, _, tall, _ = gu_ref.shape
    third = 256
    high = 3 * tall

    @pl.when(j == 0)
    def _():
        total = None
        for at in spans:
            c = nn(o_ref[at, :], wc_ref[...])
            h = h1_ref[at, :] + c
            h_scr[at, :] = h
            n_scr[at, :] = (h * rms_scale(h) * gain).astype(BF)
            part = jnp.sum(c * c, axis=0, keepdims=True)
            total = part if total is None else total + part
        s_ref[...] = jnp.zeros_like(s_ref)
        s_ref[0:1, :] = total
        m_scr[...] = jnp.zeros_like(m_scr)
        dn_scr[...] = jnp.zeros_like(dn_scr)

    for z in range(n_fsdp):
        for p in range(n_two):
            for t in range(3):
                at, to = pl.ds(z * high + t * tall, tall), pl.ds(p * third, third)
                wg_scr[at, to] = gu_ref[z, p, 0, :, t * third : (t + 1) * third]
                wu_scr[at, to] = gu_ref[z, p, 1, :, t * third : (t + 1) * third]
    wg, wu = wg_scr[...], wu_scr[...]
    wd = wd_ref[...].reshape(-1, wd_ref.shape[-1])
    for at in spans:
        n = n_scr[at, :]
        u = nn(n, wg)
        w = nn(n, wu)
        dhid = nt(t_ref[at, :], wd)
        square = u * u
        th = jnp.tanh(GELU_C * u * (1.0 + GELU_A * square))
        half = 0.5 * (1.0 + th)
        gel = u * half
        slope = half + 0.5 * u * (1.0 - th * th) * (GELU_C * (1.0 + 3.0 * GELU_A * square))
        hid = (gel * w).astype(BF)
        du = (dhid * w * slope).astype(BF)
        dw = (dhid * gel).astype(BF)
        hid_scr[at, :] = hid
        du_scr[at, :] = du
        dw_scr[at, :] = dw
        m_scr[at, :] += nn(hid, wd)
        dn_scr[at, :] += nt(du, wg) + nt(dw, wu)

    slot = lax.rem(j, 2)

    def copies(step_of, slot_of):
        return (
            pltpu.make_async_copy(
                gu_out.at[slot_of],
                g_out.at[:, pl.ds(step_of * n_two, n_two), pl.ds(0, 2)],
                sems.at[slot_of, 0],
            ),
            pltpu.make_async_copy(d_out.at[slot_of], g_out.at[step_of, :, 2], sems.at[slot_of, 1]),
        )

    @pl.when(j >= 2)
    def _():
        for copy in copies(j - 2, slot):
            copy.wait()

    d_out[slot] = tn(hid_scr[...], t_ref[...]).astype(BF).reshape(d_out.shape[1:])
    for side, source in ((0, du_scr), (1, dw_scr)):
        grad = tn(n_scr[...], source[...]).astype(BF)
        for z in range(n_fsdp):
            for p in range(n_two):
                for t in range(3):
                    gu_out[slot, z, p, side, :, t * third : (t + 1) * third] = grad[
                        z * high + t * tall : z * high + (t + 1) * tall,
                        p * third : (p + 1) * third,
                    ]
    for copy in copies(j, slot):
        copy.start()

    @pl.when(j == last)
    def _():
        total = gains = None
        for at in spans:
            h = h_scr[at, :]
            y = h + m_scr[at, :]
            y_ref[at, :] = y.astype(BF)
            dh, dg = norm_back(h, gain, dn_scr[at, :])
            dh = dh + t_ref[at, :].astype(F32)
            dh_ref[at, :] = dh
            dc = dh.astype(BF)
            dc_ref[at, :] = dc
            do_ref[at, :] = nt(dc, wc_ref[...]).astype(BF)
            part = jnp.sum(y * y, axis=0, keepdims=True)
            total = part if total is None else total + part
            gains = dg if gains is None else gains + dg
        s_ref[1:2, :] = total
        s_ref[2:3, :] = gains
        for copy in copies(j - 1, 1 - slot) + copies(j, slot):
            copy.wait()


def feed_forward(o, h1, w2, gain, cot, w3):
    rows, dim = o.shape
    n_fsdp, n_plane, _, tall, _ = w3.shape
    steps = n_fsdp
    two = n_plane // steps
    width = two * 256
    whole = lambda j: (0, 0)
    once = pl.Buffered(1)
    full = pl.BlockSpec((rows, dim), whole, pipeline_mode=once)
    flops = 18 * rows * dim * width * steps + 6 * rows * dim * dim
    return pl.pallas_call(
        mlp_kernel,
        grid=(steps,),
        in_specs=[
            full,
            full,
            pl.BlockSpec((dim, dim), lambda j: (0, 4), pipeline_mode=once),
            pl.BlockSpec((1, dim), whole),
            full,
            pl.BlockSpec((n_fsdp, two, 2, tall, dim), lambda j: (0, j, 0, 0, 0)),
            pl.BlockSpec((1, n_plane, 1, tall, dim), lambda j: (j, 0, 2, 0, 0)),
        ],
        out_specs=[
            full,
            full,
            full,
            full,
            pl.BlockSpec((8, dim), whole),
            pl.BlockSpec(memory_space=pl.ANY),
        ],
        out_shape=[
            jax.ShapeDtypeStruct((rows, dim), BF),
            jax.ShapeDtypeStruct((rows, dim), F32),
            jax.ShapeDtypeStruct((rows, dim), BF),
            jax.ShapeDtypeStruct((rows, dim), BF),
            jax.ShapeDtypeStruct((8, dim), F32),
            jax.ShapeDtypeStruct(w3.shape, BF),
        ],
        scratch_shapes=[
            pltpu.VMEM((rows, dim), BF),
            pltpu.VMEM((rows, dim), F32),
            pltpu.VMEM((rows, dim), F32),
            pltpu.VMEM((rows, dim), F32),
            pltpu.VMEM((rows, width), BF),
            pltpu.VMEM((rows, width), BF),
            pltpu.VMEM((rows, width), BF),
            pltpu.VMEM((dim, width), BF),
            pltpu.VMEM((dim, width), BF),
            pltpu.VMEM((2, n_fsdp, two, 2, tall, dim), BF),
            pltpu.VMEM((2, n_plane, tall, dim), BF),
            pltpu.SemaphoreType.DMA((2, 2)),
        ],
        compiler_params=params(60),
        cost_estimate=cost(flops, 40 * MIB, rows * width * steps),
        name="feed_forward",
    )(o, h1, w2, gain, cot, w3, w3)


def unpack_kernel(me_ref, p_ref, gate_ref, up_ref, down_ref):
    core, x, place = me_ref[0], me_ref[1], me_ref[2]
    tall = p_ref.shape[4]
    third = 256
    for p in range(8):
        near = (core ^ ((p // 2) % 2), x ^ (p // 4), place ^ (p % 2))
        for t in range(3):
            at, to = pl.ds(t * tall, tall), pl.ds(p * third, third)
            lane = slice(t * third, (t + 1) * third)
            gate_ref[at, to] = p_ref[near + (0, slice(None), lane)].astype(F32)
            up_ref[at, to] = p_ref[near + (1, slice(None), lane)].astype(F32)
        down_ref[pl.ds(p * tall, tall), :] = p_ref[near + (2,)].astype(F32)


def unpack(me, pieces):
    tall, dim = pieces.shape[-2:]
    vmem = pl.BlockSpec(memory_space=pltpu.VMEM)
    return pl.pallas_call(
        unpack_kernel,
        in_specs=[pl.BlockSpec(memory_space=pltpu.SMEM), vmem],
        out_specs=[vmem] * 3,
        out_shape=[
            jax.ShapeDtypeStruct((3 * tall, 8 * 256), F32),
            jax.ShapeDtypeStruct((3 * tall, 8 * 256), F32),
            jax.ShapeDtypeStruct((8 * tall, dim), F32),
        ],
        compiler_params=params(32),
        name="unpack",
    )(me, pieces)


def mid_grads_kernel(turn_ref, *refs, count):
    o_refs = refs[:count]
    da_ref, n2_ref, dq_ref, own_ref, far_ref, dk_ref, dv_ref, o2_ref, dc_ref, g_ref = refs[count:]
    m = pl.program_id(0)
    dim = g_ref.shape[0]
    width = o_refs[0].shape[1]
    ours = own_ref.shape[0]

    @pl.when(m == 0)
    def _():
        for i in range(count):
            base = pl.multiple_of(turn_ref[i] * width, width)
            term = tn(o_refs[i][...], da_ref[...]).astype(BF)

            @pl.when(base < dim)
            def _():
                g_ref[pl.ds(base, width), :] = term

    for at, right in ((2, dk_ref), (3, dv_ref)):

        @pl.when(m == at)
        def _():
            total = tn(own_ref[...], right[:ours, :]) + tn(far_ref[...], right[ours:, :])
            g_ref[...] = total.astype(BF)

    for at, left, right in ((1, n2_ref, dq_ref), (4, o2_ref, dc_ref)):

        @pl.when(m == at)
        def _():
            g_ref[...] = tn(left[...], right[...]).astype(BF)


def mid_grads(turn, pieces, da, n2, dq2, own, far, dk2, dv2, o2, dc):
    dim = n2.shape[1]
    rows = n2.shape[0]
    args = (*pieces, da, n2, dq2, own, far, dk2, dv2, o2, dc)
    shapes = [(rows, a.shape[1]) for a in pieces] + [a.shape for a in args[len(pieces) :]]
    flops = 2 * dim * dim * (3 * rows + 2 * dk2.shape[0])
    return pl.pallas_call(
        functools.partial(mid_grads_kernel, count=len(pieces)),
        grid_spec=pltpu.PrefetchScalarGridSpec(
            num_scalar_prefetch=1,
            grid=(5,),
            in_specs=[
                pl.BlockSpec(shape, lambda m, t: (0, 0), pipeline_mode=pl.Buffered(1))
                for shape in shapes
            ],
            out_specs=pl.BlockSpec((dim, dim), lambda m, t: (0, m)),
        ),
        out_shape=jax.ShapeDtypeStruct((dim, 5 * dim), BF),
        compiler_params=params(48),
        cost_estimate=cost(flops, 24 * MIB),
        name="mid_grads",
    )(turn, *args)


def enc_back_kernel(dk_ref, dv_ref, wk_ref, wv_ref, far_ref, own_ref, *, far_blocks):
    d = nt(dk_ref[...], wk_ref[...]) + nt(dv_ref[...], wv_ref[...])

    @pl.when(pl.program_id(0) < far_blocks)
    def _():
        far_ref[...] = d.astype(BF)

    @pl.when(pl.program_id(0) >= far_blocks)
    def _():
        own_ref[...] = d


def enc_backward(dk, dv, w2, own_rows):
    keys, dim = dk.shape
    block = min(512, own_rows)
    blocks, own = keys // block, own_rows // block
    far = blocks - own
    row = pl.BlockSpec((block, dim), lambda i: ((i + own) % blocks, 0))
    return pl.pallas_call(
        functools.partial(enc_back_kernel, far_blocks=far),
        grid=(blocks,),
        in_specs=[
            row,
            row,
            pl.BlockSpec((dim, dim), lambda i: (0, 2)),
            pl.BlockSpec((dim, dim), lambda i: (0, 3)),
        ],
        out_specs=[
            pl.BlockSpec((block, dim), lambda i: (jnp.minimum(i, far - 1), 0)),
            pl.BlockSpec((block, dim), lambda i: (jnp.maximum(i - far, 0), 0)),
        ],
        out_shape=[
            jax.ShapeDtypeStruct((keys - own_rows, dim), BF),
            jax.ShapeDtypeStruct((own_rows, dim), F32),
        ],
        compiler_params=params(48),
        cost_estimate=cost(4 * keys * dim * dim, 8 * keys * dim),
        name="enc_backward",
    )(dk, dv, w2, w2)


def before_self_kernel(turn_ref, dq_ref, wq_ref, h_ref, dh_ref, g_ref, *refs, count):
    w_refs = refs[:count]
    d1_ref, da_ref, s_ref = refs[count : count + 3]
    do_refs = refs[count + 3 :]
    dn = nt(dq_ref[...], wq_ref[...])
    dh, dg = norm_back(h_ref[...], g_ref[...], dn)
    d1 = dh_ref[...] + dh
    d1_ref[...] = d1
    da = d1.astype(BF)
    da_ref[...] = da
    for do_ref, w_ref in zip(do_refs, w_refs):
        do_ref[...] = nt(da, w_ref[...]).astype(BF)

    @pl.when(pl.program_id(0) == 0)
    def _():
        s_ref[...] = jnp.zeros_like(s_ref)

    s_ref[0:1, :] += dg


def before_self(turn, dq, w2, h1, dh2, gain, wo, width):
    rows, dim = dq.shape
    count = turn.shape[0]
    block = min(512, rows)
    line = lambda i, t: (i, 0)
    whole = lambda i, t: (0, 0)
    row = pl.BlockSpec((block, dim), line)
    return pl.pallas_call(
        functools.partial(before_self_kernel, count=count),
        grid_spec=pltpu.PrefetchScalarGridSpec(
            num_scalar_prefetch=1,
            grid=(rows // block,),
            in_specs=[
                row,
                pl.BlockSpec((dim, dim), lambda i, t: (0, 1)),
                row,
                row,
                pl.BlockSpec((1, dim), whole),
            ]
            + turn_specs(count, width, dim),
            out_specs=[row, row, pl.BlockSpec((8, dim), whole)]
            + [pl.BlockSpec((block, width), line)] * count,
        ),
        out_shape=[
            jax.ShapeDtypeStruct((rows, dim), F32),
            jax.ShapeDtypeStruct((rows, dim), BF),
            jax.ShapeDtypeStruct((8, dim), F32),
        ]
        + [jax.ShapeDtypeStruct((rows, width), BF)] * count,
        compiler_params=params(56),
        cost_estimate=cost(4 * rows * dim * dim, 18 * rows * dim),
        name="before_self",
    )(turn, dq, w2, h1, dh2, gain, *([wo] * count))


def normed_sum(dn, x):
    return jnp.sum(dn * (x * rms_scale(x)), axis=0, keepdims=True)


def qkv_far_kernel(order_ref, dq_ref, dk_ref, dv_ref, w_ref, x_ref, dn_ref, s_ref):
    d = jnp.concatenate([dq_ref[...], dk_ref[...], dv_ref[...]], axis=1)
    dn = nt(d, w_ref[...])
    dn_ref[...] = dn.astype(BF)

    @pl.when(pl.program_id(0) == 0)
    def _():
        s_ref[...] = jnp.zeros_like(s_ref)

    s_ref[0:1, :] += normed_sum(dn, x_ref[...].astype(F32))


def qkv_back_far(order, dq, dk, dv, w, x_far, block):
    width, dim = dq.shape[1], x_far.shape[1]
    first = order.shape[0] - x_far.shape[0] // block
    row = pl.BlockSpec((block, width), lambda i, o: (o[i + first], 0))
    line = pl.BlockSpec((block, dim), lambda i, o: (i, 0))
    whole = lambda i, o: (0, 0)
    return pl.pallas_call(
        qkv_far_kernel,
        grid_spec=pltpu.PrefetchScalarGridSpec(
            num_scalar_prefetch=1,
            grid=(x_far.shape[0] // block,),
            in_specs=[row, row, row, pl.BlockSpec(w.shape, whole), line],
            out_specs=[line, pl.BlockSpec((8, dim), whole)],
        ),
        out_shape=[
            jax.ShapeDtypeStruct(x_far.shape, BF),
            jax.ShapeDtypeStruct((8, dim), F32),
        ],
        compiler_params=params(48),
        cost_estimate=cost(6 * x_far.shape[0] * dim * width, 10 * x_far.shape[0] * dim),
        name="qkv_back_far",
    )(order, dq, dk, dv, w, x_far)


def qkv_own_kernel(
    order_ref, dq_ref, dk_ref, dv_ref, w_ref, n_ref, x_ref, far_ref, dn_ref, g_ref, acc, s_acc, *, per_dev
):
    i = pl.program_id(0)
    d = jnp.concatenate([dq_ref[...], dk_ref[...], dv_ref[...]], axis=1)
    term = tn(n_ref[...], d)

    @pl.when(i == 0)
    def _():
        acc[...] = term
        s_acc[...] = far_ref[...]

    @pl.when(i > 0)
    def _():
        acc[...] += term

    @pl.when(i < per_dev)
    def _():
        dn = nt(d, w_ref[...])
        dn_ref[...] = dn
        s_acc[0:1, :] += normed_sum(dn, x_ref[...].astype(F32))

    @pl.when(i == pl.num_programs(0) - 1)
    def _():
        width = acc.shape[1]
        g_ref[:, :width] = acc[...].astype(BF)
        g_ref[:, width:] = jnp.broadcast_to(s_acc[0:1, :], (128, s_acc.shape[1])).T.astype(BF)


def qkv_back_own(order, dq, dk, dv, w, n, x_own, far_sum, block):
    total, width = dq.shape
    dim = n.shape[1]
    per_dev = x_own.shape[0] // block
    row = pl.BlockSpec((block, width), lambda i, o: (o[i], 0))
    ours = pl.BlockSpec((block, dim), lambda i, o: (jnp.minimum(i, per_dev - 1), 0))
    whole = lambda i, o: (0, 0)
    return pl.pallas_call(
        functools.partial(qkv_own_kernel, per_dev=per_dev),
        grid_spec=pltpu.PrefetchScalarGridSpec(
            num_scalar_prefetch=1,
            grid=(total // block,),
            in_specs=[
                row,
                row,
                row,
                pl.BlockSpec(w.shape, whole),
                pl.BlockSpec((block, dim), lambda i, o: (o[i], 0)),
                ours,
                pl.BlockSpec((8, dim), whole),
            ],
            out_specs=[ours, pl.BlockSpec((dim, 3 * width + 128), whole)],
            scratch_shapes=[pltpu.VMEM((dim, 3 * width), F32), pltpu.VMEM((8, dim), F32)],
        ),
        out_shape=[
            jax.ShapeDtypeStruct(x_own.shape, F32),
            jax.ShapeDtypeStruct((dim, 3 * width + 128), BF),
        ],
        compiler_params=params(48),
        cost_estimate=cost(9 * total * dim * width, 10 * total * dim),
        name="qkv_back_own",
    )(order, dq, dk, dv, w, n, x_own, far_sum)


def turned(n, k):
    return [(i, (i + k) % n) for i in range(n)]


def rows_of(array, index, count):
    size = array.shape[0] // count
    return lax.dynamic_slice_in_dim(array, index * size, size, 0)


def assemble_kernel(place_ref, near_ref, far_ref, w_ref, g_ref):
    z, core = place_ref[0], place_ref[1]
    count, size = near_ref.shape[0], near_ref.shape[1]
    width = w_ref.shape[1]
    for d in range(count):
        base = lax.rem(z - d + count, count) * (2 * size)
        for ref, half in ((near_ref, core), (far_ref, 1 - core)):
            at = pl.ds(pl.multiple_of(base + half * size, 16), size)
            w_ref[at, :] = ref[d, :, :width]
            g_ref[at, :] = ref[d, :, width:]


def gather_first(own, z, part, n_fsdp, n_parts):
    size = own.shape[0] // 2
    width = own.shape[1] - 128
    if n_parts % 2 or size % 16:
        full = lax.all_gather(own, "fsdp", axis=0, tiled=True)
        return full[:, :width], full[:, width:]
    core = part % 2
    mine = lax.dynamic_slice_in_dim(own, core * size, size, 0)
    near = jnp.stack(
        [mine] + [lax.ppermute(mine, "fsdp", turned(n_fsdp, d)) for d in range(1, n_fsdp)]
    )
    far = lax.ppermute(near, "parts", [(i, i ^ 1) for i in range(n_parts)])
    vmem = pl.BlockSpec(memory_space=pltpu.VMEM)
    total = n_fsdp * own.shape[0]
    return pl.pallas_call(
        assemble_kernel,
        in_specs=[pl.BlockSpec(memory_space=pltpu.SMEM), vmem, vmem],
        out_specs=[vmem, vmem],
        out_shape=[
            jax.ShapeDtypeStruct((total, width), BF),
            jax.ShapeDtypeStruct((total, 128), BF),
        ],
        compiler_params=params(32),
        name="assemble",
    )(jnp.stack([z, core]).astype(jnp.int32), near, far)


def pick(array, index, axis):
    return lax.dynamic_index_in_dim(array, index, axis, keepdims=False)


class Plane:
    def __init__(self, part, place, z, n_parts, n_fsdp):
        self.core, self.x, self.place, self.z = part % 2, part // 2, place, z
        self.n_fsdp = n_fsdp
        self.swap_core = [(i, i ^ 1) for i in range(n_parts)]
        self.swap_x = [(i, i ^ 2) for i in range(n_parts)]

    def over_core(self, grad):
        rows = grad.shape[0] // (4 * self.n_fsdp)
        g = grad.reshape(self.n_fsdp, 2, 2, rows, grad.shape[1])
        got = lax.ppermute(pick(g, 1 - self.core, 2), "parts", self.swap_core).astype(F32)
        g = pick(g, self.core, 2).astype(F32)
        send = (pick(g, 1 - self.x, 1) + pick(got, 1 - self.x, 1)).astype(BF)
        keep = (pick(g, self.x, 1) + pick(got, self.x, 1)).astype(BF)
        return send, keep

    def over_x(self, send, keep):
        got = lax.ppermute(send, "parts", self.swap_x)
        return (keep.astype(F32) + got.astype(F32)).astype(BF)

    def over_fsdp(self, g):
        total = pick(g, self.z, 0).astype(F32)
        for d in range(1, self.n_fsdp):
            piece = pick(g, (self.z + d) % self.n_fsdp, 0)
            total = total + lax.ppermute(piece, "fsdp", turned(self.n_fsdp, d)).astype(F32)
        return total.astype(BF)

    def over_ctx(self, g):
        return (g.astype(F32) + lax.ppermute(g, "ctx", turned(2, 1)).astype(F32)).astype(BF)

    def widen_ctx(self, g):
        return jnp.stack([g, lax.ppermute(g, "ctx", turned(2, 1))])

    def widen(self, g):
        g = jnp.stack([g, lax.ppermute(g, "parts", self.swap_x)])
        return jnp.stack([g, lax.ppermute(g, "parts", self.swap_core)])

    def rows(self, wide):
        pieces = [
            lax.dynamic_slice(
                wide, (c ^ self.core, a ^ self.x, 0, 0), (1, 1) + wide.shape[2:]
            )[0, 0]
            for a in range(2)
            for c in range(2)
        ]
        return jnp.concatenate(pieces).astype(F32)


def sum_everywhere(value, sizes):
    for axis, size in sizes:
        bit = 1
        while bit < size:
            value = value + lax.ppermute(value, axis, [(i, i ^ bit) for i in range(size)])
            bit *= 2
    return value


def local(
    mesh_shape,
    decoder_in,
    encoder_out,
    segment_ids,
    block_order,
    prompt_len,
    self_query,
    self_key,
    self_value,
    self_output,
    cross_query,
    cross_key,
    cross_value,
    cross_output,
    gate_in,
    up_in,
    down_out,
    norm_self,
    norm_cross,
    norm_mlp,
    cotangent,
):
    n_parts, n_ctx, n_fsdp = mesh_shape
    part, place, z = lax.axis_index("parts"), lax.axis_index("ctx"), lax.axis_index("fsdp")
    plane, n_plane = part * n_ctx + place, n_parts * n_ctx
    x_own, enc_own = decoder_in[0], encoder_out[0]
    rows, dim = x_own.shape
    segs, order = segment_ids[0], block_order[0]
    total = segs.shape[0]
    slots_total = order.shape[0]
    block = total // slots_total
    per_dev = slots_total // n_ctx
    enc_rows = enc_own.shape[0]
    keys = enc_rows * n_ctx
    hidden = down_out.shape[0] * n_fsdp
    heads_here = 2 * -(-HEADS // (2 * n_ctx))
    width = heads_here * HEAD
    padded = width * n_ctx

    ring = (place + jnp.arange(n_ctx, dtype=jnp.int32)) % n_ctx
    order_here = jnp.roll(order, -per_dev * place)
    slots = jnp.argsort(order_here).astype(jnp.int32)
    counts = needed_blocks(segs, block)

    def from_ctx(value):
        pieces = [lax.ppermute(value, "ctx", turned(n_ctx, -k)) for k in range(1, n_ctx)]
        return pieces[0] if n_ctx == 2 else jnp.concatenate(pieces, axis=0)

    x_far = from_ctx(x_own)

    fast = (n_parts, n_ctx, n_fsdp) == (4, 2, 4)
    shard = dim // n_fsdp

    def own_heads(w):
        w = jnp.pad(w, ((0, 0), (0, padded - dim)))
        return lax.dynamic_slice_in_dim(w, place * width, width, 1)

    gain_cols = jnp.pad(jnp.stack([norm_self, norm_cross, norm_mlp], axis=1), ((0, 0), (0, 125)))
    w1, gains = gather_first(
        jnp.concatenate(
            [own_heads(self_query), own_heads(self_key), own_heads(self_value), gain_cols], axis=1
        ),
        z, part, n_fsdp, n_parts,
    )
    gains = gains[:, :8].astype(F32).T
    gain_self, gain_cross, gain_mlp = (gains[i : i + 1] for i in range(3))
    mats = (self_output, cross_query, cross_key, cross_value, cross_output)
    if fast:
        w2 = lax.all_gather(
            jnp.concatenate([rows_of(w, plane, n_plane) for w in mats], axis=1),
            ALL, axis=0, tiled=True,
        )

        def column_piece(w):
            cut = lax.dynamic_slice_in_dim(w, plane * 256, 256, 1)
            return jnp.concatenate([cut[t * 64 : (t + 1) * 64] for t in range(3)], axis=1)

        w3 = lax.all_gather(
            jnp.stack(
                [column_piece(gate_in), column_piece(up_in), rows_of(down_out, plane, n_plane)]
            ),
            ALL, axis=0,
        ).reshape(PIECES + (dim,))
    else:
        w2 = lax.all_gather(jnp.concatenate(mats, axis=1), "fsdp", axis=0, tiled=True)

        def packed(w):
            w = lax.all_gather(w, "fsdp", axis=0, tiled=True).reshape(4, 3, 64, 8, 256)
            return w.transpose(0, 3, 2, 1, 4).reshape(4, 8, 64, dim)

        w_down = lax.all_gather(down_out, "fsdp", axis=0, tiled=True).reshape(4, 8, 64, dim)
        w3 = jnp.stack([packed(gate_in), packed(up_in), w_down], axis=2)
    enc_far = from_ctx(enc_own)

    n1, q, k, v = qkv_forward(order_here, x_own, x_far, gain_self, w1, block)
    spot = jnp.arange(128, dtype=jnp.int32)[None, :] % HEAD
    minus = jnp.where((spot >= PART0) & (spot < PART0 + 3), -1.0, 0.0)
    seg_q = jnp.where(spot == segs[:, None], 1.0, 0.0).astype(BF)
    seg_k = jnp.where((spot < SEGS) & (spot != segs[:, None]), -BIG, minus).astype(BF)
    o1, lse1 = self_forward(counts, slots, q, k, v, seg_q, seg_k, block)
    pieces = [o1] + [
        lax.ppermute(o1[i * rows : (i + 1) * rows], "ctx", turned(n_ctx, i)) for i in range(1, n_ctx)
    ]
    turn = (place - jnp.arange(n_ctx, dtype=jnp.int32)) % n_ctx
    wo = w2 if padded == dim else jnp.pad(w2[:, :dim], ((0, padded - dim), (0, 0)))
    kv2 = enc_forward(enc_own, enc_far, w2)
    pieces[1], kv2 = lax.optimization_barrier((pieces[1], kv2))
    h1, n2, q2, stat1 = after_self(turn, x_own, pieces, wo, gain_cross, w2)

    where_key = (ring[:, None] * enc_rows + jnp.arange(enc_rows, dtype=jnp.int32)).reshape(-1, 1)
    len_q = jnp.where(spot == 0, jnp.ones((rows, 1), F32), 0.0).astype(BF)
    len_k = jnp.where((spot == 0) & (where_key >= prompt_len[0]), -BIG, minus).astype(BF)
    o2, lse2 = cross_forward(q2, kv2, len_q, len_k)

    layer_out, dh2, dc, do2, stat2, g_ff = feed_forward(o2, h1, w2, gain_mlp, cotangent[0], w3)
    if fast:
        part_ff = lax.psum_scatter(g_ff.reshape(32, 3, 64, dim), ALL, scatter_dimension=0)

    dq2, dk2, dv2 = cross_backward(q2, kv2, do2, o2, lse2, len_q, len_k)
    dh1, da, stat3, *do1 = before_self(turn, dq2, w2, h1, dh2, gain_cross, wo, width)
    do_far = [lax.ppermute(do1[i], "ctx", turned(n_ctx, -i)) for i in range(1, n_ctx)]
    do_far = do_far[0] if n_ctx == 2 else jnp.concatenate(do_far, axis=0)
    g_mid = mid_grads(turn, pieces, da, n2, dq2, enc_own, enc_far, dk2, dv2, o2, dc)
    d_far, enc_grad = enc_backward(dk2, dv2, w2, enc_rows)
    enc_got = [
        lax.ppermute(d_far[(i - 1) * enc_rows : i * enc_rows], "ctx", turned(n_ctx, i))
        for i in range(1, n_ctx)
    ]
    for piece in enc_got:
        enc_grad = enc_grad + piece.astype(F32)

    small = jnp.concatenate([stat1[:2], stat2[:3], stat3[:1], jnp.zeros((2, dim), F32)], axis=0)
    small = sum_everywhere(small, (("parts", n_parts), ("ctx", n_ctx), ("fsdp", n_fsdp)))
    entries = float(n_parts * n_ctx * n_fsdp * rows * dim)
    rms_values = jnp.sqrt(jnp.sum(small[:4], axis=1) / entries)
    grad_gmlp = lax.dynamic_slice_in_dim(small[4], z * shard, shard)
    grad_gcross = lax.dynamic_slice_in_dim(small[5], z * shard, shard)

    do_own = do1[0]
    if fast:
        net = Plane(part, place, z, n_parts, n_fsdp)
        send, keep = net.over_core(g_mid)
        do_own, do_far, send, keep, d_far = lax.optimization_barrier(
            (do_own, do_far, send, keep, d_far)
        )
        g_mid = net.over_x(send, keep)

    dq, dk, dv = self_backward(counts, slots, q, k, v, do_own, do_far, o1, lse1, seg_q, seg_k, block)
    if fast:
        dq, dk, dv, part_ff, g_mid = lax.optimization_barrier((dq, dk, dv, part_ff, g_mid))
    dn_far, far_sum = qkv_back_far(order_here, dq, dk, dv, w1, x_far, block)
    dn_got = [
        lax.ppermute(dn_far[(i - 1) * rows : i * rows], "ctx", turned(n_ctx, i))
        for i in range(1, n_ctx)
    ]
    dn_own, g_qkv = qkv_back_own(order_here, dq, dk, dv, w1, n1, x_own, far_sum, block)
    for piece in dn_got:
        dn_own = dn_own + piece.astype(F32)
    d_in, _ = norm_back(x_own.astype(F32), gain_self, dn_own)
    decoder_grad = dh1 + d_in

    if fast:
        send, keep = net.over_core(g_qkv)
        sum_mid = net.rows(net.widen(net.over_ctx(net.over_fsdp(g_mid))))
        me = jnp.stack([net.core, net.x, place]).astype(jnp.int32)
        grad_gate, grad_up, grad_down = unpack(me, net.widen(net.widen_ctx(part_ff)))
        wide = net.widen(net.widen_ctx(net.over_fsdp(net.over_x(send, keep))))
        every = jnp.stack([net.rows(pick(wide, i ^ place, 2)) for i in range(2)])
    else:

        def total(g):
            g = lax.psum_scatter(g, "fsdp", scatter_dimension=0, tiled=True).astype(F32)
            return lax.psum(g, ("parts", "ctx"))

        sum_mid = total(g_mid)
        flat = [
            g_ff[:, :, i].reshape(4, 8, 64, 3, 256).transpose(0, 3, 2, 1, 4).reshape(dim, hidden)
            for i in range(2)
        ]
        grad_gate, grad_up = total(flat[0]), total(flat[1])
        grad_down = total(g_ff[:, :, 2].reshape(hidden, dim))
        sum_qkv = lax.psum_scatter(g_qkv, "fsdp", scatter_dimension=0, tiled=True).astype(F32)
        every = lax.all_gather(lax.psum(sum_qkv, "parts"), "ctx", axis=0)
    grads_qkv = [
        jnp.concatenate([every[c, :, i * width : (i + 1) * width] for c in range(n_ctx)], axis=1)[:, :dim]
        for i in range(3)
    ]
    grad_gself = jnp.sum(every[:, :, 3 * width], axis=0)
    mids = [sum_mid[:, i * dim : (i + 1) * dim] for i in range(5)]
    return (
        layer_out[None],
        decoder_grad[None],
        enc_grad[None],
        *grads_qkv,
        *mids,
        grad_gate,
        grad_up,
        grad_down,
        grad_gself,
        grad_gcross,
        grad_gmlp,
        rms_values,
    )


def solution(mesh):
    rows3 = P(("parts", "fsdp"), "ctx", None)
    group = P(("parts", "fsdp"), None)
    matrix, vector = P("fsdp", None), P("fsdp")
    shape = tuple(mesh.shape[a] for a in ("parts", "ctx", "fsdp"))
    return jax.shard_map(
        functools.partial(local, shape),
        mesh=mesh,
        in_specs=(rows3, rows3, group, group, P(("parts", "fsdp")))
        + (matrix,) * 11
        + (vector,) * 3
        + (rows3,),
        out_specs=(rows3,) * 3 + (matrix,) * 11 + (vector,) * 3 + (P(),),
        check_vma=False,
    )
```

```python
import functools
import math

import jax
import jax.numpy as jnp
from jax import lax
from jax.experimental import pallas as pl
from jax.experimental.pallas import tpu as pltpu
from jax.sharding import PartitionSpec as P

HEADS = 12
HEAD = 64
SCALE = 0.125
EPS = 1e-06
BIG = 1e30
LN2 = math.log(2.0)
QSCALE = SCALE * math.log2(math.e)
PART0 = 16
SEGS = 16
BF = jnp.bfloat16
F32 = jnp.float32
MIB = 1 << 20
ALL = ("fsdp", "parts", "ctx")


def nn(a, b):
    return lax.dot_general(a, b, (((1,), (0,)), ((), ())), preferred_element_type=F32)


def nt(a, b):
    return lax.dot_general(a, b, (((1,), (1,)), ((), ())), preferred_element_type=F32)


def tn(a, b):
    return lax.dot_general(a, b, (((0,), (0,)), ((), ())), preferred_element_type=F32)


def lanes(shape):
    return lax.broadcasted_iota(jnp.int32, shape, len(shape) - 1)


def params(mib):
    return pltpu.CompilerParams(vmem_limit_bytes=mib * MIB)


def cost(flops, moved, exps=0):
    return pl.CostEstimate(flops=int(flops), bytes_accessed=int(moved), transcendentals=int(exps))


def rms_scale(h):
    return lax.rsqrt(jnp.mean(h * h, axis=-1, keepdims=True) + EPS)


def norm_back(h, gain, dn):
    r = rms_scale(h)
    t = dn * gain
    hr = h * r
    dh = r * (t - hr * jnp.mean(t * hr, axis=-1, keepdims=True))
    return dh, jnp.sum(dn * hr, axis=0, keepdims=True)


def with_parts(base, value):
    spot = lanes(base.shape) % HEAD
    hi = value.astype(BF)
    rest = value - hi.astype(F32)
    mid = rest.astype(BF)
    low = (rest - mid.astype(F32)).astype(BF)
    return jnp.where(
        spot == PART0, hi, jnp.where(spot == PART0 + 1, mid, jnp.where(spot == PART0 + 2, low, base))
    )


def pair_of(own, other):
    left = lanes(own.shape) < HEAD
    return jnp.where(left, own, other), jnp.where(left, other, own)


CHUNK = 512


def below(s, rows_first):
    r = lax.broadcasted_iota(jnp.int32, s.shape, 0)
    c = lanes(s.shape)
    return jnp.where(c <= r if rows_first else r <= c, s, -BIG)


def lane_max(s):
    return functools.reduce(jnp.maximum, [s[:, c : c + 128] for c in range(0, s.shape[1], 128)])


def sweep(step, lo, full, odd, grain, unroll):
    base = lo
    if odd is not None:

        @pl.when(odd == 1)
        def _():
            step(lo, 0, grain)

        base = lo + odd * grain

    def body(c, carry):
        step(pl.multiple_of(base + c * CHUNK, grain), pl.multiple_of(grain + c * CHUNK, 128), CHUNK)
        return carry

    lax.fori_loop(0, full, body, 0, unroll=unroll)
    return pl.multiple_of(base + full * CHUNK, grain)


def forward_block(
    lo, full, odd, grain, diag, q_ref, qa_ref, kx, vx, o_ref, lse_ref, s_scr, m_scr, a_scr, unroll
):
    q = q_ref[...]
    rows = q.shape[0]
    left = lanes(q.shape) < HEAD
    sides = pair_of(q, qa_ref[...])
    m_scr[...] = jnp.full_like(m_scr, -BIG)
    a_scr[...] = jnp.zeros_like(a_scr)
    last = s_scr.shape[2] - rows

    def scores(key, at, size, masked=False):
        for h in range(2):
            s = nt(sides[h], kx[h, pl.ds(key, size), :])
            s = below(s, True) if masked else s
            s_scr[h, :, pl.ds(at, size)] = s
            m_scr[h] = jnp.maximum(m_scr[h], lane_max(s))

    end = sweep(scores, lo, full, odd, grain, unroll)
    if diag:
        scores(end, last, rows, True)
    tops = [jnp.max(m_scr[h], axis=1, keepdims=True) for h in range(2)]

    def values(key, at, size):
        for h in range(2):
            p = jnp.exp2(s_scr[h, :, pl.ds(at, size)] - tops[h]).astype(BF)
            a_scr[h] += nn(p, vx[h, pl.ds(key, size), :])

    end = sweep(values, lo, full, odd, grain, unroll)
    if diag:
        values(end, last, rows)
    wide = jnp.where(left, a_scr[0], a_scr[1])
    total = jnp.where(left, a_scr[1], a_scr[0])
    o_ref[...] = (wide / pltpu.roll(total, HEAD, 1)).astype(o_ref.dtype)
    lse_ref[...] = jnp.where(left, tops[1], tops[0]) + jnp.log2(total)


def forward_scratch(block, keys):
    return [
        pltpu.VMEM((2, keys, 128), BF),
        pltpu.VMEM((2, keys, 128), BF),
        pltpu.VMEM((2, block, keys + CHUNK), F32),
        pltpu.VMEM((2, block, 128), F32),
        pltpu.VMEM((2, block, 128), F32),
    ]


def backward_scratch(block, keys):
    return (
        [pltpu.VMEM((2, keys, 128), BF)] * 3
        + [pltpu.VMEM((keys, 128), F32)] * 2
        + [pltpu.VMEM((block, 128), F32)]
    )


def forward_prep(k_ref, v_ref, ka_ref, kx, vx):
    kx[0], kx[1] = pair_of(k_ref[...], ka_ref[...])
    v = v_ref[...]
    vx[0], vx[1] = pair_of(v, jnp.ones_like(v))


def backward_prep(k_ref, v_ref, ka_ref, kx, vx, km, dk_acc, dv_acc):
    k, v = k_ref[...], v_ref[...]
    spot = lanes(v.shape) % HEAD
    neg = jnp.where((spot >= PART0) & (spot < PART0 + 3), -1.0, 0.0).astype(BF)
    kx[0], kx[1] = pair_of(k, ka_ref[...])
    vx[0], vx[1] = pair_of(v, neg)
    km[0], km[1] = pair_of(k, jnp.zeros_like(k))
    dk_acc[...] = jnp.zeros_like(dk_acc)
    dv_acc[...] = jnp.zeros_like(dv_acc)


def backward_block(
    lo, full, odd, grain, diag, q, do, o_ref, lse_ref, qa_ref, kx, vx, km,
    dq_ref, dk_acc, dv_acc, dq_acc, unroll,
):
    left = lanes(q.shape) < HEAD
    rows = q.shape[0]
    product = do.astype(F32) * o_ref[...].astype(F32)
    first = jnp.sum(jnp.where(left, product, 0.0), axis=1, keepdims=True)
    second = jnp.sum(jnp.where(left, 0.0, product), axis=1, keepdims=True)
    delta = jnp.where(left, second, first)
    zero = jnp.zeros_like(q)
    qx = pair_of(q, with_parts(qa_ref[...], lse_ref[...]))
    dx = pair_of(do, with_parts(zero, delta))
    qm = pair_of(q, zero)
    dm = pair_of(do, zero)
    dq_acc[...] = jnp.zeros_like(dq_acc)

    def step(key, _, size, masked=False):
        at = pl.ds(key, size)
        dq = dk = dv = None
        for h in range(2):
            st = nt(kx[h, at, :], qx[h])
            pt = jnp.exp2(below(st, False) if masked else st)
            dp = nt(vx[h, at, :], dx[h])
            ds = (pt * dp).astype(BF)
            tv, tk, tq = nn(pt.astype(BF), dm[h]), nn(ds, qm[h]), tn(ds, km[h, at, :])
            dv = tv if dv is None else dv + tv
            dk = tk if dk is None else dk + tk
            dq = tq if dq is None else dq + tq
        dv_acc[at, :] += dv
        dk_acc[at, :] += dk
        dq_acc[...] += dq

    end = sweep(step, lo, full, odd, grain, unroll)
    if diag:
        step(end, 0, rows, True)
    dq_ref[...] = (dq_acc[...] * SCALE).astype(dq_ref.dtype)


def cross_forward_kernel(
    q_ref, k_ref, v_ref, qa_ref, ka_ref, o_ref, lse_ref, kx, vx, s_scr, m_scr, a_scr
):
    @pl.when(pl.program_id(1) == 0)
    def _():
        forward_prep(k_ref, v_ref, ka_ref, kx, vx)

    full = k_ref.shape[0] // CHUNK
    forward_block(
        0, full, None, CHUNK, False, q_ref, qa_ref, kx, vx, o_ref, lse_ref, s_scr, m_scr, a_scr, full
    )


def cross_forward(q, kv, qa, ka):
    rows, width = q.shape
    keys = kv.shape[0]
    block = min(512, rows)
    pairs = width // 128
    row = pl.BlockSpec((block, 128), lambda h, i: (i, h))
    return pl.pallas_call(
        cross_forward_kernel,
        grid=(pairs, rows // block),
        in_specs=[
            row,
            pl.BlockSpec((keys, 128), lambda h, i: (0, h)),
            pl.BlockSpec((keys, 128), lambda h, i: (0, h + pairs)),
            pl.BlockSpec((block, 128), lambda h, i: (i, 0)),
            pl.BlockSpec((keys, 128), lambda h, i: (0, 0)),
        ],
        out_specs=[row, row],
        out_shape=[
            jax.ShapeDtypeStruct((rows, width), BF),
            jax.ShapeDtypeStruct((rows, width), F32),
        ],
        scratch_shapes=forward_scratch(block, keys),
        compiler_params=params(48),
        cost_estimate=cost(16 * rows * keys * width, 8 * rows * width, rows * keys * 12),
        name="cross_forward",
    )(q, kv, kv, qa, ka)


def cross_backward_kernel(
    q_ref, k_ref, v_ref, do_ref, o_ref, lse_ref, qa_ref, ka_ref,
    dq_ref, dk_ref, dv_ref, kx, vx, km, dk_acc, dv_acc, dq_acc,
):
    @pl.when(pl.program_id(1) == 0)
    def _():
        backward_prep(k_ref, v_ref, ka_ref, kx, vx, km, dk_acc, dv_acc)

    backward_block(
        0, k_ref.shape[0] // CHUNK, None, CHUNK, False, q_ref[...], do_ref[...], o_ref, lse_ref,
        qa_ref, kx, vx, km, dq_ref, dk_acc, dv_acc, dq_acc, 2,
    )

    @pl.when(pl.program_id(1) == pl.num_programs(1) - 1)
    def _():
        dk_ref[...] = (dk_acc[...] * LN2).astype(BF)
        dv_ref[...] = dv_acc[...].astype(BF)


def cross_backward(q, kv, do, o, lse, qa, ka):
    rows, width = q.shape
    keys = kv.shape[0]
    block = min(512, rows)
    pairs = width // 128
    row = pl.BlockSpec((block, 128), lambda h, i: (i, h))
    col = pl.BlockSpec((keys, 128), lambda h, i: (0, h))
    return pl.pallas_call(
        cross_backward_kernel,
        grid=(pairs, rows // block),
        in_specs=[
            row,
            col,
            pl.BlockSpec((keys, 128), lambda h, i: (0, h + pairs)),
            row,
            row,
            row,
            pl.BlockSpec((block, 128), lambda h, i: (i, 0)),
            pl.BlockSpec((keys, 128), lambda h, i: (0, 0)),
        ],
        out_specs=[row, col, col],
        out_shape=[
            jax.ShapeDtypeStruct((rows, width), BF),
            jax.ShapeDtypeStruct((keys, width), BF),
            jax.ShapeDtypeStruct((keys, width), BF),
        ],
        scratch_shapes=backward_scratch(block, keys),
        compiler_params=params(48),
        cost_estimate=cost(40 * rows * keys * width, 12 * rows * width, rows * keys * 12),
        name="cross_backward",
    )(q, kv, kv, do, o, lse, qa, ka)


def grain_of(block):
    return min(256, block)


def needed_blocks(segs, block):
    total = segs.shape[0]
    grain = grain_of(block)
    first = segs.reshape(total // block, block)[:, 0]
    start = jnp.sum((segs[None, :] < first[:, None]).astype(jnp.int32), axis=1)
    ends = (jnp.arange(total // block, dtype=jnp.int32) + 1) * block
    return (ends - start // grain * grain) // grain


def self_range(count, i, block):
    grain = grain_of(block)
    before = count - block // grain
    per = CHUNK // grain
    lo = pl.multiple_of((i + 1) * block - count * grain, grain)
    return lo, before // per, before % per, grain


def self_forward_kernel(
    count_ref, slot_ref, q_ref, k_ref, v_ref, qa_ref, ka_ref, o_ref, lse_ref,
    kx, vx, s_scr, m_scr, a_scr,
):
    i = pl.program_id(1)

    @pl.when(i == 0)
    def _():
        forward_prep(k_ref, v_ref, ka_ref, kx, vx)

    forward_block(
        *self_range(count_ref[i], i, q_ref.shape[0]), True, q_ref, qa_ref, kx, vx, o_ref, lse_ref,
        s_scr, m_scr, a_scr, 1,
    )


def self_forward(counts, slots, q, k, v, qa, ka, block):
    total, width = q.shape
    row = pl.BlockSpec((block, 128), lambda h, i, n, s: (i, h))
    col = pl.BlockSpec((total, 128), lambda h, i, n, s: (0, h))
    return pl.pallas_call(
        self_forward_kernel,
        grid_spec=pltpu.PrefetchScalarGridSpec(
            num_scalar_prefetch=2,
            grid=(width // 128, total // block),
            in_specs=[
                row,
                col,
                col,
                pl.BlockSpec((block, 128), lambda h, i, n, s: (i, 0)),
                pl.BlockSpec((total, 128), lambda h, i, n, s: (0, 0)),
            ],
            out_specs=[pl.BlockSpec((block, 128), lambda h, i, n, s: (s[i], h)), row],
            scratch_shapes=forward_scratch(block, total),
        ),
        out_shape=[
            jax.ShapeDtypeStruct((total, width), BF),
            jax.ShapeDtypeStruct((total, width), F32),
        ],
        compiler_params=params(48),
        cost_estimate=cost(8 * total * total * width, 8 * total * width, total * total * 3),
        name="self_forward",
    )(counts, slots, q, k, v, qa, ka)


def self_backward_kernel(
    count_ref, slot_ref, q_ref, k_ref, v_ref, own_ref, far_ref, o_ref, lse_ref, qa_ref, ka_ref,
    dq_ref, dk_ref, dv_ref, kx, vx, km, dk_acc, dv_acc, dq_acc, *, per_dev,
):
    i = pl.program_id(0)
    do = jnp.where(slot_ref[i] < per_dev, own_ref[...], far_ref[...])

    @pl.when(i == 0)
    def _():
        backward_prep(k_ref, v_ref, ka_ref, kx, vx, km, dk_acc, dv_acc)

    backward_block(
        *self_range(count_ref[i], i, q_ref.shape[0]), True, q_ref[...], do, o_ref, lse_ref, qa_ref,
        kx, vx, km, dq_ref, dk_acc, dv_acc, dq_acc, 1,
    )

    @pl.when(i == pl.num_programs(0) - 1)
    def _():
        dk_ref[...] = (dk_acc[...] * LN2).astype(BF)
        dv_ref[...] = dv_acc[...].astype(BF)


def self_backward(pair, counts, slots, q, k, v, own, far, o, lse, qa, ka, block):
    total = q.shape[0]
    per_dev = own.shape[0] // block
    row = pl.BlockSpec((block, 128), lambda i, n, s: (i, pair))
    col = pl.BlockSpec((total, 128), lambda i, n, s: (0, pair))
    whole = pl.BlockSpec((total, 128), lambda i, n, s: (0, 0))
    return pl.pallas_call(
        functools.partial(self_backward_kernel, per_dev=per_dev),
        grid_spec=pltpu.PrefetchScalarGridSpec(
            num_scalar_prefetch=2,
            grid=(total // block,),
            in_specs=[
                row,
                col,
                col,
                pl.BlockSpec((block, 128), lambda i, n, s: (jnp.minimum(s[i], per_dev - 1), pair)),
                pl.BlockSpec((block, 128), lambda i, n, s: (jnp.maximum(s[i] - per_dev, 0), pair)),
                pl.BlockSpec((block, 128), lambda i, n, s: (s[i], pair)),
                row,
                pl.BlockSpec((block, 128), lambda i, n, s: (i, 0)),
                whole,
            ],
            out_specs=[pl.BlockSpec((block, 128), lambda i, n, s: (i, 0)), whole, whole],
            scratch_shapes=backward_scratch(block, total),
        ),
        out_shape=[jax.ShapeDtypeStruct((total, 128), BF)] * 3,
        compiler_params=params(48),
        cost_estimate=cost(20 * total * total * 128, 12 * total * 128, total * total),
        name="self_backward",
    )(counts, slots, q, k, v, own, far, o, lse, qa, ka)


def qkv_kernel(order_ref, own_ref, far_ref, g_ref, w_ref, n_ref, q_ref, k_ref, v_ref, *, per_dev):
    x = jnp.where(pl.program_id(0) < per_dev, own_ref[...], far_ref[...]).astype(F32)
    n = (x * rms_scale(x) * g_ref[...]).astype(BF)
    n_ref[...] = n
    width = q_ref.shape[1]
    out = nn(n, w_ref[...])
    q_ref[...] = (out[:, :width] * QSCALE).astype(BF)
    k_ref[...] = out[:, width : 2 * width].astype(BF)
    v_ref[...] = out[:, 2 * width :].astype(BF)


def qkv_forward(order, own, far, gain, w, block):
    dim = own.shape[1]
    total = own.shape[0] + far.shape[0]
    width = w.shape[1] // 3
    per_dev = own.shape[0] // block
    here = lambda i, o: (o[i], 0)
    whole = lambda i, o: (0, 0)
    return pl.pallas_call(
        functools.partial(qkv_kernel, per_dev=per_dev),
        grid_spec=pltpu.PrefetchScalarGridSpec(
            num_scalar_prefetch=1,
            grid=(total // block,),
            in_specs=[
                pl.BlockSpec((block, dim), lambda i, o: (jnp.minimum(i, per_dev - 1), 0)),
                pl.BlockSpec((block, dim), lambda i, o: (jnp.maximum(i - per_dev, 0), 0)),
                pl.BlockSpec((1, dim), whole),
                pl.BlockSpec(w.shape, whole),
            ],
            out_specs=[pl.BlockSpec((block, dim), here)] + [pl.BlockSpec((block, width), here)] * 3,
        ),
        out_shape=[jax.ShapeDtypeStruct((total, dim), BF)]
        + [jax.ShapeDtypeStruct((total, width), BF)] * 3,
        compiler_params=params(48),
        cost_estimate=cost(6 * total * dim * width, 8 * total * dim),
        name="qkv_forward",
    )(order, own, far, gain, w)


def enc_kv_kernel(own_ref, far_ref, w_ref, kv_ref, *, own_blocks):
    enc = jnp.where(pl.program_id(0) < own_blocks, own_ref[...], far_ref[...])
    half = w_ref.shape[1] // 2
    for c in range(2):
        at = slice(c * half, (c + 1) * half)
        kv_ref[:, at] = nn(enc, w_ref[:, at]).astype(BF)


def enc_forward(own, far, w2):
    rows, dim = own.shape
    block = min(512, rows)
    keys = rows + far.shape[0]
    ours = rows // block
    return pl.pallas_call(
        functools.partial(enc_kv_kernel, own_blocks=ours),
        grid=(keys // block,),
        in_specs=[
            pl.BlockSpec((block, dim), lambda i: (jnp.minimum(i, ours - 1), 0)),
            pl.BlockSpec((block, dim), lambda i: (jnp.maximum(i - ours, 0), 0)),
            pl.BlockSpec((dim, 2 * dim), lambda i: (0, 1)),
        ],
        out_specs=pl.BlockSpec((block, 2 * dim), lambda i: (i, 0)),
        out_shape=jax.ShapeDtypeStruct((keys, 2 * dim), BF),
        compiler_params=params(48),
        cost_estimate=cost(4 * keys * dim * dim, 8 * keys * dim),
        name="enc_forward",
    )(own, far, w2)


def after_self_kernel(turn_ref, x_ref, *refs, count):
    o_refs, w_refs = refs[:count], refs[count : 2 * count]
    g_ref, wq_ref, h_ref, n_ref, q_ref, s_ref = refs[2 * count :]
    x = x_ref[...].astype(F32)
    a = nn(o_refs[0][...], w_refs[0][...])
    for o_ref, w_ref in zip(o_refs[1:], w_refs[1:]):
        a = a + nn(o_ref[...], w_ref[...])
    h = x + a
    h_ref[...] = h
    n = (h * rms_scale(h) * g_ref[...]).astype(BF)
    n_ref[...] = n
    q_ref[...] = (nn(n, wq_ref[...]) * QSCALE).astype(BF)

    @pl.when(pl.program_id(0) == 0)
    def _():
        s_ref[...] = jnp.zeros_like(s_ref)

    s_ref[0:1, :] += jnp.sum(x * x, axis=0, keepdims=True)
    s_ref[1:2, :] += jnp.sum(a * a, axis=0, keepdims=True)


def turn_specs(count, width, dim):
    return [pl.BlockSpec((width, dim), lambda i, t, k=k: (t[k], 0)) for k in range(count)]


def after_self(turn, x, pieces, wo, gain, w2):
    rows, dim = x.shape
    count, width = len(pieces), pieces[0].shape[1]
    block = min(512, rows)
    line = lambda i, t: (i, 0)
    whole = lambda i, t: (0, 0)
    row = pl.BlockSpec((block, dim), line)
    return pl.pallas_call(
        functools.partial(after_self_kernel, count=count),
        grid_spec=pltpu.PrefetchScalarGridSpec(
            num_scalar_prefetch=1,
            grid=(rows // block,),
            in_specs=[row]
            + [pl.BlockSpec((block, width), line)] * count
            + turn_specs(count, width, dim)
            + [pl.BlockSpec((1, dim), whole), pl.BlockSpec((dim, dim), lambda i, t: (0, 1))],
            out_specs=[row, row, row, pl.BlockSpec((8, dim), whole)],
        ),
        out_shape=[
            jax.ShapeDtypeStruct((rows, dim), F32),
            jax.ShapeDtypeStruct((rows, dim), BF),
            jax.ShapeDtypeStruct((rows, dim), BF),
            jax.ShapeDtypeStruct((8, dim), F32),
        ],
        compiler_params=params(56),
        cost_estimate=cost(4 * rows * dim * dim, 14 * rows * dim),
        name="after_self",
    )(turn, x, *pieces, *([wo] * count), gain, w2)


GELU_C = math.sqrt(2.0 / math.pi)
GELU_A = 0.044715


PIECES = (4, 8, 3, 64)


def mlp_kernel(
    o_ref, h1_ref, wc_ref, g_ref, t_ref, gu_ref, wd_ref,
    y_ref, dh_ref, dc_ref, do_ref, s_ref, g_out,
    n_scr, h_scr, m_scr, dn_scr, hid_scr, du_scr, dw_scr, wg_scr, wu_scr, gu_out, d_out, sems,
):
    j = pl.program_id(0)
    last = pl.num_programs(0) - 1
    rows = o_ref.shape[0]
    step = min(256, rows)
    spans = [pl.ds(r, step) for r in range(0, rows, step)]
    gain = g_ref[...]
    n_fsdp, n_two, _, tall, _ = gu_ref.shape
    third = 256
    high = 3 * tall

    @pl.when(j == 0)
    def _():
        total = None
        for at in spans:
            c = nn(o_ref[at, :], wc_ref[...])
            h = h1_ref[at, :] + c
            h_scr[at, :] = h
            n_scr[at, :] = (h * rms_scale(h) * gain).astype(BF)
            part = jnp.sum(c * c, axis=0, keepdims=True)
            total = part if total is None else total + part
        s_ref[...] = jnp.zeros_like(s_ref)
        s_ref[0:1, :] = total
        m_scr[...] = jnp.zeros_like(m_scr)
        dn_scr[...] = jnp.zeros_like(dn_scr)

    for z in range(n_fsdp):
        for p in range(n_two):
            for t in range(3):
                at, to = pl.ds(z * high + t * tall, tall), pl.ds(p * third, third)
                wg_scr[at, to] = gu_ref[z, p, 0, :, t * third : (t + 1) * third]
                wu_scr[at, to] = gu_ref[z, p, 1, :, t * third : (t + 1) * third]
    wg, wu = wg_scr[...], wu_scr[...]
    wd = wd_ref[...].reshape(-1, wd_ref.shape[-1])
    for at in spans:
        n = n_scr[at, :]
        u = nn(n, wg)
        w = nn(n, wu)
        dhid = nt(t_ref[at, :], wd)
        square = u * u
        th = jnp.tanh(GELU_C * u * (1.0 + GELU_A * square))
        half = 0.5 * (1.0 + th)
        gel = u * half
        slope = half + 0.5 * u * (1.0 - th * th) * (GELU_C * (1.0 + 3.0 * GELU_A * square))
        hid = (gel * w).astype(BF)
        du = (dhid * w * slope).astype(BF)
        dw = (dhid * gel).astype(BF)
        hid_scr[at, :] = hid
        du_scr[at, :] = du
        dw_scr[at, :] = dw
        m_scr[at, :] += nn(hid, wd)
        dn_scr[at, :] += nt(du, wg) + nt(dw, wu)

    slot = lax.rem(j, 2)

    def copies(step_of, slot_of):
        return (
            pltpu.make_async_copy(
                gu_out.at[slot_of],
                g_out.at[:, pl.ds(step_of * n_two, n_two), pl.ds(0, 2)],
                sems.at[slot_of, 0],
            ),
            pltpu.make_async_copy(d_out.at[slot_of], g_out.at[step_of, :, 2], sems.at[slot_of, 1]),
        )

    @pl.when(j >= 2)
    def _():
        for copy in copies(j - 2, slot):
            copy.wait()

    d_out[slot] = tn(hid_scr[...], t_ref[...]).astype(BF).reshape(d_out.shape[1:])
    for side, source in ((0, du_scr), (1, dw_scr)):
        grad = tn(n_scr[...], source[...]).astype(BF)
        for z in range(n_fsdp):
            for p in range(n_two):
                for t in range(3):
                    gu_out[slot, z, p, side, :, t * third : (t + 1) * third] = grad[
                        z * high + t * tall : z * high + (t + 1) * tall,
                        p * third : (p + 1) * third,
                    ]
    for copy in copies(j, slot):
        copy.start()

    @pl.when(j == last)
    def _():
        total = gains = None
        for at in spans:
            h = h_scr[at, :]
            y = h + m_scr[at, :]
            y_ref[at, :] = y.astype(BF)
            dh, dg = norm_back(h, gain, dn_scr[at, :])
            dh = dh + t_ref[at, :].astype(F32)
            dh_ref[at, :] = dh
            dc = dh.astype(BF)
            dc_ref[at, :] = dc
            do_ref[at, :] = nt(dc, wc_ref[...]).astype(BF)
            part = jnp.sum(y * y, axis=0, keepdims=True)
            total = part if total is None else total + part
            gains = dg if gains is None else gains + dg
        s_ref[1:2, :] = total
        s_ref[2:3, :] = gains
        for copy in copies(j - 1, 1 - slot) + copies(j, slot):
            copy.wait()


def feed_forward(o, h1, w2, gain, cot, w3):
    rows, dim = o.shape
    n_fsdp, n_plane, _, tall, _ = w3.shape
    steps = n_fsdp
    two = n_plane // steps
    width = two * 256
    whole = lambda j: (0, 0)
    once = pl.Buffered(1)
    full = pl.BlockSpec((rows, dim), whole, pipeline_mode=once)
    flops = 18 * rows * dim * width * steps + 6 * rows * dim * dim
    return pl.pallas_call(
        mlp_kernel,
        grid=(steps,),
        in_specs=[
            full,
            full,
            pl.BlockSpec((dim, dim), lambda j: (0, 4), pipeline_mode=once),
            pl.BlockSpec((1, dim), whole),
            full,
            pl.BlockSpec((n_fsdp, two, 2, tall, dim), lambda j: (0, j, 0, 0, 0)),
            pl.BlockSpec((1, n_plane, 1, tall, dim), lambda j: (j, 0, 2, 0, 0)),
        ],
        out_specs=[
            full,
            full,
            full,
            full,
            pl.BlockSpec((8, dim), whole),
            pl.BlockSpec(memory_space=pl.ANY),
        ],
        out_shape=[
            jax.ShapeDtypeStruct((rows, dim), BF),
            jax.ShapeDtypeStruct((rows, dim), F32),
            jax.ShapeDtypeStruct((rows, dim), BF),
            jax.ShapeDtypeStruct((rows, dim), BF),
            jax.ShapeDtypeStruct((8, dim), F32),
            jax.ShapeDtypeStruct(w3.shape, BF),
        ],
        scratch_shapes=[
            pltpu.VMEM((rows, dim), BF),
            pltpu.VMEM((rows, dim), F32),
            pltpu.VMEM((rows, dim), F32),
            pltpu.VMEM((rows, dim), F32),
            pltpu.VMEM((rows, width), BF),
            pltpu.VMEM((rows, width), BF),
            pltpu.VMEM((rows, width), BF),
            pltpu.VMEM((dim, width), BF),
            pltpu.VMEM((dim, width), BF),
            pltpu.VMEM((2, n_fsdp, two, 2, tall, dim), BF),
            pltpu.VMEM((2, n_plane, tall, dim), BF),
            pltpu.SemaphoreType.DMA((2, 2)),
        ],
        compiler_params=params(60),
        cost_estimate=cost(flops, 40 * MIB, rows * width * steps),
        name="feed_forward",
    )(o, h1, w2, gain, cot, w3, w3)


def unpack_kernel(me_ref, p_ref, gate_ref, up_ref, down_ref):
    core, x, place = me_ref[0], me_ref[1], me_ref[2]
    tall = p_ref.shape[4]
    third = 256
    for p in range(8):
        near = (core ^ ((p // 2) % 2), x ^ (p // 4), place ^ (p % 2))
        for t in range(3):
            at, to = pl.ds(t * tall, tall), pl.ds(p * third, third)
            lane = slice(t * third, (t + 1) * third)
            gate_ref[at, to] = p_ref[near + (0, slice(None), lane)].astype(F32)
            up_ref[at, to] = p_ref[near + (1, slice(None), lane)].astype(F32)
        down_ref[pl.ds(p * tall, tall), :] = p_ref[near + (2,)].astype(F32)


def unpack(me, pieces):
    tall, dim = pieces.shape[-2:]
    vmem = pl.BlockSpec(memory_space=pltpu.VMEM)
    return pl.pallas_call(
        unpack_kernel,
        in_specs=[pl.BlockSpec(memory_space=pltpu.SMEM), vmem],
        out_specs=[vmem] * 3,
        out_shape=[
            jax.ShapeDtypeStruct((3 * tall, 8 * 256), F32),
            jax.ShapeDtypeStruct((3 * tall, 8 * 256), F32),
            jax.ShapeDtypeStruct((8 * tall, dim), F32),
        ],
        compiler_params=params(32),
        name="unpack",
    )(me, pieces)


def deal_rows(core, full, send_ref, keep_ref):
    count, size = send_ref.shape[:2]
    for i in range(count):
        for ref, c in ((send_ref, 1 - core), (keep_ref, core)):
            ref[i] = full[pl.ds(pl.multiple_of((2 * i + c) * size, 16), size), :]


def mid_grads_kernel(turn_ref, core_ref, *refs, count, deal):
    o_refs = refs[:count]
    da_ref, n2_ref, dq_ref, own_ref, far_ref, dk_ref, dv_ref, o2_ref, dc_ref = refs[count : count + 9]
    outs = refs[count + 9 :]
    full = outs[-1]
    m = pl.program_id(0)
    dim = full.shape[0]
    width = o_refs[0].shape[1]
    ours = own_ref.shape[0]

    @pl.when(m == 0)
    def _():
        for i in range(count):
            base = pl.multiple_of(turn_ref[i] * width, width)
            term = tn(o_refs[i][...], da_ref[...]).astype(BF)

            @pl.when(base < dim)
            def _():
                full[pl.ds(base, width), :] = term

    for at, right in ((2, dk_ref), (3, dv_ref)):

        @pl.when(m == at)
        def _():
            total = tn(own_ref[...], right[:ours, :]) + tn(far_ref[...], right[ours:, :])
            full[...] = total.astype(BF)

    for at, left, right in ((1, n2_ref, dq_ref), (4, o2_ref, dc_ref)):

        @pl.when(m == at)
        def _():
            full[...] = tn(left[...], right[...]).astype(BF)

    if deal:
        deal_rows(core_ref[0], full, outs[0], outs[1])
    else:
        outs[0][...] = full[...]


def dealt_out(dim, block, total, index, deal):
    if not deal:
        return [pl.BlockSpec((dim, block), lambda *a: (0, index(*a)))], [
            jax.ShapeDtypeStruct((dim, total), BF)
        ]
    spec = pl.BlockSpec((8, dim // 16, block), lambda *a: (0, 0, index(*a)))
    return [spec] * 2, [jax.ShapeDtypeStruct((8, dim // 16, total), BF)] * 2


def mid_grads(turn, core, pieces, da, n2, dq2, own, far, dk2, dv2, o2, dc, deal):
    rows, dim = n2.shape
    args = (*pieces, da, n2, dq2, own, far, dk2, dv2, o2, dc)
    shapes = [(rows, a.shape[1]) for a in pieces] + [a.shape for a in args[len(pieces) :]]
    flops = 2 * dim * dim * (3 * rows + 2 * dk2.shape[0])
    specs, outs = dealt_out(dim, dim, 5 * dim, lambda m, t, c: m, deal)
    return pl.pallas_call(
        functools.partial(mid_grads_kernel, count=len(pieces), deal=deal),
        grid_spec=pltpu.PrefetchScalarGridSpec(
            num_scalar_prefetch=2,
            grid=(5,),
            in_specs=[
                pl.BlockSpec(shape, lambda m, t, c: (0, 0), pipeline_mode=pl.Buffered(1))
                for shape in shapes
            ],
            out_specs=specs,
            scratch_shapes=[pltpu.VMEM((dim, dim), BF)],
        ),
        out_shape=outs,
        compiler_params=params(48),
        cost_estimate=cost(flops, 24 * MIB),
        name="mid_grads",
    )(turn, core, *args)


def enc_back_kernel(dk_ref, dv_ref, wk_ref, wv_ref, far_ref, own_ref, *, far_blocks):
    d = nt(dk_ref[...], wk_ref[...]) + nt(dv_ref[...], wv_ref[...])

    @pl.when(pl.program_id(0) < far_blocks)
    def _():
        far_ref[...] = d.astype(BF)

    @pl.when(pl.program_id(0) >= far_blocks)
    def _():
        own_ref[...] = d


def enc_backward(dk, dv, w2, own_rows):
    keys, dim = dk.shape
    block = min(512, own_rows)
    blocks, own = keys // block, own_rows // block
    far = blocks - own
    row = pl.BlockSpec((block, dim), lambda i: ((i + own) % blocks, 0))
    return pl.pallas_call(
        functools.partial(enc_back_kernel, far_blocks=far),
        grid=(blocks,),
        in_specs=[
            row,
            row,
            pl.BlockSpec((dim, dim), lambda i: (0, 2)),
            pl.BlockSpec((dim, dim), lambda i: (0, 3)),
        ],
        out_specs=[
            pl.BlockSpec((block, dim), lambda i: (jnp.minimum(i, far - 1), 0)),
            pl.BlockSpec((block, dim), lambda i: (jnp.maximum(i - far, 0), 0)),
        ],
        out_shape=[
            jax.ShapeDtypeStruct((keys - own_rows, dim), BF),
            jax.ShapeDtypeStruct((own_rows, dim), F32),
        ],
        compiler_params=params(48),
        cost_estimate=cost(keys * dim, keys),
        name="enc_backward",
    )(dk, dv, w2, w2)


def before_self_kernel(turn_ref, dq_ref, wq_ref, h_ref, dh_ref, g_ref, *refs, count):
    w_refs = refs[:count]
    d1_ref, da_ref, s_ref = refs[count : count + 3]
    do_refs = refs[count + 3 :]
    dn = nt(dq_ref[...], wq_ref[...])
    dh, dg = norm_back(h_ref[...], g_ref[...], dn)
    d1 = dh_ref[...] + dh
    d1_ref[...] = d1
    da = d1.astype(BF)
    da_ref[...] = da
    for do_ref, w_ref in zip(do_refs, w_refs):
        do_ref[...] = nt(da, w_ref[...]).astype(BF)

    @pl.when(pl.program_id(0) == 0)
    def _():
        s_ref[...] = jnp.zeros_like(s_ref)

    s_ref[0:1, :] += dg


def before_self(turn, dq, w2, h1, dh2, gain, wo, width):
    rows, dim = dq.shape
    count = turn.shape[0]
    block = min(512, rows)
    line = lambda i, t: (i, 0)
    whole = lambda i, t: (0, 0)
    row = pl.BlockSpec((block, dim), line)
    return pl.pallas_call(
        functools.partial(before_self_kernel, count=count),
        grid_spec=pltpu.PrefetchScalarGridSpec(
            num_scalar_prefetch=1,
            grid=(rows // block,),
            in_specs=[
                row,
                pl.BlockSpec((dim, dim), lambda i, t: (0, 1)),
                row,
                row,
                pl.BlockSpec((1, dim), whole),
            ]
            + turn_specs(count, width, dim),
            out_specs=[row, row, pl.BlockSpec((8, dim), whole)]
            + [pl.BlockSpec((block, width), line)] * count,
        ),
        out_shape=[
            jax.ShapeDtypeStruct((rows, dim), F32),
            jax.ShapeDtypeStruct((rows, dim), BF),
            jax.ShapeDtypeStruct((8, dim), F32),
        ]
        + [jax.ShapeDtypeStruct((rows, width), BF)] * count,
        compiler_params=params(56),
        cost_estimate=cost(4 * rows * dim * dim, 18 * rows * dim),
        name="before_self",
    )(turn, dq, w2, h1, dh2, gain, *([wo] * count))


def joined(refs):
    return jnp.concatenate([r[...] for r in refs], axis=1)


def qkv_grads_kernel(core_ref, *refs, count, deal):
    d_refs = refs[:count]
    n_ref, w_ref, gain_ref, extra_ref = refs[count : count + 4]
    outs = refs[count + 4 :]
    acc, full = outs[-2:]
    i = pl.program_id(0)
    term = tn(n_ref[...], joined(d_refs))

    @pl.when(i == 0)
    def _():
        acc[...] = term

    @pl.when(i > 0)
    def _():
        acc[...] += term

    @pl.when(i == pl.num_programs(0) - 1)
    def _():
        width = acc.shape[1]
        grad = acc[...]
        gains = jnp.sum(grad * w_ref[...].astype(F32), axis=1, keepdims=True) / gain_ref[:, :1]
        extra = extra_ref[...]
        full[:, :width] = grad.astype(BF)
        full[:, width:] = jnp.where(lanes(extra.shape) == 0, gains, extra).astype(BF)
        if deal:
            deal_rows(core_ref[0], full, outs[0], outs[1])
        else:
            outs[0][...] = full[...]


def qkv_grads(core, ds, n, w, gain, extra, deal):
    total, dim = n.shape
    block = min(512, total)
    width = w.shape[1]
    specs, outs = dealt_out(dim, width + 128, width + 128, lambda i, c: 0, deal)
    whole = lambda i, c: (0, 0)
    return pl.pallas_call(
        functools.partial(qkv_grads_kernel, count=len(ds), deal=deal),
        grid_spec=pltpu.PrefetchScalarGridSpec(
            num_scalar_prefetch=1,
            grid=(total // block,),
            in_specs=[pl.BlockSpec((block, 128), lambda i, c: (i, 0))] * len(ds)
            + [
                pl.BlockSpec((block, dim), lambda i, c: (i, 0)),
                pl.BlockSpec(w.shape, whole),
                pl.BlockSpec((dim, 128), whole),
                pl.BlockSpec((dim, 128), whole),
            ],
            out_specs=specs,
            scratch_shapes=[pltpu.VMEM((dim, width), F32), pltpu.VMEM((dim, width + 128), BF)],
        ),
        out_shape=outs,
        compiler_params=params(48),
        cost_estimate=cost(2 * total * dim * width, 6 * total * dim),
        name="qkv_grads",
    )(core, *ds, n, w, gain, extra)


def qkv_back_kernel(order_ref, *refs, count):
    dn_ref = refs[count + 1]
    dn_ref[...] = nt(joined(refs[:count]), refs[count][...]).astype(dn_ref.dtype)


def qkv_back(order, first, ds, w, rows, dtype, block):
    dim = w.shape[0]
    return pl.pallas_call(
        functools.partial(qkv_back_kernel, count=len(ds)),
        grid_spec=pltpu.PrefetchScalarGridSpec(
            num_scalar_prefetch=1,
            grid=(rows // block,),
            in_specs=[pl.BlockSpec((block, 128), lambda i, o: (o[i + first], 0))] * len(ds)
            + [pl.BlockSpec(w.shape, lambda i, o: (0, 0))],
            out_specs=pl.BlockSpec((block, dim), lambda i, o: (i, 0)),
        ),
        out_shape=jax.ShapeDtypeStruct((rows, dim), dtype),
        compiler_params=params(48),
        cost_estimate=cost(2 * rows * dim * w.shape[1], 10 * rows * dim),
        name="qkv_back",
    )(order, *ds, w)


def finish_kernel(x_ref, dh_ref, g_ref, own_ref, *refs):
    dn = own_ref[...]
    for ref in refs[:-1]:
        dn = dn + ref[...].astype(F32)
    dh, _ = norm_back(x_ref[...].astype(F32), g_ref[...], dn)
    refs[-1][...] = dh_ref[...] + dh


def finish(x, dh1, gain, own, got):
    rows, dim = x.shape
    block = min(256, rows)
    row = pl.BlockSpec((block, dim), lambda i: (i, 0))
    return pl.pallas_call(
        finish_kernel,
        grid=(rows // block,),
        in_specs=[row, row, pl.BlockSpec((1, dim), lambda i: (0, 0)), row] + [row] * len(got),
        out_specs=row,
        out_shape=jax.ShapeDtypeStruct((rows, dim), F32),
        compiler_params=params(32),
        cost_estimate=cost(10 * rows * dim, 16 * rows * dim),
        name="finish",
    )(x, dh1, gain, own, *got)


def turned(n, k):
    return [(i, (i + k) % n) for i in range(n)]


def rows_of(array, index, count):
    size = array.shape[0] // count
    return lax.dynamic_slice_in_dim(array, index * size, size, 0)


def assemble_kernel(place_ref, near_ref, far_ref, w_ref, g_ref):
    z, core = place_ref[0], place_ref[1]
    count, size = near_ref.shape[0], near_ref.shape[1]
    width = w_ref.shape[1]
    for d in range(count):
        base = lax.rem(z - d + count, count) * (2 * size)
        for ref, half in ((near_ref, core), (far_ref, 1 - core)):
            at = pl.ds(pl.multiple_of(base + half * size, 16), size)
            w_ref[at, :] = ref[d, :, :width]
            g_ref[at, :] = ref[d, :, width:]


def gather_first(own, z, part, n_fsdp, n_parts):
    size = own.shape[0] // 2
    width = own.shape[1] - 128
    if n_parts % 2 or size % 16:
        full = lax.all_gather(own, "fsdp", axis=0, tiled=True)
        return full[:, :width], full[:, width:]
    core = part % 2
    mine = lax.dynamic_slice_in_dim(own, core * size, size, 0)
    near = jnp.stack(
        [mine] + [lax.ppermute(mine, "fsdp", turned(n_fsdp, d)) for d in range(1, n_fsdp)]
    )
    far = lax.ppermute(near, "parts", [(i, i ^ 1) for i in range(n_parts)])
    vmem = pl.BlockSpec(memory_space=pltpu.VMEM)
    total = n_fsdp * own.shape[0]
    return pl.pallas_call(
        assemble_kernel,
        in_specs=[pl.BlockSpec(memory_space=pltpu.SMEM), vmem, vmem],
        out_specs=[vmem, vmem],
        out_shape=[
            jax.ShapeDtypeStruct((total, width), BF),
            jax.ShapeDtypeStruct((total, 128), BF),
        ],
        compiler_params=params(32),
        name="assemble",
    )(jnp.stack([z, core]).astype(jnp.int32), near, far)


def pick(array, index, axis):
    return lax.dynamic_index_in_dim(array, index, axis, keepdims=False)


class Plane:
    def __init__(self, part, place, z, n_parts, n_fsdp):
        self.core, self.x, self.place, self.z = part % 2, part // 2, place, z
        self.n_fsdp = n_fsdp
        self.swap_core = [(i, i ^ 1) for i in range(n_parts)]
        self.swap_x = [(i, i ^ 2) for i in range(n_parts)]

    def over_core(self, send, keep):
        shape = (self.n_fsdp, 2) + send.shape[1:]
        got = lax.ppermute(send, "parts", self.swap_core).reshape(shape)
        keep = keep.reshape(shape)
        add = lambda i: (pick(keep, i, 1).astype(F32) + pick(got, i, 1).astype(F32)).astype(BF)
        return add(1 - self.x), add(self.x)

    def over_x(self, send, keep):
        got = lax.ppermute(send, "parts", self.swap_x)
        return (keep.astype(F32) + got.astype(F32)).astype(BF)

    def over_fsdp(self, g):
        total = pick(g, self.z, 0).astype(F32)
        for d in range(1, self.n_fsdp):
            piece = pick(g, (self.z + d) % self.n_fsdp, 0)
            total = total + lax.ppermute(piece, "fsdp", turned(self.n_fsdp, d)).astype(F32)
        return total.astype(BF)

    def over_ctx(self, g):
        return (g.astype(F32) + lax.ppermute(g, "ctx", turned(2, 1)).astype(F32)).astype(BF)

    def widen_ctx(self, g):
        return jnp.stack([g, lax.ppermute(g, "ctx", turned(2, 1))])

    def widen(self, g):
        g = jnp.stack([g, lax.ppermute(g, "parts", self.swap_x)])
        return jnp.stack([g, lax.ppermute(g, "parts", self.swap_core)])

    def rows(self, wide):
        pieces = [
            lax.dynamic_slice(
                wide, (c ^ self.core, a ^ self.x, 0, 0), (1, 1) + wide.shape[2:]
            )[0, 0]
            for a in range(2)
            for c in range(2)
        ]
        return jnp.concatenate(pieces).astype(F32)


def local(
    mesh_shape,
    decoder_in,
    encoder_out,
    segment_ids,
    block_order,
    prompt_len,
    self_query,
    self_key,
    self_value,
    self_output,
    cross_query,
    cross_key,
    cross_value,
    cross_output,
    gate_in,
    up_in,
    down_out,
    norm_self,
    norm_cross,
    norm_mlp,
    cotangent,
):
    n_parts, n_ctx, n_fsdp = mesh_shape
    part, place, z = lax.axis_index("parts"), lax.axis_index("ctx"), lax.axis_index("fsdp")
    plane, n_plane = part * n_ctx + place, n_parts * n_ctx
    x_own, enc_own = decoder_in[0], encoder_out[0]
    rows, dim = x_own.shape
    segs, order = segment_ids[0], block_order[0]
    total = segs.shape[0]
    slots_total = order.shape[0]
    block = total // slots_total
    per_dev = slots_total // n_ctx
    enc_rows = enc_own.shape[0]
    keys = enc_rows * n_ctx
    hidden = down_out.shape[0] * n_fsdp
    heads_here = 2 * -(-HEADS // (2 * n_ctx))
    width = heads_here * HEAD
    padded = width * n_ctx

    ring = (place + jnp.arange(n_ctx, dtype=jnp.int32)) % n_ctx
    order_here = jnp.roll(order, -per_dev * place)
    slots = jnp.argsort(order_here).astype(jnp.int32)
    counts = needed_blocks(segs, block)

    def from_ctx(value):
        pieces = [lax.ppermute(value, "ctx", turned(n_ctx, -k)) for k in range(1, n_ctx)]
        return pieces[0] if n_ctx == 2 else jnp.concatenate(pieces, axis=0)

    x_far = from_ctx(x_own)

    fast = (n_parts, n_ctx, n_fsdp) == (4, 2, 4)
    shard = dim // n_fsdp

    def own_heads(w):
        w = jnp.pad(w, ((0, 0), (0, padded - dim)))
        return lax.dynamic_slice_in_dim(w, place * width, width, 1)

    gain_cols = jnp.pad(jnp.stack([norm_self, norm_cross, norm_mlp], axis=1), ((0, 0), (0, 125)))
    w1, gains = gather_first(
        jnp.concatenate(
            [own_heads(self_query), own_heads(self_key), own_heads(self_value), gain_cols], axis=1
        ),
        z, part, n_fsdp, n_parts,
    )
    gains = gains[:, :8].astype(F32).T
    gain_self, gain_cross, gain_mlp = (gains[i : i + 1] for i in range(3))
    mats = (self_output, cross_query, cross_key, cross_value, cross_output)
    if fast:
        w2 = lax.all_gather(
            jnp.concatenate([rows_of(w, plane, n_plane) for w in mats], axis=1),
            ALL, axis=0, tiled=True,
        )

        def column_piece(w):
            cut = lax.dynamic_slice_in_dim(w, plane * 256, 256, 1)
            return jnp.concatenate([cut[t * 64 : (t + 1) * 64] for t in range(3)], axis=1)

        w3 = lax.all_gather(
            jnp.stack(
                [column_piece(gate_in), column_piece(up_in), rows_of(down_out, plane, n_plane)]
            ),
            ALL, axis=0,
        ).reshape(PIECES + (dim,))
    else:
        w2 = lax.all_gather(jnp.concatenate(mats, axis=1), "fsdp", axis=0, tiled=True)

        def packed(w):
            w = lax.all_gather(w, "fsdp", axis=0, tiled=True).reshape(4, 3, 64, 8, 256)
            return w.transpose(0, 3, 2, 1, 4).reshape(4, 8, 64, dim)

        w_down = lax.all_gather(down_out, "fsdp", axis=0, tiled=True).reshape(4, 8, 64, dim)
        w3 = jnp.stack([packed(gate_in), packed(up_in), w_down], axis=2)
    x_far, enc_sent = lax.optimization_barrier((x_far, enc_own))
    enc_far = from_ctx(enc_sent)

    n1, q, k, v = qkv_forward(order_here, x_own, x_far, gain_self, w1, block)
    spot = jnp.arange(128, dtype=jnp.int32)[None, :] % HEAD
    minus = jnp.where((spot >= PART0) & (spot < PART0 + 3), -1.0, 0.0)
    seg_q = jnp.where(spot == segs[:, None], 1.0, 0.0).astype(BF)
    seg_k = jnp.where((spot < SEGS) & (spot != segs[:, None]), -BIG, minus).astype(BF)
    o1, lse1 = self_forward(counts, slots, q, k, v, seg_q, seg_k, block)
    pieces = [o1] + [
        lax.ppermute(o1[i * rows : (i + 1) * rows], "ctx", turned(n_ctx, i)) for i in range(1, n_ctx)
    ]
    turn = (place - jnp.arange(n_ctx, dtype=jnp.int32)) % n_ctx
    wo = w2 if padded == dim else jnp.pad(w2[:, :dim], ((0, padded - dim), (0, 0)))
    kv2 = enc_forward(enc_own, enc_far, w2)
    pieces[1], kv2 = lax.optimization_barrier((pieces[1], kv2))
    h1, n2, q2, stat1 = after_self(turn, x_own, pieces, wo, gain_cross, w2)

    where_key = (ring[:, None] * enc_rows + jnp.arange(enc_rows, dtype=jnp.int32)).reshape(-1, 1)
    len_q = jnp.where(spot == 0, jnp.ones((rows, 1), F32), 0.0).astype(BF)
    len_k = jnp.where((spot == 0) & (where_key >= prompt_len[0]), -BIG, minus).astype(BF)
    o2, lse2 = cross_forward(q2, kv2, len_q, len_k)

    layer_out, dh2, dc, do2, stat2, g_ff = feed_forward(o2, h1, w2, gain_mlp, cotangent[0], w3)
    if fast:
        part_ff = lax.psum_scatter(g_ff.reshape(32, 3, 64, dim), ALL, scatter_dimension=0)

    dq2, dk2, dv2 = cross_backward(q2, kv2, do2, o2, lse2, len_q, len_k)
    dh1, da, stat3, *do1 = before_self(turn, dq2, w2, h1, dh2, gain_cross, wo, width)
    do_far = [lax.ppermute(do1[i], "ctx", turned(n_ctx, -i)) for i in range(1, n_ctx)]
    do_far = do_far[0] if n_ctx == 2 else jnp.concatenate(do_far, axis=0)
    do_own = do1[0]
    core = jnp.reshape(part % 2, (1,)).astype(jnp.int32)
    g_mid = mid_grads(
        turn, core, pieces, da, n2, dq2, enc_own, enc_far, dk2, dv2, o2, dc, fast
    )
    d_far, enc_grad = enc_backward(dk2, dv2, w2, enc_rows)

    sums = jnp.sum(jnp.concatenate([stat1[:2], stat2[:2]], axis=0), axis=1)
    extra = jnp.concatenate(
        [
            jnp.zeros((dim, 1), F32),
            stat2[2][:, None],
            stat3[0][:, None],
            jnp.broadcast_to(sums[None], (dim, 4)),
            jnp.zeros((dim, 121), F32),
        ],
        axis=1,
    )
    gain_wide = jnp.broadcast_to(gain_self.reshape(dim, 1), (dim, 128))

    def self_pair(pair, own, far):
        return self_backward(
            pair, counts, slots, q, k, v, own, far, o1, lse1, seg_q, seg_k, block
        )

    pairs = width // 128
    if fast:
        net = Plane(part, place, z, n_parts, n_fsdp)
        send, keep = net.over_core(*g_mid)
        do_own, do_far, send, d_far, extra = lax.optimization_barrier(
            (do_own, do_far, send, d_far, extra)
        )
    enc_got = [
        lax.ppermute(d_far[(i - 1) * enc_rows : i * enc_rows], "ctx", turned(n_ctx, i))
        for i in range(1, n_ctx)
    ]
    if fast:
        by_pair = [self_pair(0, do_own, do_far)]
        g_mid = net.over_x(send, keep)
        g_mid, do_far = lax.optimization_barrier((g_mid, by_pair[0][0], do_far))[::2]
        by_pair.append(self_pair(1, do_own, do_far))
        g_mid = net.over_fsdp(g_mid)
        g_mid, part_ff, enc_got, do_far = lax.optimization_barrier(
            (g_mid, part_ff, enc_got, do_far, by_pair[1][0])
        )[:4]
        by_pair.append(self_pair(2, do_own, do_far))
        wide_ff = net.widen_ctx(part_ff)
        g_mid = net.over_ctx(g_mid)
        by_pair[2], wide_ff, g_mid = lax.optimization_barrier((by_pair[2], wide_ff, g_mid))
    else:
        by_pair = [self_pair(i, do_own, do_far) for i in range(pairs)]
    for piece in enc_got:
        enc_grad = enc_grad + piece.astype(F32)
    ds = [d[i] for i in range(3) for d in by_pair]
    g_qkv = qkv_grads(core, ds, n1, w1, gain_wide, extra, fast)
    dn_far = qkv_back(order_here, per_dev, ds, w1, total - rows, BF, block)
    dn_got = [
        lax.ppermute(dn_far[(i - 1) * rows : i * rows], "ctx", turned(n_ctx, i))
        for i in range(1, n_ctx)
    ]
    dn_own = qkv_back(order_here, 0, ds, w1, rows, F32, block)
    decoder_grad = finish(x_own, dh1, gain_self, dn_own, dn_got)

    if fast:
        send, keep = net.over_core(*g_qkv)
        sum_mid = net.rows(net.widen(g_mid))
        me = jnp.stack([net.core, net.x, place]).astype(jnp.int32)
        grad_gate, grad_up, grad_down = unpack(me, net.widen(wide_ff))
        wide = net.widen(net.widen_ctx(net.over_fsdp(net.over_x(send, keep))))
        every = jnp.stack([net.rows(pick(wide, i ^ place, 2)) for i in range(2)])
    else:

        def total_of(g):
            g = lax.psum_scatter(g, "fsdp", scatter_dimension=0, tiled=True).astype(F32)
            return lax.psum(g, ("parts", "ctx"))

        (g_mid,), (g_qkv,) = g_mid, g_qkv
        sum_mid = total_of(g_mid)
        flat = [
            g_ff[:, :, i].reshape(4, 8, 64, 3, 256).transpose(0, 3, 2, 1, 4).reshape(dim, hidden)
            for i in range(2)
        ]
        grad_gate, grad_up = total_of(flat[0]), total_of(flat[1])
        grad_down = total_of(g_ff[:, :, 2].reshape(hidden, dim))
        sum_qkv = lax.psum_scatter(g_qkv, "fsdp", scatter_dimension=0, tiled=True).astype(F32)
        every = lax.all_gather(lax.psum(sum_qkv, "parts"), "ctx", axis=0)
    grads_qkv = [
        jnp.concatenate([every[c, :, i * width : (i + 1) * width] for c in range(n_ctx)], axis=1)[:, :dim]
        for i in range(3)
    ]
    tail = jnp.sum(every[:, :, 3 * width : 3 * width + 8], axis=0)
    grad_gself, grad_gmlp, grad_gcross = tail[:, 0], tail[:, 1], tail[:, 2]
    entries = float(n_parts * n_ctx * n_fsdp * rows * dim)
    rms_values = jnp.sqrt(tail[0, jnp.array([3, 4, 5, 6])] / entries)
    mids = [sum_mid[:, i * dim : (i + 1) * dim] for i in range(5)]
    return (
        layer_out[None],
        decoder_grad[None],
        enc_grad[None],
        *grads_qkv,
        *mids,
        grad_gate,
        grad_up,
        grad_down,
        grad_gself,
        grad_gcross,
        grad_gmlp,
        rms_values,
    )


def solution(mesh):
    rows3 = P(("parts", "fsdp"), "ctx", None)
    group = P(("parts", "fsdp"), None)
    matrix, vector = P("fsdp", None), P("fsdp")
    shape = tuple(mesh.shape[a] for a in ("parts", "ctx", "fsdp"))
    return jax.shard_map(
        functools.partial(local, shape),
        mesh=mesh,
        in_specs=(rows3, rows3, group, group, P(("parts", "fsdp")))
        + (matrix,) * 11
        + (vector,) * 3
        + (rows3,),
        out_specs=(rows3,) * 3 + (matrix,) * 11 + (vector,) * 3 + (P(),),
        check_vma=False,
    )
```

```python
import functools
import math

import jax
import jax.numpy as jnp
from jax import lax
from jax.experimental import pallas as pl
from jax.experimental.pallas import tpu as pltpu
from jax.sharding import PartitionSpec as P

HEADS = 12
HEAD = 64
SCALE = 0.125
EPS = 1e-06
BIG = 1e30
LN2 = math.log(2.0)
QSCALE = SCALE * math.log2(math.e)
PART0 = 16
SEGS = 16
BF = jnp.bfloat16
F32 = jnp.float32
MIB = 1 << 20
AROUND = ("fsdp", "parts")


def nn(a, b):
    return lax.dot_general(a, b, (((1,), (0,)), ((), ())), preferred_element_type=F32)


def nt(a, b):
    return lax.dot_general(a, b, (((1,), (1,)), ((), ())), preferred_element_type=F32)


def tn(a, b):
    return lax.dot_general(a, b, (((0,), (0,)), ((), ())), preferred_element_type=F32)


def lanes(shape):
    return lax.broadcasted_iota(jnp.int32, shape, len(shape) - 1)


def params(mib=60):
    return pltpu.CompilerParams(vmem_limit_bytes=mib * MIB)


def cost(flops, moved, exps=0):
    return pl.CostEstimate(flops=int(flops), bytes_accessed=int(moved), transcendentals=int(exps))


def rms_scale(h):
    return lax.rsqrt(jnp.mean(h * h, axis=-1, keepdims=True) + EPS)


def norm_back(h, gain, dn):
    r = rms_scale(h)
    t = dn * gain
    hr = h * r
    dh = r * (t - hr * jnp.mean(t * hr, axis=-1, keepdims=True))
    return dh, jnp.sum(dn * hr, axis=0, keepdims=True)


def with_parts(base, value):
    spot = lanes(base.shape) % HEAD
    hi = value.astype(BF)
    rest = value - hi.astype(F32)
    mid = rest.astype(BF)
    low = (rest - mid.astype(F32)).astype(BF)
    return jnp.where(
        spot == PART0, hi, jnp.where(spot == PART0 + 1, mid, jnp.where(spot == PART0 + 2, low, base))
    )


def pair_of(own, other):
    left = lanes(own.shape) < HEAD
    return jnp.where(left, own, other), jnp.where(left, other, own)


CHUNK = 512


def below(s, rows_first):
    r = lax.broadcasted_iota(jnp.int32, s.shape, 0)
    c = lanes(s.shape)
    return jnp.where(c <= r if rows_first else r <= c, s, -BIG)


def lane_max(s):
    return functools.reduce(jnp.maximum, [s[:, c : c + 128] for c in range(0, s.shape[1], 128)])


def sweep(step, lo, full, odd, grain, unroll):
    base = lo
    if odd is not None:

        @pl.when(odd == 1)
        def _():
            step(lo, 0, grain)

        base = lo + odd * grain

    def body(c, carry):
        step(pl.multiple_of(base + c * CHUNK, grain), pl.multiple_of(grain + c * CHUNK, 128), CHUNK)
        return carry

    lax.fori_loop(0, full, body, 0, unroll=unroll)
    return pl.multiple_of(base + full * CHUNK, grain)


def forward_block(
    lo, full, odd, grain, diag, q_ref, qa_ref, kx, vx, o_ref, lse_ref, s_scr, m_scr, a_scr, unroll
):
    q = q_ref[...]
    rows = q.shape[0]
    left = lanes(q.shape) < HEAD
    sides = pair_of(q, qa_ref[...])
    m_scr[...] = jnp.full_like(m_scr, -BIG)
    a_scr[...] = jnp.zeros_like(a_scr)
    last = s_scr.shape[2] - rows

    def scores(key, at, size, start=None):
        live = pl.ds(start or 0, rows - (start or 0))
        for h in range(2):
            s = nt(sides[h][start or 0 :], kx[h, pl.ds(key, size), :])
            s = s if start is None else below(s, True)
            s_scr[h, live, pl.ds(at, size)] = s
            m_scr[h, live, :] = jnp.maximum(m_scr[h, live, :], lane_max(s))

    steps = range(0, rows, grain) if diag else ()
    end = sweep(scores, lo, full, odd, grain, unroll)
    for start in steps:
        scores(end + start, last + start, grain, start)
    tops = [jnp.max(m_scr[h], axis=1, keepdims=True) for h in range(2)]

    def values(key, at, size, start=0):
        live = pl.ds(start, rows - start)
        for h in range(2):
            p = jnp.exp2(s_scr[h, live, pl.ds(at, size)] - tops[h][start:]).astype(BF)
            a_scr[h, live, :] += nn(p, vx[h, pl.ds(key, size), :])

    end = sweep(values, lo, full, odd, grain, unroll)
    for start in steps:
        values(end + start, last + start, grain, start)
    wide = jnp.where(left, a_scr[0], a_scr[1])
    total = jnp.where(left, a_scr[1], a_scr[0])
    o_ref[...] = (wide / pltpu.roll(total, HEAD, 1)).astype(o_ref.dtype)
    lse_ref[...] = jnp.where(left, tops[1], tops[0]) + jnp.log2(total)


def forward_scratch(block, keys):
    return [
        pltpu.VMEM((2, keys, 128), BF),
        pltpu.VMEM((2, keys, 128), BF),
        pltpu.VMEM((2, block, keys + CHUNK), F32),
        pltpu.VMEM((2, block, 128), F32),
        pltpu.VMEM((2, block, 128), F32),
    ]


def backward_scratch(block, keys):
    return (
        [pltpu.VMEM((2, keys, 128), BF)] * 3
        + [pltpu.VMEM((keys, 128), F32)] * 2
        + [pltpu.VMEM((block, 128), F32)]
    )


def forward_prep(k_ref, v_ref, ka_ref, kx, vx):
    kx[0], kx[1] = pair_of(k_ref[...], ka_ref[...])
    v = v_ref[...]
    vx[0], vx[1] = pair_of(v, jnp.ones_like(v))


def backward_prep(k_ref, v_ref, ka_ref, kx, vx, km, dk_acc, dv_acc):
    k, v = k_ref[...], v_ref[...]
    spot = lanes(v.shape) % HEAD
    neg = jnp.where((spot >= PART0) & (spot < PART0 + 3), -1.0, 0.0).astype(BF)
    kx[0], kx[1] = pair_of(k, ka_ref[...])
    vx[0], vx[1] = pair_of(v, neg)
    km[0], km[1] = pair_of(k, jnp.zeros_like(k))
    dk_acc[...] = jnp.zeros_like(dk_acc)
    dv_acc[...] = jnp.zeros_like(dv_acc)


def backward_block(
    lo, full, odd, grain, diag, q, do, o_ref, lse_ref, qa_ref, kx, vx, km,
    dq_ref, dk_acc, dv_acc, dq_acc, unroll,
):
    left = lanes(q.shape) < HEAD
    rows = q.shape[0]
    product = do.astype(F32) * o_ref[...].astype(F32)
    first = jnp.sum(jnp.where(left, product, 0.0), axis=1, keepdims=True)
    second = jnp.sum(jnp.where(left, 0.0, product), axis=1, keepdims=True)
    delta = jnp.where(left, second, first)
    zero = jnp.zeros_like(q)
    qx = pair_of(q, with_parts(qa_ref[...], lse_ref[...]))
    dx = pair_of(do, with_parts(zero, delta))
    qm = pair_of(q, zero)
    dm = pair_of(do, zero)
    dq_acc[...] = jnp.zeros_like(dq_acc)

    def step(key, _, size, start=None):
        at = pl.ds(key, size)
        live = slice(start or 0, rows)
        dq = dk = dv = None
        for h in range(2):
            st = nt(kx[h, at, :], qx[h][live])
            pt = jnp.exp2(st if start is None else below(st, False))
            dp = nt(vx[h, at, :], dx[h][live])
            ds = (pt * dp).astype(BF)
            tv, tk, tq = nn(pt.astype(BF), dm[h][live]), nn(ds, qm[h][live]), tn(ds, km[h, at, :])
            dv = tv if dv is None else dv + tv
            dk = tk if dk is None else dk + tk
            dq = tq if dq is None else dq + tq
        dv_acc[at, :] += dv
        dk_acc[at, :] += dk
        dq_acc[live, :] += dq

    end = sweep(step, lo, full, odd, grain, unroll)
    for start in range(0, rows, grain) if diag else ():
        step(end + start, 0, grain, start)
    dq_ref[...] = (dq_acc[...] * SCALE).astype(dq_ref.dtype)


def cross_forward_kernel(
    q_ref, k_ref, v_ref, qa_ref, ka_ref, o_ref, lse_ref, kx, vx, s_scr, m_scr, a_scr
):
    @pl.when(pl.program_id(1) == 0)
    def _():
        forward_prep(k_ref, v_ref, ka_ref, kx, vx)

    full = k_ref.shape[0] // CHUNK
    forward_block(
        0, full, None, CHUNK, False, q_ref, qa_ref, kx, vx, o_ref, lse_ref, s_scr, m_scr, a_scr, full
    )


def cross_forward(q, kv, qa, ka):
    rows, width = q.shape
    keys = kv.shape[0]
    block = min(512, rows)
    pairs = width // 128
    row = pl.BlockSpec((block, 128), lambda h, i: (i, h))
    return pl.pallas_call(
        cross_forward_kernel,
        grid=(pairs, rows // block),
        in_specs=[
            row,
            pl.BlockSpec((keys, 128), lambda h, i: (0, h)),
            pl.BlockSpec((keys, 128), lambda h, i: (0, h + pairs)),
            pl.BlockSpec((block, 128), lambda h, i: (i, 0)),
            pl.BlockSpec((keys, 128), lambda h, i: (0, 0)),
        ],
        out_specs=[row, row],
        out_shape=[
            jax.ShapeDtypeStruct((rows, width), BF),
            jax.ShapeDtypeStruct((rows, width), F32),
        ],
        scratch_shapes=forward_scratch(block, keys),
        compiler_params=params(),
        cost_estimate=cost(16 * rows * keys * width, 8 * rows * width, rows * keys * 12),
        name="cross_forward",
    )(q, kv, kv, qa, ka)


def cross_backward_kernel(
    q_ref, k_ref, v_ref, do_ref, o_ref, lse_ref, qa_ref, ka_ref,
    dq_ref, dk_ref, dv_ref, kx, vx, km, dk_acc, dv_acc, dq_acc,
):
    @pl.when(pl.program_id(1) == 0)
    def _():
        backward_prep(k_ref, v_ref, ka_ref, kx, vx, km, dk_acc, dv_acc)

    backward_block(
        0, k_ref.shape[0] // CHUNK, None, CHUNK, False, q_ref[...], do_ref[...], o_ref, lse_ref,
        qa_ref, kx, vx, km, dq_ref, dk_acc, dv_acc, dq_acc, k_ref.shape[0] // CHUNK,
    )

    @pl.when(pl.program_id(1) == pl.num_programs(1) - 1)
    def _():
        dk_ref[...] = (dk_acc[...] * LN2).astype(BF)
        dv_ref[...] = dv_acc[...].astype(BF)


def cross_backward(q, kv, do, o, lse, qa, ka):
    rows, width = q.shape
    keys = kv.shape[0]
    block = min(512, rows)
    pairs = width // 128
    row = pl.BlockSpec((block, 128), lambda h, i: (i, h))
    col = pl.BlockSpec((keys, 128), lambda h, i: (0, h))
    return pl.pallas_call(
        cross_backward_kernel,
        grid=(pairs, rows // block),
        in_specs=[
            row,
            col,
            pl.BlockSpec((keys, 128), lambda h, i: (0, h + pairs)),
            row,
            row,
            row,
            pl.BlockSpec((block, 128), lambda h, i: (i, 0)),
            pl.BlockSpec((keys, 128), lambda h, i: (0, 0)),
        ],
        out_specs=[row, col, col],
        out_shape=[
            jax.ShapeDtypeStruct((rows, width), BF),
            jax.ShapeDtypeStruct((keys, width), BF),
            jax.ShapeDtypeStruct((keys, width), BF),
        ],
        scratch_shapes=backward_scratch(block, keys),
        compiler_params=params(),
        cost_estimate=cost(40 * rows * keys * width, 12 * rows * width, rows * keys * 12),
        name="cross_backward",
    )(q, kv, kv, do, o, lse, qa, ka)


def grain_of(block):
    return min(256, block)


def needed_blocks(segs, block):
    total = segs.shape[0]
    grain = grain_of(block)
    first = segs.reshape(total // block, block)[:, 0]
    start = jnp.sum((segs[None, :] < first[:, None]).astype(jnp.int32), axis=1)
    ends = (jnp.arange(total // block, dtype=jnp.int32) + 1) * block
    return (ends - start // grain * grain) // grain


def self_range(count, i, block):
    grain = grain_of(block)
    before = count - block // grain
    per = CHUNK // grain
    lo = pl.multiple_of((i + 1) * block - count * grain, grain)
    return lo, before // per, before % per, grain


def self_forward_kernel(
    count_ref, slot_ref, q_ref, k_ref, v_ref, qa_ref, ka_ref, o_ref, lse_ref,
    kx, vx, s_scr, m_scr, a_scr,
):
    i = pl.program_id(1)

    @pl.when(i == 0)
    def _():
        forward_prep(k_ref, v_ref, ka_ref, kx, vx)

    forward_block(
        *self_range(count_ref[i], i, q_ref.shape[0]), True, q_ref, qa_ref, kx, vx, o_ref, lse_ref,
        s_scr, m_scr, a_scr, 1,
    )


def self_forward(counts, slots, q, k, v, qa, ka, block):
    total, width = q.shape
    row = pl.BlockSpec((block, 128), lambda h, i, n, s: (i, h))
    col = pl.BlockSpec((total, 128), lambda h, i, n, s: (0, h))
    return pl.pallas_call(
        self_forward_kernel,
        grid_spec=pltpu.PrefetchScalarGridSpec(
            num_scalar_prefetch=2,
            grid=(width // 128, total // block),
            in_specs=[
                row,
                col,
                col,
                pl.BlockSpec((block, 128), lambda h, i, n, s: (i, 0)),
                pl.BlockSpec((total, 128), lambda h, i, n, s: (0, 0)),
            ],
            out_specs=[pl.BlockSpec((block, 128), lambda h, i, n, s: (s[i], h)), row],
            scratch_shapes=forward_scratch(block, total),
        ),
        out_shape=[
            jax.ShapeDtypeStruct((total, width), BF),
            jax.ShapeDtypeStruct((total, width), F32),
        ],
        compiler_params=params(),
        cost_estimate=cost(8 * total * total * width, 8 * total * width, total * total * 3),
        name="self_forward",
    )(counts, slots, q, k, v, qa, ka)


def self_backward_kernel(
    count_ref, slot_ref, q_ref, k_ref, v_ref, own_ref, far_ref, o_ref, lse_ref, qa_ref, ka_ref,
    dq_ref, dk_ref, dv_ref, kx, vx, km, dk_acc, dv_acc, dq_acc, *, per_dev,
):
    i = pl.program_id(0)
    do = jnp.where(slot_ref[i] < per_dev, own_ref[...], far_ref[...])

    @pl.when(i == 0)
    def _():
        backward_prep(k_ref, v_ref, ka_ref, kx, vx, km, dk_acc, dv_acc)

    backward_block(
        *self_range(count_ref[i], i, q_ref.shape[0]), True, q_ref[...], do, o_ref, lse_ref, qa_ref,
        kx, vx, km, dq_ref, dk_acc, dv_acc, dq_acc, 1,
    )

    @pl.when(i == pl.num_programs(0) - 1)
    def _():
        dk_ref[...] = (dk_acc[...] * LN2).astype(BF)
        dv_ref[...] = dv_acc[...].astype(BF)


def self_backward(pair, counts, slots, q, k, v, own, far, o, lse, qa, ka, block):
    total = q.shape[0]
    per_dev = own.shape[0] // block
    row = pl.BlockSpec((block, 128), lambda i, n, s: (i, pair))
    col = pl.BlockSpec((total, 128), lambda i, n, s: (0, pair))
    whole = pl.BlockSpec((total, 128), lambda i, n, s: (0, 0))
    return pl.pallas_call(
        functools.partial(self_backward_kernel, per_dev=per_dev),
        grid_spec=pltpu.PrefetchScalarGridSpec(
            num_scalar_prefetch=2,
            grid=(total // block,),
            in_specs=[
                row,
                col,
                col,
                pl.BlockSpec((block, 128), lambda i, n, s: (jnp.minimum(s[i], per_dev - 1), pair)),
                pl.BlockSpec((block, 128), lambda i, n, s: (jnp.maximum(s[i] - per_dev, 0), pair)),
                pl.BlockSpec((block, 128), lambda i, n, s: (s[i], pair)),
                row,
                pl.BlockSpec((block, 128), lambda i, n, s: (i, 0)),
                whole,
            ],
            out_specs=[pl.BlockSpec((block, 128), lambda i, n, s: (i, 0)), whole, whole],
            scratch_shapes=backward_scratch(block, total),
        ),
        out_shape=[jax.ShapeDtypeStruct((total, 128), BF)] * 3,
        compiler_params=params(),
        cost_estimate=cost(20 * total * total * 128, 12 * total * 128, total * total),
        name="self_backward",
    )(counts, slots, q, k, v, own, far, o, lse, qa, ka)


def qkv_kernel(order_ref, own_ref, far_ref, g_ref, w_ref, n_ref, q_ref, k_ref, v_ref, *, per_dev):
    x = jnp.where(pl.program_id(0) < per_dev, own_ref[...], far_ref[...]).astype(F32)
    n = (x * rms_scale(x) * g_ref[...]).astype(BF)
    n_ref[...] = n
    width = q_ref.shape[1]
    out = nn(n, w_ref[...])
    q_ref[...] = (out[:, :width] * QSCALE).astype(BF)
    k_ref[...] = out[:, width : 2 * width].astype(BF)
    v_ref[...] = out[:, 2 * width :].astype(BF)


def qkv_forward(order, own, far, gain, w, block):
    dim = own.shape[1]
    total = own.shape[0] + far.shape[0]
    width = w.shape[1] // 3
    per_dev = own.shape[0] // block
    here = lambda i, o: (o[i], 0)
    whole = lambda i, o: (0, 0)
    return pl.pallas_call(
        functools.partial(qkv_kernel, per_dev=per_dev),
        grid_spec=pltpu.PrefetchScalarGridSpec(
            num_scalar_prefetch=1,
            grid=(total // block,),
            in_specs=[
                pl.BlockSpec((block, dim), lambda i, o: (jnp.minimum(i, per_dev - 1), 0)),
                pl.BlockSpec((block, dim), lambda i, o: (jnp.maximum(i - per_dev, 0), 0)),
                pl.BlockSpec((1, dim), whole),
                pl.BlockSpec(w.shape, whole),
            ],
            out_specs=[pl.BlockSpec((block, dim), here)] + [pl.BlockSpec((block, width), here)] * 3,
        ),
        out_shape=[jax.ShapeDtypeStruct((total, dim), BF)]
        + [jax.ShapeDtypeStruct((total, width), BF)] * 3,
        compiler_params=params(),
        cost_estimate=cost(6 * total * dim * width, 8 * total * dim),
        name="qkv_forward",
    )(order, own, far, gain, w)


def enc_kv_kernel(own_ref, far_ref, w_ref, kv_ref, *, own_blocks):
    enc = jnp.where(pl.program_id(0) < own_blocks, own_ref[...], far_ref[...])
    half = w_ref.shape[1] // 2
    for c in range(2):
        at = slice(c * half, (c + 1) * half)
        kv_ref[:, at] = nn(enc, w_ref[:, at]).astype(BF)


def enc_forward(own, far, w2):
    rows, dim = own.shape
    block = min(512, rows)
    keys = rows + far.shape[0]
    ours = rows // block
    return pl.pallas_call(
        functools.partial(enc_kv_kernel, own_blocks=ours),
        grid=(keys // block,),
        in_specs=[
            pl.BlockSpec((block, dim), lambda i: (jnp.minimum(i, ours - 1), 0)),
            pl.BlockSpec((block, dim), lambda i: (jnp.maximum(i - ours, 0), 0)),
            pl.BlockSpec((dim, 2 * dim), lambda i: (0, 1)),
        ],
        out_specs=pl.BlockSpec((block, 2 * dim), lambda i: (i, 0)),
        out_shape=jax.ShapeDtypeStruct((keys, 2 * dim), BF),
        compiler_params=params(),
        cost_estimate=cost(4 * keys * dim * dim, 8 * keys * dim),
        name="enc_forward",
    )(own, far, w2)


def after_self_kernel(turn_ref, x_ref, *refs, count):
    o_refs, w_refs = refs[:count], refs[count : 2 * count]
    g_ref, wq_ref, h_ref, n_ref, q_ref, s_ref = refs[2 * count :]
    x = x_ref[...].astype(F32)
    a = nn(o_refs[0][...], w_refs[0][...])
    for o_ref, w_ref in zip(o_refs[1:], w_refs[1:]):
        a = a + nn(o_ref[...], w_ref[...])
    h = x + a
    h_ref[...] = h
    n = (h * rms_scale(h) * g_ref[...]).astype(BF)
    n_ref[...] = n
    q_ref[...] = (nn(n, wq_ref[...]) * QSCALE).astype(BF)

    @pl.when(pl.program_id(0) == 0)
    def _():
        s_ref[...] = jnp.zeros_like(s_ref)

    s_ref[0:1, :] += jnp.sum(x * x, axis=0, keepdims=True)
    s_ref[1:2, :] += jnp.sum(a * a, axis=0, keepdims=True)


def turn_specs(count, width, dim):
    return [pl.BlockSpec((width, dim), lambda i, t, k=k: (t[k], 0)) for k in range(count)]


def after_self(turn, x, pieces, wo, gain, w2):
    rows, dim = x.shape
    count, width = len(pieces), pieces[0].shape[1]
    block = min(512, rows)
    line = lambda i, t: (i, 0)
    whole = lambda i, t: (0, 0)
    row = pl.BlockSpec((block, dim), line)
    return pl.pallas_call(
        functools.partial(after_self_kernel, count=count),
        grid_spec=pltpu.PrefetchScalarGridSpec(
            num_scalar_prefetch=1,
            grid=(rows // block,),
            in_specs=[row]
            + [pl.BlockSpec((block, width), line)] * count
            + turn_specs(count, width, dim)
            + [pl.BlockSpec((1, dim), whole), pl.BlockSpec((dim, dim), lambda i, t: (0, 1))],
            out_specs=[row, row, row, pl.BlockSpec((8, dim), whole)],
        ),
        out_shape=[
            jax.ShapeDtypeStruct((rows, dim), F32),
            jax.ShapeDtypeStruct((rows, dim), BF),
            jax.ShapeDtypeStruct((rows, dim), BF),
            jax.ShapeDtypeStruct((8, dim), F32),
        ],
        compiler_params=params(),
        cost_estimate=cost(4 * rows * dim * dim, 14 * rows * dim),
        name="after_self",
    )(turn, x, *pieces, *([wo] * count), gain, w2)


GELU_C = math.sqrt(2.0 / math.pi)
GELU_A = 0.044715


PIECES = (4, 8, 3, 64)


def mlp_kernel(
    o_ref, h1_ref, wc_ref, g_ref, t_ref, gu_ref, wd_ref,
    y_ref, dh_ref, dc_ref, do_ref, s_ref, g_out,
    n_scr, h_scr, m_scr, dn_scr, hid_scr, du_scr, dw_scr, wg_scr, wu_scr, gu_out, d_out, sems,
):
    j = pl.program_id(0)
    last = pl.num_programs(0) - 1
    rows = o_ref.shape[0]
    step = min(256, rows)
    spans = [pl.ds(r, step) for r in range(0, rows, step)]
    gain = g_ref[...]
    n_fsdp, n_two, _, tall, _ = gu_ref.shape
    third = 256
    high = 3 * tall

    @pl.when(j == 0)
    def _():
        total = None
        for at in spans:
            c = nn(o_ref[at, :], wc_ref[...])
            h = h1_ref[at, :] + c
            h_scr[at, :] = h
            n_scr[at, :] = (h * rms_scale(h) * gain).astype(BF)
            part = jnp.sum(c * c, axis=0, keepdims=True)
            total = part if total is None else total + part
        s_ref[...] = jnp.zeros_like(s_ref)
        s_ref[0:1, :] = total
        m_scr[...] = jnp.zeros_like(m_scr)
        dn_scr[...] = jnp.zeros_like(dn_scr)

    for z in range(n_fsdp):
        for p in range(n_two):
            for t in range(3):
                at, to = pl.ds(z * high + t * tall, tall), pl.ds(p * third, third)
                wg_scr[at, to] = gu_ref[z, p, 0, :, t * third : (t + 1) * third]
                wu_scr[at, to] = gu_ref[z, p, 1, :, t * third : (t + 1) * third]
    wg, wu = wg_scr[...], wu_scr[...]
    wd = wd_ref[...].reshape(-1, wd_ref.shape[-1])
    for at in spans:
        n = n_scr[at, :]
        u = nn(n, wg)
        w = nn(n, wu)
        dhid = nt(t_ref[at, :], wd)
        square = u * u
        th = jnp.tanh(GELU_C * u * (1.0 + GELU_A * square))
        half = 0.5 * (1.0 + th)
        gel = u * half
        slope = half + 0.5 * u * (1.0 - th * th) * (GELU_C * (1.0 + 3.0 * GELU_A * square))
        hid = (gel * w).astype(BF)
        du = (dhid * w * slope).astype(BF)
        dw = (dhid * gel).astype(BF)
        hid_scr[at, :] = hid
        du_scr[at, :] = du
        dw_scr[at, :] = dw
        m_scr[at, :] += nn(hid, wd)
        dn_scr[at, :] += nt(du, wg) + nt(dw, wu)

    slot = lax.rem(j, 2)

    def copies(step_of, slot_of):
        return (
            pltpu.make_async_copy(
                gu_out.at[slot_of],
                g_out.at[:, pl.ds(step_of * n_two, n_two), pl.ds(0, 2)],
                sems.at[slot_of, 0],
            ),
            pltpu.make_async_copy(d_out.at[slot_of], g_out.at[step_of, :, 2], sems.at[slot_of, 1]),
        )

    @pl.when(j >= 2)
    def _():
        for copy in copies(j - 2, slot):
            copy.wait()

    d_out[slot] = tn(hid_scr[...], t_ref[...]).astype(BF).reshape(d_out.shape[1:])
    for side, source in ((0, du_scr), (1, dw_scr)):
        grad = tn(n_scr[...], source[...]).astype(BF)
        for z in range(n_fsdp):
            for p in range(n_two):
                for t in range(3):
                    gu_out[slot, z, p, side, :, t * third : (t + 1) * third] = grad[
                        z * high + t * tall : z * high + (t + 1) * tall,
                        p * third : (p + 1) * third,
                    ]
    for copy in copies(j, slot):
        copy.start()

    @pl.when(j == last)
    def _():
        total = gains = None
        for at in spans:
            h = h_scr[at, :]
            y = h + m_scr[at, :]
            y_ref[at, :] = y.astype(BF)
            dh, dg = norm_back(h, gain, dn_scr[at, :])
            dh = dh + t_ref[at, :].astype(F32)
            dh_ref[at, :] = dh
            dc = dh.astype(BF)
            dc_ref[at, :] = dc
            do_ref[at, :] = nt(dc, wc_ref[...]).astype(BF)
            part = jnp.sum(y * y, axis=0, keepdims=True)
            total = part if total is None else total + part
            gains = dg if gains is None else gains + dg
        s_ref[1:2, :] = total
        s_ref[2:3, :] = gains
        for copy in copies(j - 1, 1 - slot) + copies(j, slot):
            copy.wait()


def feed_forward(o, h1, w2, gain, cot, w3):
    rows, dim = o.shape
    n_fsdp, n_plane, _, tall, _ = w3.shape
    steps = n_fsdp
    two = n_plane // steps
    width = two * 256
    whole = lambda j: (0, 0)
    once = pl.Buffered(1)
    full = pl.BlockSpec((rows, dim), whole, pipeline_mode=once)
    flops = 18 * rows * dim * width * steps + 6 * rows * dim * dim
    return pl.pallas_call(
        mlp_kernel,
        grid=(steps,),
        in_specs=[
            full,
            full,
            pl.BlockSpec((dim, dim), lambda j: (0, 4), pipeline_mode=once),
            pl.BlockSpec((1, dim), whole),
            full,
            pl.BlockSpec((n_fsdp, two, 2, tall, dim), lambda j: (0, j, 0, 0, 0)),
            pl.BlockSpec((1, n_plane, 1, tall, dim), lambda j: (j, 0, 2, 0, 0)),
        ],
        out_specs=[
            full,
            full,
            full,
            full,
            pl.BlockSpec((8, dim), whole),
            pl.BlockSpec(memory_space=pl.ANY),
        ],
        out_shape=[
            jax.ShapeDtypeStruct((rows, dim), BF),
            jax.ShapeDtypeStruct((rows, dim), F32),
            jax.ShapeDtypeStruct((rows, dim), BF),
            jax.ShapeDtypeStruct((rows, dim), BF),
            jax.ShapeDtypeStruct((8, dim), F32),
            jax.ShapeDtypeStruct(w3.shape, BF),
        ],
        scratch_shapes=[
            pltpu.VMEM((rows, dim), BF),
            pltpu.VMEM((rows, dim), F32),
            pltpu.VMEM((rows, dim), F32),
            pltpu.VMEM((rows, dim), F32),
            pltpu.VMEM((rows, width), BF),
            pltpu.VMEM((rows, width), BF),
            pltpu.VMEM((rows, width), BF),
            pltpu.VMEM((dim, width), BF),
            pltpu.VMEM((dim, width), BF),
            pltpu.VMEM((2, n_fsdp, two, 2, tall, dim), BF),
            pltpu.VMEM((2, n_plane, tall, dim), BF),
            pltpu.SemaphoreType.DMA((2, 2)),
        ],
        compiler_params=params(),
        cost_estimate=cost(flops, 40 * MIB, rows * width * steps),
        name="feed_forward",
    )(o, h1, w2, gain, cot, w3, w3)


def unpack_kernel(me_ref, p_ref, gate_ref, up_ref, down_ref):
    core, x = me_ref[0], me_ref[1]
    tall = p_ref.shape[4]
    third = 256
    for p in range(8):
        near = (core ^ ((p // 2) % 2), x ^ (p // 4), p % 2)
        for t in range(3):
            at, to = pl.ds(t * tall, tall), pl.ds(p * third, third)
            lane = slice(t * third, (t + 1) * third)
            gate_ref[at, to] = p_ref[near + (0, slice(None), lane)].astype(F32)
            up_ref[at, to] = p_ref[near + (1, slice(None), lane)].astype(F32)
        down_ref[pl.ds(p * tall, tall), :] = p_ref[near + (2,)].astype(F32)


def unpack(me, pieces):
    tall, dim = pieces.shape[-2:]
    vmem = pl.BlockSpec(memory_space=pltpu.VMEM)
    return pl.pallas_call(
        unpack_kernel,
        in_specs=[pl.BlockSpec(memory_space=pltpu.SMEM), vmem],
        out_specs=[vmem] * 3,
        out_shape=[
            jax.ShapeDtypeStruct((3 * tall, 8 * 256), F32),
            jax.ShapeDtypeStruct((3 * tall, 8 * 256), F32),
            jax.ShapeDtypeStruct((8 * tall, dim), F32),
        ],
        compiler_params=params(),
        name="unpack",
    )(me, pieces)


def deal_rows(core, full, send_ref, keep_ref):
    count, size = send_ref.shape[:2]
    for i in range(count):
        for ref, c in ((send_ref, 1 - core), (keep_ref, core)):
            ref[i] = full[pl.ds(pl.multiple_of((2 * i + c) * size, 16), size), :]


def mid_grads_kernel(turn_ref, *refs, count, far_blocks):
    n_in = count + 9
    sources = refs[:n_in]
    wk_ref, wv_ref, g_ref, far_out, own_out = refs[n_in : n_in + 5]
    buffers = refs[n_in + 5 : 2 * n_in + 5]
    sems = refs[-1]
    m = pl.program_id(0)
    dim = g_ref.shape[0]
    copies = [
        pltpu.make_async_copy(
            source.at[pl.ds(0, buffer.shape[0])] if source.shape != buffer.shape else source,
            buffer,
            sems.at[i],
        )
        for i, (source, buffer) in enumerate(zip(sources, buffers))
    ]
    n2, dq, da, *o_pieces, own, far, dk, dv, o2, dc = buffers
    ours = own.shape[0]
    width = o_pieces[0].shape[1]

    @pl.when(m == 0)
    def _():
        for copy in copies:
            copy.start()
        for copy in copies[:2]:
            copy.wait()
        g_ref[...] = tn(n2[...], dq[...]).astype(BF)

    @pl.when(m == 1)
    def _():
        for copy in copies[2 : 3 + count]:
            copy.wait()
        for i in range(count):
            base = pl.multiple_of(turn_ref[i] * width, width)
            term = tn(o_pieces[i][...], da[...]).astype(BF)

            @pl.when(base < dim)
            def _():
                g_ref[pl.ds(base, width), :] = term

    for at, right, first in ((2, dk, 3), (3, dv, 6)):

        @pl.when(m == at)
        def _():
            for copy in copies[count + first : count + 6 if at == 2 else count + 7]:
                copy.wait()
            g_ref[...] = (tn(own[...], right[:ours, :]) + tn(far[...], right[ours:, :])).astype(BF)

    @pl.when(m == 4)
    def _():
        for copy in copies[count + 7 :]:
            copy.wait()
        g_ref[...] = tn(o2[...], dc[...]).astype(BF)

    block = far_out.shape[0]
    blocks = dk.shape[0] // block

    def enc_rows(i):
        at = pl.ds(pl.multiple_of(lax.rem(i + ours // block, blocks) * block, block), block)
        return nt(dk[at, :], wk_ref[...]) + nt(dv[at, :], wv_ref[...])

    @pl.when((m >= 5) & (m < 5 + far_blocks))
    def _():
        far_out[...] = enc_rows(m - 5).astype(BF)

    @pl.when(m >= 5 + far_blocks)
    def _():
        own_out[...] = enc_rows(m - 5)


def dealt_out(dim, block, total, index, deal):
    if not deal:
        return [pl.BlockSpec((dim, block), lambda *a: (0, index(*a)))], [
            jax.ShapeDtypeStruct((dim, total), BF)
        ]
    spec = pl.BlockSpec((8, dim // 16, block), lambda *a: (0, 0, index(*a)))
    return [spec] * 2, [jax.ShapeDtypeStruct((8, dim // 16, total), BF)] * 2


def mid_grads(turn, pieces, da, n2, dq2, own, far, dk2, dv2, o2, dc, w2):
    rows, dim = n2.shape
    args = (n2, dq2, da, *pieces, own, far, dk2, dv2, o2, dc)
    shapes = [(rows, a.shape[1]) for a in args[: 3 + len(pieces)]]
    shapes += [a.shape for a in args[3 + len(pieces) :]]
    flops = 2 * dim * dim * (3 * rows + 4 * dk2.shape[0])
    block = min(512, own.shape[0])
    far_blocks, own_blocks = far.shape[0] // block, own.shape[0] // block
    once = pl.Buffered(1)
    column = lambda m, t: (0, jnp.where(m < 2, 1 - m, jnp.minimum(m, 4)))
    return pl.pallas_call(
        functools.partial(mid_grads_kernel, count=len(pieces), far_blocks=far_blocks),
        grid_spec=pltpu.PrefetchScalarGridSpec(
            num_scalar_prefetch=1,
            grid=(5 + far_blocks + own_blocks,),
            in_specs=[pl.BlockSpec(memory_space=pl.ANY)] * len(args)
            + [
                pl.BlockSpec((dim, dim), lambda m, t: (0, 2), pipeline_mode=once),
                pl.BlockSpec((dim, dim), lambda m, t: (0, 3), pipeline_mode=once),
            ],
            out_specs=[
                pl.BlockSpec((dim, dim), column),
                pl.BlockSpec((block, dim), lambda m, t: (jnp.clip(m - 5, 0, far_blocks - 1), 0)),
                pl.BlockSpec((block, dim), lambda m, t: (jnp.maximum(m - 5 - far_blocks, 0), 0)),
            ],
            scratch_shapes=[pltpu.VMEM(shape, BF) for shape in shapes]
            + [pltpu.SemaphoreType.DMA((len(args),))],
        ),
        out_shape=[
            jax.ShapeDtypeStruct((dim, 5 * dim), BF),
            jax.ShapeDtypeStruct(far.shape, BF),
            jax.ShapeDtypeStruct(own.shape, F32),
        ],
        compiler_params=params(),
        cost_estimate=cost(flops, 30 * MIB),
        name="mid_grads",
    )(turn, *args, w2, w2)


def before_self_kernel(turn_ref, dq_ref, wq_ref, h_ref, dh_ref, g_ref, *refs, count):
    w_refs = refs[:count]
    d1_ref, da_ref, s_ref = refs[count : count + 3]
    do_refs = refs[count + 3 :]
    dn = nt(dq_ref[...], wq_ref[...])
    dh, dg = norm_back(h_ref[...], g_ref[...], dn)
    d1 = dh_ref[...] + dh
    d1_ref[...] = d1
    da = d1.astype(BF)
    da_ref[...] = da
    for do_ref, w_ref in zip(do_refs, w_refs):
        do_ref[...] = nt(da, w_ref[...]).astype(BF)

    @pl.when(pl.program_id(0) == 0)
    def _():
        s_ref[...] = jnp.zeros_like(s_ref)

    s_ref[0:1, :] += dg


def before_self(turn, dq, w2, h1, dh2, gain, wo, width):
    rows, dim = dq.shape
    count = turn.shape[0]
    block = min(512, rows)
    line = lambda i, t: (i, 0)
    whole = lambda i, t: (0, 0)
    row = pl.BlockSpec((block, dim), line)
    return pl.pallas_call(
        functools.partial(before_self_kernel, count=count),
        grid_spec=pltpu.PrefetchScalarGridSpec(
            num_scalar_prefetch=1,
            grid=(rows // block,),
            in_specs=[
                row,
                pl.BlockSpec((dim, dim), lambda i, t: (0, 1)),
                row,
                row,
                pl.BlockSpec((1, dim), whole),
            ]
            + turn_specs(count, width, dim),
            out_specs=[row, row, pl.BlockSpec((8, dim), whole)]
            + [pl.BlockSpec((block, width), line)] * count,
        ),
        out_shape=[
            jax.ShapeDtypeStruct((rows, dim), F32),
            jax.ShapeDtypeStruct((rows, dim), BF),
            jax.ShapeDtypeStruct((8, dim), F32),
        ]
        + [jax.ShapeDtypeStruct((rows, width), BF)] * count,
        compiler_params=params(),
        cost_estimate=cost(4 * rows * dim * dim, 18 * rows * dim),
        name="before_self",
    )(turn, dq, w2, h1, dh2, gain, *([wo] * count))


def joined(refs):
    return jnp.concatenate([r[...] for r in refs], axis=1)


def qkv_grads_kernel(core_ref, *refs, count, deal):
    d_refs = refs[:count]
    n_ref, w_ref, gain_ref, extra_ref = refs[count : count + 4]
    outs = refs[count + 4 :]
    acc, full = outs[-2:]
    i = pl.program_id(0)
    term = tn(n_ref[...], joined(d_refs))

    @pl.when(i == 0)
    def _():
        acc[...] = term

    @pl.when(i > 0)
    def _():
        acc[...] += term

    @pl.when(i == pl.num_programs(0) - 1)
    def _():
        width = acc.shape[1]
        grad = acc[...]
        gains = jnp.sum(grad * w_ref[...].astype(F32), axis=1, keepdims=True) / gain_ref[:, :1]
        extra = extra_ref[...]
        full[:, :width] = grad.astype(BF)
        full[:, width:] = jnp.where(lanes(extra.shape) == 0, gains, extra).astype(BF)
        if deal:
            deal_rows(core_ref[0], full, outs[0], outs[1])
        else:
            outs[0][...] = full[...]


def qkv_grads(core, ds, n, w, gain, extra, deal):
    total, dim = n.shape
    block = min(512, total)
    width = w.shape[1]
    specs, outs = dealt_out(dim, width + 128, width + 128, lambda i, c: 0, deal)
    whole = lambda i, c: (0, 0)
    return pl.pallas_call(
        functools.partial(qkv_grads_kernel, count=len(ds), deal=deal),
        grid_spec=pltpu.PrefetchScalarGridSpec(
            num_scalar_prefetch=1,
            grid=(total // block,),
            in_specs=[pl.BlockSpec((block, 128), lambda i, c: (i, 0))] * len(ds)
            + [
                pl.BlockSpec((block, dim), lambda i, c: (i, 0)),
                pl.BlockSpec(w.shape, whole),
                pl.BlockSpec((dim, 128), whole),
                pl.BlockSpec((dim, 128), whole),
            ],
            out_specs=specs,
            scratch_shapes=[pltpu.VMEM((dim, width), F32), pltpu.VMEM((dim, width + 128), BF)],
        ),
        out_shape=outs,
        compiler_params=params(),
        cost_estimate=cost(2 * total * dim * width, 6 * total * dim),
        name="qkv_grads",
    )(core, *ds, n, w, gain, extra)


def qkv_back_kernel(order_ref, *refs, count):
    dn_ref = refs[count + 1]
    dn_ref[...] = nt(joined(refs[:count]), refs[count][...]).astype(dn_ref.dtype)


def qkv_back(order, first, ds, w, rows, dtype, block):
    dim = w.shape[0]
    return pl.pallas_call(
        functools.partial(qkv_back_kernel, count=len(ds)),
        grid_spec=pltpu.PrefetchScalarGridSpec(
            num_scalar_prefetch=1,
            grid=(rows // block,),
            in_specs=[pl.BlockSpec((block, 128), lambda i, o: (o[i + first], 0))] * len(ds)
            + [pl.BlockSpec(w.shape, lambda i, o: (0, 0))],
            out_specs=pl.BlockSpec((block, dim), lambda i, o: (i, 0)),
        ),
        out_shape=jax.ShapeDtypeStruct((rows, dim), dtype),
        compiler_params=params(),
        cost_estimate=cost(2 * rows * dim * w.shape[1], 10 * rows * dim),
        name="qkv_back",
    )(order, *ds, w)


def finish_kernel(x_ref, dh_ref, g_ref, own_ref, *refs):
    dn = own_ref[...]
    for ref in refs[:-1]:
        dn = dn + ref[...].astype(F32)
    dh, _ = norm_back(x_ref[...].astype(F32), g_ref[...], dn)
    refs[-1][...] = dh_ref[...] + dh


def finish(x, dh1, gain, own, got):
    rows, dim = x.shape
    block = min(256, rows)
    row = pl.BlockSpec((block, dim), lambda i: (i, 0))
    return pl.pallas_call(
        finish_kernel,
        grid=(rows // block,),
        in_specs=[row, row, pl.BlockSpec((1, dim), lambda i: (0, 0)), row] + [row] * len(got),
        out_specs=row,
        out_shape=jax.ShapeDtypeStruct((rows, dim), F32),
        compiler_params=params(),
        cost_estimate=cost(10 * rows * dim, 16 * rows * dim),
        name="finish",
    )(x, dh1, gain, own, *got)


def turned(n, k):
    return [(i, (i + k) % n) for i in range(n)]


def rows_of(array, index, count):
    size = array.shape[0] // count
    return lax.dynamic_slice_in_dim(array, index * size, size, 0)


def assemble_kernel(place_ref, near_ref, far_ref, w_ref, g_ref):
    z, core = place_ref[0], place_ref[1]
    count, size = near_ref.shape[0], near_ref.shape[1]
    width = w_ref.shape[1]
    for d in range(count):
        base = lax.rem(z - d + count, count) * (2 * size)
        for ref, half in ((near_ref, core), (far_ref, 1 - core)):
            at = pl.ds(pl.multiple_of(base + half * size, 16), size)
            w_ref[at, :] = ref[d, :, :width]
            g_ref[at, :] = ref[d, :, width:]


def gather_first(own, z, part, n_fsdp, n_parts):
    size = own.shape[0] // 2
    width = own.shape[1] - 128
    if n_parts % 2 or size % 16:
        full = lax.all_gather(own, "fsdp", axis=0, tiled=True)
        return full[:, :width], full[:, width:]
    core = part % 2
    mine = lax.dynamic_slice_in_dim(own, core * size, size, 0)
    near = jnp.stack(
        [mine] + [lax.ppermute(mine, "fsdp", turned(n_fsdp, d)) for d in range(1, n_fsdp)]
    )
    far = lax.ppermute(near, "parts", [(i, i ^ 1) for i in range(n_parts)])
    vmem = pl.BlockSpec(memory_space=pltpu.VMEM)
    total = n_fsdp * own.shape[0]
    return pl.pallas_call(
        assemble_kernel,
        in_specs=[pl.BlockSpec(memory_space=pltpu.SMEM), vmem, vmem],
        out_specs=[vmem, vmem],
        out_shape=[
            jax.ShapeDtypeStruct((total, width), BF),
            jax.ShapeDtypeStruct((total, 128), BF),
        ],
        compiler_params=params(),
        name="assemble",
    )(jnp.stack([z, core]).astype(jnp.int32), near, far)


def pick(array, index, axis):
    return lax.dynamic_index_in_dim(array, index, axis, keepdims=False)


class Plane:
    def __init__(self, part, place, z, n_parts, n_fsdp):
        self.core, self.x, self.place, self.z = part % 2, part // 2, place, z
        self.n_fsdp = n_fsdp
        self.swap_core = [(i, i ^ 1) for i in range(n_parts)]
        self.swap_x = [(i, i ^ 2) for i in range(n_parts)]

    def over_core(self, send, keep):
        shape = (self.n_fsdp, 2) + send.shape[1:]
        got = lax.ppermute(send, "parts", self.swap_core).reshape(shape)
        keep = keep.reshape(shape)
        add = lambda i: (pick(keep, i, 1).astype(F32) + pick(got, i, 1).astype(F32)).astype(BF)
        return add(1 - self.x), add(self.x)

    def over_x(self, send, keep):
        got = lax.ppermute(send, "parts", self.swap_x)
        return (keep.astype(F32) + got.astype(F32)).astype(BF)

    def over_fsdp(self, g):
        total = pick(g, self.z, 0).astype(F32)
        for d in range(1, self.n_fsdp):
            piece = pick(g, (self.z + d) % self.n_fsdp, 0)
            total = total + lax.ppermute(piece, "fsdp", turned(self.n_fsdp, d)).astype(F32)
        return total.astype(BF)

    def over_ctx(self, g):
        return (g.astype(F32) + lax.ppermute(g, "ctx", turned(2, 1)).astype(F32)).astype(BF)

    def widen_ctx(self, g):
        return jnp.stack([g, lax.ppermute(g, "ctx", turned(2, 1))])

    def widen_x(self, g):
        return jnp.stack([g, lax.ppermute(g, "parts", self.swap_x)])

    def widen_core(self, g):
        return jnp.stack([g, lax.ppermute(g, "parts", self.swap_core)])

    def widen(self, g):
        return self.widen_core(self.widen_x(g))

    def rows(self, wide):
        pieces = [
            lax.dynamic_slice(
                wide, (c ^ self.core, a ^ self.x, 0, 0), (1, 1) + wide.shape[2:]
            )[0, 0]
            for a in range(2)
            for c in range(2)
        ]
        return jnp.concatenate(pieces).astype(F32)


def local(
    mesh_shape,
    decoder_in,
    encoder_out,
    segment_ids,
    block_order,
    prompt_len,
    self_query,
    self_key,
    self_value,
    self_output,
    cross_query,
    cross_key,
    cross_value,
    cross_output,
    gate_in,
    up_in,
    down_out,
    norm_self,
    norm_cross,
    norm_mlp,
    cotangent,
):
    n_parts, n_ctx, n_fsdp = mesh_shape
    part, place, z = lax.axis_index("parts"), lax.axis_index("ctx"), lax.axis_index("fsdp")
    plane, n_plane = part * n_ctx + place, n_parts * n_ctx
    x_own, enc_own = decoder_in[0], encoder_out[0]
    rows, dim = x_own.shape
    segs, order = segment_ids[0], block_order[0]
    total = segs.shape[0]
    slots_total = order.shape[0]
    block = total // slots_total
    per_dev = slots_total // n_ctx
    enc_rows = enc_own.shape[0]
    keys = enc_rows * n_ctx
    hidden = down_out.shape[0] * n_fsdp
    heads_here = 2 * -(-HEADS // (2 * n_ctx))
    width = heads_here * HEAD
    padded = width * n_ctx

    ring = (place + jnp.arange(n_ctx, dtype=jnp.int32)) % n_ctx
    order_here = jnp.roll(order, -per_dev * place)
    slots = jnp.argsort(order_here).astype(jnp.int32)
    counts = needed_blocks(segs, block)

    def from_ctx(value):
        pieces = [lax.ppermute(value, "ctx", turned(n_ctx, -k)) for k in range(1, n_ctx)]
        return pieces[0] if n_ctx == 2 else jnp.concatenate(pieces, axis=0)

    x_far = from_ctx(x_own)

    fast = (n_parts, n_ctx, n_fsdp) == (4, 2, 4)
    shard = dim // n_fsdp

    def own_heads(w):
        w = jnp.pad(w, ((0, 0), (0, padded - dim)))
        return lax.dynamic_slice_in_dim(w, place * width, width, 1)

    gain_cols = jnp.pad(jnp.stack([norm_self, norm_cross, norm_mlp], axis=1), ((0, 0), (0, 125)))
    first = jnp.concatenate(
        [own_heads(self_query), own_heads(self_key), own_heads(self_value), gain_cols], axis=1
    )
    first, self_output, gate_in = lax.optimization_barrier((first, self_output, gate_in))
    w1, gains = gather_first(first, z, part, n_fsdp, n_parts)
    gains = gains[:, :8].astype(F32).T
    gain_self, gain_cross, gain_mlp = (gains[i : i + 1] for i in range(3))
    mats = (self_output, cross_query, cross_key, cross_value, cross_output)
    if fast:
        w2 = lax.all_gather(
            jnp.concatenate([rows_of(w, part, n_parts) for w in mats], axis=1),
            AROUND, axis=0, tiled=True,
        )

        def column_pieces(w):
            cut = lax.dynamic_slice_in_dim(w, part * 512, 512, 1).reshape(3, 64, 2, 256)
            return cut.transpose(2, 1, 0, 3).reshape(2, 64, dim)

        w3 = lax.all_gather(
            jnp.stack(
                [
                    column_pieces(gate_in),
                    column_pieces(up_in),
                    rows_of(down_out, part, n_parts).reshape(2, 64, dim),
                ],
                axis=1,
            ).reshape(-1, dim),
            AROUND, axis=0, tiled=True,
        ).reshape(PIECES + (dim,))
    else:
        w2 = lax.all_gather(jnp.concatenate(mats, axis=1), "fsdp", axis=0, tiled=True)

        def packed(w):
            w = lax.all_gather(w, "fsdp", axis=0, tiled=True).reshape(4, 3, 64, 8, 256)
            return w.transpose(0, 3, 2, 1, 4).reshape(4, 8, 64, dim)

        w_down = lax.all_gather(down_out, "fsdp", axis=0, tiled=True).reshape(4, 8, 64, dim)
        w3 = jnp.stack([packed(gate_in), packed(up_in), w_down], axis=2)
    x_far, enc_sent = lax.optimization_barrier((x_far, enc_own))
    enc_far = from_ctx(enc_sent)

    n1, q, k, v = qkv_forward(order_here, x_own, x_far, gain_self, w1, block)
    spot = jnp.arange(128, dtype=jnp.int32)[None, :] % HEAD
    minus = jnp.where((spot >= PART0) & (spot < PART0 + 3), -1.0, 0.0)
    seg_q = jnp.where(spot == segs[:, None], 1.0, 0.0).astype(BF)
    seg_k = jnp.where((spot < SEGS) & (spot != segs[:, None]), -BIG, minus).astype(BF)
    o1, lse1 = self_forward(counts, slots, q, k, v, seg_q, seg_k, block)
    pieces = [o1] + [
        lax.ppermute(o1[i * rows : (i + 1) * rows], "ctx", turned(n_ctx, i)) for i in range(1, n_ctx)
    ]
    turn = (place - jnp.arange(n_ctx, dtype=jnp.int32)) % n_ctx
    wo = w2 if padded == dim else jnp.pad(w2[:, :dim], ((0, padded - dim), (0, 0)))
    kv2 = enc_forward(enc_own, enc_far, w2)
    pieces[1], kv2 = lax.optimization_barrier((pieces[1], kv2))
    h1, n2, q2, stat1 = after_self(turn, x_own, pieces, wo, gain_cross, w2)

    where_key = (ring[:, None] * enc_rows + jnp.arange(enc_rows, dtype=jnp.int32)).reshape(-1, 1)
    len_q = jnp.where(spot == 0, jnp.ones((rows, 1), F32), 0.0).astype(BF)
    len_k = jnp.where((spot == 0) & (where_key >= prompt_len[0]), -BIG, minus).astype(BF)
    o2, lse2 = cross_forward(q2, kv2, len_q, len_k)

    layer_out, dh2, dc, do2, stat2, g_ff = feed_forward(o2, h1, w2, gain_mlp, cotangent[0], w3)
    if fast:
        part_ff = lax.psum_scatter(
            g_ff.reshape(-1, dim), AROUND, scatter_dimension=0, tiled=True
        ).reshape(2, 3, 64, dim)

    dq2, dk2, dv2 = cross_backward(q2, kv2, do2, o2, lse2, len_q, len_k)
    dh1, da, stat3, *do1 = before_self(turn, dq2, w2, h1, dh2, gain_cross, wo, width)
    do_far = [lax.ppermute(do1[i], "ctx", turned(n_ctx, -i)) for i in range(1, n_ctx)]
    do_far = do_far[0] if n_ctx == 2 else jnp.concatenate(do_far, axis=0)
    do_own = do1[0]
    core = jnp.reshape(part % 2, (1,)).astype(jnp.int32)
    g_mid, d_far, enc_grad = mid_grads(
        turn, pieces, da, n2, dq2, enc_own, enc_far, dk2, dv2, o2, dc, w2
    )

    sums = jnp.sum(jnp.concatenate([stat1[:2], stat2[:2]], axis=0), axis=1)
    extra = jnp.concatenate(
        [
            jnp.zeros((dim, 1), F32),
            stat2[2][:, None],
            stat3[0][:, None],
            jnp.broadcast_to(sums[None], (dim, 4)),
            jnp.zeros((dim, 121), F32),
        ],
        axis=1,
    )
    gain_wide = jnp.broadcast_to(gain_self.reshape(dim, 1), (dim, 128))

    def self_pair(pair, own, far):
        return self_backward(
            pair, counts, slots, q, k, v, own, far, o1, lse1, seg_q, seg_k, block
        )

    pairs = width // 128
    if fast:
        net = Plane(part, place, z, n_parts, n_fsdp)
        do_own, do_far, d_far, extra, g_mid, part_ff = lax.optimization_barrier(
            (do_own, do_far, d_far, extra, g_mid, part_ff)
        )
        part_mid = lax.psum_scatter(g_mid, AROUND, scatter_dimension=0, tiled=True)
    enc_got = [
        lax.ppermute(d_far[(i - 1) * enc_rows : i * enc_rows], "ctx", turned(n_ctx, i))
        for i in range(1, n_ctx)
    ]
    if fast:
        by_pair = [self_pair(0, do_own, do_far)]
        part_ff, do_far = lax.optimization_barrier((part_ff, do_far, by_pair[0][0]))[:2]
        by_pair += [self_pair(1, do_own, do_far), self_pair(2, do_own, do_far)]
        sum_ff = net.over_ctx(part_ff)
        by_pair, sum_ff, enc_got = lax.optimization_barrier((by_pair, sum_ff, enc_got))
    else:
        by_pair = [self_pair(i, do_own, do_far) for i in range(pairs)]
    for piece in enc_got:
        enc_grad = enc_grad + piece.astype(F32)
    ds = [d[i] for i in range(3) for d in by_pair]
    g_qkv = qkv_grads(core, ds, n1, w1, gain_wide, extra, fast)
    dn_far = qkv_back(order_here, per_dev, ds, w1, total - rows, BF, block)
    dn_got = [
        lax.ppermute(dn_far[(i - 1) * rows : i * rows], "ctx", turned(n_ctx, i))
        for i in range(1, n_ctx)
    ]
    dn_own = qkv_back(order_here, 0, ds, w1, rows, F32, block)
    if fast:
        send, keep, dn_far = lax.optimization_barrier((*net.over_core(*g_qkv), dn_far))
        g_qkv = net.over_fsdp(net.over_x(send, keep))
        dn_got, g_qkv, part_mid, sum_ff, dn_own = lax.optimization_barrier(
            (dn_got, g_qkv, part_mid, net.widen_x(sum_ff), dn_own)
        )
    decoder_grad = finish(x_own, dh1, gain_self, dn_own, dn_got)

    if fast:
        sum_mid = net.rows(net.widen(net.over_ctx(part_mid)))
        me = jnp.stack([net.core, net.x]).astype(jnp.int32)
        grad_gate, grad_up, grad_down = unpack(me, net.widen_core(sum_ff))
        wide = net.widen(net.widen_ctx(g_qkv))
        every = jnp.stack([net.rows(pick(wide, i ^ place, 2)) for i in range(2)])
    else:

        def total_of(g):
            g = lax.psum_scatter(g, "fsdp", scatter_dimension=0, tiled=True).astype(F32)
            return lax.psum(g, ("parts", "ctx"))

        (g_qkv,) = g_qkv
        sum_mid = total_of(g_mid)
        flat = [
            g_ff[:, :, i].reshape(4, 8, 64, 3, 256).transpose(0, 3, 2, 1, 4).reshape(dim, hidden)
            for i in range(2)
        ]
        grad_gate, grad_up = total_of(flat[0]), total_of(flat[1])
        grad_down = total_of(g_ff[:, :, 2].reshape(hidden, dim))
        sum_qkv = lax.psum_scatter(g_qkv, "fsdp", scatter_dimension=0, tiled=True).astype(F32)
        every = lax.all_gather(lax.psum(sum_qkv, "parts"), "ctx", axis=0)
    grads_qkv = [
        jnp.concatenate([every[c, :, i * width : (i + 1) * width] for c in range(n_ctx)], axis=1)[:, :dim]
        for i in range(3)
    ]
    tail = jnp.sum(every[:, :, 3 * width : 3 * width + 8], axis=0)
    grad_gself, grad_gmlp, grad_gcross = tail[:, 0], tail[:, 1], tail[:, 2]
    entries = float(n_parts * n_ctx * n_fsdp * rows * dim)
    rms_values = jnp.sqrt(tail[0, jnp.array([3, 4, 5, 6])] / entries)
    mids = [sum_mid[:, i * dim : (i + 1) * dim] for i in range(5)]
    return (
        layer_out[None],
        decoder_grad[None],
        enc_grad[None],
        *grads_qkv,
        *mids,
        grad_gate,
        grad_up,
        grad_down,
        grad_gself,
        grad_gcross,
        grad_gmlp,
        rms_values,
    )


def solution(mesh):
    rows3 = P(("parts", "fsdp"), "ctx", None)
    group = P(("parts", "fsdp"), None)
    matrix, vector = P("fsdp", None), P("fsdp")
    shape = tuple(mesh.shape[a] for a in ("parts", "ctx", "fsdp"))
    return jax.shard_map(
        functools.partial(local, shape),
        mesh=mesh,
        in_specs=(rows3, rows3, group, group, P(("parts", "fsdp")))
        + (matrix,) * 11
        + (vector,) * 3
        + (rows3,),
        out_specs=(rows3,) * 3 + (matrix,) * 11 + (vector,) * 3 + (P(),),
        check_vma=False,
    )
```

```python
import functools
import math

import jax
import jax.numpy as jnp
from jax import lax
from jax.experimental import pallas as pl
from jax.experimental.pallas import tpu as pltpu
from jax.sharding import PartitionSpec as P

HEADS = 12
HEAD = 64
SCALE = 0.125
EPS = 1e-06
BIG = 1e30
LN2 = math.log(2.0)
QSCALE = SCALE * math.log2(math.e)
PART0 = 16
SEGS = 16
BF = jnp.bfloat16
F32 = jnp.float32
MIB = 1 << 20
AROUND = ("fsdp", "parts")


def nn(a, b):
    return lax.dot_general(a, b, (((1,), (0,)), ((), ())), preferred_element_type=F32)


def nt(a, b):
    return lax.dot_general(a, b, (((1,), (1,)), ((), ())), preferred_element_type=F32)


def tn(a, b):
    return lax.dot_general(a, b, (((0,), (0,)), ((), ())), preferred_element_type=F32)


def lanes(shape):
    return lax.broadcasted_iota(jnp.int32, shape, len(shape) - 1)


def params(mib=60):
    return pltpu.CompilerParams(vmem_limit_bytes=mib * MIB)


def cost(flops, moved, exps=0):
    return pl.CostEstimate(flops=int(flops), bytes_accessed=int(moved), transcendentals=int(exps))


def rms_scale(h):
    return lax.rsqrt(jnp.mean(h * h, axis=-1, keepdims=True) + EPS)


def norm_back(h, gain, dn):
    r = rms_scale(h)
    t = dn * gain
    hr = h * r
    dh = r * (t - hr * jnp.mean(t * hr, axis=-1, keepdims=True))
    return dh, jnp.sum(dn * hr, axis=0, keepdims=True)


def with_parts(base, value):
    spot = lanes(base.shape) % HEAD
    hi = value.astype(BF)
    rest = value - hi.astype(F32)
    mid = rest.astype(BF)
    low = (rest - mid.astype(F32)).astype(BF)
    return jnp.where(
        spot == PART0, hi, jnp.where(spot == PART0 + 1, mid, jnp.where(spot == PART0 + 2, low, base))
    )


def pair_of(own, other):
    left = lanes(own.shape) < HEAD
    return jnp.where(left, own, other), jnp.where(left, other, own)


CHUNK = 512


def below(s, rows_first):
    r = lax.broadcasted_iota(jnp.int32, s.shape, 0)
    c = lanes(s.shape)
    return jnp.where(c <= r if rows_first else r <= c, s, -BIG)


def lane_max(s):
    return functools.reduce(jnp.maximum, [s[:, c : c + 128] for c in range(0, s.shape[1], 128)])


def sweep(step, lo, full, odd, grain, unroll):
    base = lo
    if odd is not None:

        @pl.when(odd == 1)
        def _():
            step(lo, 0, grain)

        base = lo + odd * grain

    def body(c, carry):
        step(pl.multiple_of(base + c * CHUNK, grain), pl.multiple_of(grain + c * CHUNK, 128), CHUNK)
        return carry

    lax.fori_loop(0, full, body, 0, unroll=unroll)
    return pl.multiple_of(base + full * CHUNK, grain)


def forward_block(
    lo, full, odd, grain, diag, q_ref, qa_ref, kx, vx, o_ref, lse_ref, s_scr, m_scr, a_scr, unroll
):
    q = q_ref[...]
    rows = q.shape[0]
    left = lanes(q.shape) < HEAD
    sides = pair_of(q, qa_ref[...])
    m_scr[...] = jnp.full_like(m_scr, -BIG)
    a_scr[...] = jnp.zeros_like(a_scr)
    last = s_scr.shape[2] - rows

    def scores(key, at, size, start=None):
        live = pl.ds(start or 0, rows - (start or 0))
        for h in range(2):
            s = nt(sides[h][start or 0 :], kx[h, pl.ds(key, size), :])
            s = s if start is None else below(s, True)
            s_scr[h, live, pl.ds(at, size)] = s
            m_scr[h, live, :] = jnp.maximum(m_scr[h, live, :], lane_max(s))

    steps = range(0, rows, grain) if diag else ()
    end = sweep(scores, lo, full, odd, grain, unroll)
    for start in steps:
        scores(end + start, last + start, grain, start)
    tops = [jnp.max(m_scr[h], axis=1, keepdims=True) for h in range(2)]

    def values(key, at, size, start=0):
        live = pl.ds(start, rows - start)
        for h in range(2):
            p = jnp.exp2(s_scr[h, live, pl.ds(at, size)] - tops[h][start:]).astype(BF)
            a_scr[h, live, :] += nn(p, vx[h, pl.ds(key, size), :])

    end = sweep(values, lo, full, odd, grain, unroll)
    for start in steps:
        values(end + start, last + start, grain, start)
    wide = jnp.where(left, a_scr[0], a_scr[1])
    total = jnp.where(left, a_scr[1], a_scr[0])
    o_ref[...] = (wide / pltpu.roll(total, HEAD, 1)).astype(o_ref.dtype)
    lse_ref[...] = jnp.where(left, tops[1], tops[0]) + jnp.log2(total)


def forward_scratch(block, keys):
    return [
        pltpu.VMEM((2, keys, 128), BF),
        pltpu.VMEM((2, keys, 128), BF),
        pltpu.VMEM((2, block, keys + CHUNK), F32),
        pltpu.VMEM((2, block, 128), F32),
        pltpu.VMEM((2, block, 128), F32),
    ]


def backward_scratch(block, keys):
    return (
        [pltpu.VMEM((2, keys, 128), BF)] * 3
        + [pltpu.VMEM((keys, 128), F32)] * 2
        + [pltpu.VMEM((block, 128), F32)]
    )


def forward_prep(k_ref, v_ref, ka_ref, kx, vx):
    kx[0], kx[1] = pair_of(k_ref[...], ka_ref[...])
    v = v_ref[...]
    vx[0], vx[1] = pair_of(v, jnp.ones_like(v))


def backward_prep(k_ref, v_ref, ka_ref, kx, vx, km, dk_acc, dv_acc):
    k, v = k_ref[...], v_ref[...]
    spot = lanes(v.shape) % HEAD
    neg = jnp.where((spot >= PART0) & (spot < PART0 + 3), -1.0, 0.0).astype(BF)
    kx[0], kx[1] = pair_of(k, ka_ref[...])
    vx[0], vx[1] = pair_of(v, neg)
    km[0], km[1] = pair_of(k, jnp.zeros_like(k))
    dk_acc[...] = jnp.zeros_like(dk_acc)
    dv_acc[...] = jnp.zeros_like(dv_acc)


def backward_block(
    lo, full, odd, grain, diag, q, do, o_ref, lse_ref, qa_ref, kx, vx, km,
    dq_ref, dk_acc, dv_acc, dq_acc, unroll,
):
    left = lanes(q.shape) < HEAD
    rows = q.shape[0]
    product = do.astype(F32) * o_ref[...].astype(F32)
    first = jnp.sum(jnp.where(left, product, 0.0), axis=1, keepdims=True)
    second = jnp.sum(jnp.where(left, 0.0, product), axis=1, keepdims=True)
    delta = jnp.where(left, second, first)
    zero = jnp.zeros_like(q)
    qx = pair_of(q, with_parts(qa_ref[...], lse_ref[...]))
    dx = pair_of(do, with_parts(zero, delta))
    qm = pair_of(q, zero)
    dm = pair_of(do, zero)
    dq_acc[...] = jnp.zeros_like(dq_acc)

    def step(key, _, size, start=None):
        at = pl.ds(key, size)
        live = slice(start or 0, rows)
        dq = dk = dv = None
        for h in range(2):
            st = nt(kx[h, at, :], qx[h][live])
            pt = jnp.exp2(st if start is None else below(st, False))
            dp = nt(vx[h, at, :], dx[h][live])
            ds = (pt * dp).astype(BF)
            tv, tk, tq = nn(pt.astype(BF), dm[h][live]), nn(ds, qm[h][live]), tn(ds, km[h, at, :])
            dv = tv if dv is None else dv + tv
            dk = tk if dk is None else dk + tk
            dq = tq if dq is None else dq + tq
        dv_acc[at, :] += dv
        dk_acc[at, :] += dk
        dq_acc[live, :] += dq

    end = sweep(step, lo, full, odd, grain, unroll)
    for start in range(0, rows, grain) if diag else ():
        step(end + start, 0, grain, start)
    dq_ref[...] = (dq_acc[...] * SCALE).astype(dq_ref.dtype)


def cross_forward_kernel(
    q_ref, k_ref, v_ref, qa_ref, ka_ref, o_ref, lse_ref, kx, vx, s_scr, m_scr, a_scr
):
    @pl.when(pl.program_id(1) == 0)
    def _():
        forward_prep(k_ref, v_ref, ka_ref, kx, vx)

    full = k_ref.shape[0] // CHUNK
    forward_block(
        0, full, None, CHUNK, False, q_ref, qa_ref, kx, vx, o_ref, lse_ref, s_scr, m_scr, a_scr, full
    )


def cross_forward(q, kv, qa, ka):
    rows, width = q.shape
    keys = kv.shape[0]
    block = min(512, rows)
    pairs = width // 128
    row = pl.BlockSpec((block, 128), lambda h, i: (i, h))
    return pl.pallas_call(
        cross_forward_kernel,
        grid=(pairs, rows // block),
        in_specs=[
            row,
            pl.BlockSpec((keys, 128), lambda h, i: (0, h)),
            pl.BlockSpec((keys, 128), lambda h, i: (0, h + pairs)),
            pl.BlockSpec((block, 128), lambda h, i: (i, 0)),
            pl.BlockSpec((keys, 128), lambda h, i: (0, 0)),
        ],
        out_specs=[row, row],
        out_shape=[
            jax.ShapeDtypeStruct((rows, width), BF),
            jax.ShapeDtypeStruct((rows, width), F32),
        ],
        scratch_shapes=forward_scratch(block, keys),
        compiler_params=params(),
        cost_estimate=cost(16 * rows * keys * width, 8 * rows * width, rows * keys * 12),
        name="cross_forward",
    )(q, kv, kv, qa, ka)


def cross_backward_kernel(
    q_ref, k_ref, v_ref, do_ref, o_ref, lse_ref, qa_ref, ka_ref,
    dq_ref, dk_ref, dv_ref, kx, vx, km, dk_acc, dv_acc, dq_acc,
):
    @pl.when(pl.program_id(1) == 0)
    def _():
        backward_prep(k_ref, v_ref, ka_ref, kx, vx, km, dk_acc, dv_acc)

    backward_block(
        0, k_ref.shape[0] // CHUNK, None, CHUNK, False, q_ref[...], do_ref[...], o_ref, lse_ref,
        qa_ref, kx, vx, km, dq_ref, dk_acc, dv_acc, dq_acc, k_ref.shape[0] // CHUNK,
    )

    @pl.when(pl.program_id(1) == pl.num_programs(1) - 1)
    def _():
        dk_ref[...] = (dk_acc[...] * LN2).astype(BF)
        dv_ref[...] = dv_acc[...].astype(BF)


def cross_backward(q, kv, do, o, lse, qa, ka):
    rows, width = q.shape
    keys = kv.shape[0]
    block = min(512, rows)
    pairs = width // 128
    row = pl.BlockSpec((block, 128), lambda h, i: (i, h))
    col = pl.BlockSpec((keys, 128), lambda h, i: (0, h))
    return pl.pallas_call(
        cross_backward_kernel,
        grid=(pairs, rows // block),
        in_specs=[
            row,
            col,
            pl.BlockSpec((keys, 128), lambda h, i: (0, h + pairs)),
            row,
            row,
            row,
            pl.BlockSpec((block, 128), lambda h, i: (i, 0)),
            pl.BlockSpec((keys, 128), lambda h, i: (0, 0)),
        ],
        out_specs=[row, col, col],
        out_shape=[
            jax.ShapeDtypeStruct((rows, width), BF),
            jax.ShapeDtypeStruct((keys, width), BF),
            jax.ShapeDtypeStruct((keys, width), BF),
        ],
        scratch_shapes=backward_scratch(block, keys),
        compiler_params=params(),
        cost_estimate=cost(40 * rows * keys * width, 12 * rows * width, rows * keys * 12),
        name="cross_backward",
    )(q, kv, kv, do, o, lse, qa, ka)


def grain_of(block):
    return min(256, block)


def needed_blocks(segs, block):
    total = segs.shape[0]
    grain = grain_of(block)
    first = segs.reshape(total // block, block)[:, 0]
    start = jnp.sum((segs[None, :] < first[:, None]).astype(jnp.int32), axis=1)
    ends = (jnp.arange(total // block, dtype=jnp.int32) + 1) * block
    return (ends - start // grain * grain) // grain


def self_range(count, i, block):
    grain = grain_of(block)
    before = count - block // grain
    per = CHUNK // grain
    lo = pl.multiple_of((i + 1) * block - count * grain, grain)
    return lo, before // per, before % per, grain


def self_forward_kernel(
    count_ref, slot_ref, q_ref, k_ref, v_ref, qa_ref, ka_ref, o_ref, lse_ref,
    kx, vx, s_scr, m_scr, a_scr,
):
    i = pl.program_id(1)

    @pl.when(i == 0)
    def _():
        forward_prep(k_ref, v_ref, ka_ref, kx, vx)

    forward_block(
        *self_range(count_ref[i], i, q_ref.shape[0]), True, q_ref, qa_ref, kx, vx, o_ref, lse_ref,
        s_scr, m_scr, a_scr, 1,
    )


def self_forward(counts, slots, q, k, v, qa, ka, block):
    total, width = q.shape
    row = pl.BlockSpec((block, 128), lambda h, i, n, s: (i, h))
    col = pl.BlockSpec((total, 128), lambda h, i, n, s: (0, h))
    return pl.pallas_call(
        self_forward_kernel,
        grid_spec=pltpu.PrefetchScalarGridSpec(
            num_scalar_prefetch=2,
            grid=(width // 128, total // block),
            in_specs=[
                row,
                col,
                col,
                pl.BlockSpec((block, 128), lambda h, i, n, s: (i, 0)),
                pl.BlockSpec((total, 128), lambda h, i, n, s: (0, 0)),
            ],
            out_specs=[pl.BlockSpec((block, 128), lambda h, i, n, s: (s[i], h)), row],
            scratch_shapes=forward_scratch(block, total),
        ),
        out_shape=[
            jax.ShapeDtypeStruct((total, width), BF),
            jax.ShapeDtypeStruct((total, width), F32),
        ],
        compiler_params=params(),
        cost_estimate=cost(8 * total * total * width, 8 * total * width, total * total * 3),
        name="self_forward",
    )(counts, slots, q, k, v, qa, ka)


def self_backward_kernel(
    count_ref, slot_ref, q_ref, k_ref, v_ref, own_ref, far_ref, o_ref, lse_ref, qa_ref, ka_ref,
    dq_ref, dk_ref, dv_ref, kx, vx, km, dk_acc, dv_acc, dq_acc, *, per_dev,
):
    i = pl.program_id(0)
    do = jnp.where(slot_ref[i] < per_dev, own_ref[...], far_ref[...])

    @pl.when(i == 0)
    def _():
        backward_prep(k_ref, v_ref, ka_ref, kx, vx, km, dk_acc, dv_acc)

    backward_block(
        *self_range(count_ref[i], i, q_ref.shape[0]), True, q_ref[...], do, o_ref, lse_ref, qa_ref,
        kx, vx, km, dq_ref, dk_acc, dv_acc, dq_acc, 1,
    )

    @pl.when(i == pl.num_programs(0) - 1)
    def _():
        dk_ref[...] = (dk_acc[...] * LN2).astype(BF)
        dv_ref[...] = dv_acc[...].astype(BF)


def self_backward(pair, counts, slots, q, k, v, own, far, o, lse, qa, ka, block):
    total = q.shape[0]
    per_dev = own.shape[0] // block
    row = pl.BlockSpec((block, 128), lambda i, n, s: (i, pair))
    col = pl.BlockSpec((total, 128), lambda i, n, s: (0, pair))
    whole = pl.BlockSpec((total, 128), lambda i, n, s: (0, 0))
    return pl.pallas_call(
        functools.partial(self_backward_kernel, per_dev=per_dev),
        grid_spec=pltpu.PrefetchScalarGridSpec(
            num_scalar_prefetch=2,
            grid=(total // block,),
            in_specs=[
                row,
                col,
                col,
                pl.BlockSpec((block, 128), lambda i, n, s: (jnp.minimum(s[i], per_dev - 1), pair)),
                pl.BlockSpec((block, 128), lambda i, n, s: (jnp.maximum(s[i] - per_dev, 0), pair)),
                pl.BlockSpec((block, 128), lambda i, n, s: (s[i], pair)),
                row,
                pl.BlockSpec((block, 128), lambda i, n, s: (i, 0)),
                whole,
            ],
            out_specs=[pl.BlockSpec((block, 128), lambda i, n, s: (i, 0)), whole, whole],
            scratch_shapes=backward_scratch(block, total),
        ),
        out_shape=[jax.ShapeDtypeStruct((total, 128), BF)] * 3,
        compiler_params=params(),
        cost_estimate=cost(4 * total * total * 128, 2 * total * 128),
        name="self_backward",
    )(counts, slots, q, k, v, own, far, o, lse, qa, ka)


def qkv_kernel(order_ref, own_ref, far_ref, g_ref, w_ref, n_ref, q_ref, k_ref, v_ref, *, per_dev):
    x = jnp.where(pl.program_id(0) < per_dev, own_ref[...], far_ref[...]).astype(F32)
    n = (x * rms_scale(x) * g_ref[...]).astype(BF)
    n_ref[...] = n
    width = q_ref.shape[1]
    out = nn(n, w_ref[...])
    q_ref[...] = (out[:, :width] * QSCALE).astype(BF)
    k_ref[...] = out[:, width : 2 * width].astype(BF)
    v_ref[...] = out[:, 2 * width :].astype(BF)


def qkv_forward(order, own, far, gain, w, block):
    dim = own.shape[1]
    total = own.shape[0] + far.shape[0]
    width = w.shape[1] // 3
    per_dev = own.shape[0] // block
    here = lambda i, o: (o[i], 0)
    whole = lambda i, o: (0, 0)
    return pl.pallas_call(
        functools.partial(qkv_kernel, per_dev=per_dev),
        grid_spec=pltpu.PrefetchScalarGridSpec(
            num_scalar_prefetch=1,
            grid=(total // block,),
            in_specs=[
                pl.BlockSpec((block, dim), lambda i, o: (jnp.minimum(i, per_dev - 1), 0)),
                pl.BlockSpec((block, dim), lambda i, o: (jnp.maximum(i - per_dev, 0), 0)),
                pl.BlockSpec((1, dim), whole),
                pl.BlockSpec(w.shape, whole),
            ],
            out_specs=[pl.BlockSpec((block, dim), here)] + [pl.BlockSpec((block, width), here)] * 3,
        ),
        out_shape=[jax.ShapeDtypeStruct((total, dim), BF)]
        + [jax.ShapeDtypeStruct((total, width), BF)] * 3,
        compiler_params=params(),
        cost_estimate=cost(6 * total * dim * width, 8 * total * dim),
        name="qkv_forward",
    )(order, own, far, gain, w)


def enc_kv_kernel(own_ref, far_ref, w_ref, kv_ref, *, own_blocks):
    enc = jnp.where(pl.program_id(0) < own_blocks, own_ref[...], far_ref[...])
    half = w_ref.shape[1] // 2
    for c in range(2):
        at = slice(c * half, (c + 1) * half)
        kv_ref[:, at] = nn(enc, w_ref[:, at]).astype(BF)


def enc_forward(own, far, w2):
    rows, dim = own.shape
    block = min(512, rows)
    keys = rows + far.shape[0]
    ours = rows // block
    return pl.pallas_call(
        functools.partial(enc_kv_kernel, own_blocks=ours),
        grid=(keys // block,),
        in_specs=[
            pl.BlockSpec((block, dim), lambda i: (jnp.minimum(i, ours - 1), 0)),
            pl.BlockSpec((block, dim), lambda i: (jnp.maximum(i - ours, 0), 0)),
            pl.BlockSpec((dim, 2 * dim), lambda i: (0, 1)),
        ],
        out_specs=pl.BlockSpec((block, 2 * dim), lambda i: (i, 0)),
        out_shape=jax.ShapeDtypeStruct((keys, 2 * dim), BF),
        compiler_params=params(),
        cost_estimate=cost(4 * keys * dim * dim, 8 * keys * dim),
        name="enc_forward",
    )(own, far, w2)


def after_self_kernel(turn_ref, x_ref, *refs, count):
    o_refs, w_refs = refs[:count], refs[count : 2 * count]
    g_ref, wq_ref, h_ref, n_ref, q_ref, s_ref = refs[2 * count :]
    x = x_ref[...].astype(F32)
    a = nn(o_refs[0][...], w_refs[0][...])
    for o_ref, w_ref in zip(o_refs[1:], w_refs[1:]):
        a = a + nn(o_ref[...], w_ref[...])
    h = x + a
    h_ref[...] = h
    n = (h * rms_scale(h) * g_ref[...]).astype(BF)
    n_ref[...] = n
    q_ref[...] = (nn(n, wq_ref[...]) * QSCALE).astype(BF)

    @pl.when(pl.program_id(0) == 0)
    def _():
        s_ref[...] = jnp.zeros_like(s_ref)

    s_ref[0:1, :] += jnp.sum(x * x, axis=0, keepdims=True)
    s_ref[1:2, :] += jnp.sum(a * a, axis=0, keepdims=True)


def turn_specs(count, width, dim):
    return [pl.BlockSpec((width, dim), lambda i, t, k=k: (t[k], 0)) for k in range(count)]


def after_self(turn, x, pieces, wo, gain, w2):
    rows, dim = x.shape
    count, width = len(pieces), pieces[0].shape[1]
    block = min(512, rows)
    line = lambda i, t: (i, 0)
    whole = lambda i, t: (0, 0)
    row = pl.BlockSpec((block, dim), line)
    return pl.pallas_call(
        functools.partial(after_self_kernel, count=count),
        grid_spec=pltpu.PrefetchScalarGridSpec(
            num_scalar_prefetch=1,
            grid=(rows // block,),
            in_specs=[row]
            + [pl.BlockSpec((block, width), line)] * count
            + turn_specs(count, width, dim)
            + [pl.BlockSpec((1, dim), whole), pl.BlockSpec((dim, dim), lambda i, t: (0, 1))],
            out_specs=[row, row, row, pl.BlockSpec((8, dim), whole)],
        ),
        out_shape=[
            jax.ShapeDtypeStruct((rows, dim), F32),
            jax.ShapeDtypeStruct((rows, dim), BF),
            jax.ShapeDtypeStruct((rows, dim), BF),
            jax.ShapeDtypeStruct((8, dim), F32),
        ],
        compiler_params=params(),
        cost_estimate=cost(4 * rows * dim * dim, 14 * rows * dim),
        name="after_self",
    )(turn, x, *pieces, *([wo] * count), gain, w2)


GELU_C = math.sqrt(2.0 / math.pi)
GELU_A = 0.044715


PIECES = (4, 8, 3, 64)


def mlp_kernel(
    o_ref, h1_ref, wc_ref, g_ref, t_ref, gu_ref, wd_ref,
    y_ref, dh_ref, dc_ref, do_ref, s_ref, g_out,
    n_scr, h_scr, m_scr, dn_scr, hid_scr, du_scr, dw_scr, wg_scr, wu_scr, gu_out, d_out, sems,
):
    j = pl.program_id(0)
    last = pl.num_programs(0) - 1
    rows = o_ref.shape[0]
    step = min(256, rows)
    spans = [pl.ds(r, step) for r in range(0, rows, step)]
    gain = g_ref[...]
    n_fsdp, n_two, _, tall, _ = gu_ref.shape
    third = 256
    high = 3 * tall

    @pl.when(j == 0)
    def _():
        total = None
        for at in spans:
            c = nn(o_ref[at, :], wc_ref[...])
            h = h1_ref[at, :] + c
            h_scr[at, :] = h
            n_scr[at, :] = (h * rms_scale(h) * gain).astype(BF)
            part = jnp.sum(c * c, axis=0, keepdims=True)
            total = part if total is None else total + part
        s_ref[...] = jnp.zeros_like(s_ref)
        s_ref[0:1, :] = total
        m_scr[...] = jnp.zeros_like(m_scr)
        dn_scr[...] = jnp.zeros_like(dn_scr)

    for z in range(n_fsdp):
        for p in range(n_two):
            for t in range(3):
                at, to = pl.ds(z * high + t * tall, tall), pl.ds(p * third, third)
                wg_scr[at, to] = gu_ref[z, p, 0, :, t * third : (t + 1) * third]
                wu_scr[at, to] = gu_ref[z, p, 1, :, t * third : (t + 1) * third]
    wg, wu = wg_scr[...], wu_scr[...]
    wd = wd_ref[...].reshape(-1, wd_ref.shape[-1])
    for at in spans:
        n = n_scr[at, :]
        u = nn(n, wg)
        w = nn(n, wu)
        dhid = nt(t_ref[at, :], wd)
        square = u * u
        th = jnp.tanh(GELU_C * u * (1.0 + GELU_A * square))
        half = 0.5 * (1.0 + th)
        gel = u * half
        slope = half + 0.5 * u * (1.0 - th * th) * (GELU_C * (1.0 + 3.0 * GELU_A * square))
        hid = (gel * w).astype(BF)
        du = (dhid * w * slope).astype(BF)
        dw = (dhid * gel).astype(BF)
        hid_scr[at, :] = hid
        du_scr[at, :] = du
        dw_scr[at, :] = dw
        m_scr[at, :] += nn(hid, wd)
        dn_scr[at, :] += nt(du, wg) + nt(dw, wu)

    slot = lax.rem(j, 2)

    def copies(step_of, slot_of):
        return (
            pltpu.make_async_copy(
                gu_out.at[slot_of],
                g_out.at[:, pl.ds(step_of * n_two, n_two), pl.ds(0, 2)],
                sems.at[slot_of, 0],
            ),
            pltpu.make_async_copy(d_out.at[slot_of], g_out.at[step_of, :, 2], sems.at[slot_of, 1]),
        )

    @pl.when(j >= 2)
    def _():
        for copy in copies(j - 2, slot):
            copy.wait()

    d_out[slot] = tn(hid_scr[...], t_ref[...]).astype(BF).reshape(d_out.shape[1:])
    for side, source in ((0, du_scr), (1, dw_scr)):
        grad = tn(n_scr[...], source[...]).astype(BF)
        for z in range(n_fsdp):
            for p in range(n_two):
                for t in range(3):
                    gu_out[slot, z, p, side, :, t * third : (t + 1) * third] = grad[
                        z * high + t * tall : z * high + (t + 1) * tall,
                        p * third : (p + 1) * third,
                    ]
    for copy in copies(j, slot):
        copy.start()

    @pl.when(j == last)
    def _():
        total = gains = None
        for at in spans:
            h = h_scr[at, :]
            y = h + m_scr[at, :]
            y_ref[at, :] = y.astype(BF)
            dh, dg = norm_back(h, gain, dn_scr[at, :])
            dh = dh + t_ref[at, :].astype(F32)
            dh_ref[at, :] = dh
            dc = dh.astype(BF)
            dc_ref[at, :] = dc
            do_ref[at, :] = nt(dc, wc_ref[...]).astype(BF)
            part = jnp.sum(y * y, axis=0, keepdims=True)
            total = part if total is None else total + part
            gains = dg if gains is None else gains + dg
        s_ref[1:2, :] = total
        s_ref[2:3, :] = gains
        for copy in copies(j - 1, 1 - slot) + copies(j, slot):
            copy.wait()


def feed_forward(o, h1, w2, gain, cot, w3):
    rows, dim = o.shape
    n_fsdp, n_plane, _, tall, _ = w3.shape
    steps = n_fsdp
    two = n_plane // steps
    width = two * 256
    whole = lambda j: (0, 0)
    once = pl.Buffered(1)
    full = pl.BlockSpec((rows, dim), whole, pipeline_mode=once)
    flops = 18 * rows * dim * width * steps + 6 * rows * dim * dim
    return pl.pallas_call(
        mlp_kernel,
        grid=(steps,),
        in_specs=[
            full,
            full,
            pl.BlockSpec((dim, dim), lambda j: (0, 4), pipeline_mode=once),
            pl.BlockSpec((1, dim), whole),
            full,
            pl.BlockSpec((n_fsdp, two, 2, tall, dim), lambda j: (0, j, 0, 0, 0)),
            pl.BlockSpec((1, n_plane, 1, tall, dim), lambda j: (j, 0, 2, 0, 0)),
        ],
        out_specs=[
            full,
            full,
            full,
            full,
            pl.BlockSpec((8, dim), whole),
            pl.BlockSpec(memory_space=pl.ANY),
        ],
        out_shape=[
            jax.ShapeDtypeStruct((rows, dim), BF),
            jax.ShapeDtypeStruct((rows, dim), F32),
            jax.ShapeDtypeStruct((rows, dim), BF),
            jax.ShapeDtypeStruct((rows, dim), BF),
            jax.ShapeDtypeStruct((8, dim), F32),
            jax.ShapeDtypeStruct(w3.shape, BF),
        ],
        scratch_shapes=[
            pltpu.VMEM((rows, dim), BF),
            pltpu.VMEM((rows, dim), F32),
            pltpu.VMEM((rows, dim), F32),
            pltpu.VMEM((rows, dim), F32),
            pltpu.VMEM((rows, width), BF),
            pltpu.VMEM((rows, width), BF),
            pltpu.VMEM((rows, width), BF),
            pltpu.VMEM((dim, width), BF),
            pltpu.VMEM((dim, width), BF),
            pltpu.VMEM((2, n_fsdp, two, 2, tall, dim), BF),
            pltpu.VMEM((2, n_plane, tall, dim), BF),
            pltpu.SemaphoreType.DMA((2, 2)),
        ],
        compiler_params=params(),
        cost_estimate=cost(flops, 40 * MIB, rows * width * steps),
        name="feed_forward",
    )(o, h1, w2, gain, cot, w3, w3)


def placed(me_ref, near_ref, far_ref, size):
    core, x = me_ref[0], me_ref[1]
    for c, ref in enumerate((near_ref, far_ref)):
        for a in range(2):
            yield ref.at[a], pl.multiple_of(((a ^ x) * 2 + (c ^ core)) * size, 16)


def unpack_kernel(me_ref, near_ref, far_ref, gate_ref, up_ref, down_ref):
    core, x = me_ref[0], me_ref[1]
    tall = near_ref.shape[3]
    third = 256
    for c in range(2):
        for a in range(2):
            for i in range(2):
                p = a * 4 + c * 2 + i
                piece = lambda k: jnp.where(
                    core == c, near_ref[a ^ x, i, k], far_ref[a ^ x, i, k]
                ).astype(F32)
                gate, up = piece(0), piece(1)
                for t in range(3):
                    at, to = pl.ds(t * tall, tall), pl.ds(p * third, third)
                    gate_ref[at, to] = gate[:, t * third : (t + 1) * third]
                    up_ref[at, to] = up[:, t * third : (t + 1) * third]
                down_ref[pl.ds(p * tall, tall), :] = piece(2)


def settle_mid_kernel(me_ref, near_ref, far_ref, *outs):
    dim = outs[0].shape[1]
    size = near_ref.shape[1]
    for ref, row in placed(me_ref, near_ref, far_ref, size):
        for m, out in enumerate(outs):
            out[pl.ds(row, size), :] = ref[:, m * dim : (m + 1) * dim].astype(F32)


def settle_qkv_kernel(me_ref, near_ref, far_ref, q_ref, k_ref, v_ref, tail_ref):
    place = me_ref[2]
    size = near_ref.shape[2]
    width = q_ref.shape[1] // 2
    for ref, row in placed(me_ref, near_ref, far_ref, size):
        at = pl.ds(row, size)
        tail = None
        for i in range(2):
            block = ref[i ^ place].astype(F32)
            for t, out in enumerate((q_ref, k_ref, v_ref)):
                out[at, i * width : (i + 1) * width] = block[:, t * width : (t + 1) * width]
            part = block[:, 3 * width :]
            tail = part if tail is None else tail + part
        tail_ref[at, :] = tail


def settle(kernel, me, near, far, shapes):
    vmem = pl.BlockSpec(memory_space=pltpu.VMEM)
    return pl.pallas_call(
        kernel,
        in_specs=[pl.BlockSpec(memory_space=pltpu.SMEM), vmem, vmem],
        out_specs=[vmem] * len(shapes),
        out_shape=[jax.ShapeDtypeStruct(shape, F32) for shape in shapes],
        compiler_params=params(),
        name=kernel.__name__[:-7],
    )(me, near, far)


def deal_rows(core, full, send_ref, keep_ref):
    count, size = send_ref.shape[:2]
    for i in range(count):
        for ref, c in ((send_ref, 1 - core), (keep_ref, core)):
            ref[i] = full[pl.ds(pl.multiple_of((2 * i + c) * size, 16), size), :]


def mid_grads_kernel(turn_ref, *refs, count):
    n_in = count + 9
    sources = refs[:n_in]
    wk_ref, wv_ref, g_ref, far_out = refs[n_in : n_in + 4]
    buffers = refs[n_in + 4 : 2 * n_in + 4]
    sems = refs[-1]
    m = pl.program_id(0)
    dim = g_ref.shape[0]
    copies = [
        pltpu.make_async_copy(
            source.at[pl.ds(0, buffer.shape[0])] if source.shape != buffer.shape else source,
            buffer,
            sems.at[i],
        )
        for i, (source, buffer) in enumerate(zip(sources, buffers))
    ]
    n2, dq, da, *o_pieces, own, far, dk, dv, o2, dc = buffers
    ours = own.shape[0]
    width = o_pieces[0].shape[1]

    @pl.when(m == 0)
    def _():
        for copy in copies:
            copy.start()
        for copy in copies[:2]:
            copy.wait()
        g_ref[...] = tn(n2[...], dq[...]).astype(BF)

    @pl.when(m == 1)
    def _():
        for copy in copies[2 : 3 + count]:
            copy.wait()
        for i in range(count):
            base = pl.multiple_of(turn_ref[i] * width, width)
            term = tn(o_pieces[i][...], da[...]).astype(BF)

            @pl.when(base < dim)
            def _():
                g_ref[pl.ds(base, width), :] = term

    for at, right, first in ((2, dk, 3), (3, dv, 6)):

        @pl.when(m == at)
        def _():
            for copy in copies[count + first : count + 6 if at == 2 else count + 7]:
                copy.wait()
            g_ref[...] = (tn(own[...], right[:ours, :]) + tn(far[...], right[ours:, :])).astype(BF)

    @pl.when(m == 4)
    def _():
        for copy in copies[count + 7 :]:
            copy.wait()
        g_ref[...] = tn(o2[...], dc[...]).astype(BF)

    block = far_out.shape[0]

    @pl.when(m >= 5)
    def _():
        at = pl.ds(pl.multiple_of(ours + (m - 5) * block, block), block)
        far_out[...] = (nt(dk[at, :], wk_ref[...]) + nt(dv[at, :], wv_ref[...])).astype(BF)


def dealt_out(dim, block, total, index, deal):
    if not deal:
        return [pl.BlockSpec((dim, block), lambda *a: (0, index(*a)))], [
            jax.ShapeDtypeStruct((dim, total), BF)
        ]
    spec = pl.BlockSpec((8, dim // 16, block), lambda *a: (0, 0, index(*a)))
    return [spec] * 2, [jax.ShapeDtypeStruct((8, dim // 16, total), BF)] * 2


def mid_grads(turn, pieces, da, n2, dq2, own, far, dk2, dv2, o2, dc, w2):
    rows, dim = n2.shape
    args = (n2, dq2, da, *pieces, own, far, dk2, dv2, o2, dc)
    shapes = [(rows, a.shape[1]) for a in args[: 3 + len(pieces)]]
    shapes += [a.shape for a in args[3 + len(pieces) :]]
    flops = 2 * dim * dim * (3 * rows + 2 * dk2.shape[0] + 2 * far.shape[0])
    block = min(512, own.shape[0])
    far_blocks = far.shape[0] // block
    once = pl.Buffered(1)
    column = lambda m, t: (0, jnp.where(m < 2, 1 - m, jnp.minimum(m, 4)))
    return pl.pallas_call(
        functools.partial(mid_grads_kernel, count=len(pieces)),
        grid_spec=pltpu.PrefetchScalarGridSpec(
            num_scalar_prefetch=1,
            grid=(5 + far_blocks,),
            in_specs=[pl.BlockSpec(memory_space=pl.ANY)] * len(args)
            + [
                pl.BlockSpec((dim, dim), lambda m, t: (0, 2), pipeline_mode=once),
                pl.BlockSpec((dim, dim), lambda m, t: (0, 3), pipeline_mode=once),
            ],
            out_specs=[
                pl.BlockSpec((dim, dim), column),
                pl.BlockSpec((block, dim), lambda m, t: (jnp.maximum(m - 5, 0), 0)),
            ],
            scratch_shapes=[pltpu.VMEM(shape, BF) for shape in shapes]
            + [pltpu.SemaphoreType.DMA((len(args),))],
        ),
        out_shape=[
            jax.ShapeDtypeStruct((dim, 5 * dim), BF),
            jax.ShapeDtypeStruct(far.shape, BF),
        ],
        compiler_params=params(),
        cost_estimate=cost(flops, 30 * MIB),
        name="mid_grads",
    )(turn, *args, w2, w2)


def enc_finish_kernel(dk_ref, dv_ref, wk_ref, wv_ref, *refs):
    total = nt(dk_ref[...], wk_ref[...]) + nt(dv_ref[...], wv_ref[...])
    for ref in refs[:-1]:
        total = total + ref[...].astype(F32)
    refs[-1][...] = total


def enc_finish(dk, dv, w2, got):
    rows, dim = got[0].shape
    block = min(512, rows)
    row = pl.BlockSpec((block, dim), lambda i: (i, 0))
    return pl.pallas_call(
        enc_finish_kernel,
        grid=(rows // block,),
        in_specs=[
            row,
            row,
            pl.BlockSpec((dim, dim), lambda i: (0, 2)),
            pl.BlockSpec((dim, dim), lambda i: (0, 3)),
        ]
        + [row] * len(got),
        out_specs=row,
        out_shape=jax.ShapeDtypeStruct((rows, dim), F32),
        compiler_params=params(),
        cost_estimate=cost(4 * rows * dim * dim, 12 * rows * dim),
        name="enc_finish",
    )(dk, dv, w2, w2, *got)


def before_self_kernel(turn_ref, dq_ref, wq_ref, h_ref, dh_ref, g_ref, *refs, count):
    w_refs = refs[:count]
    d1_ref, da_ref, s_ref = refs[count : count + 3]
    do_refs = refs[count + 3 :]
    dn = nt(dq_ref[...], wq_ref[...])
    dh, dg = norm_back(h_ref[...], g_ref[...], dn)
    d1 = dh_ref[...] + dh
    d1_ref[...] = d1
    da = d1.astype(BF)
    da_ref[...] = da
    for do_ref, w_ref in zip(do_refs, w_refs):
        do_ref[...] = nt(da, w_ref[...]).astype(BF)

    @pl.when(pl.program_id(0) == 0)
    def _():
        s_ref[...] = jnp.zeros_like(s_ref)

    s_ref[0:1, :] += dg


def before_self(turn, dq, w2, h1, dh2, gain, wo, width):
    rows, dim = dq.shape
    count = turn.shape[0]
    block = min(512, rows)
    line = lambda i, t: (i, 0)
    whole = lambda i, t: (0, 0)
    row = pl.BlockSpec((block, dim), line)
    return pl.pallas_call(
        functools.partial(before_self_kernel, count=count),
        grid_spec=pltpu.PrefetchScalarGridSpec(
            num_scalar_prefetch=1,
            grid=(rows // block,),
            in_specs=[
                row,
                pl.BlockSpec((dim, dim), lambda i, t: (0, 1)),
                row,
                row,
                pl.BlockSpec((1, dim), whole),
            ]
            + turn_specs(count, width, dim),
            out_specs=[row, row, pl.BlockSpec((8, dim), whole)]
            + [pl.BlockSpec((block, width), line)] * count,
        ),
        out_shape=[
            jax.ShapeDtypeStruct((rows, dim), F32),
            jax.ShapeDtypeStruct((rows, dim), BF),
            jax.ShapeDtypeStruct((8, dim), F32),
        ]
        + [jax.ShapeDtypeStruct((rows, width), BF)] * count,
        compiler_params=params(),
        cost_estimate=cost(4 * rows * dim * dim, 18 * rows * dim),
        name="before_self",
    )(turn, dq, w2, h1, dh2, gain, *([wo] * count))


def joined(refs):
    return jnp.concatenate([r[...] for r in refs], axis=1)


def qkv_grads_kernel(core_ref, *refs, count, deal):
    d_refs = refs[:count]
    n_ref, w_ref, gain_ref, extra_ref = refs[count : count + 4]
    outs = refs[count + 4 :]
    acc, full = outs[-2:]
    i = pl.program_id(0)
    term = tn(n_ref[...], joined(d_refs))

    @pl.when(i == 0)
    def _():
        acc[...] = term

    @pl.when(i > 0)
    def _():
        acc[...] += term

    @pl.when(i == pl.num_programs(0) - 1)
    def _():
        width = acc.shape[1]
        grad = acc[...]
        gains = jnp.sum(grad * w_ref[...].astype(F32), axis=1, keepdims=True) / gain_ref[:, :1]
        extra = extra_ref[...]
        full[:, :width] = grad.astype(BF)
        full[:, width:] = jnp.where(lanes(extra.shape) == 0, gains, extra).astype(BF)
        if deal:
            deal_rows(core_ref[0], full, outs[0], outs[1])
        else:
            outs[0][...] = full[...]


def qkv_grads(core, ds, n, w, gain, extra, deal):
    total, dim = n.shape
    block = min(512, total)
    width = w.shape[1]
    specs, outs = dealt_out(dim, width + 128, width + 128, lambda i, c: 0, deal)
    whole = lambda i, c: (0, 0)
    return pl.pallas_call(
        functools.partial(qkv_grads_kernel, count=len(ds), deal=deal),
        grid_spec=pltpu.PrefetchScalarGridSpec(
            num_scalar_prefetch=1,
            grid=(total // block,),
            in_specs=[pl.BlockSpec((block, 128), lambda i, c: (i, 0))] * len(ds)
            + [
                pl.BlockSpec((block, dim), lambda i, c: (i, 0)),
                pl.BlockSpec(w.shape, whole),
                pl.BlockSpec((dim, 128), whole),
                pl.BlockSpec((dim, 128), whole),
            ],
            out_specs=specs,
            scratch_shapes=[pltpu.VMEM((dim, width), F32), pltpu.VMEM((dim, width + 128), BF)],
        ),
        out_shape=outs,
        compiler_params=params(),
        cost_estimate=cost(total * dim, total),
        name="qkv_grads",
    )(core, *ds, n, w, gain, extra)


def qkv_back_kernel(order_ref, *refs, count):
    dn_ref = refs[count + 1]
    dn_ref[...] = nt(joined(refs[:count]), refs[count][...]).astype(dn_ref.dtype)


def qkv_back(order, first, ds, w, rows, dtype, block):
    dim = w.shape[0]
    return pl.pallas_call(
        functools.partial(qkv_back_kernel, count=len(ds)),
        grid_spec=pltpu.PrefetchScalarGridSpec(
            num_scalar_prefetch=1,
            grid=(rows // block,),
            in_specs=[pl.BlockSpec((block, 128), lambda i, o: (o[i + first], 0))] * len(ds)
            + [pl.BlockSpec(w.shape, lambda i, o: (0, 0))],
            out_specs=pl.BlockSpec((block, dim), lambda i, o: (i, 0)),
        ),
        out_shape=jax.ShapeDtypeStruct((rows, dim), dtype),
        compiler_params=params(),
        cost_estimate=cost(rows * dim, rows),
        name="qkv_back",
    )(order, *ds, w)


def finish_kernel(x_ref, dh_ref, g_ref, own_ref, *refs):
    dn = own_ref[...]
    for ref in refs[:-1]:
        dn = dn + ref[...].astype(F32)
    dh, _ = norm_back(x_ref[...].astype(F32), g_ref[...], dn)
    refs[-1][...] = dh_ref[...] + dh


def finish(x, dh1, gain, own, got):
    rows, dim = x.shape
    block = min(256, rows)
    row = pl.BlockSpec((block, dim), lambda i: (i, 0))
    return pl.pallas_call(
        finish_kernel,
        grid=(rows // block,),
        in_specs=[row, row, pl.BlockSpec((1, dim), lambda i: (0, 0)), row] + [row] * len(got),
        out_specs=row,
        out_shape=jax.ShapeDtypeStruct((rows, dim), F32),
        compiler_params=params(),
        cost_estimate=cost(10 * rows * dim, 16 * rows * dim),
        name="finish",
    )(x, dh1, gain, own, *got)


def turned(n, k):
    return [(i, (i + k) % n) for i in range(n)]


def rows_of(array, index, count):
    size = array.shape[0] // count
    return lax.dynamic_slice_in_dim(array, index * size, size, 0)


def assemble_kernel(place_ref, near_ref, far_ref, w_ref, g_ref):
    z, core = place_ref[0], place_ref[1]
    count, size = near_ref.shape[0], near_ref.shape[1]
    width = w_ref.shape[1]
    for d in range(count):
        base = lax.rem(z - d + count, count) * (2 * size)
        for ref, half in ((near_ref, core), (far_ref, 1 - core)):
            at = pl.ds(pl.multiple_of(base + half * size, 16), size)
            w_ref[at, :] = ref[d, :, :width]
            g_ref[at, :] = ref[d, :, width:]


def gather_first(own, z, part, n_fsdp, n_parts):
    size = own.shape[0] // 2
    width = own.shape[1] - 128
    if n_parts % 2 or size % 16:
        full = lax.all_gather(own, "fsdp", axis=0, tiled=True)
        return full[:, :width], full[:, width:]
    core = part % 2
    mine = lax.dynamic_slice_in_dim(own, core * size, size, 0)
    near = jnp.stack(
        [mine] + [lax.ppermute(mine, "fsdp", turned(n_fsdp, d)) for d in range(1, n_fsdp)]
    )
    far = lax.ppermute(near, "parts", [(i, i ^ 1) for i in range(n_parts)])
    vmem = pl.BlockSpec(memory_space=pltpu.VMEM)
    total = n_fsdp * own.shape[0]
    return pl.pallas_call(
        assemble_kernel,
        in_specs=[pl.BlockSpec(memory_space=pltpu.SMEM), vmem, vmem],
        out_specs=[vmem, vmem],
        out_shape=[
            jax.ShapeDtypeStruct((total, width), BF),
            jax.ShapeDtypeStruct((total, 128), BF),
        ],
        compiler_params=params(),
        name="assemble",
    )(jnp.stack([z, core]).astype(jnp.int32), near, far)


def pick(array, index, axis):
    return lax.dynamic_index_in_dim(array, index, axis, keepdims=False)


class Plane:
    def __init__(self, part, place, z, n_parts, n_fsdp):
        self.core, self.x, self.place, self.z = part % 2, part // 2, place, z
        self.n_fsdp = n_fsdp
        self.swap_core = [(i, i ^ 1) for i in range(n_parts)]
        self.swap_x = [(i, i ^ 2) for i in range(n_parts)]

    def over_core(self, send, keep):
        shape = (self.n_fsdp, 2) + send.shape[1:]
        got = lax.ppermute(send, "parts", self.swap_core).reshape(shape)
        keep = keep.reshape(shape)
        add = lambda i: (pick(keep, i, 1).astype(F32) + pick(got, i, 1).astype(F32)).astype(BF)
        return add(1 - self.x), add(self.x)

    def over_x(self, send, keep):
        got = lax.ppermute(send, "parts", self.swap_x)
        return (keep.astype(F32) + got.astype(F32)).astype(BF)

    def over_fsdp(self, g):
        total = pick(g, self.z, 0).astype(F32)
        for d in range(1, self.n_fsdp):
            piece = pick(g, (self.z + d) % self.n_fsdp, 0)
            total = total + lax.ppermute(piece, "fsdp", turned(self.n_fsdp, d)).astype(F32)
        return total.astype(BF)

    def over_ctx(self, g):
        return (g.astype(F32) + lax.ppermute(g, "ctx", turned(2, 1)).astype(F32)).astype(BF)

    def widen_ctx(self, g):
        return jnp.stack([g, lax.ppermute(g, "ctx", turned(2, 1))])

    def widen_x(self, g):
        return jnp.stack([g, lax.ppermute(g, "parts", self.swap_x)])

    def from_core(self, g):
        return lax.ppermute(g, "parts", self.swap_core)


def local(
    mesh_shape,
    decoder_in,
    encoder_out,
    segment_ids,
    block_order,
    prompt_len,
    self_query,
    self_key,
    self_value,
    self_output,
    cross_query,
    cross_key,
    cross_value,
    cross_output,
    gate_in,
    up_in,
    down_out,
    norm_self,
    norm_cross,
    norm_mlp,
    cotangent,
):
    n_parts, n_ctx, n_fsdp = mesh_shape
    part, place, z = lax.axis_index("parts"), lax.axis_index("ctx"), lax.axis_index("fsdp")
    plane, n_plane = part * n_ctx + place, n_parts * n_ctx
    x_own, enc_own = decoder_in[0], encoder_out[0]
    rows, dim = x_own.shape
    segs, order = segment_ids[0], block_order[0]
    total = segs.shape[0]
    slots_total = order.shape[0]
    block = total // slots_total
    per_dev = slots_total // n_ctx
    enc_rows = enc_own.shape[0]
    keys = enc_rows * n_ctx
    hidden = down_out.shape[0] * n_fsdp
    heads_here = 2 * -(-HEADS // (2 * n_ctx))
    width = heads_here * HEAD
    padded = width * n_ctx

    ring = (place + jnp.arange(n_ctx, dtype=jnp.int32)) % n_ctx
    order_here = jnp.roll(order, -per_dev * place)
    slots = jnp.argsort(order_here).astype(jnp.int32)
    counts = needed_blocks(segs, block)

    def from_ctx(value):
        pieces = [lax.ppermute(value, "ctx", turned(n_ctx, -k)) for k in range(1, n_ctx)]
        return pieces[0] if n_ctx == 2 else jnp.concatenate(pieces, axis=0)

    x_far = from_ctx(x_own)

    fast = (n_parts, n_ctx, n_fsdp) == (4, 2, 4)
    shard = dim // n_fsdp

    def own_heads(w):
        w = jnp.pad(w, ((0, 0), (0, padded - dim)))
        return lax.dynamic_slice_in_dim(w, place * width, width, 1)

    gain_cols = jnp.pad(jnp.stack([norm_self, norm_cross, norm_mlp], axis=1), ((0, 0), (0, 125)))
    first = jnp.concatenate(
        [own_heads(self_query), own_heads(self_key), own_heads(self_value), gain_cols], axis=1
    )
    w1, gains = gather_first(first, z, part, n_fsdp, n_parts)
    gains = gains[:, :8].astype(F32).T
    gain_self, gain_cross, gain_mlp = (gains[i : i + 1] for i in range(3))
    mats = (self_output, cross_query, cross_key, cross_value, cross_output)
    if fast:
        w2 = lax.all_gather(
            jnp.concatenate([rows_of(w, part, n_parts) for w in mats], axis=1),
            AROUND, axis=0, tiled=True,
        )

        def column_pieces(w):
            cut = lax.dynamic_slice_in_dim(w, part * 512, 512, 1).reshape(3, 64, 2, 256)
            return cut.transpose(2, 1, 0, 3).reshape(2, 64, dim)

        w3 = lax.all_gather(
            jnp.stack(
                [
                    column_pieces(gate_in),
                    column_pieces(up_in),
                    rows_of(down_out, part, n_parts).reshape(2, 64, dim),
                ],
                axis=1,
            ).reshape(-1, dim),
            AROUND, axis=0, tiled=True,
        ).reshape(PIECES + (dim,))
    else:
        w2 = lax.all_gather(jnp.concatenate(mats, axis=1), "fsdp", axis=0, tiled=True)

        def packed(w):
            w = lax.all_gather(w, "fsdp", axis=0, tiled=True).reshape(4, 3, 64, 8, 256)
            return w.transpose(0, 3, 2, 1, 4).reshape(4, 8, 64, dim)

        w_down = lax.all_gather(down_out, "fsdp", axis=0, tiled=True).reshape(4, 8, 64, dim)
        w3 = jnp.stack([packed(gate_in), packed(up_in), w_down], axis=2)
    x_far, enc_sent = lax.optimization_barrier((x_far, enc_own))
    enc_far = from_ctx(enc_sent)

    n1, q, k, v = qkv_forward(order_here, x_own, x_far, gain_self, w1, block)
    spot = jnp.arange(128, dtype=jnp.int32)[None, :] % HEAD
    minus = jnp.where((spot >= PART0) & (spot < PART0 + 3), -1.0, 0.0)
    seg_q = jnp.where(spot == segs[:, None], 1.0, 0.0).astype(BF)
    seg_k = jnp.where((spot < SEGS) & (spot != segs[:, None]), -BIG, minus).astype(BF)
    o1, lse1 = self_forward(counts, slots, q, k, v, seg_q, seg_k, block)
    pieces = [o1] + [
        lax.ppermute(o1[i * rows : (i + 1) * rows], "ctx", turned(n_ctx, i)) for i in range(1, n_ctx)
    ]
    turn = (place - jnp.arange(n_ctx, dtype=jnp.int32)) % n_ctx
    wo = w2 if padded == dim else jnp.pad(w2[:, :dim], ((0, padded - dim), (0, 0)))
    kv2 = enc_forward(enc_own, enc_far, w2)
    pieces[1], kv2 = lax.optimization_barrier((pieces[1], kv2))
    h1, n2, q2, stat1 = after_self(turn, x_own, pieces, wo, gain_cross, w2)

    where_key = (ring[:, None] * enc_rows + jnp.arange(enc_rows, dtype=jnp.int32)).reshape(-1, 1)
    len_q = jnp.where(spot == 0, jnp.ones((rows, 1), F32), 0.0).astype(BF)
    len_k = jnp.where((spot == 0) & (where_key >= prompt_len[0]), -BIG, minus).astype(BF)
    o2, lse2 = cross_forward(q2, kv2, len_q, len_k)

    layer_out, dh2, dc, do2, stat2, g_ff = feed_forward(o2, h1, w2, gain_mlp, cotangent[0], w3)
    if fast:
        part_ff = lax.psum_scatter(
            g_ff.reshape(-1, dim), AROUND, scatter_dimension=0, tiled=True
        ).reshape(2, 3, 64, dim)

    dq2, dk2, dv2 = cross_backward(q2, kv2, do2, o2, lse2, len_q, len_k)
    dh1, da, stat3, *do1 = before_self(turn, dq2, w2, h1, dh2, gain_cross, wo, width)
    do_far = [lax.ppermute(do1[i], "ctx", turned(n_ctx, -i)) for i in range(1, n_ctx)]
    do_far = do_far[0] if n_ctx == 2 else jnp.concatenate(do_far, axis=0)
    do_own = do1[0]
    core = jnp.reshape(part % 2, (1,)).astype(jnp.int32)
    g_mid, d_far = mid_grads(
        turn, pieces, da, n2, dq2, enc_own, enc_far, dk2, dv2, o2, dc, w2
    )

    sums = jnp.sum(jnp.concatenate([stat1[:2], stat2[:2]], axis=0), axis=1)
    extra = jnp.concatenate(
        [
            jnp.zeros((dim, 1), F32),
            stat2[2][:, None],
            stat3[0][:, None],
            jnp.broadcast_to(sums[None], (dim, 4)),
            jnp.zeros((dim, 121), F32),
        ],
        axis=1,
    )
    gain_wide = jnp.broadcast_to(gain_self.reshape(dim, 1), (dim, 128))

    def self_pair(pair, own, far):
        return self_backward(
            pair, counts, slots, q, k, v, own, far, o1, lse1, seg_q, seg_k, block
        )

    pairs = width // 128
    if fast:
        net = Plane(part, place, z, n_parts, n_fsdp)
        do_own, do_far, d_far, extra, g_mid, part_ff = lax.optimization_barrier(
            (do_own, do_far, d_far, extra, g_mid, part_ff)
        )
        part_mid = lax.psum_scatter(g_mid, AROUND, scatter_dimension=0, tiled=True)
    enc_got = [
        lax.ppermute(d_far[(i - 1) * enc_rows : i * enc_rows], "ctx", turned(n_ctx, i))
        for i in range(1, n_ctx)
    ]
    if fast:
        by_pair = [self_pair(0, do_own, do_far)]
        part_ff, do_far = lax.optimization_barrier((part_ff, do_far, by_pair[0][0]))[:2]
        by_pair += [self_pair(1, do_own, do_far), self_pair(2, do_own, do_far)]
        sum_ff = net.over_ctx(part_ff)
        by_pair, sum_ff, enc_got = lax.optimization_barrier((by_pair, sum_ff, enc_got))
    else:
        by_pair = [self_pair(i, do_own, do_far) for i in range(pairs)]
    ds = [d[i] for i in range(3) for d in by_pair]
    dn_far = qkv_back(order_here, per_dev, ds, w1, total - rows, BF, block)
    dn_got = [
        lax.ppermute(dn_far[(i - 1) * rows : i * rows], "ctx", turned(n_ctx, i))
        for i in range(1, n_ctx)
    ]
    ds, dn_far = lax.optimization_barrier((ds, dn_far))
    g_qkv = qkv_grads(core, ds, n1, w1, gain_wide, extra, fast)
    dn_own = qkv_back(order_here, 0, ds, w1, rows, F32, block)
    if fast:
        sum_ff = net.widen_x(sum_ff)
        g_qkv = net.over_fsdp(net.over_x(*net.over_core(*g_qkv)))
        dn_got, part_mid, dn_own = lax.optimization_barrier((dn_got, part_mid, dn_own))
    decoder_grad = finish(x_own, dh1, gain_self, dn_own, dn_got)
    enc_grad = enc_finish(dk2, dv2, w2, enc_got)

    if fast:
        me = jnp.stack([net.core, net.x, place]).astype(jnp.int32)
        g_qkv = net.widen_x(net.widen_ctx(g_qkv))
        sum_mid = net.widen_x(net.over_ctx(part_mid))
        square = (shard, dim)
        *grads_qkv, tail = settle(
            settle_qkv_kernel, me, g_qkv, net.from_core(g_qkv), [square] * 3 + [(shard, 128)]
        )
        mids = settle(settle_mid_kernel, me, sum_mid, net.from_core(sum_mid), [square] * 5)
        grad_gate, grad_up, grad_down = settle(
            unpack_kernel, me, sum_ff, net.from_core(sum_ff),
            [(shard, hidden), (shard, hidden), (hidden // n_fsdp, dim)],
        )
    else:

        def total_of(g):
            g = lax.psum_scatter(g, "fsdp", scatter_dimension=0, tiled=True).astype(F32)
            return lax.psum(g, ("parts", "ctx"))

        (g_qkv,) = g_qkv
        sum_mid = total_of(g_mid)
        flat = [
            g_ff[:, :, i].reshape(4, 8, 64, 3, 256).transpose(0, 3, 2, 1, 4).reshape(dim, hidden)
            for i in range(2)
        ]
        grad_gate, grad_up = total_of(flat[0]), total_of(flat[1])
        grad_down = total_of(g_ff[:, :, 2].reshape(hidden, dim))
        sum_qkv = lax.psum_scatter(g_qkv, "fsdp", scatter_dimension=0, tiled=True).astype(F32)
        every = lax.all_gather(lax.psum(sum_qkv, "parts"), "ctx", axis=0)
        grads_qkv = [
            jnp.concatenate(
                [every[c, :, i * width : (i + 1) * width] for c in range(n_ctx)], axis=1
            )[:, :dim]
            for i in range(3)
        ]
        tail = jnp.sum(every[:, :, 3 * width :], axis=0)
        mids = [sum_mid[:, i * dim : (i + 1) * dim] for i in range(5)]
    grad_gself, grad_gmlp, grad_gcross = tail[:, 0], tail[:, 1], tail[:, 2]
    entries = float(n_parts * n_ctx * n_fsdp * rows * dim)
    rms_values = jnp.sqrt(tail[0, 3:7] / entries)
    return (
        layer_out[None],
        decoder_grad[None],
        enc_grad[None],
        *grads_qkv,
        *mids,
        grad_gate,
        grad_up,
        grad_down,
        grad_gself,
        grad_gcross,
        grad_gmlp,
        rms_values,
    )


def solution(mesh):
    rows3 = P(("parts", "fsdp"), "ctx", None)
    group = P(("parts", "fsdp"), None)
    matrix, vector = P("fsdp", None), P("fsdp")
    shape = tuple(mesh.shape[a] for a in ("parts", "ctx", "fsdp"))
    return jax.shard_map(
        functools.partial(local, shape),
        mesh=mesh,
        in_specs=(rows3, rows3, group, group, P(("parts", "fsdp")))
        + (matrix,) * 11
        + (vector,) * 3
        + (rows3,),
        out_specs=(rows3,) * 3 + (matrix,) * 11 + (vector,) * 3 + (P(),),
        check_vma=False,
    )
```

```python
import functools
import math

import jax
import jax.numpy as jnp
from jax import lax
from jax.experimental import pallas as pl
from jax.experimental.pallas import tpu as pltpu
from jax.sharding import PartitionSpec as P

HEADS = 12
HEAD = 64
SCALE = 0.125
EPS = 1e-06
BIG = 1e30
LN2 = math.log(2.0)
QSCALE = SCALE * math.log2(math.e)
PART0 = 16
SEGS = 16
BF = jnp.bfloat16
F32 = jnp.float32
MIB = 1 << 20
AROUND = ("fsdp", "parts")


def nn(a, b):
    return lax.dot_general(a, b, (((1,), (0,)), ((), ())), preferred_element_type=F32)


def nt(a, b):
    return lax.dot_general(a, b, (((1,), (1,)), ((), ())), preferred_element_type=F32)


def tn(a, b):
    return lax.dot_general(a, b, (((0,), (0,)), ((), ())), preferred_element_type=F32)


def lanes(shape):
    return lax.broadcasted_iota(jnp.int32, shape, len(shape) - 1)


def params(mib=60):
    return pltpu.CompilerParams(vmem_limit_bytes=mib * MIB)


def cost(flops, moved, exps=0):
    return pl.CostEstimate(flops=int(flops), bytes_accessed=int(moved), transcendentals=int(exps))


def rms_scale(h):
    return lax.rsqrt(jnp.mean(h * h, axis=-1, keepdims=True) + EPS)


def norm_back(h, gain, dn):
    r = rms_scale(h)
    t = dn * gain
    hr = h * r
    dh = r * (t - hr * jnp.mean(t * hr, axis=-1, keepdims=True))
    return dh, jnp.sum(dn * hr, axis=0, keepdims=True)


def with_parts(base, value):
    spot = lanes(base.shape) % HEAD
    hi = value.astype(BF)
    rest = value - hi.astype(F32)
    mid = rest.astype(BF)
    low = (rest - mid.astype(F32)).astype(BF)
    return jnp.where(
        spot == PART0, hi, jnp.where(spot == PART0 + 1, mid, jnp.where(spot == PART0 + 2, low, base))
    )


def pair_of(own, other):
    left = lanes(own.shape) < HEAD
    return jnp.where(left, own, other), jnp.where(left, other, own)


CHUNK = 512


def below(s, rows_first):
    r = lax.broadcasted_iota(jnp.int32, s.shape, 0)
    c = lanes(s.shape)
    return jnp.where(c <= r if rows_first else r <= c, s, -BIG)


def lane_max(s):
    return functools.reduce(jnp.maximum, [s[:, c : c + 128] for c in range(0, s.shape[1], 128)])


def sweep(step, lo, full, odd, grain, unroll):
    base = lo
    if odd is not None:

        @pl.when(odd == 1)
        def _():
            step(lo, 0, grain)

        base = lo + odd * grain

    def body(c, carry):
        step(pl.multiple_of(base + c * CHUNK, grain), pl.multiple_of(grain + c * CHUNK, 128), CHUNK)
        return carry

    lax.fori_loop(0, full, body, 0, unroll=unroll)
    return pl.multiple_of(base + full * CHUNK, grain)


def forward_block(
    lo, full, odd, grain, diag, q_ref, qa_ref, kx, vx, o_ref, lse_ref, s_scr, m_scr, a_scr, unroll
):
    q = q_ref[...]
    rows = q.shape[0]
    left = lanes(q.shape) < HEAD
    sides = pair_of(q, qa_ref[...])
    m_scr[...] = jnp.full_like(m_scr, -BIG)
    a_scr[...] = jnp.zeros_like(a_scr)
    last = s_scr.shape[2] - rows

    def scores(key, at, size, start=None):
        live = pl.ds(start or 0, rows - (start or 0))
        for h in range(2):
            s = nt(sides[h][start or 0 :], kx[h, pl.ds(key, size), :])
            s = s if start is None else below(s, True)
            s_scr[h, live, pl.ds(at, size)] = s
            m_scr[h, live, :] = jnp.maximum(m_scr[h, live, :], lane_max(s))

    steps = range(0, rows, grain) if diag else ()
    end = sweep(scores, lo, full, odd, grain, unroll)
    for start in steps:
        scores(end + start, last + start, grain, start)
    tops = [jnp.max(m_scr[h], axis=1, keepdims=True) for h in range(2)]

    def values(key, at, size, start=0):
        live = pl.ds(start, rows - start)
        for h in range(2):
            p = jnp.exp2(s_scr[h, live, pl.ds(at, size)] - tops[h][start:]).astype(BF)
            a_scr[h, live, :] += nn(p, vx[h, pl.ds(key, size), :])

    end = sweep(values, lo, full, odd, grain, unroll)
    for start in steps:
        values(end + start, last + start, grain, start)
    wide = jnp.where(left, a_scr[0], a_scr[1])
    total = jnp.where(left, a_scr[1], a_scr[0])
    o_ref[...] = (wide / pltpu.roll(total, HEAD, 1)).astype(o_ref.dtype)
    lse_ref[...] = jnp.where(left, tops[1], tops[0]) + jnp.log2(total)


def forward_scratch(block, keys):
    return [
        pltpu.VMEM((2, keys, 128), BF),
        pltpu.VMEM((2, keys, 128), BF),
        pltpu.VMEM((2, block, keys + CHUNK), F32),
        pltpu.VMEM((2, block, 128), F32),
        pltpu.VMEM((2, block, 128), F32),
    ]


def backward_scratch(block, keys):
    return (
        [pltpu.VMEM((2, keys, 128), BF)] * 3
        + [pltpu.VMEM((keys, 128), F32)] * 2
        + [pltpu.VMEM((block, 128), F32)]
    )


def forward_prep(k_ref, v_ref, ka_ref, kx, vx):
    kx[0], kx[1] = pair_of(k_ref[...], ka_ref[...])
    v = v_ref[...]
    vx[0], vx[1] = pair_of(v, jnp.ones_like(v))


def backward_prep(k_ref, v_ref, ka_ref, kx, vx, km, dk_acc, dv_acc):
    k, v = k_ref[...], v_ref[...]
    spot = lanes(v.shape) % HEAD
    neg = jnp.where((spot >= PART0) & (spot < PART0 + 3), -1.0, 0.0).astype(BF)
    kx[0], kx[1] = pair_of(k, ka_ref[...])
    vx[0], vx[1] = pair_of(v, neg)
    km[0], km[1] = pair_of(k, jnp.zeros_like(k))
    dk_acc[...] = jnp.zeros_like(dk_acc)
    dv_acc[...] = jnp.zeros_like(dv_acc)


def backward_block(
    lo, full, odd, grain, diag, q, do, o_ref, lse_ref, qa_ref, kx, vx, km,
    dq_ref, dk_acc, dv_acc, dq_acc, unroll,
):
    left = lanes(q.shape) < HEAD
    rows = q.shape[0]
    product = do.astype(F32) * o_ref[...].astype(F32)
    first = jnp.sum(jnp.where(left, product, 0.0), axis=1, keepdims=True)
    second = jnp.sum(jnp.where(left, 0.0, product), axis=1, keepdims=True)
    delta = jnp.where(left, second, first)
    zero = jnp.zeros_like(q)
    qx = pair_of(q, with_parts(qa_ref[...], lse_ref[...]))
    dx = pair_of(do, with_parts(zero, delta))
    qm = pair_of(q, zero)
    dm = pair_of(do, zero)
    dq_acc[...] = jnp.zeros_like(dq_acc)

    def step(key, _, size, start=None):
        at = pl.ds(key, size)
        live = slice(start or 0, rows)
        dq = dk = dv = None
        for h in range(2):
            st = nt(kx[h, at, :], qx[h][live])
            pt = jnp.exp2(st if start is None else below(st, False))
            dp = nt(vx[h, at, :], dx[h][live])
            ds = (pt * dp).astype(BF)
            tv, tk, tq = nn(pt.astype(BF), dm[h][live]), nn(ds, qm[h][live]), tn(ds, km[h, at, :])
            dv = tv if dv is None else dv + tv
            dk = tk if dk is None else dk + tk
            dq = tq if dq is None else dq + tq
        dv_acc[at, :] += dv
        dk_acc[at, :] += dk
        dq_acc[live, :] += dq

    end = sweep(step, lo, full, odd, grain, unroll)
    for start in range(0, rows, grain) if diag else ():
        step(end + start, 0, grain, start)
    dq_ref[...] = (dq_acc[...] * SCALE).astype(dq_ref.dtype)


def cross_forward_kernel(
    q_ref, k_ref, v_ref, qa_ref, ka_ref, o_ref, lse_ref, kx, vx, s_scr, m_scr, a_scr
):
    @pl.when(pl.program_id(1) == 0)
    def _():
        forward_prep(k_ref, v_ref, ka_ref, kx, vx)

    full = k_ref.shape[0] // CHUNK
    forward_block(
        0, full, None, CHUNK, False, q_ref, qa_ref, kx, vx, o_ref, lse_ref, s_scr, m_scr, a_scr, full
    )


def cross_forward(q, kv, qa, ka):
    rows, width = q.shape
    keys = kv.shape[0]
    block = min(512, rows)
    pairs = width // 128
    row = pl.BlockSpec((block, 128), lambda h, i: (i, h))
    return pl.pallas_call(
        cross_forward_kernel,
        grid=(pairs, rows // block),
        in_specs=[
            row,
            pl.BlockSpec((keys, 128), lambda h, i: (0, h)),
            pl.BlockSpec((keys, 128), lambda h, i: (0, h + pairs)),
            pl.BlockSpec((block, 128), lambda h, i: (i, 0)),
            pl.BlockSpec((keys, 128), lambda h, i: (0, 0)),
        ],
        out_specs=[row, row],
        out_shape=[
            jax.ShapeDtypeStruct((rows, width), BF),
            jax.ShapeDtypeStruct((rows, width), F32),
        ],
        scratch_shapes=forward_scratch(block, keys),
        compiler_params=params(),
        cost_estimate=cost(16 * rows * keys * width, 8 * rows * width, rows * keys * 12),
        name="cross_forward",
    )(q, kv, kv, qa, ka)


def cross_backward_kernel(
    q_ref, k_ref, v_ref, do_ref, o_ref, lse_ref, qa_ref, ka_ref,
    dq_ref, dk_ref, dv_ref, kx, vx, km, dk_acc, dv_acc, dq_acc,
):
    @pl.when(pl.program_id(1) == 0)
    def _():
        backward_prep(k_ref, v_ref, ka_ref, kx, vx, km, dk_acc, dv_acc)

    backward_block(
        0, k_ref.shape[0] // CHUNK, None, CHUNK, False, q_ref[...], do_ref[...], o_ref, lse_ref,
        qa_ref, kx, vx, km, dq_ref, dk_acc, dv_acc, dq_acc, k_ref.shape[0] // CHUNK,
    )

    @pl.when(pl.program_id(1) == pl.num_programs(1) - 1)
    def _():
        dk_ref[...] = (dk_acc[...] * LN2).astype(BF)
        dv_ref[...] = dv_acc[...].astype(BF)


def cross_backward(q, kv, do, o, lse, qa, ka):
    rows, width = q.shape
    keys = kv.shape[0]
    block = min(512, rows)
    pairs = width // 128
    row = pl.BlockSpec((block, 128), lambda h, i: (i, h))
    col = pl.BlockSpec((keys, 128), lambda h, i: (0, h))
    return pl.pallas_call(
        cross_backward_kernel,
        grid=(pairs, rows // block),
        in_specs=[
            row,
            col,
            pl.BlockSpec((keys, 128), lambda h, i: (0, h + pairs)),
            row,
            row,
            row,
            pl.BlockSpec((block, 128), lambda h, i: (i, 0)),
            pl.BlockSpec((keys, 128), lambda h, i: (0, 0)),
        ],
        out_specs=[row, col, col],
        out_shape=[
            jax.ShapeDtypeStruct((rows, width), BF),
            jax.ShapeDtypeStruct((keys, width), BF),
            jax.ShapeDtypeStruct((keys, width), BF),
        ],
        scratch_shapes=backward_scratch(block, keys),
        compiler_params=params(),
        cost_estimate=cost(40 * rows * keys * width, 12 * rows * width, rows * keys * 12),
        name="cross_backward",
    )(q, kv, kv, do, o, lse, qa, ka)


def grain_of(block):
    return min(256, block)


def needed_blocks(segs, block):
    total = segs.shape[0]
    grain = grain_of(block)
    first = segs.reshape(total // block, block)[:, 0]
    start = jnp.sum((segs[None, :] < first[:, None]).astype(jnp.int32), axis=1)
    ends = (jnp.arange(total // block, dtype=jnp.int32) + 1) * block
    return (ends - start // grain * grain) // grain


def self_range(count, i, block):
    grain = grain_of(block)
    before = count - block // grain
    per = CHUNK // grain
    lo = pl.multiple_of((i + 1) * block - count * grain, grain)
    return lo, before // per, before % per, grain


def self_forward_kernel(
    count_ref, slot_ref, q_ref, k_ref, v_ref, qa_ref, ka_ref, o_ref, lse_ref,
    kx, vx, s_scr, m_scr, a_scr,
):
    i = pl.program_id(1)

    @pl.when(i == 0)
    def _():
        forward_prep(k_ref, v_ref, ka_ref, kx, vx)

    forward_block(
        *self_range(count_ref[i], i, q_ref.shape[0]), True, q_ref, qa_ref, kx, vx, o_ref, lse_ref,
        s_scr, m_scr, a_scr, 1,
    )


def self_forward(counts, slots, q, k, v, qa, ka, block):
    total, width = q.shape
    row = pl.BlockSpec((block, 128), lambda h, i, n, s: (i, h))
    col = pl.BlockSpec((total, 128), lambda h, i, n, s: (0, h))
    return pl.pallas_call(
        self_forward_kernel,
        grid_spec=pltpu.PrefetchScalarGridSpec(
            num_scalar_prefetch=2,
            grid=(width // 128, total // block),
            in_specs=[
                row,
                col,
                col,
                pl.BlockSpec((block, 128), lambda h, i, n, s: (i, 0)),
                pl.BlockSpec((total, 128), lambda h, i, n, s: (0, 0)),
            ],
            out_specs=[pl.BlockSpec((block, 128), lambda h, i, n, s: (s[i], h)), row],
            scratch_shapes=forward_scratch(block, total),
        ),
        out_shape=[
            jax.ShapeDtypeStruct((total, width), BF),
            jax.ShapeDtypeStruct((total, width), F32),
        ],
        compiler_params=params(),
        cost_estimate=cost(8 * total * total * width, 8 * total * width, total * total * 3),
        name="self_forward",
    )(counts, slots, q, k, v, qa, ka)


def self_backward_kernel(
    count_ref, slot_ref, q_ref, k_ref, v_ref, own_ref, far_ref, o_ref, lse_ref, qa_ref, ka_ref,
    dq_ref, dk_ref, dv_ref, kx, vx, km, dk_acc, dv_acc, dq_acc, *, per_dev,
):
    i = pl.program_id(1)
    do = jnp.where(slot_ref[i] < per_dev, own_ref[...], far_ref[...])

    @pl.when(i == 0)
    def _():
        backward_prep(k_ref, v_ref, ka_ref, kx, vx, km, dk_acc, dv_acc)

    backward_block(
        *self_range(count_ref[i], i, q_ref.shape[0]), True, q_ref[...], do, o_ref, lse_ref, qa_ref,
        kx, vx, km, dq_ref, dk_acc, dv_acc, dq_acc, 1,
    )

    @pl.when(i == pl.num_programs(1) - 1)
    def _():
        dk_ref[...] = (dk_acc[...] * LN2).astype(BF)
        dv_ref[...] = dv_acc[...].astype(BF)


def self_backward(counts, slots, q, k, v, own, far, o, lse, qa, ka, block):
    total, width = q.shape
    per_dev = own.shape[0] // block
    row = pl.BlockSpec((block, 128), lambda h, i, n, s: (i, h))
    col = pl.BlockSpec((total, 128), lambda h, i, n, s: (0, h))
    return pl.pallas_call(
        functools.partial(self_backward_kernel, per_dev=per_dev),
        grid_spec=pltpu.PrefetchScalarGridSpec(
            num_scalar_prefetch=2,
            grid=(width // 128, total // block),
            in_specs=[
                row,
                col,
                col,
                pl.BlockSpec((block, 128), lambda h, i, n, s: (jnp.minimum(s[i], per_dev - 1), h)),
                pl.BlockSpec((block, 128), lambda h, i, n, s: (jnp.maximum(s[i] - per_dev, 0), h)),
                pl.BlockSpec((block, 128), lambda h, i, n, s: (s[i], h)),
                row,
                pl.BlockSpec((block, 128), lambda h, i, n, s: (i, 0)),
                pl.BlockSpec((total, 128), lambda h, i, n, s: (0, 0)),
            ],
            out_specs=[row, col, col],
            scratch_shapes=backward_scratch(block, total),
        ),
        out_shape=[jax.ShapeDtypeStruct((total, width), BF)] * 3,
        compiler_params=params(),
        cost_estimate=cost(4 * total * total * width, 2 * total * width),
        name="self_backward",
    )(counts, slots, q, k, v, own, far, o, lse, qa, ka)


def qkv_kernel(order_ref, own_ref, far_ref, g_ref, w_ref, n_ref, q_ref, k_ref, v_ref, *, per_dev):
    x = jnp.where(pl.program_id(0) < per_dev, own_ref[...], far_ref[...]).astype(F32)
    n = (x * rms_scale(x) * g_ref[...]).astype(BF)
    n_ref[...] = n
    width = q_ref.shape[1]
    out = nn(n, w_ref[...])
    q_ref[...] = (out[:, :width] * QSCALE).astype(BF)
    k_ref[...] = out[:, width : 2 * width].astype(BF)
    v_ref[...] = out[:, 2 * width :].astype(BF)


def qkv_forward(order, own, far, gain, w, block):
    dim = own.shape[1]
    total = own.shape[0] + far.shape[0]
    width = w.shape[1] // 3
    per_dev = own.shape[0] // block
    here = lambda i, o: (o[i], 0)
    whole = lambda i, o: (0, 0)
    return pl.pallas_call(
        functools.partial(qkv_kernel, per_dev=per_dev),
        grid_spec=pltpu.PrefetchScalarGridSpec(
            num_scalar_prefetch=1,
            grid=(total // block,),
            in_specs=[
                pl.BlockSpec((block, dim), lambda i, o: (jnp.minimum(i, per_dev - 1), 0)),
                pl.BlockSpec((block, dim), lambda i, o: (jnp.maximum(i - per_dev, 0), 0)),
                pl.BlockSpec((1, dim), whole),
                pl.BlockSpec(w.shape, whole),
            ],
            out_specs=[pl.BlockSpec((block, dim), here)] + [pl.BlockSpec((block, width), here)] * 3,
        ),
        out_shape=[jax.ShapeDtypeStruct((total, dim), BF)]
        + [jax.ShapeDtypeStruct((total, width), BF)] * 3,
        compiler_params=params(),
        cost_estimate=cost(6 * total * dim * width, 8 * total * dim),
        name="qkv_forward",
    )(order, own, far, gain, w)


def enc_kv_kernel(own_ref, far_ref, w_ref, kv_ref, *, own_blocks):
    enc = jnp.where(pl.program_id(0) < own_blocks, own_ref[...], far_ref[...])
    half = w_ref.shape[1] // 2
    for c in range(2):
        at = slice(c * half, (c + 1) * half)
        kv_ref[:, at] = nn(enc, w_ref[:, at]).astype(BF)


def enc_forward(own, far, w2):
    rows, dim = own.shape
    block = min(512, rows)
    keys = rows + far.shape[0]
    ours = rows // block
    return pl.pallas_call(
        functools.partial(enc_kv_kernel, own_blocks=ours),
        grid=(keys // block,),
        in_specs=[
            pl.BlockSpec((block, dim), lambda i: (jnp.minimum(i, ours - 1), 0)),
            pl.BlockSpec((block, dim), lambda i: (jnp.maximum(i - ours, 0), 0)),
            pl.BlockSpec((dim, 2 * dim), lambda i: (0, 1)),
        ],
        out_specs=pl.BlockSpec((block, 2 * dim), lambda i: (i, 0)),
        out_shape=jax.ShapeDtypeStruct((keys, 2 * dim), BF),
        compiler_params=params(),
        cost_estimate=cost(4 * keys * dim * dim, 8 * keys * dim),
        name="enc_forward",
    )(own, far, w2)


def after_self_kernel(turn_ref, x_ref, *refs, count):
    o_refs, w_refs = refs[:count], refs[count : 2 * count]
    g_ref, wq_ref, h_ref, n_ref, q_ref, s_ref = refs[2 * count :]
    x = x_ref[...].astype(F32)
    a = nn(o_refs[0][...], w_refs[0][...])
    for o_ref, w_ref in zip(o_refs[1:], w_refs[1:]):
        a = a + nn(o_ref[...], w_ref[...])
    h = x + a
    h_ref[...] = h
    n = (h * rms_scale(h) * g_ref[...]).astype(BF)
    n_ref[...] = n
    q_ref[...] = (nn(n, wq_ref[...]) * QSCALE).astype(BF)

    @pl.when(pl.program_id(0) == 0)
    def _():
        s_ref[...] = jnp.zeros_like(s_ref)

    s_ref[0:1, :] += jnp.sum(x * x, axis=0, keepdims=True)
    s_ref[1:2, :] += jnp.sum(a * a, axis=0, keepdims=True)


def turn_specs(count, width, dim):
    return [pl.BlockSpec((width, dim), lambda i, t, k=k: (t[k], 0)) for k in range(count)]


def after_self(turn, x, pieces, wo, gain, w2):
    rows, dim = x.shape
    count, width = len(pieces), pieces[0].shape[1]
    block = min(512, rows)
    line = lambda i, t: (i, 0)
    whole = lambda i, t: (0, 0)
    row = pl.BlockSpec((block, dim), line)
    return pl.pallas_call(
        functools.partial(after_self_kernel, count=count),
        grid_spec=pltpu.PrefetchScalarGridSpec(
            num_scalar_prefetch=1,
            grid=(rows // block,),
            in_specs=[row]
            + [pl.BlockSpec((block, width), line)] * count
            + turn_specs(count, width, dim)
            + [pl.BlockSpec((1, dim), whole), pl.BlockSpec((dim, dim), lambda i, t: (0, 1))],
            out_specs=[row, row, row, pl.BlockSpec((8, dim), whole)],
        ),
        out_shape=[
            jax.ShapeDtypeStruct((rows, dim), F32),
            jax.ShapeDtypeStruct((rows, dim), BF),
            jax.ShapeDtypeStruct((rows, dim), BF),
            jax.ShapeDtypeStruct((8, dim), F32),
        ],
        compiler_params=params(),
        cost_estimate=cost(4 * rows * dim * dim, 14 * rows * dim),
        name="after_self",
    )(turn, x, *pieces, *([wo] * count), gain, w2)


GELU_C = math.sqrt(2.0 / math.pi)
GELU_A = 0.044715


PIECES = (4, 8, 3, 64)


def mlp_kernel(
    o_ref, h1_ref, wc_ref, g_ref, t_ref, gu_ref, wd_ref,
    y_ref, dh_ref, dc_ref, do_ref, s_ref, g_out,
    n_scr, h_scr, m_scr, dn_scr, hid_scr, du_scr, dw_scr, wg_scr, wu_scr, gu_out, d_out, sems,
):
    j = pl.program_id(0)
    last = pl.num_programs(0) - 1
    rows = o_ref.shape[0]
    step = min(256, rows)
    spans = [pl.ds(r, step) for r in range(0, rows, step)]
    gain = g_ref[...]
    n_fsdp, n_two, _, tall, _ = gu_ref.shape
    third = 256
    high = 3 * tall

    @pl.when(j == 0)
    def _():
        total = None
        for at in spans:
            c = nn(o_ref[at, :], wc_ref[...])
            h = h1_ref[at, :] + c
            h_scr[at, :] = h
            n_scr[at, :] = (h * rms_scale(h) * gain).astype(BF)
            part = jnp.sum(c * c, axis=0, keepdims=True)
            total = part if total is None else total + part
        s_ref[...] = jnp.zeros_like(s_ref)
        s_ref[0:1, :] = total
        m_scr[...] = jnp.zeros_like(m_scr)
        dn_scr[...] = jnp.zeros_like(dn_scr)

    for z in range(n_fsdp):
        for p in range(n_two):
            for t in range(3):
                at, to = pl.ds(z * high + t * tall, tall), pl.ds(p * third, third)
                wg_scr[at, to] = gu_ref[z, p, 0, :, t * third : (t + 1) * third]
                wu_scr[at, to] = gu_ref[z, p, 1, :, t * third : (t + 1) * third]
    wg, wu = wg_scr[...], wu_scr[...]
    wd = wd_ref[...].reshape(-1, wd_ref.shape[-1])
    for at in spans:
        n = n_scr[at, :]
        u = nn(n, wg)
        w = nn(n, wu)
        dhid = nt(t_ref[at, :], wd)
        square = u * u
        th = jnp.tanh(GELU_C * u * (1.0 + GELU_A * square))
        half = 0.5 * (1.0 + th)
        gel = u * half
        slope = half + 0.5 * u * (1.0 - th * th) * (GELU_C * (1.0 + 3.0 * GELU_A * square))
        hid = (gel * w).astype(BF)
        du = (dhid * w * slope).astype(BF)
        dw = (dhid * gel).astype(BF)
        hid_scr[at, :] = hid
        du_scr[at, :] = du
        dw_scr[at, :] = dw
        m_scr[at, :] += nn(hid, wd)
        dn_scr[at, :] += nt(du, wg) + nt(dw, wu)

    slot = lax.rem(j, 2)

    def copies(step_of, slot_of):
        return (
            pltpu.make_async_copy(
                gu_out.at[slot_of],
                g_out.at[:, pl.ds(step_of * n_two, n_two), pl.ds(0, 2)],
                sems.at[slot_of, 0],
            ),
            pltpu.make_async_copy(d_out.at[slot_of], g_out.at[step_of, :, 2], sems.at[slot_of, 1]),
        )

    @pl.when(j >= 2)
    def _():
        for copy in copies(j - 2, slot):
            copy.wait()

    d_out[slot] = tn(hid_scr[...], t_ref[...]).astype(BF).reshape(d_out.shape[1:])
    for side, source in ((0, du_scr), (1, dw_scr)):
        grad = tn(n_scr[...], source[...]).astype(BF)
        for z in range(n_fsdp):
            for p in range(n_two):
                for t in range(3):
                    gu_out[slot, z, p, side, :, t * third : (t + 1) * third] = grad[
                        z * high + t * tall : z * high + (t + 1) * tall,
                        p * third : (p + 1) * third,
                    ]
    for copy in copies(j, slot):
        copy.start()

    @pl.when(j == last)
    def _():
        total = gains = None
        for at in spans:
            h = h_scr[at, :]
            y = h + m_scr[at, :]
            y_ref[at, :] = y.astype(BF)
            dh, dg = norm_back(h, gain, dn_scr[at, :])
            dh = dh + t_ref[at, :].astype(F32)
            dh_ref[at, :] = dh
            dc = dh.astype(BF)
            dc_ref[at, :] = dc
            do_ref[at, :] = nt(dc, wc_ref[...]).astype(BF)
            part = jnp.sum(y * y, axis=0, keepdims=True)
            total = part if total is None else total + part
            gains = dg if gains is None else gains + dg
        s_ref[1:2, :] = total
        s_ref[2:3, :] = gains
        for copy in copies(j - 1, 1 - slot) + copies(j, slot):
            copy.wait()


def feed_forward(o, h1, w2, gain, cot, w3):
    rows, dim = o.shape
    n_fsdp, n_plane, _, tall, _ = w3.shape
    steps = n_fsdp
    two = n_plane // steps
    width = two * 256
    whole = lambda j: (0, 0)
    once = pl.Buffered(1)
    full = pl.BlockSpec((rows, dim), whole, pipeline_mode=once)
    flops = 18 * rows * dim * width * steps + 6 * rows * dim * dim
    return pl.pallas_call(
        mlp_kernel,
        grid=(steps,),
        in_specs=[
            full,
            full,
            pl.BlockSpec((dim, dim), lambda j: (0, 4), pipeline_mode=once),
            pl.BlockSpec((1, dim), whole),
            full,
            pl.BlockSpec((n_fsdp, two, 2, tall, dim), lambda j: (0, j, 0, 0, 0)),
            pl.BlockSpec((1, n_plane, 1, tall, dim), lambda j: (j, 0, 2, 0, 0)),
        ],
        out_specs=[
            full,
            full,
            full,
            full,
            pl.BlockSpec((8, dim), whole),
            pl.BlockSpec(memory_space=pl.ANY),
        ],
        out_shape=[
            jax.ShapeDtypeStruct((rows, dim), BF),
            jax.ShapeDtypeStruct((rows, dim), F32),
            jax.ShapeDtypeStruct((rows, dim), BF),
            jax.ShapeDtypeStruct((rows, dim), BF),
            jax.ShapeDtypeStruct((8, dim), F32),
            jax.ShapeDtypeStruct(w3.shape, BF),
        ],
        scratch_shapes=[
            pltpu.VMEM((rows, dim), BF),
            pltpu.VMEM((rows, dim), F32),
            pltpu.VMEM((rows, dim), F32),
            pltpu.VMEM((rows, dim), F32),
            pltpu.VMEM((rows, width), BF),
            pltpu.VMEM((rows, width), BF),
            pltpu.VMEM((rows, width), BF),
            pltpu.VMEM((dim, width), BF),
            pltpu.VMEM((dim, width), BF),
            pltpu.VMEM((2, n_fsdp, two, 2, tall, dim), BF),
            pltpu.VMEM((2, n_plane, tall, dim), BF),
            pltpu.SemaphoreType.DMA((2, 2)),
        ],
        compiler_params=params(),
        cost_estimate=cost(flops, 40 * MIB, rows * width * steps),
        name="feed_forward",
    )(o, h1, w2, gain, cot, w3, w3)


def placed(me_ref, near_ref, far_ref, size):
    core, x = me_ref[0], me_ref[1]
    for c, ref in enumerate((near_ref, far_ref)):
        for a in range(2):
            yield ref.at[a], pl.multiple_of(((a ^ x) * 2 + (c ^ core)) * size, 16)


def unpack_kernel(me_ref, near_ref, far_ref, gate_ref, up_ref, down_ref):
    core, x = me_ref[0], me_ref[1]
    tall = near_ref.shape[3]
    third = 256
    for c in range(2):
        for a in range(2):
            for i in range(2):
                p = a * 4 + c * 2 + i
                piece = lambda k: jnp.where(
                    core == c, near_ref[a ^ x, i, k], far_ref[a ^ x, i, k]
                ).astype(F32)
                gate, up = piece(0), piece(1)
                for t in range(3):
                    at, to = pl.ds(t * tall, tall), pl.ds(p * third, third)
                    gate_ref[at, to] = gate[:, t * third : (t + 1) * third]
                    up_ref[at, to] = up[:, t * third : (t + 1) * third]
                down_ref[pl.ds(p * tall, tall), :] = piece(2)


def settle_mid_kernel(me_ref, near_ref, far_ref, *outs):
    dim = outs[0].shape[1]
    size = near_ref.shape[1]
    for ref, row in placed(me_ref, near_ref, far_ref, size):
        for m, out in enumerate(outs):
            out[pl.ds(row, size), :] = ref[:, m * dim : (m + 1) * dim].astype(F32)


def settle_qkv_kernel(me_ref, near_ref, far_ref, q_ref, k_ref, v_ref, tail_ref):
    place = me_ref[2]
    size = near_ref.shape[2]
    width = q_ref.shape[1] // 2
    for ref, row in placed(me_ref, near_ref, far_ref, size):
        at = pl.ds(row, size)
        tail = None
        for i in range(2):
            block = ref[i ^ place].astype(F32)
            for t, out in enumerate((q_ref, k_ref, v_ref)):
                out[at, i * width : (i + 1) * width] = block[:, t * width : (t + 1) * width]
            part = block[:, 3 * width :]
            tail = part if tail is None else tail + part
        tail_ref[at, :] = tail


def settle(kernel, me, near, far, shapes):
    vmem = pl.BlockSpec(memory_space=pltpu.VMEM)
    return pl.pallas_call(
        kernel,
        in_specs=[pl.BlockSpec(memory_space=pltpu.SMEM), vmem, vmem],
        out_specs=[vmem] * len(shapes),
        out_shape=[jax.ShapeDtypeStruct(shape, F32) for shape in shapes],
        compiler_params=params(),
        name=kernel.__name__[:-7],
    )(me, near, far)


def deal_rows(core, full, send_ref, keep_ref):
    count, size = send_ref.shape[:2]
    for i in range(count):
        for ref, c in ((send_ref, 1 - core), (keep_ref, core)):
            ref[i] = full[pl.ds(pl.multiple_of((2 * i + c) * size, 16), size), :]


def mid_grads_kernel(turn_ref, *refs, count):
    n_in = count + 9
    sources = refs[:n_in]
    wk_ref, wv_ref, g_ref, far_out = refs[n_in : n_in + 4]
    buffers = refs[n_in + 4 : 2 * n_in + 4]
    sems = refs[-1]
    m = pl.program_id(0)
    dim = g_ref.shape[0]
    copies = [
        pltpu.make_async_copy(
            source.at[pl.ds(0, buffer.shape[0])] if source.shape != buffer.shape else source,
            buffer,
            sems.at[i],
        )
        for i, (source, buffer) in enumerate(zip(sources, buffers))
    ]
    n2, dq, da, *o_pieces, own, far, dk, dv, o2, dc = buffers
    ours = own.shape[0]
    width = o_pieces[0].shape[1]

    @pl.when(m == 0)
    def _():
        for copy in copies:
            copy.start()
        for copy in copies[:2]:
            copy.wait()
        g_ref[...] = tn(n2[...], dq[...]).astype(BF)

    @pl.when(m == 1)
    def _():
        for copy in copies[2 : 3 + count]:
            copy.wait()
        for i in range(count):
            base = pl.multiple_of(turn_ref[i] * width, width)
            term = tn(o_pieces[i][...], da[...]).astype(BF)

            @pl.when(base < dim)
            def _():
                g_ref[pl.ds(base, width), :] = term

    for at, right, first in ((2, dk, 3), (3, dv, 6)):

        @pl.when(m == at)
        def _():
            for copy in copies[count + first : count + 6 if at == 2 else count + 7]:
                copy.wait()
            g_ref[...] = (tn(own[...], right[:ours, :]) + tn(far[...], right[ours:, :])).astype(BF)

    @pl.when(m == 4)
    def _():
        for copy in copies[count + 7 :]:
            copy.wait()
        g_ref[...] = tn(o2[...], dc[...]).astype(BF)

    block = far_out.shape[0]

    @pl.when(m >= 5)
    def _():
        at = pl.ds(pl.multiple_of(ours + (m - 5) * block, block), block)
        far_out[...] = (nt(dk[at, :], wk_ref[...]) + nt(dv[at, :], wv_ref[...])).astype(BF)


def dealt_out(dim, block, total, index, deal):
    if not deal:
        return [pl.BlockSpec((dim, block), lambda *a: (0, index(*a)))], [
            jax.ShapeDtypeStruct((dim, total), BF)
        ]
    spec = pl.BlockSpec((8, dim // 16, block), lambda *a: (0, 0, index(*a)))
    return [spec] * 2, [jax.ShapeDtypeStruct((8, dim // 16, total), BF)] * 2


def mid_grads(turn, pieces, da, n2, dq2, own, far, dk2, dv2, o2, dc, w2):
    rows, dim = n2.shape
    args = (n2, dq2, da, *pieces, own, far, dk2, dv2, o2, dc)
    shapes = [(rows, a.shape[1]) for a in args[: 3 + len(pieces)]]
    shapes += [a.shape for a in args[3 + len(pieces) :]]
    flops = 2 * dim * dim * (3 * rows + 2 * dk2.shape[0] + 2 * far.shape[0])
    block = min(512, own.shape[0])
    far_blocks = far.shape[0] // block
    once = pl.Buffered(1)
    column = lambda m, t: (0, jnp.where(m < 2, 1 - m, jnp.minimum(m, 4)))
    return pl.pallas_call(
        functools.partial(mid_grads_kernel, count=len(pieces)),
        grid_spec=pltpu.PrefetchScalarGridSpec(
            num_scalar_prefetch=1,
            grid=(5 + far_blocks,),
            in_specs=[pl.BlockSpec(memory_space=pl.ANY)] * len(args)
            + [
                pl.BlockSpec((dim, dim), lambda m, t: (0, 2), pipeline_mode=once),
                pl.BlockSpec((dim, dim), lambda m, t: (0, 3), pipeline_mode=once),
            ],
            out_specs=[
                pl.BlockSpec((dim, dim), column),
                pl.BlockSpec((block, dim), lambda m, t: (jnp.maximum(m - 5, 0), 0)),
            ],
            scratch_shapes=[pltpu.VMEM(shape, BF) for shape in shapes]
            + [pltpu.SemaphoreType.DMA((len(args),))],
        ),
        out_shape=[
            jax.ShapeDtypeStruct((dim, 5 * dim), BF),
            jax.ShapeDtypeStruct(far.shape, BF),
        ],
        compiler_params=params(),
        cost_estimate=cost(flops, 30 * MIB),
        name="mid_grads",
    )(turn, *args, w2, w2)


def enc_finish_kernel(dk_ref, dv_ref, wk_ref, wv_ref, *refs):
    total = nt(dk_ref[...], wk_ref[...]) + nt(dv_ref[...], wv_ref[...])
    for ref in refs[:-1]:
        total = total + ref[...].astype(F32)
    refs[-1][...] = total


def enc_finish(dk, dv, w2, got):
    rows, dim = got[0].shape
    block = min(512, rows)
    row = pl.BlockSpec((block, dim), lambda i: (i, 0))
    return pl.pallas_call(
        enc_finish_kernel,
        grid=(rows // block,),
        in_specs=[
            row,
            row,
            pl.BlockSpec((dim, dim), lambda i: (0, 2)),
            pl.BlockSpec((dim, dim), lambda i: (0, 3)),
        ]
        + [row] * len(got),
        out_specs=row,
        out_shape=jax.ShapeDtypeStruct((rows, dim), F32),
        compiler_params=params(),
        cost_estimate=cost(4 * rows * dim * dim, 12 * rows * dim),
        name="enc_finish",
    )(dk, dv, w2, w2, *got)


def before_self_kernel(turn_ref, dq_ref, wq_ref, h_ref, dh_ref, g_ref, *refs, count):
    w_refs = refs[:count]
    d1_ref, da_ref, s_ref = refs[count : count + 3]
    do_refs = refs[count + 3 :]
    dn = nt(dq_ref[...], wq_ref[...])
    dh, dg = norm_back(h_ref[...], g_ref[...], dn)
    d1 = dh_ref[...] + dh
    d1_ref[...] = d1
    da = d1.astype(BF)
    da_ref[...] = da
    for do_ref, w_ref in zip(do_refs, w_refs):
        do_ref[...] = nt(da, w_ref[...]).astype(BF)

    @pl.when(pl.program_id(0) == 0)
    def _():
        s_ref[...] = jnp.zeros_like(s_ref)

    s_ref[0:1, :] += dg


def before_self(turn, dq, w2, h1, dh2, gain, wo, width):
    rows, dim = dq.shape
    count = turn.shape[0]
    block = min(512, rows)
    line = lambda i, t: (i, 0)
    whole = lambda i, t: (0, 0)
    row = pl.BlockSpec((block, dim), line)
    return pl.pallas_call(
        functools.partial(before_self_kernel, count=count),
        grid_spec=pltpu.PrefetchScalarGridSpec(
            num_scalar_prefetch=1,
            grid=(rows // block,),
            in_specs=[
                row,
                pl.BlockSpec((dim, dim), lambda i, t: (0, 1)),
                row,
                row,
                pl.BlockSpec((1, dim), whole),
            ]
            + turn_specs(count, width, dim),
            out_specs=[row, row, pl.BlockSpec((8, dim), whole)]
            + [pl.BlockSpec((block, width), line)] * count,
        ),
        out_shape=[
            jax.ShapeDtypeStruct((rows, dim), F32),
            jax.ShapeDtypeStruct((rows, dim), BF),
            jax.ShapeDtypeStruct((8, dim), F32),
        ]
        + [jax.ShapeDtypeStruct((rows, width), BF)] * count,
        compiler_params=params(),
        cost_estimate=cost(4 * rows * dim * dim, 18 * rows * dim),
        name="before_self",
    )(turn, dq, w2, h1, dh2, gain, *([wo] * count))


def joined(refs):
    return jnp.concatenate([r[...] for r in refs], axis=1)


def qkv_grads_kernel(core_ref, *refs, count, deal):
    d_refs = refs[:count]
    n_ref, w_ref, gain_ref, extra_ref = refs[count : count + 4]
    outs = refs[count + 4 :]
    acc, full = outs[-2:]
    i = pl.program_id(0)
    term = tn(n_ref[...], joined(d_refs))

    @pl.when(i == 0)
    def _():
        acc[...] = term

    @pl.when(i > 0)
    def _():
        acc[...] += term

    @pl.when(i == pl.num_programs(0) - 1)
    def _():
        width = acc.shape[1]
        grad = acc[...]
        gains = jnp.sum(grad * w_ref[...].astype(F32), axis=1, keepdims=True) / gain_ref[:, :1]
        extra = extra_ref[...]
        full[:, :width] = grad.astype(BF)
        full[:, width:] = jnp.where(lanes(extra.shape) == 0, gains, extra).astype(BF)
        if deal:
            deal_rows(core_ref[0], full, outs[0], outs[1])
        else:
            outs[0][...] = full[...]


def qkv_grads(core, ds, n, w, gain, extra, deal):
    total, dim = n.shape
    block = min(512, total)
    width = w.shape[1]
    specs, outs = dealt_out(dim, width + 128, width + 128, lambda i, c: 0, deal)
    whole = lambda i, c: (0, 0)
    return pl.pallas_call(
        functools.partial(qkv_grads_kernel, count=len(ds), deal=deal),
        grid_spec=pltpu.PrefetchScalarGridSpec(
            num_scalar_prefetch=1,
            grid=(total // block,),
            in_specs=[pl.BlockSpec((block, width // 3), lambda i, c: (i, 0))] * len(ds)
            + [
                pl.BlockSpec((block, dim), lambda i, c: (i, 0)),
                pl.BlockSpec(w.shape, whole),
                pl.BlockSpec((dim, 128), whole),
                pl.BlockSpec((dim, 128), whole),
            ],
            out_specs=specs,
            scratch_shapes=[pltpu.VMEM((dim, width), F32), pltpu.VMEM((dim, width + 128), BF)],
        ),
        out_shape=outs,
        compiler_params=params(),
        cost_estimate=cost(total * dim, total),
        name="qkv_grads",
    )(core, *ds, n, w, gain, extra)


def qkv_back_kernel(order_ref, *refs, count):
    dn_ref = refs[count + 1]
    dn_ref[...] = nt(joined(refs[:count]), refs[count][...]).astype(dn_ref.dtype)


def qkv_back(order, first, ds, w, rows, dtype, block):
    dim = w.shape[0]
    return pl.pallas_call(
        functools.partial(qkv_back_kernel, count=len(ds)),
        grid_spec=pltpu.PrefetchScalarGridSpec(
            num_scalar_prefetch=1,
            grid=(rows // block,),
            in_specs=[pl.BlockSpec((block, w.shape[1] // 3), lambda i, o: (o[i + first], 0))] * len(ds)
            + [pl.BlockSpec(w.shape, lambda i, o: (0, 0))],
            out_specs=pl.BlockSpec((block, dim), lambda i, o: (i, 0)),
        ),
        out_shape=jax.ShapeDtypeStruct((rows, dim), dtype),
        compiler_params=params(),
        cost_estimate=cost(rows * dim, rows),
        name="qkv_back",
    )(order, *ds, w)


def finish_kernel(x_ref, dh_ref, g_ref, own_ref, *refs):
    dn = own_ref[...]
    for ref in refs[:-1]:
        dn = dn + ref[...].astype(F32)
    dh, _ = norm_back(x_ref[...].astype(F32), g_ref[...], dn)
    refs[-1][...] = dh_ref[...] + dh


def finish(x, dh1, gain, own, got):
    rows, dim = x.shape
    block = min(256, rows)
    row = pl.BlockSpec((block, dim), lambda i: (i, 0))
    return pl.pallas_call(
        finish_kernel,
        grid=(rows // block,),
        in_specs=[row, row, pl.BlockSpec((1, dim), lambda i: (0, 0)), row] + [row] * len(got),
        out_specs=row,
        out_shape=jax.ShapeDtypeStruct((rows, dim), F32),
        compiler_params=params(),
        cost_estimate=cost(10 * rows * dim, 16 * rows * dim),
        name="finish",
    )(x, dh1, gain, own, *got)


def turned(n, k):
    return [(i, (i + k) % n) for i in range(n)]


def rows_of(array, index, count):
    size = array.shape[0] // count
    return lax.dynamic_slice_in_dim(array, index * size, size, 0)


def assemble_kernel(place_ref, near_ref, far_ref, w_ref, g_ref):
    z, core = place_ref[0], place_ref[1]
    count, size = near_ref.shape[0], near_ref.shape[1]
    width = w_ref.shape[1]
    for d in range(count):
        base = lax.rem(z - d + count, count) * (2 * size)
        for ref, half in ((near_ref, core), (far_ref, 1 - core)):
            at = pl.ds(pl.multiple_of(base + half * size, 16), size)
            w_ref[at, :] = ref[d, :, :width]
            g_ref[at, :] = ref[d, :, width:]


def gather_first(own, z, part, n_fsdp, n_parts):
    size = own.shape[0] // 2
    width = own.shape[1] - 128
    if n_parts % 2 or size % 16:
        full = lax.all_gather(own, "fsdp", axis=0, tiled=True)
        return full[:, :width], full[:, width:]
    core = part % 2
    mine = lax.dynamic_slice_in_dim(own, core * size, size, 0)
    near = jnp.stack(
        [mine] + [lax.ppermute(mine, "fsdp", turned(n_fsdp, d)) for d in range(1, n_fsdp)]
    )
    far = lax.ppermute(near, "parts", [(i, i ^ 1) for i in range(n_parts)])
    vmem = pl.BlockSpec(memory_space=pltpu.VMEM)
    total = n_fsdp * own.shape[0]
    return pl.pallas_call(
        assemble_kernel,
        in_specs=[pl.BlockSpec(memory_space=pltpu.SMEM), vmem, vmem],
        out_specs=[vmem, vmem],
        out_shape=[
            jax.ShapeDtypeStruct((total, width), BF),
            jax.ShapeDtypeStruct((total, 128), BF),
        ],
        compiler_params=params(),
        name="assemble",
    )(jnp.stack([z, core]).astype(jnp.int32), near, far)


def pick(array, index, axis):
    return lax.dynamic_index_in_dim(array, index, axis, keepdims=False)


class Plane:
    def __init__(self, part, place, z, n_parts, n_fsdp):
        self.core, self.x, self.place, self.z = part % 2, part // 2, place, z
        self.n_fsdp = n_fsdp
        self.swap_core = [(i, i ^ 1) for i in range(n_parts)]
        self.swap_x = [(i, i ^ 2) for i in range(n_parts)]

    def over_core(self, send, keep):
        shape = (self.n_fsdp, 2) + send.shape[1:]
        got = lax.ppermute(send, "parts", self.swap_core).reshape(shape)
        keep = keep.reshape(shape)
        add = lambda i: (pick(keep, i, 1).astype(F32) + pick(got, i, 1).astype(F32)).astype(BF)
        return add(1 - self.x), add(self.x)

    def over_x(self, send, keep):
        got = lax.ppermute(send, "parts", self.swap_x)
        return (keep.astype(F32) + got.astype(F32)).astype(BF)

    def over_fsdp(self, g):
        total = pick(g, self.z, 0).astype(F32)
        for d in range(1, self.n_fsdp):
            piece = pick(g, (self.z + d) % self.n_fsdp, 0)
            total = total + lax.ppermute(piece, "fsdp", turned(self.n_fsdp, d)).astype(F32)
        return total.astype(BF)

    def over_ctx(self, g):
        return (g.astype(F32) + lax.ppermute(g, "ctx", turned(2, 1)).astype(F32)).astype(BF)

    def widen_ctx(self, g):
        return jnp.stack([g, lax.ppermute(g, "ctx", turned(2, 1))])

    def widen_x(self, g):
        return jnp.stack([g, lax.ppermute(g, "parts", self.swap_x)])

    def from_core(self, g):
        return lax.ppermute(g, "parts", self.swap_core)


def local(
    mesh_shape,
    decoder_in,
    encoder_out,
    segment_ids,
    block_order,
    prompt_len,
    self_query,
    self_key,
    self_value,
    self_output,
    cross_query,
    cross_key,
    cross_value,
    cross_output,
    gate_in,
    up_in,
    down_out,
    norm_self,
    norm_cross,
    norm_mlp,
    cotangent,
):
    n_parts, n_ctx, n_fsdp = mesh_shape
    part, place, z = lax.axis_index("parts"), lax.axis_index("ctx"), lax.axis_index("fsdp")
    plane, n_plane = part * n_ctx + place, n_parts * n_ctx
    x_own, enc_own = decoder_in[0], encoder_out[0]
    rows, dim = x_own.shape
    segs, order = segment_ids[0], block_order[0]
    total = segs.shape[0]
    slots_total = order.shape[0]
    block = total // slots_total
    per_dev = slots_total // n_ctx
    enc_rows = enc_own.shape[0]
    keys = enc_rows * n_ctx
    hidden = down_out.shape[0] * n_fsdp
    heads_here = 2 * -(-HEADS // (2 * n_ctx))
    width = heads_here * HEAD
    padded = width * n_ctx

    ring = (place + jnp.arange(n_ctx, dtype=jnp.int32)) % n_ctx
    order_here = jnp.roll(order, -per_dev * place)
    slots = jnp.argsort(order_here).astype(jnp.int32)
    counts = needed_blocks(segs, block)

    def from_ctx(value):
        pieces = [lax.ppermute(value, "ctx", turned(n_ctx, -k)) for k in range(1, n_ctx)]
        return pieces[0] if n_ctx == 2 else jnp.concatenate(pieces, axis=0)

    x_far = from_ctx(x_own)

    fast = (n_parts, n_ctx, n_fsdp) == (4, 2, 4)
    shard = dim // n_fsdp

    def own_heads(w):
        w = jnp.pad(w, ((0, 0), (0, padded - dim)))
        return lax.dynamic_slice_in_dim(w, place * width, width, 1)

    gain_cols = jnp.pad(jnp.stack([norm_self, norm_cross, norm_mlp], axis=1), ((0, 0), (0, 125)))
    first = jnp.concatenate(
        [own_heads(self_query), own_heads(self_key), own_heads(self_value), gain_cols], axis=1
    )
    w1, gains = gather_first(first, z, part, n_fsdp, n_parts)
    gains = gains[:, :8].astype(F32).T
    gain_self, gain_cross, gain_mlp = (gains[i : i + 1] for i in range(3))
    mats = (self_output, cross_query, cross_key, cross_value, cross_output)
    if fast:
        w2 = lax.all_gather(
            jnp.concatenate([rows_of(w, part, n_parts) for w in mats], axis=1),
            AROUND, axis=0, tiled=True,
        )

        def column_pieces(w):
            cut = lax.dynamic_slice_in_dim(w, part * 512, 512, 1).reshape(3, 64, 2, 256)
            return cut.transpose(2, 1, 0, 3).reshape(2, 64, dim)

        w3 = lax.all_gather(
            jnp.stack(
                [
                    column_pieces(gate_in),
                    column_pieces(up_in),
                    rows_of(down_out, part, n_parts).reshape(2, 64, dim),
                ],
                axis=1,
            ).reshape(-1, dim),
            AROUND, axis=0, tiled=True,
        ).reshape(PIECES + (dim,))
    else:
        w2 = lax.all_gather(jnp.concatenate(mats, axis=1), "fsdp", axis=0, tiled=True)

        def packed(w):
            w = lax.all_gather(w, "fsdp", axis=0, tiled=True).reshape(4, 3, 64, 8, 256)
            return w.transpose(0, 3, 2, 1, 4).reshape(4, 8, 64, dim)

        w_down = lax.all_gather(down_out, "fsdp", axis=0, tiled=True).reshape(4, 8, 64, dim)
        w3 = jnp.stack([packed(gate_in), packed(up_in), w_down], axis=2)
    x_far, enc_sent = lax.optimization_barrier((x_far, enc_own))
    enc_far = from_ctx(enc_sent)

    n1, q, k, v = qkv_forward(order_here, x_own, x_far, gain_self, w1, block)
    spot = jnp.arange(128, dtype=jnp.int32)[None, :] % HEAD
    minus = jnp.where((spot >= PART0) & (spot < PART0 + 3), -1.0, 0.0)
    seg_q = jnp.where(spot == segs[:, None], 1.0, 0.0).astype(BF)
    seg_k = jnp.where((spot < SEGS) & (spot != segs[:, None]), -BIG, minus).astype(BF)
    o1, lse1 = self_forward(counts, slots, q, k, v, seg_q, seg_k, block)
    pieces = [o1] + [
        lax.ppermute(o1[i * rows : (i + 1) * rows], "ctx", turned(n_ctx, i)) for i in range(1, n_ctx)
    ]
    turn = (place - jnp.arange(n_ctx, dtype=jnp.int32)) % n_ctx
    wo = w2 if padded == dim else jnp.pad(w2[:, :dim], ((0, padded - dim), (0, 0)))
    kv2 = enc_forward(enc_own, enc_far, w2)
    pieces[1], kv2 = lax.optimization_barrier((pieces[1], kv2))
    h1, n2, q2, stat1 = after_self(turn, x_own, pieces, wo, gain_cross, w2)

    where_key = (ring[:, None] * enc_rows + jnp.arange(enc_rows, dtype=jnp.int32)).reshape(-1, 1)
    len_q = jnp.where(spot == 0, jnp.ones((rows, 1), F32), 0.0).astype(BF)
    len_k = jnp.where((spot == 0) & (where_key >= prompt_len[0]), -BIG, minus).astype(BF)
    o2, lse2 = cross_forward(q2, kv2, len_q, len_k)

    layer_out, dh2, dc, do2, stat2, g_ff = feed_forward(o2, h1, w2, gain_mlp, cotangent[0], w3)
    if fast:
        part_ff = lax.psum_scatter(
            g_ff.reshape(-1, dim), AROUND, scatter_dimension=0, tiled=True
        ).reshape(2, 3, 64, dim)

    dq2, dk2, dv2 = cross_backward(q2, kv2, do2, o2, lse2, len_q, len_k)
    dh1, da, stat3, *do1 = before_self(turn, dq2, w2, h1, dh2, gain_cross, wo, width)
    do_far = [lax.ppermute(do1[i], "ctx", turned(n_ctx, -i)) for i in range(1, n_ctx)]
    do_far = do_far[0] if n_ctx == 2 else jnp.concatenate(do_far, axis=0)
    do_own = do1[0]
    core = jnp.reshape(part % 2, (1,)).astype(jnp.int32)
    g_mid, d_far = mid_grads(
        turn, pieces, da, n2, dq2, enc_own, enc_far, dk2, dv2, o2, dc, w2
    )

    sums = jnp.sum(jnp.concatenate([stat1[:2], stat2[:2]], axis=0), axis=1)
    extra = jnp.concatenate(
        [
            jnp.zeros((dim, 1), F32),
            stat2[2][:, None],
            stat3[0][:, None],
            jnp.broadcast_to(sums[None], (dim, 4)),
            jnp.zeros((dim, 121), F32),
        ],
        axis=1,
    )
    gain_wide = jnp.broadcast_to(gain_self.reshape(dim, 1), (dim, 128))

    if fast:
        net = Plane(part, place, z, n_parts, n_fsdp)
        do_own, do_far, d_far, extra, gain_wide, g_mid, part_ff = lax.optimization_barrier(
            (do_own, do_far, d_far, extra, gain_wide, g_mid, part_ff)
        )
        part_mid = lax.psum_scatter(g_mid, AROUND, scatter_dimension=0, tiled=True)
        sum_ff = net.over_ctx(part_ff)
    enc_got = [
        lax.ppermute(d_far[(i - 1) * enc_rows : i * enc_rows], "ctx", turned(n_ctx, i))
        for i in range(1, n_ctx)
    ]
    ds = self_backward(counts, slots, q, k, v, do_own, do_far, o1, lse1, seg_q, seg_k, block)
    if fast:
        ds, sum_ff, enc_got = lax.optimization_barrier((ds, sum_ff, enc_got))
    g_qkv = qkv_grads(core, ds, n1, w1, gain_wide, extra, fast)
    ds, g_qkv = lax.optimization_barrier((ds, g_qkv))
    dn_far = qkv_back(order_here, per_dev, ds, w1, total - rows, BF, block)
    dn_got = [
        lax.ppermute(dn_far[(i - 1) * rows : i * rows], "ctx", turned(n_ctx, i))
        for i in range(1, n_ctx)
    ]
    dn_own = qkv_back(order_here, 0, ds, w1, rows, F32, block)
    enc_grad = enc_finish(dk2, dv2, w2, enc_got)
    if fast:
        send, keep = net.over_core(*g_qkv)
        send, keep, dn_far = lax.optimization_barrier((send, keep, dn_far))
        sum_ff = net.widen_x(sum_ff)
        g_qkv, enc_grad = lax.optimization_barrier((net.over_x(send, keep), enc_grad))
        g_qkv = net.over_fsdp(g_qkv)
        dn_got, part_mid, dn_own = lax.optimization_barrier((dn_got, part_mid, dn_own))
        g_qkv, part_mid = lax.optimization_barrier((g_qkv, part_mid))
    decoder_grad = finish(x_own, dh1, gain_self, dn_own, dn_got)

    if fast:
        me = jnp.stack([net.core, net.x, place]).astype(jnp.int32)
        square = (shard, dim)
        ff = settle(
            unpack_kernel, me, sum_ff, net.from_core(sum_ff),
            [(shard, hidden), (shard, hidden), (hidden // n_fsdp, dim)],
        )
        g_qkv, decoder_grad = lax.optimization_barrier((net.widen_ctx(g_qkv), decoder_grad))
        g_qkv, ff = lax.optimization_barrier((net.widen_x(g_qkv), ff))
        grad_gate, grad_up, grad_down = ff
        sum_mid = net.widen_x(net.over_ctx(part_mid))
        *grads_qkv, tail = settle(
            settle_qkv_kernel, me, g_qkv, net.from_core(g_qkv), [square] * 3 + [(shard, 128)]
        )
        mids = settle(settle_mid_kernel, me, sum_mid, net.from_core(sum_mid), [square] * 5)
    else:

        def total_of(g):
            g = lax.psum_scatter(g, "fsdp", scatter_dimension=0, tiled=True).astype(F32)
            return lax.psum(g, ("parts", "ctx"))

        (g_qkv,) = g_qkv
        sum_mid = total_of(g_mid)
        flat = [
            g_ff[:, :, i].reshape(4, 8, 64, 3, 256).transpose(0, 3, 2, 1, 4).reshape(dim, hidden)
            for i in range(2)
        ]
        grad_gate, grad_up = total_of(flat[0]), total_of(flat[1])
        grad_down = total_of(g_ff[:, :, 2].reshape(hidden, dim))
        sum_qkv = lax.psum_scatter(g_qkv, "fsdp", scatter_dimension=0, tiled=True).astype(F32)
        every = lax.all_gather(lax.psum(sum_qkv, "parts"), "ctx", axis=0)
        grads_qkv = [
            jnp.concatenate(
                [every[c, :, i * width : (i + 1) * width] for c in range(n_ctx)], axis=1
            )[:, :dim]
            for i in range(3)
        ]
        tail = jnp.sum(every[:, :, 3 * width :], axis=0)
        mids = [sum_mid[:, i * dim : (i + 1) * dim] for i in range(5)]
    grad_gself, grad_gmlp, grad_gcross = tail[:, 0], tail[:, 1], tail[:, 2]
    entries = float(n_parts * n_ctx * n_fsdp * rows * dim)
    rms_values = jnp.sqrt(tail[0, 3:7] / entries)
    return (
        layer_out[None],
        decoder_grad[None],
        enc_grad[None],
        *grads_qkv,
        *mids,
        grad_gate,
        grad_up,
        grad_down,
        grad_gself,
        grad_gcross,
        grad_gmlp,
        rms_values,
    )


def solution(mesh):
    rows3 = P(("parts", "fsdp"), "ctx", None)
    group = P(("parts", "fsdp"), None)
    matrix, vector = P("fsdp", None), P("fsdp")
    shape = tuple(mesh.shape[a] for a in ("parts", "ctx", "fsdp"))
    return jax.shard_map(
        functools.partial(local, shape),
        mesh=mesh,
        in_specs=(rows3, rows3, group, group, P(("parts", "fsdp")))
        + (matrix,) * 11
        + (vector,) * 3
        + (rows3,),
        out_specs=(rows3,) * 3 + (matrix,) * 11 + (vector,) * 3 + (P(),),
        check_vma=False,
    )
```

```python
import functools
import math

import jax
import jax.numpy as jnp
from jax import lax
from jax.experimental import pallas as pl
from jax.experimental.pallas import tpu as pltpu
from jax.sharding import PartitionSpec as P

HEADS = 12
HEAD = 64
SCALE = 0.125
EPS = 1e-06
BIG = 1e30
LN2 = math.log(2.0)
QSCALE = SCALE * math.log2(math.e)
PART0 = 16
SEGS = 16
BF = jnp.bfloat16
F32 = jnp.float32
MIB = 1 << 20
AROUND = ("fsdp", "parts")


def nn(a, b):
    return lax.dot_general(a, b, (((1,), (0,)), ((), ())), preferred_element_type=F32)


def nt(a, b):
    return lax.dot_general(a, b, (((1,), (1,)), ((), ())), preferred_element_type=F32)


def tn(a, b):
    return lax.dot_general(a, b, (((0,), (0,)), ((), ())), preferred_element_type=F32)


def lanes(shape):
    return lax.broadcasted_iota(jnp.int32, shape, len(shape) - 1)


def params(mib=60):
    return pltpu.CompilerParams(vmem_limit_bytes=mib * MIB)


def cost(flops, moved, exps=0):
    return pl.CostEstimate(flops=int(flops), bytes_accessed=int(moved), transcendentals=int(exps))


def rms_scale(h):
    return lax.rsqrt(jnp.mean(h * h, axis=-1, keepdims=True) + EPS)


def norm_back(h, gain, dn):
    r = rms_scale(h)
    t = dn * gain
    hr = h * r
    dh = r * (t - hr * jnp.mean(t * hr, axis=-1, keepdims=True))
    return dh, jnp.sum(dn * hr, axis=0, keepdims=True)


def with_parts(base, value):
    spot = lanes(base.shape) % HEAD
    hi = value.astype(BF)
    rest = value - hi.astype(F32)
    mid = rest.astype(BF)
    low = (rest - mid.astype(F32)).astype(BF)
    return jnp.where(
        spot == PART0, hi, jnp.where(spot == PART0 + 1, mid, jnp.where(spot == PART0 + 2, low, base))
    )


def pair_of(own, other):
    left = lanes(own.shape) < HEAD
    return jnp.where(left, own, other), jnp.where(left, other, own)


CHUNK = 512


def below(s, rows_first):
    r = lax.broadcasted_iota(jnp.int32, s.shape, 0)
    c = lanes(s.shape)
    return jnp.where(c <= r if rows_first else r <= c, s, -BIG)


def lane_max(s):
    return functools.reduce(jnp.maximum, [s[:, c : c + 128] for c in range(0, s.shape[1], 128)])


def sweep(step, lo, full, odd, grain, unroll):
    base = lo
    if odd is not None:

        @pl.when(odd == 1)
        def _():
            step(lo, 0, grain)

        base = lo + odd * grain

    def body(c, carry):
        step(pl.multiple_of(base + c * CHUNK, grain), pl.multiple_of(grain + c * CHUNK, 128), CHUNK)
        return carry

    lax.fori_loop(0, full, body, 0, unroll=unroll)
    return pl.multiple_of(base + full * CHUNK, grain)


def forward_block(
    lo, full, odd, grain, diag, q_ref, qa_ref, kx, vx, o_ref, lse_ref, s_scr, m_scr, a_scr, unroll
):
    q = q_ref[...]
    rows = q.shape[0]
    left = lanes(q.shape) < HEAD
    sides = pair_of(q, qa_ref[...])
    m_scr[...] = jnp.full_like(m_scr, -BIG)
    a_scr[...] = jnp.zeros_like(a_scr)
    last = s_scr.shape[2] - rows

    def scores(key, at, size, start=None):
        live = pl.ds(start or 0, rows - (start or 0))
        for h in range(2):
            s = nt(sides[h][start or 0 :], kx[h, pl.ds(key, size), :])
            s = s if start is None else below(s, True)
            s_scr[h, live, pl.ds(at, size)] = s
            m_scr[h, live, :] = jnp.maximum(m_scr[h, live, :], lane_max(s))

    steps = range(0, rows, grain) if diag else ()
    end = sweep(scores, lo, full, odd, grain, unroll)
    for start in steps:
        scores(end + start, last + start, grain, start)
    tops = [jnp.max(m_scr[h], axis=1, keepdims=True) for h in range(2)]

    def values(key, at, size, start=0):
        live = pl.ds(start, rows - start)
        for h in range(2):
            p = jnp.exp2(s_scr[h, live, pl.ds(at, size)] - tops[h][start:]).astype(BF)
            a_scr[h, live, :] += nn(p, vx[h, pl.ds(key, size), :])

    end = sweep(values, lo, full, odd, grain, unroll)
    for start in steps:
        values(end + start, last + start, grain, start)
    wide = jnp.where(left, a_scr[0], a_scr[1])
    total = jnp.where(left, a_scr[1], a_scr[0])
    o_ref[...] = (wide / pltpu.roll(total, HEAD, 1)).astype(o_ref.dtype)
    lse_ref[...] = jnp.where(left, tops[1], tops[0]) + jnp.log2(total)


def forward_scratch(block, keys):
    return [
        pltpu.VMEM((2, keys, 128), BF),
        pltpu.VMEM((2, keys, 128), BF),
        pltpu.VMEM((2, block, keys + CHUNK), F32),
        pltpu.VMEM((2, block, 128), F32),
        pltpu.VMEM((2, block, 128), F32),
    ]


def backward_scratch(block, keys):
    return (
        [pltpu.VMEM((2, keys, 128), BF)] * 3
        + [pltpu.VMEM((keys, 128), F32)] * 2
        + [pltpu.VMEM((block, 128), F32)]
    )


def forward_prep(k_ref, v_ref, ka_ref, kx, vx):
    kx[0], kx[1] = pair_of(k_ref[...], ka_ref[...])
    v = v_ref[...]
    vx[0], vx[1] = pair_of(v, jnp.ones_like(v))


def backward_prep(k_ref, v_ref, ka_ref, kx, vx, km, dk_acc, dv_acc):
    k, v = k_ref[...], v_ref[...]
    spot = lanes(v.shape) % HEAD
    neg = jnp.where((spot >= PART0) & (spot < PART0 + 3), -1.0, 0.0).astype(BF)
    kx[0], kx[1] = pair_of(k, ka_ref[...])
    vx[0], vx[1] = pair_of(v, neg)
    km[0], km[1] = pair_of(k, jnp.zeros_like(k))
    dk_acc[...] = jnp.zeros_like(dk_acc)
    dv_acc[...] = jnp.zeros_like(dv_acc)


def backward_block(
    lo, full, odd, grain, diag, q, do, o_ref, lse_ref, qa_ref, kx, vx, km,
    dq_ref, dk_acc, dv_acc, dq_acc, unroll,
):
    left = lanes(q.shape) < HEAD
    rows = q.shape[0]
    product = do.astype(F32) * o_ref[...].astype(F32)
    first = jnp.sum(jnp.where(left, product, 0.0), axis=1, keepdims=True)
    second = jnp.sum(jnp.where(left, 0.0, product), axis=1, keepdims=True)
    delta = jnp.where(left, second, first)
    zero = jnp.zeros_like(q)
    qx = pair_of(q, with_parts(qa_ref[...], lse_ref[...]))
    dx = pair_of(do, with_parts(zero, delta))
    qm = pair_of(q, zero)
    dm = pair_of(do, zero)
    dq_acc[...] = jnp.zeros_like(dq_acc)

    def step(key, _, size, start=None):
        at = pl.ds(key, size)
        live = slice(start or 0, rows)
        dq = dk = dv = None
        for h in range(2):
            st = nt(kx[h, at, :], qx[h][live])
            pt = jnp.exp2(st if start is None else below(st, False))
            dp = nt(vx[h, at, :], dx[h][live])
            ds = (pt * dp).astype(BF)
            tv, tk, tq = nn(pt.astype(BF), dm[h][live]), nn(ds, qm[h][live]), tn(ds, km[h, at, :])
            dv = tv if dv is None else dv + tv
            dk = tk if dk is None else dk + tk
            dq = tq if dq is None else dq + tq
        dv_acc[at, :] += dv
        dk_acc[at, :] += dk
        dq_acc[live, :] += dq

    end = sweep(step, lo, full, odd, grain, unroll)
    for start in range(0, rows, grain) if diag else ():
        step(end + start, 0, grain, start)
    dq_ref[...] = (dq_acc[...] * SCALE).astype(dq_ref.dtype)


def cross_forward_kernel(
    q_ref, k_ref, v_ref, qa_ref, ka_ref, o_ref, inv_ref, p_ref, kx, vx, s_scr, m_scr, a_scr
):
    @pl.when(pl.program_id(1) == 0)
    def _():
        forward_prep(k_ref, v_ref, ka_ref, kx, vx)

    q = q_ref[...]
    keys = k_ref.shape[0]
    left = lanes(q.shape) < HEAD
    sides = pair_of(q, qa_ref[...])
    chunks = [pl.ds(c, CHUNK) for c in range(0, keys, CHUNK)]
    m_scr[...] = jnp.full_like(m_scr, -BIG)
    a_scr[...] = jnp.zeros_like(a_scr)
    for at in chunks:
        for h in range(2):
            s = nt(sides[h], kx[h, at, :])
            s_scr[h, :, at] = s
            m_scr[h] = jnp.maximum(m_scr[h], lane_max(s))
    tops = [jnp.max(m_scr[h], axis=1, keepdims=True) for h in range(2)]
    for at in chunks:
        for h in range(2):
            p = jnp.exp2(s_scr[h, :, at] - tops[h]).astype(BF)
            p_ref[:, pl.ds(h * keys + at.start, CHUNK)] = p
            a_scr[h] += nn(p, vx[h, at, :])
    wide = jnp.where(left, a_scr[0], a_scr[1])
    inv = 1.0 / jnp.where(left, a_scr[1], a_scr[0])
    o_ref[...] = (wide * pltpu.roll(inv, HEAD, 1)).astype(o_ref.dtype)
    inv_ref[...] = inv


def cross_forward(q, kv, qa, ka):
    rows, width = q.shape
    keys = kv.shape[0]
    block = min(512, rows)
    pairs = width // 128
    row = pl.BlockSpec((block, 128), lambda h, i: (i, h))
    return pl.pallas_call(
        cross_forward_kernel,
        grid=(pairs, rows // block),
        in_specs=[
            row,
            pl.BlockSpec((keys, 128), lambda h, i: (0, h)),
            pl.BlockSpec((keys, 128), lambda h, i: (0, h + pairs)),
            pl.BlockSpec((block, 128), lambda h, i: (i, 0)),
            pl.BlockSpec((keys, 128), lambda h, i: (0, 0)),
        ],
        out_specs=[row, row, pl.BlockSpec((block, 2 * keys), lambda h, i: (i, h))],
        out_shape=[
            jax.ShapeDtypeStruct((rows, width), BF),
            jax.ShapeDtypeStruct((rows, width), F32),
            jax.ShapeDtypeStruct((rows, 2 * pairs * keys), BF),
        ],
        scratch_shapes=forward_scratch(block, keys),
        compiler_params=params(),
        cost_estimate=cost(16 * rows * keys * width, 8 * rows * width, rows * keys * 12),
        name="cross_forward",
    )(q, kv, kv, qa, ka)


def cross_backward_kernel(
    q_ref, k_ref, v_ref, do_ref, o_ref, inv_ref, p_ref,
    dq_ref, dk_ref, dv_ref, vx, km, dk_acc, dv_acc,
):
    keys = k_ref.shape[0]

    @pl.when(pl.program_id(1) == 0)
    def _():
        k, v = k_ref[...], v_ref[...]
        spot = lanes(v.shape) % HEAD
        neg = jnp.where((spot >= PART0) & (spot < PART0 + 3), -1.0, 0.0).astype(BF)
        vx[0], vx[1] = pair_of(v, neg)
        km[0], km[1] = pair_of(k, jnp.zeros_like(k))
        dk_acc[...] = jnp.zeros_like(dk_acc)
        dv_acc[...] = jnp.zeros_like(dv_acc)

    q, do = q_ref[...], do_ref[...].astype(F32)
    left = lanes(q.shape) < HEAD
    zero = jnp.zeros_like(q)
    inv = inv_ref[...]
    product = do * o_ref[...].astype(F32)
    first = jnp.sum(jnp.where(left, product, 0.0), axis=1, keepdims=True)
    second = jnp.sum(jnp.where(left, 0.0, product), axis=1, keepdims=True)
    delta = jnp.where(left, second, first) * inv
    do = (do * pltpu.roll(inv, HEAD, 1)).astype(BF)
    dx = pair_of(do, with_parts(zero, delta))
    qm = pair_of(q, zero)
    dm = pair_of(do, zero)
    dq = None
    for c in range(0, keys, CHUNK):
        at = pl.ds(c, CHUNK)
        dk = dv = None
        for h in range(2):
            p = p_ref[:, pl.ds(h * keys + c, CHUNK)]
            ds = (p.astype(F32) * nt(dx[h], vx[h, at, :])).astype(BF)
            tv, tk, tq = tn(p, dm[h]), tn(ds, qm[h]), nn(ds, km[h, at, :])
            dv = tv if dv is None else dv + tv
            dk = tk if dk is None else dk + tk
            dq = tq if dq is None else dq + tq
        dv_acc[at, :] += dv
        dk_acc[at, :] += dk
    dq_ref[...] = (dq * SCALE).astype(BF)

    @pl.when(pl.program_id(1) == pl.num_programs(1) - 1)
    def _():
        dk_ref[...] = (dk_acc[...] * LN2).astype(BF)
        dv_ref[...] = dv_acc[...].astype(BF)


def cross_backward(q, kv, do, o, inv, p):
    rows, width = q.shape
    keys = kv.shape[0]
    block = min(512, rows)
    pairs = width // 128
    row = pl.BlockSpec((block, 128), lambda h, i: (i, h))
    col = pl.BlockSpec((keys, 128), lambda h, i: (0, h))
    return pl.pallas_call(
        cross_backward_kernel,
        grid=(pairs, rows // block),
        in_specs=[
            row,
            col,
            pl.BlockSpec((keys, 128), lambda h, i: (0, h + pairs)),
            row,
            row,
            row,
            pl.BlockSpec((block, 2 * keys), lambda h, i: (i, h)),
        ],
        out_specs=[row, col, col],
        out_shape=[
            jax.ShapeDtypeStruct((rows, width), BF),
            jax.ShapeDtypeStruct((keys, width), BF),
            jax.ShapeDtypeStruct((keys, width), BF),
        ],
        scratch_shapes=[pltpu.VMEM((2, keys, 128), BF)] * 2 + [pltpu.VMEM((keys, 128), F32)] * 2,
        compiler_params=params(),
        cost_estimate=cost(32 * rows * keys * width, 12 * rows * width),
        name="cross_backward",
    )(q, kv, kv, do, o, inv, p)


def grain_of(block):
    return min(256, block)


def needed_blocks(segs, block):
    total = segs.shape[0]
    grain = grain_of(block)
    first = segs.reshape(total // block, block)[:, 0]
    start = jnp.sum((segs[None, :] < first[:, None]).astype(jnp.int32), axis=1)
    ends = (jnp.arange(total // block, dtype=jnp.int32) + 1) * block
    return (ends - start // grain * grain) // grain


def self_range(count, i, block):
    grain = grain_of(block)
    before = count - block // grain
    per = CHUNK // grain
    lo = pl.multiple_of((i + 1) * block - count * grain, grain)
    return lo, before // per, before % per, grain


def self_forward_kernel(
    count_ref, slot_ref, q_ref, k_ref, v_ref, qa_ref, ka_ref, o_ref, lse_ref,
    kx, vx, s_scr, m_scr, a_scr,
):
    i = pl.program_id(1)

    @pl.when(i == 0)
    def _():
        forward_prep(k_ref, v_ref, ka_ref, kx, vx)

    forward_block(
        *self_range(count_ref[i], i, q_ref.shape[0]), True, q_ref, qa_ref, kx, vx, o_ref, lse_ref,
        s_scr, m_scr, a_scr, 1,
    )


def self_forward(counts, slots, q, k, v, qa, ka, block):
    total, width = q.shape
    row = pl.BlockSpec((block, 128), lambda h, i, n, s: (i, h))
    col = pl.BlockSpec((total, 128), lambda h, i, n, s: (0, h))
    return pl.pallas_call(
        self_forward_kernel,
        grid_spec=pltpu.PrefetchScalarGridSpec(
            num_scalar_prefetch=2,
            grid=(width // 128, total // block),
            in_specs=[
                row,
                col,
                col,
                pl.BlockSpec((block, 128), lambda h, i, n, s: (i, 0)),
                pl.BlockSpec((total, 128), lambda h, i, n, s: (0, 0)),
            ],
            out_specs=[pl.BlockSpec((block, 128), lambda h, i, n, s: (s[i], h)), row],
            scratch_shapes=forward_scratch(block, total),
        ),
        out_shape=[
            jax.ShapeDtypeStruct((total, width), BF),
            jax.ShapeDtypeStruct((total, width), F32),
        ],
        compiler_params=params(),
        cost_estimate=cost(8 * total * total * width, 8 * total * width, total * total * 3),
        name="self_forward",
    )(counts, slots, q, k, v, qa, ka)


def self_backward_kernel(
    count_ref, slot_ref, q_ref, k_ref, v_ref, own_ref, far_ref, o_ref, lse_ref, qa_ref, ka_ref,
    dq_ref, dk_ref, dv_ref, kx, vx, km, dk_acc, dv_acc, dq_acc, *, per_dev,
):
    i = pl.program_id(1)
    do = jnp.where(slot_ref[i] < per_dev, own_ref[...], far_ref[...])

    @pl.when(i == 0)
    def _():
        backward_prep(k_ref, v_ref, ka_ref, kx, vx, km, dk_acc, dv_acc)

    backward_block(
        *self_range(count_ref[i], i, q_ref.shape[0]), True, q_ref[...], do, o_ref, lse_ref, qa_ref,
        kx, vx, km, dq_ref, dk_acc, dv_acc, dq_acc, 1,
    )

    @pl.when(i == pl.num_programs(1) - 1)
    def _():
        dk_ref[...] = (dk_acc[...] * LN2).astype(BF)
        dv_ref[...] = dv_acc[...].astype(BF)


def self_backward(counts, slots, q, k, v, own, far, o, lse, qa, ka, block):
    total, width = q.shape
    per_dev = own.shape[0] // block
    row = pl.BlockSpec((block, 128), lambda h, i, n, s: (i, h))
    col = pl.BlockSpec((total, 128), lambda h, i, n, s: (0, h))
    return pl.pallas_call(
        functools.partial(self_backward_kernel, per_dev=per_dev),
        grid_spec=pltpu.PrefetchScalarGridSpec(
            num_scalar_prefetch=2,
            grid=(width // 128, total // block),
            in_specs=[
                row,
                col,
                col,
                pl.BlockSpec((block, 128), lambda h, i, n, s: (jnp.minimum(s[i], per_dev - 1), h)),
                pl.BlockSpec((block, 128), lambda h, i, n, s: (jnp.maximum(s[i] - per_dev, 0), h)),
                pl.BlockSpec((block, 128), lambda h, i, n, s: (s[i], h)),
                row,
                pl.BlockSpec((block, 128), lambda h, i, n, s: (i, 0)),
                pl.BlockSpec((total, 128), lambda h, i, n, s: (0, 0)),
            ],
            out_specs=[row, col, col],
            scratch_shapes=backward_scratch(block, total),
        ),
        out_shape=[jax.ShapeDtypeStruct((total, width), BF)] * 3,
        compiler_params=params(),
        cost_estimate=cost(4 * total * total * width, 2 * total * width),
        name="self_backward",
    )(counts, slots, q, k, v, own, far, o, lse, qa, ka)


def qkv_kernel(order_ref, own_ref, far_ref, g_ref, w_ref, n_ref, q_ref, k_ref, v_ref, *, per_dev):
    x = jnp.where(pl.program_id(0) < per_dev, own_ref[...], far_ref[...]).astype(F32)
    n = (x * rms_scale(x) * g_ref[...]).astype(BF)
    n_ref[...] = n
    width = q_ref.shape[1]
    out = nn(n, w_ref[...])
    q_ref[...] = (out[:, :width] * QSCALE).astype(BF)
    k_ref[...] = out[:, width : 2 * width].astype(BF)
    v_ref[...] = out[:, 2 * width :].astype(BF)


def qkv_forward(order, own, far, gain, w, block):
    dim = own.shape[1]
    total = own.shape[0] + far.shape[0]
    width = w.shape[1] // 3
    per_dev = own.shape[0] // block
    here = lambda i, o: (o[i], 0)
    whole = lambda i, o: (0, 0)
    return pl.pallas_call(
        functools.partial(qkv_kernel, per_dev=per_dev),
        grid_spec=pltpu.PrefetchScalarGridSpec(
            num_scalar_prefetch=1,
            grid=(total // block,),
            in_specs=[
                pl.BlockSpec((block, dim), lambda i, o: (jnp.minimum(i, per_dev - 1), 0)),
                pl.BlockSpec((block, dim), lambda i, o: (jnp.maximum(i - per_dev, 0), 0)),
                pl.BlockSpec((1, dim), whole),
                pl.BlockSpec(w.shape, whole),
            ],
            out_specs=[pl.BlockSpec((block, dim), here)] + [pl.BlockSpec((block, width), here)] * 3,
        ),
        out_shape=[jax.ShapeDtypeStruct((total, dim), BF)]
        + [jax.ShapeDtypeStruct((total, width), BF)] * 3,
        compiler_params=params(),
        cost_estimate=cost(6 * total * dim * width, 8 * total * dim),
        name="qkv_forward",
    )(order, own, far, gain, w)


def enc_kv_kernel(own_ref, far_ref, w_ref, kv_ref, *, own_blocks):
    enc = jnp.where(pl.program_id(0) < own_blocks, own_ref[...], far_ref[...])
    half = w_ref.shape[1] // 2
    for c in range(2):
        at = slice(c * half, (c + 1) * half)
        kv_ref[:, at] = nn(enc, w_ref[:, at]).astype(BF)


def enc_forward(own, far, w2):
    rows, dim = own.shape
    block = min(512, rows)
    keys = rows + far.shape[0]
    ours = rows // block
    return pl.pallas_call(
        functools.partial(enc_kv_kernel, own_blocks=ours),
        grid=(keys // block,),
        in_specs=[
            pl.BlockSpec((block, dim), lambda i: (jnp.minimum(i, ours - 1), 0)),
            pl.BlockSpec((block, dim), lambda i: (jnp.maximum(i - ours, 0), 0)),
            pl.BlockSpec((dim, 2 * dim), lambda i: (0, 1)),
        ],
        out_specs=pl.BlockSpec((block, 2 * dim), lambda i: (i, 0)),
        out_shape=jax.ShapeDtypeStruct((keys, 2 * dim), BF),
        compiler_params=params(),
        cost_estimate=cost(4 * keys * dim * dim, 8 * keys * dim),
        name="enc_forward",
    )(own, far, w2)


def after_self_kernel(turn_ref, x_ref, *refs, count):
    o_refs, w_refs = refs[:count], refs[count : 2 * count]
    g_ref, wq_ref, h_ref, n_ref, q_ref, s_ref = refs[2 * count :]
    x = x_ref[...].astype(F32)
    a = nn(o_refs[0][...], w_refs[0][...])
    for o_ref, w_ref in zip(o_refs[1:], w_refs[1:]):
        a = a + nn(o_ref[...], w_ref[...])
    h = x + a
    h_ref[...] = h
    n = (h * rms_scale(h) * g_ref[...]).astype(BF)
    n_ref[...] = n
    q_ref[...] = (nn(n, wq_ref[...]) * QSCALE).astype(BF)

    @pl.when(pl.program_id(0) == 0)
    def _():
        s_ref[...] = jnp.zeros_like(s_ref)

    s_ref[0:1, :] += jnp.sum(x * x, axis=0, keepdims=True)
    s_ref[1:2, :] += jnp.sum(a * a, axis=0, keepdims=True)


def turn_specs(count, width, dim):
    return [pl.BlockSpec((width, dim), lambda i, t, k=k: (t[k], 0)) for k in range(count)]


def after_self(turn, x, pieces, wo, gain, w2):
    rows, dim = x.shape
    count, width = len(pieces), pieces[0].shape[1]
    block = min(512, rows)
    line = lambda i, t: (i, 0)
    whole = lambda i, t: (0, 0)
    row = pl.BlockSpec((block, dim), line)
    return pl.pallas_call(
        functools.partial(after_self_kernel, count=count),
        grid_spec=pltpu.PrefetchScalarGridSpec(
            num_scalar_prefetch=1,
            grid=(rows // block,),
            in_specs=[row]
            + [pl.BlockSpec((block, width), line)] * count
            + turn_specs(count, width, dim)
            + [pl.BlockSpec((1, dim), whole), pl.BlockSpec((dim, dim), lambda i, t: (0, 1))],
            out_specs=[row, row, row, pl.BlockSpec((8, dim), whole)],
        ),
        out_shape=[
            jax.ShapeDtypeStruct((rows, dim), F32),
            jax.ShapeDtypeStruct((rows, dim), BF),
            jax.ShapeDtypeStruct((rows, dim), BF),
            jax.ShapeDtypeStruct((8, dim), F32),
        ],
        compiler_params=params(),
        cost_estimate=cost(4 * rows * dim * dim, 14 * rows * dim),
        name="after_self",
    )(turn, x, *pieces, *([wo] * count), gain, w2)


GELU_C = math.sqrt(2.0 / math.pi)
GELU_A = 0.044715


PIECES = (4, 8, 3, 64)


def mlp_kernel(
    o_ref, h1_ref, wc_ref, g_ref, t_ref, gu_ref, wd_ref,
    y_ref, dh_ref, dc_ref, do_ref, s_ref, g_out,
    n_scr, h_scr, m_scr, dn_scr, hid_scr, du_scr, dw_scr, wg_scr, wu_scr, gu_out, d_out, sems,
):
    j = pl.program_id(0)
    last = pl.num_programs(0) - 1
    rows = o_ref.shape[0]
    step = min(256, rows)
    spans = [pl.ds(r, step) for r in range(0, rows, step)]
    gain = g_ref[...]
    n_fsdp, n_two, _, tall, _ = gu_ref.shape
    third = 256
    high = 3 * tall

    @pl.when(j == 0)
    def _():
        total = None
        for at in spans:
            c = nn(o_ref[at, :], wc_ref[...])
            h = h1_ref[at, :] + c
            h_scr[at, :] = h
            n_scr[at, :] = (h * rms_scale(h) * gain).astype(BF)
            part = jnp.sum(c * c, axis=0, keepdims=True)
            total = part if total is None else total + part
        s_ref[...] = jnp.zeros_like(s_ref)
        s_ref[0:1, :] = total
        m_scr[...] = jnp.zeros_like(m_scr)
        dn_scr[...] = jnp.zeros_like(dn_scr)

    for z in range(n_fsdp):
        for p in range(n_two):
            for t in range(3):
                at, to = pl.ds(z * high + t * tall, tall), pl.ds(p * third, third)
                wg_scr[at, to] = gu_ref[z, p, 0, :, t * third : (t + 1) * third]
                wu_scr[at, to] = gu_ref[z, p, 1, :, t * third : (t + 1) * third]
    wg, wu = wg_scr[...], wu_scr[...]
    wd = wd_ref[...].reshape(-1, wd_ref.shape[-1])
    for at in spans:
        n = n_scr[at, :]
        u = nn(n, wg)
        w = nn(n, wu)
        dhid = nt(t_ref[at, :], wd)
        square = u * u
        th = jnp.tanh(GELU_C * u * (1.0 + GELU_A * square))
        half = 0.5 * (1.0 + th)
        gel = u * half
        slope = half + 0.5 * u * (1.0 - th * th) * (GELU_C * (1.0 + 3.0 * GELU_A * square))
        hid = (gel * w).astype(BF)
        du = (dhid * w * slope).astype(BF)
        dw = (dhid * gel).astype(BF)
        hid_scr[at, :] = hid
        du_scr[at, :] = du
        dw_scr[at, :] = dw
        m_scr[at, :] += nn(hid, wd)
        dn_scr[at, :] += nt(du, wg) + nt(dw, wu)

    slot = lax.rem(j, 2)

    def copies(step_of, slot_of):
        return (
            pltpu.make_async_copy(
                gu_out.at[slot_of],
                g_out.at[:, pl.ds(step_of * n_two, n_two), pl.ds(0, 2)],
                sems.at[slot_of, 0],
            ),
            pltpu.make_async_copy(d_out.at[slot_of], g_out.at[step_of, :, 2], sems.at[slot_of, 1]),
        )

    @pl.when(j >= 2)
    def _():
        for copy in copies(j - 2, slot):
            copy.wait()

    d_out[slot] = tn(hid_scr[...], t_ref[...]).astype(BF).reshape(d_out.shape[1:])
    for side, source in ((0, du_scr), (1, dw_scr)):
        grad = tn(n_scr[...], source[...]).astype(BF)
        for z in range(n_fsdp):
            for p in range(n_two):
                for t in range(3):
                    gu_out[slot, z, p, side, :, t * third : (t + 1) * third] = grad[
                        z * high + t * tall : z * high + (t + 1) * tall,
                        p * third : (p + 1) * third,
                    ]
    for copy in copies(j, slot):
        copy.start()

    @pl.when(j == last)
    def _():
        total = gains = None
        for at in spans:
            h = h_scr[at, :]
            y = h + m_scr[at, :]
            y_ref[at, :] = y.astype(BF)
            dh, dg = norm_back(h, gain, dn_scr[at, :])
            dh = dh + t_ref[at, :].astype(F32)
            dh_ref[at, :] = dh
            dc = dh.astype(BF)
            dc_ref[at, :] = dc
            do_ref[at, :] = nt(dc, wc_ref[...]).astype(BF)
            part = jnp.sum(y * y, axis=0, keepdims=True)
            total = part if total is None else total + part
            gains = dg if gains is None else gains + dg
        s_ref[1:2, :] = total
        s_ref[2:3, :] = gains
        for copy in copies(j - 1, 1 - slot) + copies(j, slot):
            copy.wait()


def feed_forward(o, h1, w2, gain, cot, w3):
    rows, dim = o.shape
    n_fsdp, n_plane, _, tall, _ = w3.shape
    steps = n_fsdp
    two = n_plane // steps
    width = two * 256
    whole = lambda j: (0, 0)
    once = pl.Buffered(1)
    full = pl.BlockSpec((rows, dim), whole, pipeline_mode=once)
    flops = 18 * rows * dim * width * steps + 6 * rows * dim * dim
    return pl.pallas_call(
        mlp_kernel,
        grid=(steps,),
        in_specs=[
            full,
            full,
            pl.BlockSpec((dim, dim), lambda j: (0, 4), pipeline_mode=once),
            pl.BlockSpec((1, dim), whole),
            full,
            pl.BlockSpec((n_fsdp, two, 2, tall, dim), lambda j: (0, j, 0, 0, 0)),
            pl.BlockSpec((1, n_plane, 1, tall, dim), lambda j: (j, 0, 2, 0, 0)),
        ],
        out_specs=[
            full,
            full,
            full,
            full,
            pl.BlockSpec((8, dim), whole),
            pl.BlockSpec(memory_space=pl.ANY),
        ],
        out_shape=[
            jax.ShapeDtypeStruct((rows, dim), BF),
            jax.ShapeDtypeStruct((rows, dim), F32),
            jax.ShapeDtypeStruct((rows, dim), BF),
            jax.ShapeDtypeStruct((rows, dim), BF),
            jax.ShapeDtypeStruct((8, dim), F32),
            jax.ShapeDtypeStruct(w3.shape, BF),
        ],
        scratch_shapes=[
            pltpu.VMEM((rows, dim), BF),
            pltpu.VMEM((rows, dim), F32),
            pltpu.VMEM((rows, dim), F32),
            pltpu.VMEM((rows, dim), F32),
            pltpu.VMEM((rows, width), BF),
            pltpu.VMEM((rows, width), BF),
            pltpu.VMEM((rows, width), BF),
            pltpu.VMEM((dim, width), BF),
            pltpu.VMEM((dim, width), BF),
            pltpu.VMEM((2, n_fsdp, two, 2, tall, dim), BF),
            pltpu.VMEM((2, n_plane, tall, dim), BF),
            pltpu.SemaphoreType.DMA((2, 2)),
        ],
        compiler_params=params(),
        cost_estimate=cost(flops, 40 * MIB, rows * width * steps),
        name="feed_forward",
    )(o, h1, w2, gain, cot, w3, w3)


def placed(me_ref, near_ref, far_ref, size):
    core, x = me_ref[0], me_ref[1]
    for c, ref in enumerate((near_ref, far_ref)):
        for a in range(2):
            yield ref.at[a], pl.multiple_of(((a ^ x) * 2 + (c ^ core)) * size, 16)


def unpack_kernel(me_ref, near_ref, far_ref, gate_ref, up_ref, down_ref):
    core, x = me_ref[0], me_ref[1]
    tall = near_ref.shape[3]
    third = 256
    for c in range(2):
        for a in range(2):
            for i in range(2):
                p = a * 4 + c * 2 + i
                piece = lambda k: jnp.where(
                    core == c, near_ref[a ^ x, i, k], far_ref[a ^ x, i, k]
                ).astype(F32)
                gate, up = piece(0), piece(1)
                for t in range(3):
                    at, to = pl.ds(t * tall, tall), pl.ds(p * third, third)
                    gate_ref[at, to] = gate[:, t * third : (t + 1) * third]
                    up_ref[at, to] = up[:, t * third : (t + 1) * third]
                down_ref[pl.ds(p * tall, tall), :] = piece(2)


def settle_mid_kernel(me_ref, near_ref, far_ref, *outs):
    dim = outs[0].shape[1]
    size = near_ref.shape[1]
    for ref, row in placed(me_ref, near_ref, far_ref, size):
        for m, out in enumerate(outs):
            out[pl.ds(row, size), :] = ref[:, m * dim : (m + 1) * dim].astype(F32)


def settle_qkv_kernel(
    me_ref, near_ref, far_ref, q_ref, k_ref, v_ref, self_ref, mlp_ref, cross_ref, rms_ref, tail_ref,
    *, entries,
):
    place = me_ref[2]
    size = near_ref.shape[2]
    width = q_ref.shape[1] // 2
    for ref, row in placed(me_ref, near_ref, far_ref, size):
        at = pl.ds(row, size)
        tail = None
        for i in range(2):
            block = ref[i ^ place].astype(F32)
            for t, out in enumerate((q_ref, k_ref, v_ref)):
                out[at, i * width : (i + 1) * width] = block[:, t * width : (t + 1) * width]
            part = block[:, 3 * width :]
            tail = part if tail is None else tail + part
        tail_ref[at, :] = tail
    rms_ref[...] = jnp.sqrt(pltpu.roll(tail_ref[0:8, :], 128 - 3, 1)[0:1, :4] / entries)
    turned_tail = tail_ref[...].T
    for i, ref in enumerate((self_ref, mlp_ref, cross_ref)):
        ref[...] = turned_tail[i : i + 1, :]


def settle(kernel, me, near, far, shapes, scratch=(), **given):
    vmem = pl.BlockSpec(memory_space=pltpu.VMEM)
    return pl.pallas_call(
        functools.partial(kernel, **given),
        in_specs=[pl.BlockSpec(memory_space=pltpu.SMEM), vmem, vmem],
        out_specs=[vmem] * len(shapes),
        out_shape=[jax.ShapeDtypeStruct(shape, F32) for shape in shapes],
        scratch_shapes=scratch,
        compiler_params=params(),
        name=kernel.__name__[:-7],
    )(me, near, far)


def deal_rows(core, full, send_ref, keep_ref):
    count, size = send_ref.shape[:2]
    for i in range(count):
        for ref, c in ((send_ref, 1 - core), (keep_ref, core)):
            ref[i] = full[pl.ds(pl.multiple_of((2 * i + c) * size, 16), size), :]


def mid_grads_kernel(turn_ref, *refs, count):
    n_in = count + 9
    sources = refs[:n_in]
    wk_ref, wv_ref, g_ref, far_out = refs[n_in : n_in + 4]
    buffers = refs[n_in + 4 : 2 * n_in + 4]
    sems = refs[-1]
    m = pl.program_id(0)
    dim = g_ref.shape[0]
    copies = [
        pltpu.make_async_copy(
            source.at[pl.ds(0, buffer.shape[0])] if source.shape != buffer.shape else source,
            buffer,
            sems.at[i],
        )
        for i, (source, buffer) in enumerate(zip(sources, buffers))
    ]
    n2, dq, da, *o_pieces, own, far, dk, dv, o2, dc = buffers
    ours = own.shape[0]
    width = o_pieces[0].shape[1]

    @pl.when(m == 0)
    def _():
        for copy in copies:
            copy.start()
        for copy in copies[:2]:
            copy.wait()
        g_ref[...] = tn(n2[...], dq[...]).astype(BF)

    @pl.when(m == 1)
    def _():
        for copy in copies[2 : 3 + count]:
            copy.wait()
        for i in range(count):
            base = pl.multiple_of(turn_ref[i] * width, width)
            term = tn(o_pieces[i][...], da[...]).astype(BF)

            @pl.when(base < dim)
            def _():
                g_ref[pl.ds(base, width), :] = term

    for at, right, first in ((2, dk, 3), (3, dv, 6)):

        @pl.when(m == at)
        def _():
            for copy in copies[count + first : count + 6 if at == 2 else count + 7]:
                copy.wait()
            g_ref[...] = (tn(own[...], right[:ours, :]) + tn(far[...], right[ours:, :])).astype(BF)

    @pl.when(m == 4)
    def _():
        for copy in copies[count + 7 :]:
            copy.wait()
        g_ref[...] = tn(o2[...], dc[...]).astype(BF)

    block = far_out.shape[0]

    @pl.when(m >= 5)
    def _():
        at = pl.ds(pl.multiple_of(ours + (m - 5) * block, block), block)
        far_out[...] = (nt(dk[at, :], wk_ref[...]) + nt(dv[at, :], wv_ref[...])).astype(BF)


def dealt_out(dim, block, total, index, deal):
    if not deal:
        return [pl.BlockSpec((dim, block), lambda *a: (0, index(*a)))], [
            jax.ShapeDtypeStruct((dim, total), BF)
        ]
    spec = pl.BlockSpec((8, dim // 16, block), lambda *a: (0, 0, index(*a)))
    return [spec] * 2, [jax.ShapeDtypeStruct((8, dim // 16, total), BF)] * 2


def mid_grads(turn, pieces, da, n2, dq2, own, far, dk2, dv2, o2, dc, w2):
    rows, dim = n2.shape
    args = (n2, dq2, da, *pieces, own, far, dk2, dv2, o2, dc)
    shapes = [(rows, a.shape[1]) for a in args[: 3 + len(pieces)]]
    shapes += [a.shape for a in args[3 + len(pieces) :]]
    flops = 2 * dim * dim * (3 * rows + 2 * dk2.shape[0] + 2 * far.shape[0])
    block = min(512, own.shape[0])
    far_blocks = far.shape[0] // block
    once = pl.Buffered(1)
    column = lambda m, t: (0, jnp.where(m < 2, 1 - m, jnp.minimum(m, 4)))
    return pl.pallas_call(
        functools.partial(mid_grads_kernel, count=len(pieces)),
        grid_spec=pltpu.PrefetchScalarGridSpec(
            num_scalar_prefetch=1,
            grid=(5 + far_blocks,),
            in_specs=[pl.BlockSpec(memory_space=pl.ANY)] * len(args)
            + [
                pl.BlockSpec((dim, dim), lambda m, t: (0, 2), pipeline_mode=once),
                pl.BlockSpec((dim, dim), lambda m, t: (0, 3), pipeline_mode=once),
            ],
            out_specs=[
                pl.BlockSpec((dim, dim), column),
                pl.BlockSpec((block, dim), lambda m, t: (jnp.maximum(m - 5, 0), 0)),
            ],
            scratch_shapes=[pltpu.VMEM(shape, BF) for shape in shapes]
            + [pltpu.SemaphoreType.DMA((len(args),))],
        ),
        out_shape=[
            jax.ShapeDtypeStruct((dim, 5 * dim), BF),
            jax.ShapeDtypeStruct(far.shape, BF),
        ],
        compiler_params=params(),
        cost_estimate=cost(flops, 30 * MIB),
        name="mid_grads",
    )(turn, *args, w2, w2)


def enc_finish_kernel(dk_ref, dv_ref, wk_ref, wv_ref, *refs):
    total = nt(dk_ref[...], wk_ref[...]) + nt(dv_ref[...], wv_ref[...])
    for ref in refs[:-1]:
        total = total + ref[...].astype(F32)
    refs[-1][...] = total


def enc_finish(dk, dv, w2, got):
    rows, dim = got[0].shape
    block = min(512, rows)
    row = pl.BlockSpec((block, dim), lambda i: (i, 0))
    return pl.pallas_call(
        enc_finish_kernel,
        grid=(rows // block,),
        in_specs=[
            row,
            row,
            pl.BlockSpec((dim, dim), lambda i: (0, 2)),
            pl.BlockSpec((dim, dim), lambda i: (0, 3)),
        ]
        + [row] * len(got),
        out_specs=row,
        out_shape=jax.ShapeDtypeStruct((rows, dim), F32),
        compiler_params=params(),
        cost_estimate=cost(4 * rows * dim * dim, 12 * rows * dim),
        name="enc_finish",
    )(dk, dv, w2, w2, *got)


def before_self_kernel(turn_ref, dq_ref, wq_ref, h_ref, dh_ref, g_ref, *refs, count):
    w_refs = refs[:count]
    d1_ref, da_ref, s_ref = refs[count : count + 3]
    do_refs = refs[count + 3 :]
    dn = nt(dq_ref[...], wq_ref[...])
    dh, dg = norm_back(h_ref[...], g_ref[...], dn)
    d1 = dh_ref[...] + dh
    d1_ref[...] = d1
    da = d1.astype(BF)
    da_ref[...] = da
    for do_ref, w_ref in zip(do_refs, w_refs):
        do_ref[...] = nt(da, w_ref[...]).astype(BF)

    @pl.when(pl.program_id(0) == 0)
    def _():
        s_ref[...] = jnp.zeros_like(s_ref)

    s_ref[0:1, :] += dg


def before_self(turn, dq, w2, h1, dh2, gain, wo, width):
    rows, dim = dq.shape
    count = turn.shape[0]
    block = min(512, rows)
    line = lambda i, t: (i, 0)
    whole = lambda i, t: (0, 0)
    row = pl.BlockSpec((block, dim), line)
    return pl.pallas_call(
        functools.partial(before_self_kernel, count=count),
        grid_spec=pltpu.PrefetchScalarGridSpec(
            num_scalar_prefetch=1,
            grid=(rows // block,),
            in_specs=[
                row,
                pl.BlockSpec((dim, dim), lambda i, t: (0, 1)),
                row,
                row,
                pl.BlockSpec((1, dim), whole),
            ]
            + turn_specs(count, width, dim),
            out_specs=[row, row, pl.BlockSpec((8, dim), whole)]
            + [pl.BlockSpec((block, width), line)] * count,
        ),
        out_shape=[
            jax.ShapeDtypeStruct((rows, dim), F32),
            jax.ShapeDtypeStruct((rows, dim), BF),
            jax.ShapeDtypeStruct((8, dim), F32),
        ]
        + [jax.ShapeDtypeStruct((rows, width), BF)] * count,
        compiler_params=params(),
        cost_estimate=cost(4 * rows * dim * dim, 18 * rows * dim),
        name="before_self",
    )(turn, dq, w2, h1, dh2, gain, *([wo] * count))


def joined(refs):
    return jnp.concatenate([r[...] for r in refs], axis=1)


def qkv_grads_kernel(core_ref, *refs, count, deal):
    d_refs = refs[:count]
    n_ref, w_ref, gain_ref, one_ref, two_ref, three_ref = refs[count : count + 6]
    outs = refs[count + 6 :]
    acc, full = outs[-2:]
    i = pl.program_id(0)
    term = tn(n_ref[...], joined(d_refs))

    @pl.when(i == 0)
    def _():
        acc[...] = term

    @pl.when(i > 0)
    def _():
        acc[...] += term

    @pl.when(i == pl.num_programs(0) - 1)
    def _():
        width = acc.shape[1]
        grad = acc[...]
        dim = grad.shape[0]
        totals = [
            jnp.broadcast_to(jnp.sum(row, axis=1, keepdims=True), (1, dim))
            for row in (one_ref[0:1, :], one_ref[1:2, :], two_ref[0:1, :], two_ref[1:2, :])
        ]
        lines = [gain_ref[...], two_ref[2:3, :], three_ref[0:1, :], *totals]
        lines.append(jnp.zeros((128 - len(lines), dim), F32))
        extra = jnp.concatenate(lines, axis=0).T
        gains = jnp.sum(grad * w_ref[...].astype(F32), axis=1, keepdims=True) / extra[:, :1]
        full[:, :width] = grad.astype(BF)
        full[:, width:] = jnp.where(lanes(extra.shape) == 0, gains, extra).astype(BF)
        if deal:
            deal_rows(core_ref[0], full, outs[0], outs[1])
        else:
            outs[0][...] = full[...]


def qkv_grads(core, ds, n, w, gain, stats, deal):
    total, dim = n.shape
    block = min(512, total)
    width = w.shape[1]
    specs, outs = dealt_out(dim, width + 128, width + 128, lambda i, c: 0, deal)
    whole = lambda i, c: (0, 0)
    return pl.pallas_call(
        functools.partial(qkv_grads_kernel, count=len(ds), deal=deal),
        grid_spec=pltpu.PrefetchScalarGridSpec(
            num_scalar_prefetch=1,
            grid=(total // block,),
            in_specs=[pl.BlockSpec((block, width // 3), lambda i, c: (i, 0))] * len(ds)
            + [
                pl.BlockSpec((block, dim), lambda i, c: (i, 0)),
                pl.BlockSpec(w.shape, whole),
                pl.BlockSpec((1, dim), whole),
            ]
            + [pl.BlockSpec((8, dim), whole)] * 3,
            out_specs=specs,
            scratch_shapes=[pltpu.VMEM((dim, width), F32), pltpu.VMEM((dim, width + 128), BF)],
        ),
        out_shape=outs,
        compiler_params=params(),
        cost_estimate=cost(total * dim, total),
        name="qkv_grads",
    )(core, *ds, n, w, gain, *stats)


def qkv_back_kernel(order_ref, *refs, count):
    dn_ref = refs[count + 1]
    dn_ref[...] = nt(joined(refs[:count]), refs[count][...]).astype(dn_ref.dtype)


def qkv_back(order, first, ds, w, rows, dtype, block):
    dim = w.shape[0]
    return pl.pallas_call(
        functools.partial(qkv_back_kernel, count=len(ds)),
        grid_spec=pltpu.PrefetchScalarGridSpec(
            num_scalar_prefetch=1,
            grid=(rows // block,),
            in_specs=[pl.BlockSpec((block, w.shape[1] // 3), lambda i, o: (o[i + first], 0))] * len(ds)
            + [pl.BlockSpec(w.shape, lambda i, o: (0, 0))],
            out_specs=pl.BlockSpec((block, dim), lambda i, o: (i, 0)),
        ),
        out_shape=jax.ShapeDtypeStruct((rows, dim), dtype),
        compiler_params=params(),
        cost_estimate=cost(rows * dim, rows),
        name="qkv_back",
    )(order, *ds, w)


def finish_kernel(x_ref, dh_ref, g_ref, own_ref, *refs):
    dn = own_ref[...]
    for ref in refs[:-1]:
        dn = dn + ref[...].astype(F32)
    dh, _ = norm_back(x_ref[...].astype(F32), g_ref[...], dn)
    refs[-1][...] = dh_ref[...] + dh


def finish(x, dh1, gain, own, got):
    rows, dim = x.shape
    block = min(256, rows)
    row = pl.BlockSpec((block, dim), lambda i: (i, 0))
    return pl.pallas_call(
        finish_kernel,
        grid=(rows // block,),
        in_specs=[row, row, pl.BlockSpec((1, dim), lambda i: (0, 0)), row] + [row] * len(got),
        out_specs=row,
        out_shape=jax.ShapeDtypeStruct((rows, dim), F32),
        compiler_params=params(),
        cost_estimate=cost(10 * rows * dim, 16 * rows * dim),
        name="finish",
    )(x, dh1, gain, own, *got)


def turned(n, k):
    return [(i, (i + k) % n) for i in range(n)]


def rows_of(array, index, count):
    size = array.shape[0] // count
    return lax.dynamic_slice_in_dim(array, index * size, size, 0)


def assemble_kernel(place_ref, near_ref, far_ref, w_ref, gain_ref, g_ref):
    z, core = place_ref[0], place_ref[1]
    count, size = near_ref.shape[0], near_ref.shape[1]
    width = w_ref.shape[1]
    for d in range(count):
        base = lax.rem(z - d + count, count) * (2 * size)
        for ref, half in ((near_ref, core), (far_ref, 1 - core)):
            at = pl.ds(pl.multiple_of(base + half * size, 16), size)
            w_ref[at, :] = ref[d, :, :width]
            g_ref[at, :] = ref[d, :, width:].astype(F32)
    gain_ref[...] = g_ref[...].T[:8, :]


def gather_first(own, z, part, n_fsdp, n_parts):
    size = own.shape[0] // 2
    width = own.shape[1] - 128
    if n_parts % 2 or size % 16:
        full = lax.all_gather(own, "fsdp", axis=0, tiled=True)
        return full[:, :width], full[:, width : width + 8].astype(F32).T
    core = part % 2
    mine = lax.dynamic_slice_in_dim(own, core * size, size, 0)
    near = jnp.stack(
        [mine] + [lax.ppermute(mine, "fsdp", turned(n_fsdp, d)) for d in range(1, n_fsdp)]
    )
    far = lax.ppermute(near, "parts", [(i, i ^ 1) for i in range(n_parts)])
    vmem = pl.BlockSpec(memory_space=pltpu.VMEM)
    total = n_fsdp * own.shape[0]
    return pl.pallas_call(
        assemble_kernel,
        in_specs=[pl.BlockSpec(memory_space=pltpu.SMEM), vmem, vmem],
        out_specs=[vmem, vmem],
        out_shape=[
            jax.ShapeDtypeStruct((total, width), BF),
            jax.ShapeDtypeStruct((8, total), F32),
        ],
        scratch_shapes=[pltpu.VMEM((total, 128), F32)],
        compiler_params=params(),
        name="assemble",
    )(jnp.stack([z, core]).astype(jnp.int32), near, far)


def pick(array, index, axis):
    return lax.dynamic_index_in_dim(array, index, axis, keepdims=False)


class Plane:
    def __init__(self, part, place, z, n_parts, n_fsdp):
        self.core, self.x, self.place, self.z = part % 2, part // 2, place, z
        self.n_fsdp = n_fsdp
        self.swap_core = [(i, i ^ 1) for i in range(n_parts)]
        self.swap_x = [(i, i ^ 2) for i in range(n_parts)]

    def over_core(self, send, keep):
        shape = (self.n_fsdp, 2) + send.shape[1:]
        got = lax.ppermute(send, "parts", self.swap_core).reshape(shape)
        keep = keep.reshape(shape)
        add = lambda i: (pick(keep, i, 1).astype(F32) + pick(got, i, 1).astype(F32)).astype(BF)
        return add(1 - self.x), add(self.x)

    def over_x(self, send, keep):
        got = lax.ppermute(send, "parts", self.swap_x)
        return (keep.astype(F32) + got.astype(F32)).astype(BF)

    def over_fsdp(self, g):
        total = pick(g, self.z, 0).astype(F32)
        for d in range(1, self.n_fsdp):
            piece = pick(g, (self.z + d) % self.n_fsdp, 0)
            total = total + lax.ppermute(piece, "fsdp", turned(self.n_fsdp, d)).astype(F32)
        return total.astype(BF)

    def over_ctx(self, g):
        return (g.astype(F32) + lax.ppermute(g, "ctx", turned(2, 1)).astype(F32)).astype(BF)

    def widen_ctx(self, g):
        return jnp.stack([g, lax.ppermute(g, "ctx", turned(2, 1))])

    def widen_x(self, g):
        return jnp.stack([g, lax.ppermute(g, "parts", self.swap_x)])

    def from_core(self, g):
        return lax.ppermute(g, "parts", self.swap_core)


def local(
    mesh_shape,
    decoder_in,
    encoder_out,
    segment_ids,
    block_order,
    prompt_len,
    self_query,
    self_key,
    self_value,
    self_output,
    cross_query,
    cross_key,
    cross_value,
    cross_output,
    gate_in,
    up_in,
    down_out,
    norm_self,
    norm_cross,
    norm_mlp,
    cotangent,
):
    n_parts, n_ctx, n_fsdp = mesh_shape
    part, place, z = lax.axis_index("parts"), lax.axis_index("ctx"), lax.axis_index("fsdp")
    plane, n_plane = part * n_ctx + place, n_parts * n_ctx
    x_own, enc_own = decoder_in[0], encoder_out[0]
    rows, dim = x_own.shape
    segs, order = segment_ids[0], block_order[0]
    total = segs.shape[0]
    slots_total = order.shape[0]
    block = total // slots_total
    per_dev = slots_total // n_ctx
    enc_rows = enc_own.shape[0]
    keys = enc_rows * n_ctx
    hidden = down_out.shape[0] * n_fsdp
    heads_here = 2 * -(-HEADS // (2 * n_ctx))
    width = heads_here * HEAD
    padded = width * n_ctx

    ring = (place + jnp.arange(n_ctx, dtype=jnp.int32)) % n_ctx
    order_here = jnp.roll(order, -per_dev * place)
    slots = jnp.argsort(order_here).astype(jnp.int32)
    counts = needed_blocks(segs, block)

    def from_ctx(value):
        pieces = [lax.ppermute(value, "ctx", turned(n_ctx, -k)) for k in range(1, n_ctx)]
        return pieces[0] if n_ctx == 2 else jnp.concatenate(pieces, axis=0)

    x_far = from_ctx(x_own)

    fast = (n_parts, n_ctx, n_fsdp) == (4, 2, 4)
    shard = dim // n_fsdp

    def own_heads(w):
        w = jnp.pad(w, ((0, 0), (0, padded - dim)))
        return lax.dynamic_slice_in_dim(w, place * width, width, 1)

    gain_cols = jnp.pad(jnp.stack([norm_self, norm_cross, norm_mlp], axis=1), ((0, 0), (0, 125)))
    first = jnp.concatenate(
        [own_heads(self_query), own_heads(self_key), own_heads(self_value), gain_cols], axis=1
    )
    w1, gains = gather_first(first, z, part, n_fsdp, n_parts)
    gain_self, gain_cross, gain_mlp = (gains[i : i + 1] for i in range(3))
    mats = (self_output, cross_query, cross_key, cross_value, cross_output)
    if fast:
        w2 = lax.all_gather(
            jnp.concatenate([rows_of(w, part, n_parts) for w in mats], axis=1),
            AROUND, axis=0, tiled=True,
        )

        def column_pieces(w):
            cut = lax.dynamic_slice_in_dim(w, part * 512, 512, 1).reshape(3, 64, 2, 256)
            return cut.transpose(2, 1, 0, 3).reshape(2, 64, dim)

        w3 = lax.all_gather(
            jnp.stack(
                [
                    column_pieces(gate_in),
                    column_pieces(up_in),
                    rows_of(down_out, part, n_parts).reshape(2, 64, dim),
                ],
                axis=1,
            ).reshape(-1, dim),
            AROUND, axis=0, tiled=True,
        ).reshape(PIECES + (dim,))
    else:
        w2 = lax.all_gather(jnp.concatenate(mats, axis=1), "fsdp", axis=0, tiled=True)

        def packed(w):
            w = lax.all_gather(w, "fsdp", axis=0, tiled=True).reshape(4, 3, 64, 8, 256)
            return w.transpose(0, 3, 2, 1, 4).reshape(4, 8, 64, dim)

        w_down = lax.all_gather(down_out, "fsdp", axis=0, tiled=True).reshape(4, 8, 64, dim)
        w3 = jnp.stack([packed(gate_in), packed(up_in), w_down], axis=2)
    x_far, enc_sent = lax.optimization_barrier((x_far, enc_own))
    enc_far = from_ctx(enc_sent)

    n1, q, k, v = qkv_forward(order_here, x_own, x_far, gain_self, w1, block)
    spot = jnp.arange(128, dtype=jnp.int32)[None, :] % HEAD
    minus = jnp.where((spot >= PART0) & (spot < PART0 + 3), -1.0, 0.0)
    seg_q = jnp.where(spot == segs[:, None], 1.0, 0.0).astype(BF)
    seg_k = jnp.where((spot < SEGS) & (spot != segs[:, None]), -BIG, minus).astype(BF)
    o1, lse1 = self_forward(counts, slots, q, k, v, seg_q, seg_k, block)
    pieces = [o1] + [
        lax.ppermute(o1[i * rows : (i + 1) * rows], "ctx", turned(n_ctx, i)) for i in range(1, n_ctx)
    ]
    turn = (place - jnp.arange(n_ctx, dtype=jnp.int32)) % n_ctx
    wo = w2 if padded == dim else jnp.pad(w2[:, :dim], ((0, padded - dim), (0, 0)))
    kv2 = enc_forward(enc_own, enc_far, w2)
    pieces[1], kv2 = lax.optimization_barrier((pieces[1], kv2))
    h1, n2, q2, stat1 = after_self(turn, x_own, pieces, wo, gain_cross, w2)

    where_key = (ring[:, None] * enc_rows + jnp.arange(enc_rows, dtype=jnp.int32)).reshape(-1, 1)
    len_q = jnp.where(spot == 0, jnp.ones((rows, 1), F32), 0.0).astype(BF)
    len_k = jnp.where((spot == 0) & (where_key >= prompt_len[0]), -BIG, minus).astype(BF)
    o2, inv2, p2 = cross_forward(q2, kv2, len_q, len_k)

    layer_out, dh2, dc, do2, stat2, g_ff = feed_forward(o2, h1, w2, gain_mlp, cotangent[0], w3)
    if fast:
        part_ff = lax.psum_scatter(
            g_ff.reshape(-1, dim), AROUND, scatter_dimension=0, tiled=True
        ).reshape(2, 3, 64, dim)

    dq2, dk2, dv2 = cross_backward(q2, kv2, do2, o2, inv2, p2)
    dh1, da, stat3, *do1 = before_self(turn, dq2, w2, h1, dh2, gain_cross, wo, width)
    do_far = [lax.ppermute(do1[i], "ctx", turned(n_ctx, -i)) for i in range(1, n_ctx)]
    do_far = do_far[0] if n_ctx == 2 else jnp.concatenate(do_far, axis=0)
    do_own = do1[0]
    core = jnp.reshape(part % 2, (1,)).astype(jnp.int32)
    g_mid, d_far = mid_grads(
        turn, pieces, da, n2, dq2, enc_own, enc_far, dk2, dv2, o2, dc, w2
    )

    entries = float(n_parts * n_ctx * n_fsdp * rows * dim)

    if fast:
        net = Plane(part, place, z, n_parts, n_fsdp)
        do_own, do_far, d_far, g_mid, part_ff = lax.optimization_barrier(
            (do_own, do_far, d_far, g_mid, part_ff)
        )
        part_mid = lax.psum_scatter(g_mid, AROUND, scatter_dimension=0, tiled=True)
        sum_ff = net.over_ctx(part_ff)
    enc_got = [
        lax.ppermute(d_far[(i - 1) * enc_rows : i * enc_rows], "ctx", turned(n_ctx, i))
        for i in range(1, n_ctx)
    ]
    ds = self_backward(counts, slots, q, k, v, do_own, do_far, o1, lse1, seg_q, seg_k, block)
    if fast:
        ds, sum_ff, enc_got = lax.optimization_barrier((ds, sum_ff, enc_got))
    g_qkv = qkv_grads(core, ds, n1, w1, gain_self, (stat1, stat2, stat3), fast)
    ds, g_qkv = lax.optimization_barrier((ds, g_qkv))
    dn_far = qkv_back(order_here, per_dev, ds, w1, total - rows, BF, block)
    dn_got = [
        lax.ppermute(dn_far[(i - 1) * rows : i * rows], "ctx", turned(n_ctx, i))
        for i in range(1, n_ctx)
    ]
    dn_own = qkv_back(order_here, 0, ds, w1, rows, F32, block)
    enc_grad = enc_finish(dk2, dv2, w2, enc_got)
    if fast:
        send, keep = net.over_core(*g_qkv)
        send, keep, dn_far = lax.optimization_barrier((send, keep, dn_far))
        sum_ff = net.widen_x(sum_ff)
        g_qkv, enc_grad = lax.optimization_barrier((net.over_x(send, keep), enc_grad))
        g_qkv = net.over_fsdp(g_qkv)
        dn_got, part_mid, dn_own = lax.optimization_barrier((dn_got, part_mid, dn_own))
        g_qkv, part_mid = lax.optimization_barrier((g_qkv, part_mid))
    decoder_grad = finish(x_own, dh1, gain_self, dn_own, dn_got)

    if fast:
        me = jnp.stack([net.core, net.x, place]).astype(jnp.int32)
        square = (shard, dim)
        ff = settle(
            unpack_kernel, me, sum_ff, net.from_core(sum_ff),
            [(shard, hidden), (shard, hidden), (hidden // n_fsdp, dim)],
        )
        g_qkv, decoder_grad = lax.optimization_barrier((net.widen_ctx(g_qkv), decoder_grad))
        g_qkv, ff = lax.optimization_barrier((net.widen_x(g_qkv), ff))
        grad_gate, grad_up, grad_down = ff
        sum_mid = net.widen_x(net.over_ctx(part_mid))
        *grads_qkv, grad_gself, grad_gmlp, grad_gcross, rms_values = settle(
            settle_qkv_kernel, me, g_qkv, net.from_core(g_qkv),
            [square] * 3 + [(1, shard)] * 3 + [(1, 4)],
            [pltpu.VMEM((shard, 128), F32)], entries=entries,
        )
        mids = settle(settle_mid_kernel, me, sum_mid, net.from_core(sum_mid), [square] * 5)
    else:

        def total_of(g):
            g = lax.psum_scatter(g, "fsdp", scatter_dimension=0, tiled=True).astype(F32)
            return lax.psum(g, ("parts", "ctx"))

        (g_qkv,) = g_qkv
        sum_mid = total_of(g_mid)
        flat = [
            g_ff[:, :, i].reshape(4, 8, 64, 3, 256).transpose(0, 3, 2, 1, 4).reshape(dim, hidden)
            for i in range(2)
        ]
        grad_gate, grad_up = total_of(flat[0]), total_of(flat[1])
        grad_down = total_of(g_ff[:, :, 2].reshape(hidden, dim))
        sum_qkv = lax.psum_scatter(g_qkv, "fsdp", scatter_dimension=0, tiled=True).astype(F32)
        every = lax.all_gather(lax.psum(sum_qkv, "parts"), "ctx", axis=0)
        grads_qkv = [
            jnp.concatenate(
                [every[c, :, i * width : (i + 1) * width] for c in range(n_ctx)], axis=1
            )[:, :dim]
            for i in range(3)
        ]
        tail = jnp.sum(every[:, :, 3 * width :], axis=0)
        mids = [sum_mid[:, i * dim : (i + 1) * dim] for i in range(5)]
        grad_gself, grad_gmlp, grad_gcross = tail[:, 0], tail[:, 1], tail[:, 2]
        rms_values = jnp.sqrt(tail[0, 3:7] / entries)
    return (
        layer_out[None],
        decoder_grad[None],
        enc_grad[None],
        *grads_qkv,
        *mids,
        grad_gate,
        grad_up,
        grad_down,
        grad_gself.reshape(shard),
        grad_gcross.reshape(shard),
        grad_gmlp.reshape(shard),
        rms_values.reshape(4),
    )


def solution(mesh):
    rows3 = P(("parts", "fsdp"), "ctx", None)
    group = P(("parts", "fsdp"), None)
    matrix, vector = P("fsdp", None), P("fsdp")
    shape = tuple(mesh.shape[a] for a in ("parts", "ctx", "fsdp"))
    return jax.shard_map(
        functools.partial(local, shape),
        mesh=mesh,
        in_specs=(rows3, rows3, group, group, P(("parts", "fsdp")))
        + (matrix,) * 11
        + (vector,) * 3
        + (rows3,),
        out_specs=(rows3,) * 3 + (matrix,) * 11 + (vector,) * 3 + (P(),),
        check_vma=False,
    )
```

```python
import functools
import math

import jax
import jax.numpy as jnp
from jax import lax
from jax.experimental import pallas as pl
from jax.experimental.pallas import tpu as pltpu
from jax.sharding import PartitionSpec as P

HEADS = 12
HEAD = 64
SCALE = 0.125
EPS = 1e-06
BIG = 1e30
LN2 = math.log(2.0)
QSCALE = SCALE * math.log2(math.e)
PART0 = 16
SEGS = 16
BF = jnp.bfloat16
F32 = jnp.float32
MIB = 1 << 20
AROUND = ("fsdp", "parts")


def nn(a, b):
    return lax.dot_general(a, b, (((1,), (0,)), ((), ())), preferred_element_type=F32)


def nt(a, b):
    return lax.dot_general(a, b, (((1,), (1,)), ((), ())), preferred_element_type=F32)


def tn(a, b):
    return lax.dot_general(a, b, (((0,), (0,)), ((), ())), preferred_element_type=F32)


def lanes(shape):
    return lax.broadcasted_iota(jnp.int32, shape, len(shape) - 1)


def params(mib=60):
    return pltpu.CompilerParams(vmem_limit_bytes=mib * MIB)


def cost(flops, moved, exps=0):
    return pl.CostEstimate(flops=int(flops), bytes_accessed=int(moved), transcendentals=int(exps))


def rms_scale(h):
    return lax.rsqrt(jnp.mean(h * h, axis=-1, keepdims=True) + EPS)


def norm_back(h, gain, dn):
    r = rms_scale(h)
    t = dn * gain
    hr = h * r
    dh = r * (t - hr * jnp.mean(t * hr, axis=-1, keepdims=True))
    return dh, jnp.sum(dn * hr, axis=0, keepdims=True)


def with_parts(base, value):
    spot = lanes(base.shape) % HEAD
    hi = value.astype(BF)
    rest = value - hi.astype(F32)
    mid = rest.astype(BF)
    low = (rest - mid.astype(F32)).astype(BF)
    return jnp.where(
        spot == PART0, hi, jnp.where(spot == PART0 + 1, mid, jnp.where(spot == PART0 + 2, low, base))
    )


def pair_of(own, other):
    left = lanes(own.shape) < HEAD
    return jnp.where(left, own, other), jnp.where(left, other, own)


CHUNK = 512


def below(s, rows_first):
    r = lax.broadcasted_iota(jnp.int32, s.shape, 0)
    c = lanes(s.shape)
    return jnp.where(c <= r if rows_first else r <= c, s, -BIG)


def lane_max(s):
    return functools.reduce(jnp.maximum, [s[:, c : c + 128] for c in range(0, s.shape[1], 128)])


def sweep(step, lo, full, odd, grain, unroll):
    base = lo
    if odd is not None:

        @pl.when(odd == 1)
        def _():
            step(lo, 0, grain)

        base = lo + odd * grain

    def body(c, carry):
        step(pl.multiple_of(base + c * CHUNK, grain), pl.multiple_of(grain + c * CHUNK, 128), CHUNK)
        return carry

    lax.fori_loop(0, full, body, 0, unroll=unroll)
    return pl.multiple_of(base + full * CHUNK, grain)


def forward_block(
    lo, full, odd, grain, diag, q_ref, qa_ref, kx, vx, o_ref, lse_ref, s_scr, m_scr, a_scr, unroll
):
    q = q_ref[...]
    rows = q.shape[0]
    left = lanes(q.shape) < HEAD
    sides = pair_of(q, qa_ref[...])
    m_scr[...] = jnp.full_like(m_scr, -BIG)
    a_scr[...] = jnp.zeros_like(a_scr)
    last = s_scr.shape[2] - rows

    def scores(key, at, size, start=None):
        live = pl.ds(start or 0, rows - (start or 0))
        for h in range(2):
            s = nt(sides[h][start or 0 :], kx[h, pl.ds(key, size), :])
            s = s if start is None else below(s, True)
            s_scr[h, live, pl.ds(at, size)] = s
            m_scr[h, live, :] = jnp.maximum(m_scr[h, live, :], lane_max(s))

    steps = range(0, rows, grain) if diag else ()
    end = sweep(scores, lo, full, odd, grain, unroll)
    for start in steps:
        scores(end + start, last + start, grain, start)
    tops = [jnp.max(m_scr[h], axis=1, keepdims=True) for h in range(2)]

    def values(key, at, size, start=0):
        live = pl.ds(start, rows - start)
        for h in range(2):
            p = jnp.exp2(s_scr[h, live, pl.ds(at, size)] - tops[h][start:]).astype(BF)
            a_scr[h, live, :] += nn(p, vx[h, pl.ds(key, size), :])

    end = sweep(values, lo, full, odd, grain, unroll)
    for start in steps:
        values(end + start, last + start, grain, start)
    wide = jnp.where(left, a_scr[0], a_scr[1])
    total = jnp.where(left, a_scr[1], a_scr[0])
    o_ref[...] = (wide / pltpu.roll(total, HEAD, 1)).astype(o_ref.dtype)
    lse_ref[...] = jnp.where(left, tops[1], tops[0]) + jnp.log2(total)


def forward_scratch(block, keys):
    return [
        pltpu.VMEM((2, keys, 128), BF),
        pltpu.VMEM((2, keys, 128), BF),
        pltpu.VMEM((2, block, keys + CHUNK), F32),
        pltpu.VMEM((2, block, 128), F32),
        pltpu.VMEM((2, block, 128), F32),
    ]


def backward_scratch(block, keys):
    return (
        [pltpu.VMEM((2, keys, 128), BF)] * 3
        + [pltpu.VMEM((keys, 128), F32)] * 2
        + [pltpu.VMEM((block, 128), F32)]
    )


def forward_prep(k_ref, v_ref, ka_ref, kx, vx):
    kx[0], kx[1] = pair_of(k_ref[...], ka_ref[...])
    v = v_ref[...]
    vx[0], vx[1] = pair_of(v, jnp.ones_like(v))


def backward_prep(k_ref, v_ref, ka_ref, kx, vx, km, dk_acc, dv_acc):
    k, v = k_ref[...], v_ref[...]
    spot = lanes(v.shape) % HEAD
    neg = jnp.where((spot >= PART0) & (spot < PART0 + 3), -1.0, 0.0).astype(BF)
    kx[0], kx[1] = pair_of(k, ka_ref[...])
    vx[0], vx[1] = pair_of(v, neg)
    km[0], km[1] = pair_of(k, jnp.zeros_like(k))
    dk_acc[...] = jnp.zeros_like(dk_acc)
    dv_acc[...] = jnp.zeros_like(dv_acc)


def backward_block(
    lo, full, odd, grain, diag, q, do, o_ref, lse_ref, qa_ref, kx, vx, km,
    dq_ref, dk_acc, dv_acc, dq_acc, unroll,
):
    left = lanes(q.shape) < HEAD
    rows = q.shape[0]
    product = do.astype(F32) * o_ref[...].astype(F32)
    first = jnp.sum(jnp.where(left, product, 0.0), axis=1, keepdims=True)
    second = jnp.sum(jnp.where(left, 0.0, product), axis=1, keepdims=True)
    delta = jnp.where(left, second, first)
    zero = jnp.zeros_like(q)
    qx = pair_of(q, with_parts(qa_ref[...], lse_ref[...]))
    dx = pair_of(do, with_parts(zero, delta))
    qm = pair_of(q, zero)
    dm = pair_of(do, zero)
    dq_acc[...] = jnp.zeros_like(dq_acc)

    def step(key, _, size, start=None):
        at = pl.ds(key, size)
        live = slice(start or 0, rows)
        dq = dk = dv = None
        for h in range(2):
            st = nt(kx[h, at, :], qx[h][live])
            pt = jnp.exp2(st if start is None else below(st, False))
            dp = nt(vx[h, at, :], dx[h][live])
            ds = (pt * dp).astype(BF)
            tv, tk, tq = nn(pt.astype(BF), dm[h][live]), nn(ds, qm[h][live]), tn(ds, km[h, at, :])
            dv = tv if dv is None else dv + tv
            dk = tk if dk is None else dk + tk
            dq = tq if dq is None else dq + tq
        dv_acc[at, :] += dv
        dk_acc[at, :] += dk
        dq_acc[live, :] += dq

    end = sweep(step, lo, full, odd, grain, unroll)
    for start in range(0, rows, grain) if diag else ():
        step(end + start, 0, grain, start)
    dq_ref[...] = (dq_acc[...] * SCALE).astype(dq_ref.dtype)


def cross_forward_kernel(
    q_ref, k_ref, v_ref, qa_ref, ka_ref, o_ref, inv_ref, p_ref, kx, vx, s_scr, m_scr, a_scr
):
    @pl.when(pl.program_id(1) == 0)
    def _():
        forward_prep(k_ref, v_ref, ka_ref, kx, vx)

    q = q_ref[...]
    keys = k_ref.shape[0]
    left = lanes(q.shape) < HEAD
    sides = pair_of(q, qa_ref[...])
    chunks = [pl.ds(c, CHUNK) for c in range(0, keys, CHUNK)]
    m_scr[...] = jnp.full_like(m_scr, -BIG)
    a_scr[...] = jnp.zeros_like(a_scr)
    for at in chunks:
        for h in range(2):
            s = nt(sides[h], kx[h, at, :])
            s_scr[h, :, at] = s
            m_scr[h] = jnp.maximum(m_scr[h], lane_max(s))
    tops = [jnp.max(m_scr[h], axis=1, keepdims=True) for h in range(2)]
    for at in chunks:
        for h in range(2):
            p = jnp.exp2(s_scr[h, :, at] - tops[h]).astype(BF)
            p_ref[:, pl.ds(h * keys + at.start, CHUNK)] = p
            a_scr[h] += nn(p, vx[h, at, :])
    wide = jnp.where(left, a_scr[0], a_scr[1])
    inv = 1.0 / jnp.where(left, a_scr[1], a_scr[0])
    o_ref[...] = (wide * pltpu.roll(inv, HEAD, 1)).astype(o_ref.dtype)
    inv_ref[...] = inv


def cross_forward(q, kv, qa, ka):
    rows, width = q.shape
    keys = kv.shape[0]
    block = min(512, rows)
    pairs = width // 128
    row = pl.BlockSpec((block, 128), lambda h, i: (i, h))
    return pl.pallas_call(
        cross_forward_kernel,
        grid=(pairs, rows // block),
        in_specs=[
            row,
            pl.BlockSpec((keys, 128), lambda h, i: (0, h)),
            pl.BlockSpec((keys, 128), lambda h, i: (0, h + pairs)),
            pl.BlockSpec((block, 128), lambda h, i: (i, 0)),
            pl.BlockSpec((keys, 128), lambda h, i: (0, 0)),
        ],
        out_specs=[row, row, pl.BlockSpec((block, 2 * keys), lambda h, i: (i, h))],
        out_shape=[
            jax.ShapeDtypeStruct((rows, width), BF),
            jax.ShapeDtypeStruct((rows, width), F32),
            jax.ShapeDtypeStruct((rows, 2 * pairs * keys), BF),
        ],
        scratch_shapes=forward_scratch(block, keys),
        compiler_params=params(),
        cost_estimate=cost(16 * rows * keys * width, 8 * rows * width, rows * keys * 12),
        name="cross_forward",
    )(q, kv, kv, qa, ka)


def cross_backward_kernel(
    q_ref, k_ref, v_ref, do_ref, o_ref, inv_ref, p_ref,
    dq_ref, dk_ref, dv_ref, vx, km, dk_acc, dv_acc,
):
    keys = k_ref.shape[0]

    @pl.when(pl.program_id(1) == 0)
    def _():
        k, v = k_ref[...], v_ref[...]
        spot = lanes(v.shape) % HEAD
        neg = jnp.where((spot >= PART0) & (spot < PART0 + 3), -1.0, 0.0).astype(BF)
        vx[0], vx[1] = pair_of(v, neg)
        km[0], km[1] = pair_of(k, jnp.zeros_like(k))
        dk_acc[...] = jnp.zeros_like(dk_acc)
        dv_acc[...] = jnp.zeros_like(dv_acc)

    q, do = q_ref[...], do_ref[...].astype(F32)
    left = lanes(q.shape) < HEAD
    zero = jnp.zeros_like(q)
    inv = inv_ref[...]
    product = do * o_ref[...].astype(F32)
    first = jnp.sum(jnp.where(left, product, 0.0), axis=1, keepdims=True)
    second = jnp.sum(jnp.where(left, 0.0, product), axis=1, keepdims=True)
    delta = jnp.where(left, second, first) * inv
    do = (do * pltpu.roll(inv, HEAD, 1)).astype(BF)
    dx = pair_of(do, with_parts(zero, delta))
    qm = pair_of(q, zero)
    dm = pair_of(do, zero)
    dq = None
    for c in range(0, keys, CHUNK):
        at = pl.ds(c, CHUNK)
        dk = dv = None
        for h in range(2):
            p = p_ref[:, pl.ds(h * keys + c, CHUNK)]
            ds = (p.astype(F32) * nt(dx[h], vx[h, at, :])).astype(BF)
            tv, tk, tq = tn(p, dm[h]), tn(ds, qm[h]), nn(ds, km[h, at, :])
            dv = tv if dv is None else dv + tv
            dk = tk if dk is None else dk + tk
            dq = tq if dq is None else dq + tq
        dv_acc[at, :] += dv
        dk_acc[at, :] += dk
    dq_ref[...] = (dq * SCALE).astype(BF)

    @pl.when(pl.program_id(1) == pl.num_programs(1) - 1)
    def _():
        dk_ref[...] = (dk_acc[...] * LN2).astype(BF)
        dv_ref[...] = dv_acc[...].astype(BF)


def cross_backward(q, kv, do, o, inv, p):
    rows, width = q.shape
    keys = kv.shape[0]
    block = min(512, rows)
    pairs = width // 128
    row = pl.BlockSpec((block, 128), lambda h, i: (i, h))
    col = pl.BlockSpec((keys, 128), lambda h, i: (0, h))
    return pl.pallas_call(
        cross_backward_kernel,
        grid=(pairs, rows // block),
        in_specs=[
            row,
            col,
            pl.BlockSpec((keys, 128), lambda h, i: (0, h + pairs)),
            row,
            row,
            row,
            pl.BlockSpec((block, 2 * keys), lambda h, i: (i, h)),
        ],
        out_specs=[row, col, col],
        out_shape=[
            jax.ShapeDtypeStruct((rows, width), BF),
            jax.ShapeDtypeStruct((keys, width), BF),
            jax.ShapeDtypeStruct((keys, width), BF),
        ],
        scratch_shapes=[pltpu.VMEM((2, keys, 128), BF)] * 2 + [pltpu.VMEM((keys, 128), F32)] * 2,
        compiler_params=params(),
        cost_estimate=cost(32 * rows * keys * width, 12 * rows * width),
        name="cross_backward",
    )(q, kv, kv, do, o, inv, p)


def grain_of(block):
    return min(256, block)


def needed_blocks(segs, block):
    total = segs.shape[0]
    grain = grain_of(block)
    first = segs.reshape(total // block, block)[:, 0]
    start = jnp.sum((segs[None, :] < first[:, None]).astype(jnp.int32), axis=1)
    ends = (jnp.arange(total // block, dtype=jnp.int32) + 1) * block
    return (ends - start // grain * grain) // grain


def self_range(count, i, block):
    grain = grain_of(block)
    before = count - block // grain
    per = CHUNK // grain
    lo = pl.multiple_of((i + 1) * block - count * grain, grain)
    return lo, before // per, before % per, grain


def self_forward_kernel(
    count_ref, slot_ref, q_ref, k_ref, v_ref, qa_ref, ka_ref, o_ref, lse_ref,
    kx, vx, s_scr, m_scr, a_scr,
):
    i = pl.program_id(1)

    @pl.when(i == 0)
    def _():
        forward_prep(k_ref, v_ref, ka_ref, kx, vx)

    forward_block(
        *self_range(count_ref[i], i, q_ref.shape[0]), True, q_ref, qa_ref, kx, vx, o_ref, lse_ref,
        s_scr, m_scr, a_scr, 1,
    )


def self_forward(counts, slots, q, k, v, qa, ka, block):
    total, width = q.shape
    row = pl.BlockSpec((block, 128), lambda h, i, n, s: (i, h))
    col = pl.BlockSpec((total, 128), lambda h, i, n, s: (0, h))
    return pl.pallas_call(
        self_forward_kernel,
        grid_spec=pltpu.PrefetchScalarGridSpec(
            num_scalar_prefetch=2,
            grid=(width // 128, total // block),
            in_specs=[
                row,
                col,
                col,
                pl.BlockSpec((block, 128), lambda h, i, n, s: (i, 0)),
                pl.BlockSpec((total, 128), lambda h, i, n, s: (0, 0)),
            ],
            out_specs=[pl.BlockSpec((block, 128), lambda h, i, n, s: (s[i], h)), row],
            scratch_shapes=forward_scratch(block, total),
        ),
        out_shape=[
            jax.ShapeDtypeStruct((total, width), BF),
            jax.ShapeDtypeStruct((total, width), F32),
        ],
        compiler_params=params(),
        cost_estimate=cost(8 * total * total * width, 8 * total * width, total * total * 3),
        name="self_forward",
    )(counts, slots, q, k, v, qa, ka)


def self_backward_kernel(
    count_ref, slot_ref, q_ref, k_ref, v_ref, own_ref, far_ref, o_ref, lse_ref, qa_ref, ka_ref,
    dq_ref, dk_ref, dv_ref, kx, vx, km, dk_acc, dv_acc, dq_acc, *, per_dev,
):
    i = pl.program_id(1)
    do = jnp.where(slot_ref[i] < per_dev, own_ref[...], far_ref[...])

    @pl.when(i == 0)
    def _():
        backward_prep(k_ref, v_ref, ka_ref, kx, vx, km, dk_acc, dv_acc)

    backward_block(
        *self_range(count_ref[i], i, q_ref.shape[0]), True, q_ref[...], do, o_ref, lse_ref, qa_ref,
        kx, vx, km, dq_ref, dk_acc, dv_acc, dq_acc, 1,
    )

    @pl.when(i == pl.num_programs(1) - 1)
    def _():
        dk_ref[...] = (dk_acc[...] * LN2).astype(BF)
        dv_ref[...] = dv_acc[...].astype(BF)


def self_backward(counts, slots, q, k, v, own, far, o, lse, qa, ka, block):
    total, width = q.shape
    per_dev = own.shape[0] // block
    row = pl.BlockSpec((block, 128), lambda h, i, n, s: (i, h))
    col = pl.BlockSpec((total, 128), lambda h, i, n, s: (0, h))
    return pl.pallas_call(
        functools.partial(self_backward_kernel, per_dev=per_dev),
        grid_spec=pltpu.PrefetchScalarGridSpec(
            num_scalar_prefetch=2,
            grid=(width // 128, total // block),
            in_specs=[
                row,
                col,
                col,
                pl.BlockSpec((block, 128), lambda h, i, n, s: (jnp.minimum(s[i], per_dev - 1), h)),
                pl.BlockSpec((block, 128), lambda h, i, n, s: (jnp.maximum(s[i] - per_dev, 0), h)),
                pl.BlockSpec((block, 128), lambda h, i, n, s: (s[i], h)),
                row,
                pl.BlockSpec((block, 128), lambda h, i, n, s: (i, 0)),
                pl.BlockSpec((total, 128), lambda h, i, n, s: (0, 0)),
            ],
            out_specs=[row, col, col],
            scratch_shapes=backward_scratch(block, total),
        ),
        out_shape=[jax.ShapeDtypeStruct((total, width), BF)] * 3,
        compiler_params=params(),
        cost_estimate=cost(4 * total * total * width, 2 * total * width),
        name="self_backward",
    )(counts, slots, q, k, v, own, far, o, lse, qa, ka)


def qkv_kernel(order_ref, own_ref, far_ref, g_ref, w_ref, n_ref, q_ref, k_ref, v_ref, *, per_dev):
    x = jnp.where(pl.program_id(0) < per_dev, own_ref[...], far_ref[...]).astype(F32)
    n = (x * rms_scale(x) * g_ref[...]).astype(BF)
    n_ref[...] = n
    width = q_ref.shape[1]
    out = nn(n, w_ref[...])
    q_ref[...] = (out[:, :width] * QSCALE).astype(BF)
    k_ref[...] = out[:, width : 2 * width].astype(BF)
    v_ref[...] = out[:, 2 * width :].astype(BF)


def qkv_forward(order, own, far, gain, w, block):
    dim = own.shape[1]
    total = own.shape[0] + far.shape[0]
    width = w.shape[1] // 3
    per_dev = own.shape[0] // block
    here = lambda i, o: (o[i], 0)
    whole = lambda i, o: (0, 0)
    return pl.pallas_call(
        functools.partial(qkv_kernel, per_dev=per_dev),
        grid_spec=pltpu.PrefetchScalarGridSpec(
            num_scalar_prefetch=1,
            grid=(total // block,),
            in_specs=[
                pl.BlockSpec((block, dim), lambda i, o: (jnp.minimum(i, per_dev - 1), 0)),
                pl.BlockSpec((block, dim), lambda i, o: (jnp.maximum(i - per_dev, 0), 0)),
                pl.BlockSpec((1, dim), whole),
                pl.BlockSpec(w.shape, whole),
            ],
            out_specs=[pl.BlockSpec((block, dim), here)] + [pl.BlockSpec((block, width), here)] * 3,
        ),
        out_shape=[jax.ShapeDtypeStruct((total, dim), BF)]
        + [jax.ShapeDtypeStruct((total, width), BF)] * 3,
        compiler_params=params(),
        cost_estimate=cost(6 * total * dim * width, 8 * total * dim),
        name="qkv_forward",
    )(order, own, far, gain, w)


def enc_kv_kernel(own_ref, far_ref, w_ref, kv_ref, *, own_blocks):
    enc = jnp.where(pl.program_id(0) < own_blocks, own_ref[...], far_ref[...])
    half = w_ref.shape[1] // 2
    for c in range(2):
        at = slice(c * half, (c + 1) * half)
        kv_ref[:, at] = nn(enc, w_ref[:, at]).astype(BF)


def enc_forward(own, far, w2):
    rows, dim = own.shape
    block = min(512, rows)
    keys = rows + far.shape[0]
    ours = rows // block
    return pl.pallas_call(
        functools.partial(enc_kv_kernel, own_blocks=ours),
        grid=(keys // block,),
        in_specs=[
            pl.BlockSpec((block, dim), lambda i: (jnp.minimum(i, ours - 1), 0)),
            pl.BlockSpec((block, dim), lambda i: (jnp.maximum(i - ours, 0), 0)),
            pl.BlockSpec((dim, 2 * dim), lambda i: (0, 1)),
        ],
        out_specs=pl.BlockSpec((block, 2 * dim), lambda i: (i, 0)),
        out_shape=jax.ShapeDtypeStruct((keys, 2 * dim), BF),
        compiler_params=params(),
        cost_estimate=cost(4 * keys * dim * dim, 8 * keys * dim),
        name="enc_forward",
    )(own, far, w2)


def after_self_kernel(turn_ref, x_ref, *refs, count):
    o_refs, w_refs = refs[:count], refs[count : 2 * count]
    g_ref, wq_ref, h_ref, n_ref, q_ref, s_ref = refs[2 * count :]
    x = x_ref[...].astype(F32)
    a = nn(o_refs[0][...], w_refs[0][...])
    for o_ref, w_ref in zip(o_refs[1:], w_refs[1:]):
        a = a + nn(o_ref[...], w_ref[...])
    h = x + a
    h_ref[...] = h
    n = (h * rms_scale(h) * g_ref[...]).astype(BF)
    n_ref[...] = n
    q_ref[...] = (nn(n, wq_ref[...]) * QSCALE).astype(BF)

    @pl.when(pl.program_id(0) == 0)
    def _():
        s_ref[...] = jnp.zeros_like(s_ref)

    s_ref[0:1, :] += jnp.sum(x * x, axis=0, keepdims=True)
    s_ref[1:2, :] += jnp.sum(a * a, axis=0, keepdims=True)


def turn_specs(count, width, dim):
    return [pl.BlockSpec((width, dim), lambda i, t, k=k: (t[k], 0)) for k in range(count)]


def after_self(turn, x, pieces, wo, gain, w2):
    rows, dim = x.shape
    count, width = len(pieces), pieces[0].shape[1]
    block = min(512, rows)
    line = lambda i, t: (i, 0)
    whole = lambda i, t: (0, 0)
    row = pl.BlockSpec((block, dim), line)
    return pl.pallas_call(
        functools.partial(after_self_kernel, count=count),
        grid_spec=pltpu.PrefetchScalarGridSpec(
            num_scalar_prefetch=1,
            grid=(rows // block,),
            in_specs=[row]
            + [pl.BlockSpec((block, width), line)] * count
            + turn_specs(count, width, dim)
            + [pl.BlockSpec((1, dim), whole), pl.BlockSpec((dim, dim), lambda i, t: (0, 1))],
            out_specs=[row, row, row, pl.BlockSpec((8, dim), whole)],
        ),
        out_shape=[
            jax.ShapeDtypeStruct((rows, dim), F32),
            jax.ShapeDtypeStruct((rows, dim), BF),
            jax.ShapeDtypeStruct((rows, dim), BF),
            jax.ShapeDtypeStruct((8, dim), F32),
        ],
        compiler_params=params(),
        cost_estimate=cost(4 * rows * dim * dim, 14 * rows * dim),
        name="after_self",
    )(turn, x, *pieces, *([wo] * count), gain, w2)


GELU_C = math.sqrt(2.0 / math.pi)
GELU_A = 0.044715


PIECES = (4, 8, 3, 64)


def mlp_kernel(
    o_ref, h1_ref, wc_ref, g_ref, t_ref, gu_ref, wd_ref,
    y_ref, dh_ref, dc_ref, do_ref, s_ref, g_out,
    n_scr, h_scr, m_scr, dn_scr, hid_scr, du_scr, dw_scr, wg_scr, wu_scr, gu_out, d_out, sems,
):
    j = pl.program_id(0)
    last = pl.num_programs(0) - 1
    rows = o_ref.shape[0]
    step = min(256, rows)
    spans = [pl.ds(r, step) for r in range(0, rows, step)]
    gain = g_ref[...]
    n_fsdp, n_two, _, tall, _ = gu_ref.shape
    third = 256
    high = 3 * tall

    @pl.when(j == 0)
    def _():
        total = None
        for at in spans:
            c = nn(o_ref[at, :], wc_ref[...])
            h = h1_ref[at, :] + c
            h_scr[at, :] = h
            n_scr[at, :] = (h * rms_scale(h) * gain).astype(BF)
            part = jnp.sum(c * c, axis=0, keepdims=True)
            total = part if total is None else total + part
        s_ref[...] = jnp.zeros_like(s_ref)
        s_ref[0:1, :] = total
        m_scr[...] = jnp.zeros_like(m_scr)
        dn_scr[...] = jnp.zeros_like(dn_scr)

    for z in range(n_fsdp):
        for p in range(n_two):
            for t in range(3):
                at, to = pl.ds(z * high + t * tall, tall), pl.ds(p * third, third)
                wg_scr[at, to] = gu_ref[z, p, 0, :, t * third : (t + 1) * third]
                wu_scr[at, to] = gu_ref[z, p, 1, :, t * third : (t + 1) * third]
    wg, wu = wg_scr[...], wu_scr[...]
    wd = wd_ref[...].reshape(-1, wd_ref.shape[-1])
    for at in spans:
        n = n_scr[at, :]
        u = nn(n, wg)
        w = nn(n, wu)
        dhid = nt(t_ref[at, :], wd)
        square = u * u
        th = jnp.tanh(GELU_C * u * (1.0 + GELU_A * square))
        half = 0.5 * (1.0 + th)
        gel = u * half
        slope = half + 0.5 * u * (1.0 - th * th) * (GELU_C * (1.0 + 3.0 * GELU_A * square))
        hid = (gel * w).astype(BF)
        du = (dhid * w * slope).astype(BF)
        dw = (dhid * gel).astype(BF)
        hid_scr[at, :] = hid
        du_scr[at, :] = du
        dw_scr[at, :] = dw
        m_scr[at, :] += nn(hid, wd)
        dn_scr[at, :] += nt(du, wg) + nt(dw, wu)

    slot = lax.rem(j, 2)

    def copies(step_of, slot_of):
        return (
            pltpu.make_async_copy(
                gu_out.at[slot_of],
                g_out.at[:, pl.ds(step_of * n_two, n_two), pl.ds(0, 2)],
                sems.at[slot_of, 0],
            ),
            pltpu.make_async_copy(d_out.at[slot_of], g_out.at[step_of, :, 2], sems.at[slot_of, 1]),
        )

    @pl.when(j >= 2)
    def _():
        for copy in copies(j - 2, slot):
            copy.wait()

    d_out[slot] = tn(hid_scr[...], t_ref[...]).astype(BF).reshape(d_out.shape[1:])
    for side, source in ((0, du_scr), (1, dw_scr)):
        grad = tn(n_scr[...], source[...]).astype(BF)
        for z in range(n_fsdp):
            for p in range(n_two):
                for t in range(3):
                    gu_out[slot, z, p, side, :, t * third : (t + 1) * third] = grad[
                        z * high + t * tall : z * high + (t + 1) * tall,
                        p * third : (p + 1) * third,
                    ]
    for copy in copies(j, slot):
        copy.start()

    @pl.when(j == last)
    def _():
        total = gains = None
        for at in spans:
            h = h_scr[at, :]
            y = h + m_scr[at, :]
            y_ref[at, :] = y.astype(BF)
            dh, dg = norm_back(h, gain, dn_scr[at, :])
            dh = dh + t_ref[at, :].astype(F32)
            dh_ref[at, :] = dh
            dc = dh.astype(BF)
            dc_ref[at, :] = dc
            do_ref[at, :] = nt(dc, wc_ref[...]).astype(BF)
            part = jnp.sum(y * y, axis=0, keepdims=True)
            total = part if total is None else total + part
            gains = dg if gains is None else gains + dg
        s_ref[1:2, :] = total
        s_ref[2:3, :] = gains
        for copy in copies(j - 1, 1 - slot) + copies(j, slot):
            copy.wait()


def feed_forward(o, h1, w2, gain, cot, w3):
    rows, dim = o.shape
    n_fsdp, n_plane, _, tall, _ = w3.shape
    steps = n_fsdp
    two = n_plane // steps
    width = two * 256
    whole = lambda j: (0, 0)
    once = pl.Buffered(1)
    full = pl.BlockSpec((rows, dim), whole, pipeline_mode=once)
    flops = 18 * rows * dim * width * steps + 6 * rows * dim * dim
    return pl.pallas_call(
        mlp_kernel,
        grid=(steps,),
        in_specs=[
            full,
            full,
            pl.BlockSpec((dim, dim), lambda j: (0, 4), pipeline_mode=once),
            pl.BlockSpec((1, dim), whole),
            full,
            pl.BlockSpec((n_fsdp, two, 2, tall, dim), lambda j: (0, j, 0, 0, 0)),
            pl.BlockSpec((1, n_plane, 1, tall, dim), lambda j: (j, 0, 2, 0, 0)),
        ],
        out_specs=[
            full,
            full,
            full,
            full,
            pl.BlockSpec((8, dim), whole),
            pl.BlockSpec(memory_space=pl.ANY),
        ],
        out_shape=[
            jax.ShapeDtypeStruct((rows, dim), BF),
            jax.ShapeDtypeStruct((rows, dim), F32),
            jax.ShapeDtypeStruct((rows, dim), BF),
            jax.ShapeDtypeStruct((rows, dim), BF),
            jax.ShapeDtypeStruct((8, dim), F32),
            jax.ShapeDtypeStruct(w3.shape, BF),
        ],
        scratch_shapes=[
            pltpu.VMEM((rows, dim), BF),
            pltpu.VMEM((rows, dim), F32),
            pltpu.VMEM((rows, dim), F32),
            pltpu.VMEM((rows, dim), F32),
            pltpu.VMEM((rows, width), BF),
            pltpu.VMEM((rows, width), BF),
            pltpu.VMEM((rows, width), BF),
            pltpu.VMEM((dim, width), BF),
            pltpu.VMEM((dim, width), BF),
            pltpu.VMEM((2, n_fsdp, two, 2, tall, dim), BF),
            pltpu.VMEM((2, n_plane, tall, dim), BF),
            pltpu.SemaphoreType.DMA((2, 2)),
        ],
        compiler_params=params(),
        cost_estimate=cost(flops, 40 * MIB, rows * width * steps),
        name="feed_forward",
    )(o, h1, w2, gain, cot, w3, w3)


def placed(me_ref, near_ref, far_ref, size):
    core, x = me_ref[0], me_ref[1]
    for c, ref in enumerate((near_ref, far_ref)):
        for a in range(2):
            yield ref.at[a], pl.multiple_of(((a ^ x) * 2 + (c ^ core)) * size, 16)


def unpack_kernel(me_ref, near_ref, far_ref, gate_ref, up_ref, down_ref):
    core, x = me_ref[0], me_ref[1]
    tall = near_ref.shape[3]
    third = 256
    for c in range(2):
        for a in range(2):
            for i in range(2):
                p = a * 4 + c * 2 + i
                piece = lambda k: jnp.where(
                    core == c, near_ref[a ^ x, i, k], far_ref[a ^ x, i, k]
                ).astype(F32)
                gate, up = piece(0), piece(1)
                for t in range(3):
                    at, to = pl.ds(t * tall, tall), pl.ds(p * third, third)
                    gate_ref[at, to] = gate[:, t * third : (t + 1) * third]
                    up_ref[at, to] = up[:, t * third : (t + 1) * third]
                down_ref[pl.ds(p * tall, tall), :] = piece(2)


def settle_mid_kernel(me_ref, near_ref, far_ref, *outs):
    dim = outs[0].shape[1]
    size = near_ref.shape[1]
    for ref, row in placed(me_ref, near_ref, far_ref, size):
        for m, out in enumerate(outs):
            out[pl.ds(row, size), :] = ref[:, m * dim : (m + 1) * dim].astype(F32)


def settle_qkv_kernel(
    me_ref, near_ref, far_ref, q_ref, k_ref, v_ref, self_ref, mlp_ref, cross_ref, rms_ref, tail_ref,
    *, entries,
):
    place = me_ref[2]
    size = near_ref.shape[2]
    width = q_ref.shape[1] // 2
    for ref, row in placed(me_ref, near_ref, far_ref, size):
        at = pl.ds(row, size)
        tail = None
        for i in range(2):
            block = ref[i ^ place].astype(F32)
            for t, out in enumerate((q_ref, k_ref, v_ref)):
                out[at, i * width : (i + 1) * width] = block[:, t * width : (t + 1) * width]
            part = block[:, 3 * width :]
            tail = part if tail is None else tail + part
        tail_ref[at, :] = tail
    rms_ref[...] = jnp.sqrt(pltpu.roll(tail_ref[0:8, :], 128 - 3, 1)[0:1, :4] / entries)
    turned_tail = tail_ref[...].T
    for i, ref in enumerate((self_ref, mlp_ref, cross_ref)):
        ref[...] = turned_tail[i : i + 1, :]


def settle(kernel, me, near, far, shapes, scratch=(), **given):
    vmem = pl.BlockSpec(memory_space=pltpu.VMEM)
    return pl.pallas_call(
        functools.partial(kernel, **given),
        in_specs=[pl.BlockSpec(memory_space=pltpu.SMEM), vmem, vmem],
        out_specs=[vmem] * len(shapes),
        out_shape=[jax.ShapeDtypeStruct(shape, F32) for shape in shapes],
        scratch_shapes=scratch,
        compiler_params=params(),
        name=kernel.__name__[:-7],
    )(me, near, far)


def deal_rows(core, full, send_ref, keep_ref):
    count, size = send_ref.shape[:2]
    for i in range(count):
        for ref, c in ((send_ref, 1 - core), (keep_ref, core)):
            ref[i] = full[pl.ds(pl.multiple_of((2 * i + c) * size, 16), size), :]


def mid_grads_kernel(turn_ref, *refs, count):
    n_in = count + 9
    sources = refs[:n_in]
    wk_ref, wv_ref, g_ref, far_out = refs[n_in : n_in + 4]
    buffers = refs[n_in + 4 : 2 * n_in + 4]
    sems = refs[-1]
    m = pl.program_id(0)
    dim = g_ref.shape[0]
    copies = [
        pltpu.make_async_copy(
            source.at[pl.ds(0, buffer.shape[0])] if source.shape != buffer.shape else source,
            buffer,
            sems.at[i],
        )
        for i, (source, buffer) in enumerate(zip(sources, buffers))
    ]
    n2, dq, da, *o_pieces, own, far, dk, dv, o2, dc = buffers
    ours = own.shape[0]
    width = o_pieces[0].shape[1]

    @pl.when(m == 0)
    def _():
        for copy in copies:
            copy.start()
        for copy in copies[:2]:
            copy.wait()
        g_ref[...] = tn(n2[...], dq[...]).astype(BF)

    @pl.when(m == 1)
    def _():
        for copy in copies[2 : 3 + count]:
            copy.wait()
        for i in range(count):
            base = pl.multiple_of(turn_ref[i] * width, width)
            term = tn(o_pieces[i][...], da[...]).astype(BF)

            @pl.when(base < dim)
            def _():
                g_ref[pl.ds(base, width), :] = term

    for at, right, first in ((2, dk, 3), (3, dv, 6)):

        @pl.when(m == at)
        def _():
            for copy in copies[count + first : count + 6 if at == 2 else count + 7]:
                copy.wait()
            g_ref[...] = (tn(own[...], right[:ours, :]) + tn(far[...], right[ours:, :])).astype(BF)

    @pl.when(m == 4)
    def _():
        for copy in copies[count + 7 :]:
            copy.wait()
        g_ref[...] = tn(o2[...], dc[...]).astype(BF)

    block = far_out.shape[0]

    @pl.when(m >= 5)
    def _():
        at = pl.ds(pl.multiple_of(ours + (m - 5) * block, block), block)
        far_out[...] = (nt(dk[at, :], wk_ref[...]) + nt(dv[at, :], wv_ref[...])).astype(BF)


def dealt_out(dim, block, total, index, deal):
    if not deal:
        return [pl.BlockSpec((dim, block), lambda *a: (0, index(*a)))], [
            jax.ShapeDtypeStruct((dim, total), BF)
        ]
    spec = pl.BlockSpec((8, dim // 16, block), lambda *a: (0, 0, index(*a)))
    return [spec] * 2, [jax.ShapeDtypeStruct((8, dim // 16, total), BF)] * 2


def mid_grads(turn, pieces, da, n2, dq2, own, far, dk2, dv2, o2, dc, w2):
    rows, dim = n2.shape
    args = (n2, dq2, da, *pieces, own, far, dk2, dv2, o2, dc)
    shapes = [(rows, a.shape[1]) for a in args[: 3 + len(pieces)]]
    shapes += [a.shape for a in args[3 + len(pieces) :]]
    flops = 2 * dim * dim * (3 * rows + 2 * dk2.shape[0] + 2 * far.shape[0])
    block = min(512, own.shape[0])
    far_blocks = far.shape[0] // block
    once = pl.Buffered(1)
    column = lambda m, t: (0, jnp.where(m < 2, 1 - m, jnp.minimum(m, 4)))
    return pl.pallas_call(
        functools.partial(mid_grads_kernel, count=len(pieces)),
        grid_spec=pltpu.PrefetchScalarGridSpec(
            num_scalar_prefetch=1,
            grid=(5 + far_blocks,),
            in_specs=[pl.BlockSpec(memory_space=pl.ANY)] * len(args)
            + [
                pl.BlockSpec((dim, dim), lambda m, t: (0, 2), pipeline_mode=once),
                pl.BlockSpec((dim, dim), lambda m, t: (0, 3), pipeline_mode=once),
            ],
            out_specs=[
                pl.BlockSpec((dim, dim), column),
                pl.BlockSpec((block, dim), lambda m, t: (jnp.maximum(m - 5, 0), 0)),
            ],
            scratch_shapes=[pltpu.VMEM(shape, BF) for shape in shapes]
            + [pltpu.SemaphoreType.DMA((len(args),))],
        ),
        out_shape=[
            jax.ShapeDtypeStruct((dim, 5 * dim), BF),
            jax.ShapeDtypeStruct(far.shape, BF),
        ],
        compiler_params=params(),
        cost_estimate=cost(flops, 30 * MIB),
        name="mid_grads",
    )(turn, *args, w2, w2)


def enc_finish_kernel(dk_ref, dv_ref, wk_ref, wv_ref, *refs):
    total = nt(dk_ref[...], wk_ref[...]) + nt(dv_ref[...], wv_ref[...])
    for ref in refs[:-1]:
        total = total + ref[...].astype(F32)
    refs[-1][...] = total


def enc_finish(dk, dv, w2, got):
    rows, dim = got[0].shape
    block = min(512, rows)
    row = pl.BlockSpec((block, dim), lambda i: (i, 0))
    return pl.pallas_call(
        enc_finish_kernel,
        grid=(rows // block,),
        in_specs=[
            row,
            row,
            pl.BlockSpec((dim, dim), lambda i: (0, 2)),
            pl.BlockSpec((dim, dim), lambda i: (0, 3)),
        ]
        + [row] * len(got),
        out_specs=row,
        out_shape=jax.ShapeDtypeStruct((rows, dim), F32),
        compiler_params=params(),
        cost_estimate=cost(4 * rows * dim * dim, 12 * rows * dim),
        name="enc_finish",
    )(dk, dv, w2, w2, *got)


def before_self_kernel(turn_ref, dq_ref, wq_ref, h_ref, dh_ref, g_ref, *refs, count):
    w_refs = refs[:count]
    d1_ref, da_ref, s_ref = refs[count : count + 3]
    do_refs = refs[count + 3 :]
    dn = nt(dq_ref[...], wq_ref[...])
    dh, dg = norm_back(h_ref[...], g_ref[...], dn)
    d1 = dh_ref[...] + dh
    d1_ref[...] = d1
    da = d1.astype(BF)
    da_ref[...] = da
    for do_ref, w_ref in zip(do_refs, w_refs):
        do_ref[...] = nt(da, w_ref[...]).astype(BF)

    @pl.when(pl.program_id(0) == 0)
    def _():
        s_ref[...] = jnp.zeros_like(s_ref)

    s_ref[0:1, :] += dg


def before_self(turn, dq, w2, h1, dh2, gain, wo, width):
    rows, dim = dq.shape
    count = turn.shape[0]
    block = min(512, rows)
    line = lambda i, t: (i, 0)
    whole = lambda i, t: (0, 0)
    row = pl.BlockSpec((block, dim), line)
    return pl.pallas_call(
        functools.partial(before_self_kernel, count=count),
        grid_spec=pltpu.PrefetchScalarGridSpec(
            num_scalar_prefetch=1,
            grid=(rows // block,),
            in_specs=[
                row,
                pl.BlockSpec((dim, dim), lambda i, t: (0, 1)),
                row,
                row,
                pl.BlockSpec((1, dim), whole),
            ]
            + turn_specs(count, width, dim),
            out_specs=[row, row, pl.BlockSpec((8, dim), whole)]
            + [pl.BlockSpec((block, width), line)] * count,
        ),
        out_shape=[
            jax.ShapeDtypeStruct((rows, dim), F32),
            jax.ShapeDtypeStruct((rows, dim), BF),
            jax.ShapeDtypeStruct((8, dim), F32),
        ]
        + [jax.ShapeDtypeStruct((rows, width), BF)] * count,
        compiler_params=params(),
        cost_estimate=cost(4 * rows * dim * dim, 18 * rows * dim),
        name="before_self",
    )(turn, dq, w2, h1, dh2, gain, *([wo] * count))


def joined(refs):
    return jnp.concatenate([r[...] for r in refs], axis=1)


def qkv_grads_kernel(core_ref, *refs, count, deal):
    d_refs = refs[:count]
    n_ref, w_ref, gain_ref, one_ref, two_ref, three_ref = refs[count : count + 6]
    outs = refs[count + 6 :]
    acc, full = outs[-2:]
    i = pl.program_id(0)
    term = tn(n_ref[...], joined(d_refs))

    @pl.when(i == 0)
    def _():
        acc[...] = term

    @pl.when(i > 0)
    def _():
        acc[...] += term

    @pl.when(i == pl.num_programs(0) - 1)
    def _():
        width = acc.shape[1]
        grad = acc[...]
        dim = grad.shape[0]
        totals = [
            jnp.broadcast_to(jnp.sum(row, axis=1, keepdims=True), (1, dim))
            for row in (one_ref[0:1, :], one_ref[1:2, :], two_ref[0:1, :], two_ref[1:2, :])
        ]
        lines = [gain_ref[...], two_ref[2:3, :], three_ref[0:1, :], *totals]
        lines.append(jnp.zeros((128 - len(lines), dim), F32))
        extra = jnp.concatenate(lines, axis=0).T
        gains = jnp.sum(grad * w_ref[...].astype(F32), axis=1, keepdims=True) / extra[:, :1]
        full[:, :width] = grad.astype(BF)
        full[:, width:] = jnp.where(lanes(extra.shape) == 0, gains, extra).astype(BF)
        if deal:
            deal_rows(core_ref[0], full, outs[0], outs[1])
        else:
            outs[0][...] = full[...]


def qkv_grads(core, ds, n, w, gain, stats, deal):
    total, dim = n.shape
    block = min(512, total)
    width = w.shape[1]
    specs, outs = dealt_out(dim, width + 128, width + 128, lambda i, c: 0, deal)
    whole = lambda i, c: (0, 0)
    return pl.pallas_call(
        functools.partial(qkv_grads_kernel, count=len(ds), deal=deal),
        grid_spec=pltpu.PrefetchScalarGridSpec(
            num_scalar_prefetch=1,
            grid=(total // block,),
            in_specs=[pl.BlockSpec((block, width // 3), lambda i, c: (i, 0))] * len(ds)
            + [
                pl.BlockSpec((block, dim), lambda i, c: (i, 0)),
                pl.BlockSpec(w.shape, whole),
                pl.BlockSpec((1, dim), whole),
            ]
            + [pl.BlockSpec((8, dim), whole)] * 3,
            out_specs=specs,
            scratch_shapes=[pltpu.VMEM((dim, width), F32), pltpu.VMEM((dim, width + 128), BF)],
        ),
        out_shape=outs,
        compiler_params=params(),
        cost_estimate=cost(total * dim, total),
        name="qkv_grads",
    )(core, *ds, n, w, gain, *stats)


def qkv_back_kernel(order_ref, *refs, count):
    dn_ref = refs[count + 1]
    dn_ref[...] = nt(joined(refs[:count]), refs[count][...]).astype(dn_ref.dtype)


def qkv_back(order, first, ds, w, rows, dtype, block):
    dim = w.shape[0]
    return pl.pallas_call(
        functools.partial(qkv_back_kernel, count=len(ds)),
        grid_spec=pltpu.PrefetchScalarGridSpec(
            num_scalar_prefetch=1,
            grid=(rows // block,),
            in_specs=[pl.BlockSpec((block, w.shape[1] // 3), lambda i, o: (o[i + first], 0))] * len(ds)
            + [pl.BlockSpec(w.shape, lambda i, o: (0, 0))],
            out_specs=pl.BlockSpec((block, dim), lambda i, o: (i, 0)),
        ),
        out_shape=jax.ShapeDtypeStruct((rows, dim), dtype),
        compiler_params=params(),
        cost_estimate=cost(rows * dim, rows),
        name="qkv_back",
    )(order, *ds, w)


def finish_kernel(x_ref, dh_ref, g_ref, own_ref, *refs):
    dn = own_ref[...]
    for ref in refs[:-1]:
        dn = dn + ref[...].astype(F32)
    dh, _ = norm_back(x_ref[...].astype(F32), g_ref[...], dn)
    refs[-1][...] = dh_ref[...] + dh


def finish(x, dh1, gain, own, got):
    rows, dim = x.shape
    block = min(256, rows)
    row = pl.BlockSpec((block, dim), lambda i: (i, 0))
    return pl.pallas_call(
        finish_kernel,
        grid=(rows // block,),
        in_specs=[row, row, pl.BlockSpec((1, dim), lambda i: (0, 0)), row] + [row] * len(got),
        out_specs=row,
        out_shape=jax.ShapeDtypeStruct((rows, dim), F32),
        compiler_params=params(),
        cost_estimate=cost(10 * rows * dim, 16 * rows * dim),
        name="finish",
    )(x, dh1, gain, own, *got)


def turned(n, k):
    return [(i, (i + k) % n) for i in range(n)]


def rows_of(array, index, count):
    size = array.shape[0] // count
    return lax.dynamic_slice_in_dim(array, index * size, size, 0)


def assemble_kernel(place_ref, near_ref, far_ref, w_ref, gain_ref, g_ref):
    z, core = place_ref[0], place_ref[1]
    count, size = near_ref.shape[0], near_ref.shape[1]
    width = w_ref.shape[1]
    for d in range(count):
        base = lax.rem(z - d + count, count) * (2 * size)
        for ref, half in ((near_ref, core), (far_ref, 1 - core)):
            at = pl.ds(pl.multiple_of(base + half * size, 16), size)
            w_ref[at, :] = ref[d, :, :width]
            g_ref[at, :] = ref[d, :, width:].astype(F32)
    gain_ref[...] = g_ref[...].T[:8, :]


def gather_first(own, z, part, n_fsdp, n_parts):
    size = own.shape[0] // 2
    width = own.shape[1] - 128
    if n_parts % 2 or size % 16:
        full = lax.all_gather(own, "fsdp", axis=0, tiled=True)
        return full[:, :width], full[:, width : width + 8].astype(F32).T
    core = part % 2
    mine = lax.dynamic_slice_in_dim(own, core * size, size, 0)
    near = jnp.stack(
        [mine] + [lax.ppermute(mine, "fsdp", turned(n_fsdp, d)) for d in range(1, n_fsdp)]
    )
    far = lax.ppermute(near, "parts", [(i, i ^ 1) for i in range(n_parts)])
    vmem = pl.BlockSpec(memory_space=pltpu.VMEM)
    total = n_fsdp * own.shape[0]
    return pl.pallas_call(
        assemble_kernel,
        in_specs=[pl.BlockSpec(memory_space=pltpu.SMEM), vmem, vmem],
        out_specs=[vmem, vmem],
        out_shape=[
            jax.ShapeDtypeStruct((total, width), BF),
            jax.ShapeDtypeStruct((8, total), F32),
        ],
        scratch_shapes=[pltpu.VMEM((total, 128), F32)],
        compiler_params=params(),
        name="assemble",
    )(jnp.stack([z, core]).astype(jnp.int32), near, far)


def pick(array, index, axis):
    return lax.dynamic_index_in_dim(array, index, axis, keepdims=False)


class Plane:
    def __init__(self, part, place, z, n_parts, n_fsdp):
        self.core, self.x, self.place, self.z = part % 2, part // 2, place, z
        self.n_fsdp = n_fsdp
        self.swap_core = [(i, i ^ 1) for i in range(n_parts)]
        self.swap_x = [(i, i ^ 2) for i in range(n_parts)]

    def over_core(self, send, keep):
        shape = (self.n_fsdp, 2) + send.shape[1:]
        got = lax.ppermute(send, "parts", self.swap_core).reshape(shape)
        keep = keep.reshape(shape)
        add = lambda i: (pick(keep, i, 1).astype(F32) + pick(got, i, 1).astype(F32)).astype(BF)
        return add(1 - self.x), add(self.x)

    def over_x(self, send, keep):
        got = lax.ppermute(send, "parts", self.swap_x)
        return (keep.astype(F32) + got.astype(F32)).astype(BF)

    def from_fsdp(self, g):
        return [pick(g, self.z, 0)] + [
            lax.ppermute(pick(g, (self.z + d) % self.n_fsdp, 0), "fsdp", turned(self.n_fsdp, d))
            for d in range(1, self.n_fsdp)
        ]

    def over_ctx(self, g):
        return (g.astype(F32) + lax.ppermute(g, "ctx", turned(2, 1)).astype(F32)).astype(BF)

    def widen_ctx(self, g):
        return jnp.stack([g, lax.ppermute(g, "ctx", turned(2, 1))])

    def widen_x(self, g):
        return jnp.stack([g, lax.ppermute(g, "parts", self.swap_x)])

    def from_core(self, g):
        return lax.ppermute(g, "parts", self.swap_core)


def local(
    mesh_shape,
    decoder_in,
    encoder_out,
    segment_ids,
    block_order,
    prompt_len,
    self_query,
    self_key,
    self_value,
    self_output,
    cross_query,
    cross_key,
    cross_value,
    cross_output,
    gate_in,
    up_in,
    down_out,
    norm_self,
    norm_cross,
    norm_mlp,
    cotangent,
):
    n_parts, n_ctx, n_fsdp = mesh_shape
    part, place, z = lax.axis_index("parts"), lax.axis_index("ctx"), lax.axis_index("fsdp")
    plane, n_plane = part * n_ctx + place, n_parts * n_ctx
    x_own, enc_own = decoder_in[0], encoder_out[0]
    rows, dim = x_own.shape
    segs, order = segment_ids[0], block_order[0]
    total = segs.shape[0]
    slots_total = order.shape[0]
    block = total // slots_total
    per_dev = slots_total // n_ctx
    enc_rows = enc_own.shape[0]
    keys = enc_rows * n_ctx
    hidden = down_out.shape[0] * n_fsdp
    heads_here = 2 * -(-HEADS // (2 * n_ctx))
    width = heads_here * HEAD
    padded = width * n_ctx

    ring = (place + jnp.arange(n_ctx, dtype=jnp.int32)) % n_ctx
    order_here = jnp.roll(order, -per_dev * place)
    slots = jnp.argsort(order_here).astype(jnp.int32)
    counts = needed_blocks(segs, block)

    def from_ctx(value):
        pieces = [lax.ppermute(value, "ctx", turned(n_ctx, -k)) for k in range(1, n_ctx)]
        return pieces[0] if n_ctx == 2 else jnp.concatenate(pieces, axis=0)

    x_far = from_ctx(x_own)

    fast = (n_parts, n_ctx, n_fsdp) == (4, 2, 4)
    shard = dim // n_fsdp

    def own_heads(w):
        w = jnp.pad(w, ((0, 0), (0, padded - dim)))
        return lax.dynamic_slice_in_dim(w, place * width, width, 1)

    gain_cols = jnp.pad(jnp.stack([norm_self, norm_cross, norm_mlp], axis=1), ((0, 0), (0, 125)))
    first = jnp.concatenate(
        [own_heads(self_query), own_heads(self_key), own_heads(self_value), gain_cols], axis=1
    )
    w1, gains = gather_first(first, z, part, n_fsdp, n_parts)
    gain_self, gain_cross, gain_mlp = (gains[i : i + 1] for i in range(3))
    mats = (self_output, cross_query, cross_key, cross_value, cross_output)
    if fast:
        w2 = lax.all_gather(
            jnp.concatenate([rows_of(w, part, n_parts) for w in mats], axis=1),
            AROUND, axis=0, tiled=True,
        )

        def column_pieces(w):
            cut = lax.dynamic_slice_in_dim(w, part * 512, 512, 1).reshape(3, 64, 2, 256)
            return cut.transpose(2, 1, 0, 3).reshape(2, 64, dim)

        w3 = lax.all_gather(
            jnp.stack(
                [
                    column_pieces(gate_in),
                    column_pieces(up_in),
                    rows_of(down_out, part, n_parts).reshape(2, 64, dim),
                ],
                axis=1,
            ).reshape(-1, dim),
            AROUND, axis=0, tiled=True,
        ).reshape(PIECES + (dim,))
    else:
        w2 = lax.all_gather(jnp.concatenate(mats, axis=1), "fsdp", axis=0, tiled=True)

        def packed(w):
            w = lax.all_gather(w, "fsdp", axis=0, tiled=True).reshape(4, 3, 64, 8, 256)
            return w.transpose(0, 3, 2, 1, 4).reshape(4, 8, 64, dim)

        w_down = lax.all_gather(down_out, "fsdp", axis=0, tiled=True).reshape(4, 8, 64, dim)
        w3 = jnp.stack([packed(gate_in), packed(up_in), w_down], axis=2)
    x_far, enc_sent = lax.optimization_barrier((x_far, enc_own))
    enc_far = from_ctx(enc_sent)

    n1, q, k, v = qkv_forward(order_here, x_own, x_far, gain_self, w1, block)
    spot = jnp.arange(128, dtype=jnp.int32)[None, :] % HEAD
    minus = jnp.where((spot >= PART0) & (spot < PART0 + 3), -1.0, 0.0)
    seg_q = jnp.where(spot == segs[:, None], 1.0, 0.0).astype(BF)
    seg_k = jnp.where((spot < SEGS) & (spot != segs[:, None]), -BIG, minus).astype(BF)
    o1, lse1 = self_forward(counts, slots, q, k, v, seg_q, seg_k, block)
    pieces = [o1] + [
        lax.ppermute(o1[i * rows : (i + 1) * rows], "ctx", turned(n_ctx, i)) for i in range(1, n_ctx)
    ]
    turn = (place - jnp.arange(n_ctx, dtype=jnp.int32)) % n_ctx
    wo = w2 if padded == dim else jnp.pad(w2[:, :dim], ((0, padded - dim), (0, 0)))
    kv2 = enc_forward(enc_own, enc_far, w2)
    pieces[1], kv2 = lax.optimization_barrier((pieces[1], kv2))
    h1, n2, q2, stat1 = after_self(turn, x_own, pieces, wo, gain_cross, w2)

    where_key = (ring[:, None] * enc_rows + jnp.arange(enc_rows, dtype=jnp.int32)).reshape(-1, 1)
    len_q = jnp.where(spot == 0, jnp.ones((rows, 1), F32), 0.0).astype(BF)
    len_k = jnp.where((spot == 0) & (where_key >= prompt_len[0]), -BIG, minus).astype(BF)
    o2, inv2, p2 = cross_forward(q2, kv2, len_q, len_k)

    layer_out, dh2, dc, do2, stat2, g_ff = feed_forward(o2, h1, w2, gain_mlp, cotangent[0], w3)
    if fast:
        part_ff = lax.psum_scatter(
            g_ff.reshape(-1, dim), AROUND, scatter_dimension=0, tiled=True
        ).reshape(2, 3, 64, dim)

    dq2, dk2, dv2 = cross_backward(q2, kv2, do2, o2, inv2, p2)
    dh1, da, stat3, *do1 = before_self(turn, dq2, w2, h1, dh2, gain_cross, wo, width)
    do_far = [lax.ppermute(do1[i], "ctx", turned(n_ctx, -i)) for i in range(1, n_ctx)]
    do_far = do_far[0] if n_ctx == 2 else jnp.concatenate(do_far, axis=0)
    do_own = do1[0]
    core = jnp.reshape(part % 2, (1,)).astype(jnp.int32)
    g_mid, d_far = mid_grads(
        turn, pieces, da, n2, dq2, enc_own, enc_far, dk2, dv2, o2, dc, w2
    )

    entries = float(n_parts * n_ctx * n_fsdp * rows * dim)

    if fast:
        net = Plane(part, place, z, n_parts, n_fsdp)
        do_own, do_far, d_far, g_mid, part_ff = lax.optimization_barrier(
            (do_own, do_far, d_far, g_mid, part_ff)
        )
        part_mid = lax.psum_scatter(g_mid, AROUND, scatter_dimension=0, tiled=True)
        sum_ff = net.over_ctx(part_ff)
    enc_got = [
        lax.ppermute(d_far[(i - 1) * enc_rows : i * enc_rows], "ctx", turned(n_ctx, i))
        for i in range(1, n_ctx)
    ]
    ds = self_backward(counts, slots, q, k, v, do_own, do_far, o1, lse1, seg_q, seg_k, block)
    if fast:
        ds, sum_ff, enc_got = lax.optimization_barrier((ds, sum_ff, enc_got))
    g_qkv = qkv_grads(core, ds, n1, w1, gain_self, (stat1, stat2, stat3), fast)
    ds, g_qkv = lax.optimization_barrier((ds, g_qkv))
    dn_far = qkv_back(order_here, per_dev, ds, w1, total - rows, BF, block)
    dn_got = [
        lax.ppermute(dn_far[(i - 1) * rows : i * rows], "ctx", turned(n_ctx, i))
        for i in range(1, n_ctx)
    ]
    dn_own = qkv_back(order_here, 0, ds, w1, rows, F32, block)
    enc_grad = enc_finish(dk2, dv2, w2, enc_got)
    if fast:
        send, keep = net.over_core(*g_qkv)
        send, keep, dn_far = lax.optimization_barrier((send, keep, dn_far))
        g_qkv, enc_grad, sum_ff, dn_own = lax.optimization_barrier(
            (net.over_x(send, keep), enc_grad, sum_ff, dn_own)
        )
        sum_ff = net.widen_x(sum_ff)
        shares = net.from_fsdp(g_qkv)
        shares[1], part_mid = lax.optimization_barrier((shares[1], part_mid))
        got_mid = lax.ppermute(part_mid, "ctx", turned(2, 1))
        g_qkv = functools.reduce(jnp.add, [share.astype(F32) for share in shares]).astype(BF)
        g_qkv, dn_got, got_mid = lax.optimization_barrier((g_qkv, dn_got, got_mid))
        part_mid = (part_mid.astype(F32) + got_mid.astype(F32)).astype(BF)
    decoder_grad = finish(x_own, dh1, gain_self, dn_own, dn_got)

    if fast:
        me = jnp.stack([net.core, net.x, place]).astype(jnp.int32)
        square = (shard, dim)
        ff = settle(
            unpack_kernel, me, sum_ff, net.from_core(sum_ff),
            [(shard, hidden), (shard, hidden), (hidden // n_fsdp, dim)],
        )
        g_qkv, decoder_grad = lax.optimization_barrier((net.widen_ctx(g_qkv), decoder_grad))
        g_qkv, ff = lax.optimization_barrier((net.widen_x(g_qkv), ff))
        grad_gate, grad_up, grad_down = ff
        sum_mid = net.widen_x(part_mid)
        *grads_qkv, grad_gself, grad_gmlp, grad_gcross, rms_values = settle(
            settle_qkv_kernel, me, g_qkv, net.from_core(g_qkv),
            [square] * 3 + [(1, shard)] * 3 + [(1, 4)],
            [pltpu.VMEM((shard, 128), F32)], entries=entries,
        )
        mids = settle(settle_mid_kernel, me, sum_mid, net.from_core(sum_mid), [square] * 5)
    else:

        def total_of(g):
            g = lax.psum_scatter(g, "fsdp", scatter_dimension=0, tiled=True).astype(F32)
            return lax.psum(g, ("parts", "ctx"))

        (g_qkv,) = g_qkv
        sum_mid = total_of(g_mid)
        flat = [
            g_ff[:, :, i].reshape(4, 8, 64, 3, 256).transpose(0, 3, 2, 1, 4).reshape(dim, hidden)
            for i in range(2)
        ]
        grad_gate, grad_up = total_of(flat[0]), total_of(flat[1])
        grad_down = total_of(g_ff[:, :, 2].reshape(hidden, dim))
        sum_qkv = lax.psum_scatter(g_qkv, "fsdp", scatter_dimension=0, tiled=True).astype(F32)
        every = lax.all_gather(lax.psum(sum_qkv, "parts"), "ctx", axis=0)
        grads_qkv = [
            jnp.concatenate(
                [every[c, :, i * width : (i + 1) * width] for c in range(n_ctx)], axis=1
            )[:, :dim]
            for i in range(3)
        ]
        tail = jnp.sum(every[:, :, 3 * width :], axis=0)
        mids = [sum_mid[:, i * dim : (i + 1) * dim] for i in range(5)]
        grad_gself, grad_gmlp, grad_gcross = tail[:, 0], tail[:, 1], tail[:, 2]
        rms_values = jnp.sqrt(tail[0, 3:7] / entries)
    return (
        layer_out[None],
        decoder_grad[None],
        enc_grad[None],
        *grads_qkv,
        *mids,
        grad_gate,
        grad_up,
        grad_down,
        grad_gself.reshape(shard),
        grad_gcross.reshape(shard),
        grad_gmlp.reshape(shard),
        rms_values.reshape(4),
    )


def solution(mesh):
    rows3 = P(("parts", "fsdp"), "ctx", None)
    group = P(("parts", "fsdp"), None)
    matrix, vector = P("fsdp", None), P("fsdp")
    shape = tuple(mesh.shape[a] for a in ("parts", "ctx", "fsdp"))
    return jax.shard_map(
        functools.partial(local, shape),
        mesh=mesh,
        in_specs=(rows3, rows3, group, group, P(("parts", "fsdp")))
        + (matrix,) * 11
        + (vector,) * 3
        + (rows3,),
        out_specs=(rows3,) * 3 + (matrix,) * 11 + (vector,) * 3 + (P(),),
        check_vma=False,
    )
```

```python
import functools
import math

import jax
import jax.numpy as jnp
from jax import lax
from jax.experimental import pallas as pl
from jax.experimental.pallas import tpu as pltpu
from jax.sharding import PartitionSpec as P

HEADS = 12
HEAD = 64
SCALE = 0.125
EPS = 1e-06
BIG = 1e30
LN2 = math.log(2.0)
QSCALE = SCALE * math.log2(math.e)
PART0 = 16
SEGS = 16
BF = jnp.bfloat16
F32 = jnp.float32
MIB = 1 << 20
AROUND = ("fsdp", "parts")


def nn(a, b):
    return lax.dot_general(a, b, (((1,), (0,)), ((), ())), preferred_element_type=F32)


def nt(a, b):
    return lax.dot_general(a, b, (((1,), (1,)), ((), ())), preferred_element_type=F32)


def tn(a, b):
    return lax.dot_general(a, b, (((0,), (0,)), ((), ())), preferred_element_type=F32)


def lanes(shape):
    return lax.broadcasted_iota(jnp.int32, shape, len(shape) - 1)


def params(mib=60):
    return pltpu.CompilerParams(vmem_limit_bytes=mib * MIB)


def cost(flops, moved, exps=0):
    return pl.CostEstimate(flops=int(flops), bytes_accessed=int(moved), transcendentals=int(exps))


def rms_scale(h):
    return lax.rsqrt(jnp.mean(h * h, axis=-1, keepdims=True) + EPS)


def norm_back(h, gain, dn):
    r = rms_scale(h)
    t = dn * gain
    hr = h * r
    dh = r * (t - hr * jnp.mean(t * hr, axis=-1, keepdims=True))
    return dh, jnp.sum(dn * hr, axis=0, keepdims=True)


def with_parts(base, value):
    spot = lanes(base.shape) % HEAD
    hi = value.astype(BF)
    rest = value - hi.astype(F32)
    mid = rest.astype(BF)
    low = (rest - mid.astype(F32)).astype(BF)
    return jnp.where(
        spot == PART0, hi, jnp.where(spot == PART0 + 1, mid, jnp.where(spot == PART0 + 2, low, base))
    )


def pair_of(own, other):
    left = lanes(own.shape) < HEAD
    return jnp.where(left, own, other), jnp.where(left, other, own)


CHUNK = 512


def below(s, rows_first):
    r = lax.broadcasted_iota(jnp.int32, s.shape, 0)
    c = lanes(s.shape)
    return jnp.where(c <= r if rows_first else r <= c, s, -BIG)


def lane_max(s):
    return functools.reduce(jnp.maximum, [s[:, c : c + 128] for c in range(0, s.shape[1], 128)])


def sweep(step, lo, full, odd, grain, unroll):
    base = lo
    if odd is not None:

        @pl.when(odd == 1)
        def _():
            step(lo, 0, grain)

        base = lo + odd * grain

    def body(c, carry):
        step(pl.multiple_of(base + c * CHUNK, grain), pl.multiple_of(grain + c * CHUNK, 128), CHUNK)
        return carry

    lax.fori_loop(0, full, body, 0, unroll=unroll)
    return pl.multiple_of(base + full * CHUNK, grain)


def forward_block(
    lo, full, odd, grain, diag, q_ref, qa_ref, kx, vx, o_ref, lse_ref, s_scr, m_scr, a_scr, unroll
):
    q = q_ref[...]
    rows = q.shape[0]
    left = lanes(q.shape) < HEAD
    sides = pair_of(q, qa_ref[...])
    m_scr[...] = jnp.full_like(m_scr, -BIG)
    a_scr[...] = jnp.zeros_like(a_scr)
    last = s_scr.shape[2] - rows

    def scores(key, at, size, start=None):
        live = pl.ds(start or 0, rows - (start or 0))
        for h in range(2):
            s = nt(sides[h][start or 0 :], kx[h, pl.ds(key, size), :])
            s = s if start is None else below(s, True)
            s_scr[h, live, pl.ds(at, size)] = s
            m_scr[h, live, :] = jnp.maximum(m_scr[h, live, :], lane_max(s))

    steps = range(0, rows, grain) if diag else ()
    end = sweep(scores, lo, full, odd, grain, unroll)
    for start in steps:
        scores(end + start, last + start, grain, start)
    tops = [jnp.max(m_scr[h], axis=1, keepdims=True) for h in range(2)]

    def values(key, at, size, start=0):
        live = pl.ds(start, rows - start)
        for h in range(2):
            p = jnp.exp2(s_scr[h, live, pl.ds(at, size)] - tops[h][start:]).astype(BF)
            a_scr[h, live, :] += nn(p, vx[h, pl.ds(key, size), :])

    end = sweep(values, lo, full, odd, grain, unroll)
    for start in steps:
        values(end + start, last + start, grain, start)
    wide = jnp.where(left, a_scr[0], a_scr[1])
    total = jnp.where(left, a_scr[1], a_scr[0])
    o_ref[...] = (wide / pltpu.roll(total, HEAD, 1)).astype(o_ref.dtype)
    lse_ref[...] = jnp.where(left, tops[1], tops[0]) + jnp.log2(total)


def forward_scratch(block, keys):
    return [
        pltpu.VMEM((2, keys, 128), BF),
        pltpu.VMEM((2, keys, 128), BF),
        pltpu.VMEM((2, block, keys + CHUNK), F32),
        pltpu.VMEM((2, block, 128), F32),
        pltpu.VMEM((2, block, 128), F32),
    ]


def backward_scratch(block, keys):
    return (
        [pltpu.VMEM((2, keys, 128), BF)] * 3
        + [pltpu.VMEM((keys, 128), F32)] * 2
        + [pltpu.VMEM((block, 128), F32)]
    )


def forward_prep(k_ref, v_ref, ka_ref, kx, vx):
    kx[0], kx[1] = pair_of(k_ref[...], ka_ref[...])
    v = v_ref[...]
    vx[0], vx[1] = pair_of(v, jnp.ones_like(v))


def backward_prep(k_ref, v_ref, ka_ref, kx, vx, km, dk_acc, dv_acc):
    k, v = k_ref[...], v_ref[...]
    spot = lanes(v.shape) % HEAD
    neg = jnp.where((spot >= PART0) & (spot < PART0 + 3), -1.0, 0.0).astype(BF)
    kx[0], kx[1] = pair_of(k, ka_ref[...])
    vx[0], vx[1] = pair_of(v, neg)
    km[0], km[1] = pair_of(k, jnp.zeros_like(k))
    dk_acc[...] = jnp.zeros_like(dk_acc)
    dv_acc[...] = jnp.zeros_like(dv_acc)


def backward_block(
    lo, full, odd, grain, diag, q, do, o_ref, lse_ref, qa_ref, kx, vx, km,
    dq_ref, dk_acc, dv_acc, dq_acc, unroll,
):
    left = lanes(q.shape) < HEAD
    rows = q.shape[0]
    product = do.astype(F32) * o_ref[...].astype(F32)
    first = jnp.sum(jnp.where(left, product, 0.0), axis=1, keepdims=True)
    second = jnp.sum(jnp.where(left, 0.0, product), axis=1, keepdims=True)
    delta = jnp.where(left, second, first)
    zero = jnp.zeros_like(q)
    qx = pair_of(q, with_parts(qa_ref[...], lse_ref[...]))
    dx = pair_of(do, with_parts(zero, delta))
    qm = pair_of(q, zero)
    dm = pair_of(do, zero)
    dq_acc[...] = jnp.zeros_like(dq_acc)

    def step(key, _, size, start=None):
        at = pl.ds(key, size)
        live = slice(start or 0, rows)
        dq = dk = dv = None
        for h in range(2):
            st = nt(kx[h, at, :], qx[h][live])
            pt = jnp.exp2(st if start is None else below(st, False))
            dp = nt(vx[h, at, :], dx[h][live])
            ds = (pt * dp).astype(BF)
            tv, tk, tq = nn(pt.astype(BF), dm[h][live]), nn(ds, qm[h][live]), tn(ds, km[h, at, :])
            dv = tv if dv is None else dv + tv
            dk = tk if dk is None else dk + tk
            dq = tq if dq is None else dq + tq
        dv_acc[at, :] += dv
        dk_acc[at, :] += dk
        dq_acc[live, :] += dq

    end = sweep(step, lo, full, odd, grain, unroll)
    for start in range(0, rows, grain) if diag else ():
        step(end + start, 0, grain, start)
    dq_ref[...] = (dq_acc[...] * SCALE).astype(dq_ref.dtype)


def cross_forward_kernel(
    q_ref, k_ref, v_ref, qa_ref, ka_ref, o_ref, inv_ref, p_ref, kx, vx, s_scr, m_scr, a_scr
):
    @pl.when(pl.program_id(1) == 0)
    def _():
        forward_prep(k_ref, v_ref, ka_ref, kx, vx)

    q = q_ref[...]
    keys = k_ref.shape[0]
    left = lanes(q.shape) < HEAD
    sides = pair_of(q, qa_ref[...])
    chunks = [pl.ds(c, CHUNK) for c in range(0, keys, CHUNK)]
    m_scr[...] = jnp.full_like(m_scr, -BIG)
    a_scr[...] = jnp.zeros_like(a_scr)
    for at in chunks:
        for h in range(2):
            s = nt(sides[h], kx[h, at, :])
            s_scr[h, :, at] = s
            m_scr[h] = jnp.maximum(m_scr[h], lane_max(s))
    tops = [jnp.max(m_scr[h], axis=1, keepdims=True) for h in range(2)]
    for at in chunks:
        for h in range(2):
            p = jnp.exp2(s_scr[h, :, at] - tops[h]).astype(BF)
            p_ref[:, pl.ds(h * keys + at.start, CHUNK)] = p
            a_scr[h] += nn(p, vx[h, at, :])
    wide = jnp.where(left, a_scr[0], a_scr[1])
    inv = 1.0 / jnp.where(left, a_scr[1], a_scr[0])
    o_ref[...] = (wide * pltpu.roll(inv, HEAD, 1)).astype(o_ref.dtype)
    inv_ref[...] = inv


def cross_forward(q, kv, qa, ka):
    rows, width = q.shape
    keys = kv.shape[0]
    block = min(512, rows)
    pairs = width // 128
    row = pl.BlockSpec((block, 128), lambda h, i: (i, h))
    return pl.pallas_call(
        cross_forward_kernel,
        grid=(pairs, rows // block),
        in_specs=[
            row,
            pl.BlockSpec((keys, 128), lambda h, i: (0, h)),
            pl.BlockSpec((keys, 128), lambda h, i: (0, h + pairs)),
            pl.BlockSpec((block, 128), lambda h, i: (i, 0)),
            pl.BlockSpec((keys, 128), lambda h, i: (0, 0)),
        ],
        out_specs=[row, row, pl.BlockSpec((block, 2 * keys), lambda h, i: (i, h))],
        out_shape=[
            jax.ShapeDtypeStruct((rows, width), BF),
            jax.ShapeDtypeStruct((rows, width), F32),
            jax.ShapeDtypeStruct((rows, 2 * pairs * keys), BF),
        ],
        scratch_shapes=forward_scratch(block, keys),
        compiler_params=params(),
        cost_estimate=cost(16 * rows * keys * width, 8 * rows * width, rows * keys * 12),
        name="cross_forward",
    )(q, kv, kv, qa, ka)


def cross_backward_kernel(
    q_ref, k_ref, v_ref, do_ref, o_ref, inv_ref, p_ref,
    dq_ref, dk_ref, dv_ref, vx, km, dk_acc, dv_acc,
):
    keys = k_ref.shape[0]

    @pl.when(pl.program_id(1) == 0)
    def _():
        k, v = k_ref[...], v_ref[...]
        spot = lanes(v.shape) % HEAD
        neg = jnp.where((spot >= PART0) & (spot < PART0 + 3), -1.0, 0.0).astype(BF)
        vx[0], vx[1] = pair_of(v, neg)
        km[0], km[1] = pair_of(k, jnp.zeros_like(k))
        dk_acc[...] = jnp.zeros_like(dk_acc)
        dv_acc[...] = jnp.zeros_like(dv_acc)

    q, do = q_ref[...], do_ref[...].astype(F32)
    left = lanes(q.shape) < HEAD
    zero = jnp.zeros_like(q)
    inv = inv_ref[...]
    product = do * o_ref[...].astype(F32)
    first = jnp.sum(jnp.where(left, product, 0.0), axis=1, keepdims=True)
    second = jnp.sum(jnp.where(left, 0.0, product), axis=1, keepdims=True)
    delta = jnp.where(left, second, first) * inv
    do = (do * pltpu.roll(inv, HEAD, 1)).astype(BF)
    dx = pair_of(do, with_parts(zero, delta))
    qm = pair_of(q, zero)
    dm = pair_of(do, zero)
    dq = None
    for c in range(0, keys, CHUNK):
        at = pl.ds(c, CHUNK)
        dk = dv = None
        for h in range(2):
            p = p_ref[:, pl.ds(h * keys + c, CHUNK)]
            ds = (p.astype(F32) * nt(dx[h], vx[h, at, :])).astype(BF)
            tv, tk, tq = tn(p, dm[h]), tn(ds, qm[h]), nn(ds, km[h, at, :])
            dv = tv if dv is None else dv + tv
            dk = tk if dk is None else dk + tk
            dq = tq if dq is None else dq + tq
        dv_acc[at, :] += dv
        dk_acc[at, :] += dk
    dq_ref[...] = (dq * SCALE).astype(BF)

    @pl.when(pl.program_id(1) == pl.num_programs(1) - 1)
    def _():
        dk_ref[...] = (dk_acc[...] * LN2).astype(BF)
        dv_ref[...] = dv_acc[...].astype(BF)


def cross_backward(q, kv, do, o, inv, p):
    rows, width = q.shape
    keys = kv.shape[0]
    block = min(512, rows)
    pairs = width // 128
    row = pl.BlockSpec((block, 128), lambda h, i: (i, h))
    col = pl.BlockSpec((keys, 128), lambda h, i: (0, h))
    return pl.pallas_call(
        cross_backward_kernel,
        grid=(pairs, rows // block),
        in_specs=[
            row,
            col,
            pl.BlockSpec((keys, 128), lambda h, i: (0, h + pairs)),
            row,
            row,
            row,
            pl.BlockSpec((block, 2 * keys), lambda h, i: (i, h)),
        ],
        out_specs=[row, col, col],
        out_shape=[
            jax.ShapeDtypeStruct((rows, width), BF),
            jax.ShapeDtypeStruct((keys, width), BF),
            jax.ShapeDtypeStruct((keys, width), BF),
        ],
        scratch_shapes=[pltpu.VMEM((2, keys, 128), BF)] * 2 + [pltpu.VMEM((keys, 128), F32)] * 2,
        compiler_params=params(),
        cost_estimate=cost(32 * rows * keys * width, 12 * rows * width),
        name="cross_backward",
    )(q, kv, kv, do, o, inv, p)


def grain_of(block):
    return min(256, block)


def needed_blocks(segs, block):
    total = segs.shape[0]
    grain = grain_of(block)
    first = segs.reshape(total // block, block)[:, 0]
    start = jnp.sum((segs[None, :] < first[:, None]).astype(jnp.int32), axis=1)
    ends = (jnp.arange(total // block, dtype=jnp.int32) + 1) * block
    return (ends - start // grain * grain) // grain


def self_range(count, i, block):
    grain = grain_of(block)
    before = count - block // grain
    per = CHUNK // grain
    lo = pl.multiple_of((i + 1) * block - count * grain, grain)
    return lo, before // per, before % per, grain


def self_forward_kernel(
    count_ref, slot_ref, q_ref, k_ref, v_ref, qa_ref, ka_ref, o_ref, lse_ref,
    kx, vx, s_scr, m_scr, a_scr,
):
    i = pl.program_id(1)

    @pl.when(i == 0)
    def _():
        forward_prep(k_ref, v_ref, ka_ref, kx, vx)

    forward_block(
        *self_range(count_ref[i], i, q_ref.shape[0]), True, q_ref, qa_ref, kx, vx, o_ref, lse_ref,
        s_scr, m_scr, a_scr, 1,
    )


def self_forward(counts, slots, q, k, v, qa, ka, block):
    total, width = q.shape
    row = pl.BlockSpec((block, 128), lambda h, i, n, s: (i, h))
    col = pl.BlockSpec((total, 128), lambda h, i, n, s: (0, h))
    return pl.pallas_call(
        self_forward_kernel,
        grid_spec=pltpu.PrefetchScalarGridSpec(
            num_scalar_prefetch=2,
            grid=(width // 128, total // block),
            in_specs=[
                row,
                col,
                col,
                pl.BlockSpec((block, 128), lambda h, i, n, s: (i, 0)),
                pl.BlockSpec((total, 128), lambda h, i, n, s: (0, 0)),
            ],
            out_specs=[pl.BlockSpec((block, 128), lambda h, i, n, s: (s[i], h)), row],
            scratch_shapes=forward_scratch(block, total),
        ),
        out_shape=[
            jax.ShapeDtypeStruct((total, width), BF),
            jax.ShapeDtypeStruct((total, width), F32),
        ],
        compiler_params=params(),
        cost_estimate=cost(8 * total * total * width, 8 * total * width, total * total * 3),
        name="self_forward",
    )(counts, slots, q, k, v, qa, ka)


def self_backward_kernel(
    count_ref, slot_ref, q_ref, k_ref, v_ref, own_ref, far_ref, o_ref, lse_ref, qa_ref, ka_ref,
    dq_ref, dk_ref, dv_ref, kx, vx, km, dk_acc, dv_acc, dq_acc, *, per_dev,
):
    i = pl.program_id(1)
    do = jnp.where(slot_ref[i] < per_dev, own_ref[...], far_ref[...])

    @pl.when(i == 0)
    def _():
        backward_prep(k_ref, v_ref, ka_ref, kx, vx, km, dk_acc, dv_acc)

    backward_block(
        *self_range(count_ref[i], i, q_ref.shape[0]), True, q_ref[...], do, o_ref, lse_ref, qa_ref,
        kx, vx, km, dq_ref, dk_acc, dv_acc, dq_acc, 1,
    )

    @pl.when(i == pl.num_programs(1) - 1)
    def _():
        dk_ref[...] = (dk_acc[...] * LN2).astype(BF)
        dv_ref[...] = dv_acc[...].astype(BF)


def self_backward(counts, slots, q, k, v, own, far, o, lse, qa, ka, block):
    total, width = q.shape
    per_dev = own.shape[0] // block
    row = pl.BlockSpec((block, 128), lambda h, i, n, s: (i, h))
    col = pl.BlockSpec((total, 128), lambda h, i, n, s: (0, h))
    return pl.pallas_call(
        functools.partial(self_backward_kernel, per_dev=per_dev),
        grid_spec=pltpu.PrefetchScalarGridSpec(
            num_scalar_prefetch=2,
            grid=(width // 128, total // block),
            in_specs=[
                row,
                col,
                col,
                pl.BlockSpec((block, 128), lambda h, i, n, s: (jnp.minimum(s[i], per_dev - 1), h)),
                pl.BlockSpec((block, 128), lambda h, i, n, s: (jnp.maximum(s[i] - per_dev, 0), h)),
                pl.BlockSpec((block, 128), lambda h, i, n, s: (s[i], h)),
                row,
                pl.BlockSpec((block, 128), lambda h, i, n, s: (i, 0)),
                pl.BlockSpec((total, 128), lambda h, i, n, s: (0, 0)),
            ],
            out_specs=[row, col, col],
            scratch_shapes=backward_scratch(block, total),
        ),
        out_shape=[jax.ShapeDtypeStruct((total, width), BF)] * 3,
        compiler_params=params(),
        cost_estimate=cost(4 * total * total * width, 2 * total * width),
        name="self_backward",
    )(counts, slots, q, k, v, own, far, o, lse, qa, ka)


def qkv_kernel(order_ref, own_ref, far_ref, g_ref, w_ref, n_ref, q_ref, k_ref, v_ref, *, per_dev):
    x = jnp.where(pl.program_id(0) < per_dev, own_ref[...], far_ref[...]).astype(F32)
    n = (x * rms_scale(x) * g_ref[...]).astype(BF)
    n_ref[...] = n
    width = q_ref.shape[1]
    out = nn(n, w_ref[...])
    q_ref[...] = (out[:, :width] * QSCALE).astype(BF)
    k_ref[...] = out[:, width : 2 * width].astype(BF)
    v_ref[...] = out[:, 2 * width :].astype(BF)


def qkv_forward(order, own, far, gain, w, block):
    dim = own.shape[1]
    total = own.shape[0] + far.shape[0]
    width = w.shape[1] // 3
    per_dev = own.shape[0] // block
    here = lambda i, o: (o[i], 0)
    whole = lambda i, o: (0, 0)
    return pl.pallas_call(
        functools.partial(qkv_kernel, per_dev=per_dev),
        grid_spec=pltpu.PrefetchScalarGridSpec(
            num_scalar_prefetch=1,
            grid=(total // block,),
            in_specs=[
                pl.BlockSpec((block, dim), lambda i, o: (jnp.minimum(i, per_dev - 1), 0)),
                pl.BlockSpec((block, dim), lambda i, o: (jnp.maximum(i - per_dev, 0), 0)),
                pl.BlockSpec((1, dim), whole),
                pl.BlockSpec(w.shape, whole),
            ],
            out_specs=[pl.BlockSpec((block, dim), here)] + [pl.BlockSpec((block, width), here)] * 3,
        ),
        out_shape=[jax.ShapeDtypeStruct((total, dim), BF)]
        + [jax.ShapeDtypeStruct((total, width), BF)] * 3,
        compiler_params=params(),
        cost_estimate=cost(6 * total * dim * width, 8 * total * dim),
        name="qkv_forward",
    )(order, own, far, gain, w)


def enc_kv_kernel(own_ref, far_ref, w_ref, kv_ref, *, own_blocks):
    enc = jnp.where(pl.program_id(0) < own_blocks, own_ref[...], far_ref[...])
    half = w_ref.shape[1] // 2
    for c in range(2):
        at = slice(c * half, (c + 1) * half)
        kv_ref[:, at] = nn(enc, w_ref[:, at]).astype(BF)


def enc_forward(own, far, w2):
    rows, dim = own.shape
    block = min(512, rows)
    keys = rows + far.shape[0]
    ours = rows // block
    return pl.pallas_call(
        functools.partial(enc_kv_kernel, own_blocks=ours),
        grid=(keys // block,),
        in_specs=[
            pl.BlockSpec((block, dim), lambda i: (jnp.minimum(i, ours - 1), 0)),
            pl.BlockSpec((block, dim), lambda i: (jnp.maximum(i - ours, 0), 0)),
            pl.BlockSpec((dim, 2 * dim), lambda i: (0, 1)),
        ],
        out_specs=pl.BlockSpec((block, 2 * dim), lambda i: (i, 0)),
        out_shape=jax.ShapeDtypeStruct((keys, 2 * dim), BF),
        compiler_params=params(),
        cost_estimate=cost(4 * keys * dim * dim, 8 * keys * dim),
        name="enc_forward",
    )(own, far, w2)


def after_self_kernel(turn_ref, x_ref, *refs, count):
    o_refs, w_refs = refs[:count], refs[count : 2 * count]
    g_ref, wq_ref, h_ref, n_ref, q_ref, s_ref = refs[2 * count :]
    x = x_ref[...].astype(F32)
    a = nn(o_refs[0][...], w_refs[0][...])
    for o_ref, w_ref in zip(o_refs[1:], w_refs[1:]):
        a = a + nn(o_ref[...], w_ref[...])
    h = x + a
    h_ref[...] = h
    n = (h * rms_scale(h) * g_ref[...]).astype(BF)
    n_ref[...] = n
    q_ref[...] = (nn(n, wq_ref[...]) * QSCALE).astype(BF)

    @pl.when(pl.program_id(0) == 0)
    def _():
        s_ref[...] = jnp.zeros_like(s_ref)

    s_ref[0:1, :] += jnp.sum(x * x, axis=0, keepdims=True)
    s_ref[1:2, :] += jnp.sum(a * a, axis=0, keepdims=True)


def turn_specs(count, width, dim):
    return [pl.BlockSpec((width, dim), lambda i, t, k=k: (t[k], 0)) for k in range(count)]


def after_self(turn, x, pieces, wo, gain, w2):
    rows, dim = x.shape
    count, width = len(pieces), pieces[0].shape[1]
    block = min(512, rows)
    line = lambda i, t: (i, 0)
    whole = lambda i, t: (0, 0)
    row = pl.BlockSpec((block, dim), line)
    return pl.pallas_call(
        functools.partial(after_self_kernel, count=count),
        grid_spec=pltpu.PrefetchScalarGridSpec(
            num_scalar_prefetch=1,
            grid=(rows // block,),
            in_specs=[row]
            + [pl.BlockSpec((block, width), line)] * count
            + turn_specs(count, width, dim)
            + [pl.BlockSpec((1, dim), whole), pl.BlockSpec((dim, dim), lambda i, t: (0, 1))],
            out_specs=[row, row, row, pl.BlockSpec((8, dim), whole)],
        ),
        out_shape=[
            jax.ShapeDtypeStruct((rows, dim), F32),
            jax.ShapeDtypeStruct((rows, dim), BF),
            jax.ShapeDtypeStruct((rows, dim), BF),
            jax.ShapeDtypeStruct((8, dim), F32),
        ],
        compiler_params=params(),
        cost_estimate=cost(4 * rows * dim * dim, 14 * rows * dim),
        name="after_self",
    )(turn, x, *pieces, *([wo] * count), gain, w2)


GELU_C = math.sqrt(2.0 / math.pi)
GELU_A = 0.044715


PIECES = (4, 8, 3, 64)


def mlp_kernel(
    o_ref, h1_ref, wc_ref, g_ref, t_ref, gu_ref, wd_ref,
    y_ref, dh_ref, dc_ref, do_ref, s_ref, g_out,
    n_scr, h_scr, m_scr, dn_scr, hid_scr, du_scr, dw_scr, wg_scr, wu_scr, gu_out, d_out, sems,
):
    j = pl.program_id(0)
    last = pl.num_programs(0) - 1
    rows = o_ref.shape[0]
    step = min(256, rows)
    spans = [pl.ds(r, step) for r in range(0, rows, step)]
    gain = g_ref[...]
    n_fsdp, n_two, _, tall, _ = gu_ref.shape
    third = 256
    high = 3 * tall

    @pl.when(j == 0)
    def _():
        total = None
        for at in spans:
            c = nn(o_ref[at, :], wc_ref[...])
            h = h1_ref[at, :] + c
            h_scr[at, :] = h
            n_scr[at, :] = (h * rms_scale(h) * gain).astype(BF)
            part = jnp.sum(c * c, axis=0, keepdims=True)
            total = part if total is None else total + part
        s_ref[...] = jnp.zeros_like(s_ref)
        s_ref[0:1, :] = total
        m_scr[...] = jnp.zeros_like(m_scr)
        dn_scr[...] = jnp.zeros_like(dn_scr)

    for z in range(n_fsdp):
        for p in range(n_two):
            for t in range(3):
                at, to = pl.ds(z * high + t * tall, tall), pl.ds(p * third, third)
                wg_scr[at, to] = gu_ref[z, p, 0, :, t * third : (t + 1) * third]
                wu_scr[at, to] = gu_ref[z, p, 1, :, t * third : (t + 1) * third]
    wg, wu = wg_scr[...], wu_scr[...]
    wd = wd_ref[...].reshape(-1, wd_ref.shape[-1])
    for at in spans:
        n = n_scr[at, :]
        u = nn(n, wg)
        w = nn(n, wu)
        dhid = nt(t_ref[at, :], wd)
        square = u * u
        th = jnp.tanh(GELU_C * u * (1.0 + GELU_A * square))
        half = 0.5 * (1.0 + th)
        gel = u * half
        slope = half + 0.5 * u * (1.0 - th * th) * (GELU_C * (1.0 + 3.0 * GELU_A * square))
        hid = (gel * w).astype(BF)
        du = (dhid * w * slope).astype(BF)
        dw = (dhid * gel).astype(BF)
        hid_scr[at, :] = hid
        du_scr[at, :] = du
        dw_scr[at, :] = dw
        m_scr[at, :] += nn(hid, wd)
        dn_scr[at, :] += nt(du, wg) + nt(dw, wu)

    slot = lax.rem(j, 2)

    def copies(step_of, slot_of):
        return (
            pltpu.make_async_copy(
                gu_out.at[slot_of],
                g_out.at[:, pl.ds(step_of * n_two, n_two), pl.ds(0, 2)],
                sems.at[slot_of, 0],
            ),
            pltpu.make_async_copy(d_out.at[slot_of], g_out.at[step_of, :, 2], sems.at[slot_of, 1]),
        )

    @pl.when(j >= 2)
    def _():
        for copy in copies(j - 2, slot):
            copy.wait()

    d_out[slot] = tn(hid_scr[...], t_ref[...]).astype(BF).reshape(d_out.shape[1:])
    for side, source in ((0, du_scr), (1, dw_scr)):
        grad = tn(n_scr[...], source[...]).astype(BF)
        for z in range(n_fsdp):
            for p in range(n_two):
                for t in range(3):
                    gu_out[slot, z, p, side, :, t * third : (t + 1) * third] = grad[
                        z * high + t * tall : z * high + (t + 1) * tall,
                        p * third : (p + 1) * third,
                    ]
    for copy in copies(j, slot):
        copy.start()

    @pl.when(j == last)
    def _():
        total = gains = None
        for at in spans:
            h = h_scr[at, :]
            y = h + m_scr[at, :]
            y_ref[at, :] = y.astype(BF)
            dh, dg = norm_back(h, gain, dn_scr[at, :])
            dh = dh + t_ref[at, :].astype(F32)
            dh_ref[at, :] = dh
            dc = dh.astype(BF)
            dc_ref[at, :] = dc
            do_ref[at, :] = nt(dc, wc_ref[...]).astype(BF)
            part = jnp.sum(y * y, axis=0, keepdims=True)
            total = part if total is None else total + part
            gains = dg if gains is None else gains + dg
        s_ref[1:2, :] = total
        s_ref[2:3, :] = gains
        for copy in copies(j - 1, 1 - slot) + copies(j, slot):
            copy.wait()


def feed_forward(o, h1, w2, gain, cot, w3):
    rows, dim = o.shape
    n_fsdp, n_plane, _, tall, _ = w3.shape
    steps = n_fsdp
    two = n_plane // steps
    width = two * 256
    whole = lambda j: (0, 0)
    once = pl.Buffered(1)
    full = pl.BlockSpec((rows, dim), whole, pipeline_mode=once)
    flops = 18 * rows * dim * width * steps + 6 * rows * dim * dim
    return pl.pallas_call(
        mlp_kernel,
        grid=(steps,),
        in_specs=[
            full,
            full,
            pl.BlockSpec((dim, dim), lambda j: (0, 4), pipeline_mode=once),
            pl.BlockSpec((1, dim), whole),
            full,
            pl.BlockSpec((n_fsdp, two, 2, tall, dim), lambda j: (0, j, 0, 0, 0)),
            pl.BlockSpec((1, n_plane, 1, tall, dim), lambda j: (j, 0, 2, 0, 0)),
        ],
        out_specs=[
            full,
            full,
            full,
            full,
            pl.BlockSpec((8, dim), whole),
            pl.BlockSpec(memory_space=pl.ANY),
        ],
        out_shape=[
            jax.ShapeDtypeStruct((rows, dim), BF),
            jax.ShapeDtypeStruct((rows, dim), F32),
            jax.ShapeDtypeStruct((rows, dim), BF),
            jax.ShapeDtypeStruct((rows, dim), BF),
            jax.ShapeDtypeStruct((8, dim), F32),
            jax.ShapeDtypeStruct(w3.shape, BF),
        ],
        scratch_shapes=[
            pltpu.VMEM((rows, dim), BF),
            pltpu.VMEM((rows, dim), F32),
            pltpu.VMEM((rows, dim), F32),
            pltpu.VMEM((rows, dim), F32),
            pltpu.VMEM((rows, width), BF),
            pltpu.VMEM((rows, width), BF),
            pltpu.VMEM((rows, width), BF),
            pltpu.VMEM((dim, width), BF),
            pltpu.VMEM((dim, width), BF),
            pltpu.VMEM((2, n_fsdp, two, 2, tall, dim), BF),
            pltpu.VMEM((2, n_plane, tall, dim), BF),
            pltpu.SemaphoreType.DMA((2, 2)),
        ],
        compiler_params=params(),
        cost_estimate=cost(flops, 40 * MIB, rows * width * steps),
        name="feed_forward",
    )(o, h1, w2, gain, cot, w3, w3)


def placed(me_ref, near_ref, far_ref, size):
    core, x = me_ref[0], me_ref[1]
    for c, ref in enumerate((near_ref, far_ref)):
        for a in range(2):
            yield ref.at[a], pl.multiple_of(((a ^ x) * 2 + (c ^ core)) * size, 16)


def unpack_kernel(me_ref, near_ref, far_ref, gate_ref, up_ref, down_ref):
    core, x = me_ref[0], me_ref[1]
    tall = near_ref.shape[3]
    third = 256
    for c in range(2):
        for a in range(2):
            for i in range(2):
                p = a * 4 + c * 2 + i
                piece = lambda k: jnp.where(
                    core == c, near_ref[a ^ x, i, k], far_ref[a ^ x, i, k]
                ).astype(F32)
                gate, up = piece(0), piece(1)
                for t in range(3):
                    at, to = pl.ds(t * tall, tall), pl.ds(p * third, third)
                    gate_ref[at, to] = gate[:, t * third : (t + 1) * third]
                    up_ref[at, to] = up[:, t * third : (t + 1) * third]
                down_ref[pl.ds(p * tall, tall), :] = piece(2)


def settle_mid_kernel(me_ref, near_ref, far_ref, *outs):
    dim = outs[0].shape[1]
    size = near_ref.shape[1]
    for ref, row in placed(me_ref, near_ref, far_ref, size):
        for m, out in enumerate(outs):
            out[pl.ds(row, size), :] = ref[:, m * dim : (m + 1) * dim].astype(F32)


def settle_qkv_kernel(
    me_ref, near_ref, far_ref, q_ref, k_ref, v_ref, self_ref, mlp_ref, cross_ref, rms_ref, tail_ref,
    *, entries,
):
    place = me_ref[2]
    size = near_ref.shape[2]
    width = q_ref.shape[1] // 2
    for ref, row in placed(me_ref, near_ref, far_ref, size):
        at = pl.ds(row, size)
        tail = None
        for i in range(2):
            block = ref[i ^ place].astype(F32)
            for t, out in enumerate((q_ref, k_ref, v_ref)):
                out[at, i * width : (i + 1) * width] = block[:, t * width : (t + 1) * width]
            part = block[:, 3 * width :]
            tail = part if tail is None else tail + part
        tail_ref[at, :] = tail
    rms_ref[...] = jnp.sqrt(pltpu.roll(tail_ref[0:8, :], 128 - 3, 1)[0:1, :4] / entries)
    turned_tail = tail_ref[...].T
    for i, ref in enumerate((self_ref, mlp_ref, cross_ref)):
        ref[...] = turned_tail[i : i + 1, :]


def settle(kernel, me, near, far, shapes, scratch=(), **given):
    vmem = pl.BlockSpec(memory_space=pltpu.VMEM)
    return pl.pallas_call(
        functools.partial(kernel, **given),
        in_specs=[pl.BlockSpec(memory_space=pltpu.SMEM), vmem, vmem],
        out_specs=[vmem] * len(shapes),
        out_shape=[jax.ShapeDtypeStruct(shape, F32) for shape in shapes],
        scratch_shapes=scratch,
        compiler_params=params(),
        name=kernel.__name__[:-7],
    )(me, near, far)


def deal_rows(core, full, send_ref, keep_ref):
    count, size = send_ref.shape[:2]
    for i in range(count):
        for ref, c in ((send_ref, 1 - core), (keep_ref, core)):
            ref[i] = full[pl.ds(pl.multiple_of((2 * i + c) * size, 16), size), :]


def mid_grads_kernel(turn_ref, *refs, count):
    n_in = count + 9
    sources = refs[:n_in]
    wk_ref, wv_ref, g_ref, far_out = refs[n_in : n_in + 4]
    buffers = refs[n_in + 4 : 2 * n_in + 4]
    sems = refs[-1]
    m = pl.program_id(0)
    dim = g_ref.shape[0]
    copies = [
        pltpu.make_async_copy(
            source.at[pl.ds(0, buffer.shape[0])] if source.shape != buffer.shape else source,
            buffer,
            sems.at[i],
        )
        for i, (source, buffer) in enumerate(zip(sources, buffers))
    ]
    n2, dq, da, *o_pieces, own, far, dk, dv, o2, dc = buffers
    ours = own.shape[0]
    width = o_pieces[0].shape[1]

    @pl.when(m == 0)
    def _():
        for copy in copies:
            copy.start()
        for copy in copies[:2]:
            copy.wait()
        g_ref[...] = tn(n2[...], dq[...]).astype(BF)

    @pl.when(m == 1)
    def _():
        for copy in copies[2 : 3 + count]:
            copy.wait()
        for i in range(count):
            base = pl.multiple_of(turn_ref[i] * width, width)
            term = tn(o_pieces[i][...], da[...]).astype(BF)

            @pl.when(base < dim)
            def _():
                g_ref[pl.ds(base, width), :] = term

    for at, right, first in ((2, dk, 3), (3, dv, 6)):

        @pl.when(m == at)
        def _():
            for copy in copies[count + first : count + 6 if at == 2 else count + 7]:
                copy.wait()
            g_ref[...] = (tn(own[...], right[:ours, :]) + tn(far[...], right[ours:, :])).astype(BF)

    @pl.when(m == 4)
    def _():
        for copy in copies[count + 7 :]:
            copy.wait()
        g_ref[...] = tn(o2[...], dc[...]).astype(BF)

    block = far_out.shape[0]

    @pl.when(m >= 5)
    def _():
        at = pl.ds(pl.multiple_of(ours + (m - 5) * block, block), block)
        far_out[...] = (nt(dk[at, :], wk_ref[...]) + nt(dv[at, :], wv_ref[...])).astype(BF)


def dealt_out(dim, block, total, index, deal):
    if not deal:
        return [pl.BlockSpec((dim, block), lambda *a: (0, index(*a)))], [
            jax.ShapeDtypeStruct((dim, total), BF)
        ]
    spec = pl.BlockSpec((8, dim // 16, block), lambda *a: (0, 0, index(*a)))
    return [spec] * 2, [jax.ShapeDtypeStruct((8, dim // 16, total), BF)] * 2


def mid_grads(turn, pieces, da, n2, dq2, own, far, dk2, dv2, o2, dc, w2):
    rows, dim = n2.shape
    args = (n2, dq2, da, *pieces, own, far, dk2, dv2, o2, dc)
    shapes = [(rows, a.shape[1]) for a in args[: 3 + len(pieces)]]
    shapes += [a.shape for a in args[3 + len(pieces) :]]
    flops = 2 * dim * dim * (3 * rows + 2 * dk2.shape[0] + 2 * far.shape[0])
    block = min(512, own.shape[0])
    far_blocks = far.shape[0] // block
    once = pl.Buffered(1)
    column = lambda m, t: (0, jnp.where(m < 2, 1 - m, jnp.minimum(m, 4)))
    return pl.pallas_call(
        functools.partial(mid_grads_kernel, count=len(pieces)),
        grid_spec=pltpu.PrefetchScalarGridSpec(
            num_scalar_prefetch=1,
            grid=(5 + far_blocks,),
            in_specs=[pl.BlockSpec(memory_space=pl.ANY)] * len(args)
            + [
                pl.BlockSpec((dim, dim), lambda m, t: (0, 2), pipeline_mode=once),
                pl.BlockSpec((dim, dim), lambda m, t: (0, 3), pipeline_mode=once),
            ],
            out_specs=[
                pl.BlockSpec((dim, dim), column),
                pl.BlockSpec((block, dim), lambda m, t: (jnp.maximum(m - 5, 0), 0)),
            ],
            scratch_shapes=[pltpu.VMEM(shape, BF) for shape in shapes]
            + [pltpu.SemaphoreType.DMA((len(args),))],
        ),
        out_shape=[
            jax.ShapeDtypeStruct((dim, 5 * dim), BF),
            jax.ShapeDtypeStruct(far.shape, BF),
        ],
        compiler_params=params(),
        cost_estimate=cost(flops, 30 * MIB),
        name="mid_grads",
    )(turn, *args, w2, w2)


def enc_finish_kernel(dk_ref, dv_ref, wk_ref, wv_ref, *refs):
    total = nt(dk_ref[...], wk_ref[...]) + nt(dv_ref[...], wv_ref[...])
    for ref in refs[:-1]:
        total = total + ref[...].astype(F32)
    refs[-1][...] = total


def enc_finish(dk, dv, w2, got):
    rows, dim = got[0].shape
    block = min(512, rows)
    row = pl.BlockSpec((block, dim), lambda i: (i, 0))
    return pl.pallas_call(
        enc_finish_kernel,
        grid=(rows // block,),
        in_specs=[
            row,
            row,
            pl.BlockSpec((dim, dim), lambda i: (0, 2)),
            pl.BlockSpec((dim, dim), lambda i: (0, 3)),
        ]
        + [row] * len(got),
        out_specs=row,
        out_shape=jax.ShapeDtypeStruct((rows, dim), F32),
        compiler_params=params(),
        cost_estimate=cost(rows * dim, rows),
        name="enc_finish",
    )(dk, dv, w2, w2, *got)


def before_self_kernel(turn_ref, dq_ref, wq_ref, h_ref, dh_ref, g_ref, *refs, count):
    w_refs = refs[:count]
    d1_ref, da_ref, s_ref = refs[count : count + 3]
    do_refs = refs[count + 3 :]
    dn = nt(dq_ref[...], wq_ref[...])
    dh, dg = norm_back(h_ref[...], g_ref[...], dn)
    d1 = dh_ref[...] + dh
    d1_ref[...] = d1
    da = d1.astype(BF)
    da_ref[...] = da
    for do_ref, w_ref in zip(do_refs, w_refs):
        do_ref[...] = nt(da, w_ref[...]).astype(BF)

    @pl.when(pl.program_id(0) == 0)
    def _():
        s_ref[...] = jnp.zeros_like(s_ref)

    s_ref[0:1, :] += dg


def before_self(turn, dq, w2, h1, dh2, gain, wo, width):
    rows, dim = dq.shape
    count = turn.shape[0]
    block = min(512, rows)
    line = lambda i, t: (i, 0)
    whole = lambda i, t: (0, 0)
    row = pl.BlockSpec((block, dim), line)
    return pl.pallas_call(
        functools.partial(before_self_kernel, count=count),
        grid_spec=pltpu.PrefetchScalarGridSpec(
            num_scalar_prefetch=1,
            grid=(rows // block,),
            in_specs=[
                row,
                pl.BlockSpec((dim, dim), lambda i, t: (0, 1)),
                row,
                row,
                pl.BlockSpec((1, dim), whole),
            ]
            + turn_specs(count, width, dim),
            out_specs=[row, row, pl.BlockSpec((8, dim), whole)]
            + [pl.BlockSpec((block, width), line)] * count,
        ),
        out_shape=[
            jax.ShapeDtypeStruct((rows, dim), F32),
            jax.ShapeDtypeStruct((rows, dim), BF),
            jax.ShapeDtypeStruct((8, dim), F32),
        ]
        + [jax.ShapeDtypeStruct((rows, width), BF)] * count,
        compiler_params=params(),
        cost_estimate=cost(4 * rows * dim * dim, 18 * rows * dim),
        name="before_self",
    )(turn, dq, w2, h1, dh2, gain, *([wo] * count))


def joined(refs):
    return jnp.concatenate([r[...] for r in refs], axis=1)


def qkv_grads_kernel(core_ref, *refs, count, deal):
    d_refs = refs[:count]
    n_ref, w_ref, gain_ref, one_ref, two_ref, three_ref = refs[count : count + 6]
    outs = refs[count + 6 :]
    acc, full = outs[-2:]
    i = pl.program_id(0)
    term = tn(n_ref[...], joined(d_refs))

    @pl.when(i == 0)
    def _():
        acc[...] = term

    @pl.when(i > 0)
    def _():
        acc[...] += term

    @pl.when(i == pl.num_programs(0) - 1)
    def _():
        width = acc.shape[1]
        grad = acc[...]
        dim = grad.shape[0]
        totals = [
            jnp.broadcast_to(jnp.sum(row, axis=1, keepdims=True), (1, dim))
            for row in (one_ref[0:1, :], one_ref[1:2, :], two_ref[0:1, :], two_ref[1:2, :])
        ]
        lines = [gain_ref[...], two_ref[2:3, :], three_ref[0:1, :], *totals]
        lines.append(jnp.zeros((128 - len(lines), dim), F32))
        extra = jnp.concatenate(lines, axis=0).T
        gains = jnp.sum(grad * w_ref[...].astype(F32), axis=1, keepdims=True) / extra[:, :1]
        full[:, :width] = grad.astype(BF)
        full[:, width:] = jnp.where(lanes(extra.shape) == 0, gains, extra).astype(BF)
        if deal:
            deal_rows(core_ref[0], full, outs[0], outs[1])
        else:
            outs[0][...] = full[...]


def qkv_grads(core, ds, n, w, gain, stats, deal):
    total, dim = n.shape
    block = min(512, total)
    width = w.shape[1]
    specs, outs = dealt_out(dim, width + 128, width + 128, lambda i, c: 0, deal)
    whole = lambda i, c: (0, 0)
    return pl.pallas_call(
        functools.partial(qkv_grads_kernel, count=len(ds), deal=deal),
        grid_spec=pltpu.PrefetchScalarGridSpec(
            num_scalar_prefetch=1,
            grid=(total // block,),
            in_specs=[pl.BlockSpec((block, width // 3), lambda i, c: (i, 0))] * len(ds)
            + [
                pl.BlockSpec((block, dim), lambda i, c: (i, 0)),
                pl.BlockSpec(w.shape, whole),
                pl.BlockSpec((1, dim), whole),
            ]
            + [pl.BlockSpec((8, dim), whole)] * 3,
            out_specs=specs,
            scratch_shapes=[pltpu.VMEM((dim, width), F32), pltpu.VMEM((dim, width + 128), BF)],
        ),
        out_shape=outs,
        compiler_params=params(),
        cost_estimate=cost(total * dim, total),
        name="qkv_grads",
    )(core, *ds, n, w, gain, *stats)


def qkv_back_kernel(order_ref, *refs, count):
    dn_ref = refs[count + 1]
    dn_ref[...] = nt(joined(refs[:count]), refs[count][...]).astype(dn_ref.dtype)


def qkv_back(order, first, ds, w, rows, dtype, block):
    dim = w.shape[0]
    return pl.pallas_call(
        functools.partial(qkv_back_kernel, count=len(ds)),
        grid_spec=pltpu.PrefetchScalarGridSpec(
            num_scalar_prefetch=1,
            grid=(rows // block,),
            in_specs=[pl.BlockSpec((block, w.shape[1] // 3), lambda i, o: (o[i + first], 0))] * len(ds)
            + [pl.BlockSpec(w.shape, lambda i, o: (0, 0))],
            out_specs=pl.BlockSpec((block, dim), lambda i, o: (i, 0)),
        ),
        out_shape=jax.ShapeDtypeStruct((rows, dim), dtype),
        compiler_params=params(),
        cost_estimate=cost(rows * dim, rows),
        name="qkv_back",
    )(order, *ds, w)


def finish_kernel(x_ref, dh_ref, g_ref, own_ref, *refs):
    dn = own_ref[...]
    for ref in refs[:-1]:
        dn = dn + ref[...].astype(F32)
    dh, _ = norm_back(x_ref[...].astype(F32), g_ref[...], dn)
    refs[-1][...] = dh_ref[...] + dh


def finish(x, dh1, gain, own, got):
    rows, dim = x.shape
    block = min(256, rows)
    row = pl.BlockSpec((block, dim), lambda i: (i, 0))
    return pl.pallas_call(
        finish_kernel,
        grid=(rows // block,),
        in_specs=[row, row, pl.BlockSpec((1, dim), lambda i: (0, 0)), row] + [row] * len(got),
        out_specs=row,
        out_shape=jax.ShapeDtypeStruct((rows, dim), F32),
        compiler_params=params(),
        cost_estimate=cost(rows * dim, rows),
        name="finish",
    )(x, dh1, gain, own, *got)


def turned(n, k):
    return [(i, (i + k) % n) for i in range(n)]


def rows_of(array, index, count):
    size = array.shape[0] // count
    return lax.dynamic_slice_in_dim(array, index * size, size, 0)


def assemble_kernel(place_ref, near_ref, far_ref, w_ref, gain_ref, g_ref):
    z, core = place_ref[0], place_ref[1]
    count, size = near_ref.shape[0], near_ref.shape[1]
    width = w_ref.shape[1]
    for d in range(count):
        base = lax.rem(z - d + count, count) * (2 * size)
        for ref, half in ((near_ref, core), (far_ref, 1 - core)):
            at = pl.ds(pl.multiple_of(base + half * size, 16), size)
            w_ref[at, :] = ref[d, :, :width]
            g_ref[at, :] = ref[d, :, width:].astype(F32)
    gain_ref[...] = g_ref[...].T[:8, :]


def gather_first(own, z, part, n_fsdp, n_parts):
    size = own.shape[0] // 2
    width = own.shape[1] - 128
    if n_parts % 2 or size % 16:
        full = lax.all_gather(own, "fsdp", axis=0, tiled=True)
        return full[:, :width], full[:, width : width + 8].astype(F32).T
    core = part % 2
    mine = lax.dynamic_slice_in_dim(own, core * size, size, 0)
    near = jnp.stack(
        [mine] + [lax.ppermute(mine, "fsdp", turned(n_fsdp, d)) for d in range(1, n_fsdp)]
    )
    far = lax.ppermute(near, "parts", [(i, i ^ 1) for i in range(n_parts)])
    vmem = pl.BlockSpec(memory_space=pltpu.VMEM)
    total = n_fsdp * own.shape[0]
    return pl.pallas_call(
        assemble_kernel,
        in_specs=[pl.BlockSpec(memory_space=pltpu.SMEM), vmem, vmem],
        out_specs=[vmem, vmem],
        out_shape=[
            jax.ShapeDtypeStruct((total, width), BF),
            jax.ShapeDtypeStruct((8, total), F32),
        ],
        scratch_shapes=[pltpu.VMEM((total, 128), F32)],
        compiler_params=params(),
        name="assemble",
    )(jnp.stack([z, core]).astype(jnp.int32), near, far)


def pick(array, index, axis):
    return lax.dynamic_index_in_dim(array, index, axis, keepdims=False)


class Plane:
    def __init__(self, part, place, z, n_parts, n_fsdp):
        self.core, self.x, self.place, self.z = part % 2, part // 2, place, z
        self.n_fsdp = n_fsdp
        self.swap_core = [(i, i ^ 1) for i in range(n_parts)]
        self.swap_x = [(i, i ^ 2) for i in range(n_parts)]

    def over_core(self, send, keep):
        shape = (self.n_fsdp, 2) + send.shape[1:]
        got = lax.ppermute(send, "parts", self.swap_core).reshape(shape)
        keep = keep.reshape(shape)
        add = lambda i: (pick(keep, i, 1).astype(F32) + pick(got, i, 1).astype(F32)).astype(BF)
        return add(1 - self.x), add(self.x)

    def over_x(self, send, keep):
        got = lax.ppermute(send, "parts", self.swap_x)
        return (keep.astype(F32) + got.astype(F32)).astype(BF)

    def from_fsdp(self, g):
        return [pick(g, self.z, 0)] + [
            lax.ppermute(pick(g, (self.z + d) % self.n_fsdp, 0), "fsdp", turned(self.n_fsdp, d))
            for d in range(1, self.n_fsdp)
        ]

    def over_ctx(self, g):
        return (g.astype(F32) + lax.ppermute(g, "ctx", turned(2, 1)).astype(F32)).astype(BF)

    def widen_ctx(self, g):
        return jnp.stack([g, lax.ppermute(g, "ctx", turned(2, 1))])

    def widen_x(self, g):
        return jnp.stack([g, lax.ppermute(g, "parts", self.swap_x)])

    def from_core(self, g):
        return lax.ppermute(g, "parts", self.swap_core)


def local(
    mesh_shape,
    decoder_in,
    encoder_out,
    segment_ids,
    block_order,
    prompt_len,
    self_query,
    self_key,
    self_value,
    self_output,
    cross_query,
    cross_key,
    cross_value,
    cross_output,
    gate_in,
    up_in,
    down_out,
    norm_self,
    norm_cross,
    norm_mlp,
    cotangent,
):
    n_parts, n_ctx, n_fsdp = mesh_shape
    part, place, z = lax.axis_index("parts"), lax.axis_index("ctx"), lax.axis_index("fsdp")
    plane, n_plane = part * n_ctx + place, n_parts * n_ctx
    x_own, enc_own = decoder_in[0], encoder_out[0]
    rows, dim = x_own.shape
    segs, order = segment_ids[0], block_order[0]
    total = segs.shape[0]
    slots_total = order.shape[0]
    block = total // slots_total
    per_dev = slots_total // n_ctx
    enc_rows = enc_own.shape[0]
    keys = enc_rows * n_ctx
    hidden = down_out.shape[0] * n_fsdp
    heads_here = 2 * -(-HEADS // (2 * n_ctx))
    width = heads_here * HEAD
    padded = width * n_ctx

    ring = (place + jnp.arange(n_ctx, dtype=jnp.int32)) % n_ctx
    order_here = jnp.roll(order, -per_dev * place)
    slots = jnp.argsort(order_here).astype(jnp.int32)
    counts = needed_blocks(segs, block)

    def from_ctx(value):
        pieces = [lax.ppermute(value, "ctx", turned(n_ctx, -k)) for k in range(1, n_ctx)]
        return pieces[0] if n_ctx == 2 else jnp.concatenate(pieces, axis=0)

    x_far = from_ctx(x_own)

    fast = (n_parts, n_ctx, n_fsdp) == (4, 2, 4)
    shard = dim // n_fsdp

    def own_heads(w):
        w = jnp.pad(w, ((0, 0), (0, padded - dim)))
        return lax.dynamic_slice_in_dim(w, place * width, width, 1)

    gain_cols = jnp.pad(jnp.stack([norm_self, norm_cross, norm_mlp], axis=1), ((0, 0), (0, 125)))
    first = jnp.concatenate(
        [own_heads(self_query), own_heads(self_key), own_heads(self_value), gain_cols], axis=1
    )
    w1, gains = gather_first(first, z, part, n_fsdp, n_parts)
    gain_self, gain_cross, gain_mlp = (gains[i : i + 1] for i in range(3))
    mats = (self_output, cross_query, cross_key, cross_value, cross_output)
    if fast:
        w2 = lax.all_gather(
            jnp.concatenate([rows_of(w, part, n_parts) for w in mats], axis=1),
            AROUND, axis=0, tiled=True,
        )

        def column_pieces(w):
            cut = lax.dynamic_slice_in_dim(w, part * 512, 512, 1).reshape(3, 64, 2, 256)
            return cut.transpose(2, 1, 0, 3).reshape(2, 64, dim)

        w3 = lax.all_gather(
            jnp.stack(
                [
                    column_pieces(gate_in),
                    column_pieces(up_in),
                    rows_of(down_out, part, n_parts).reshape(2, 64, dim),
                ],
                axis=1,
            ).reshape(-1, dim),
            AROUND, axis=0, tiled=True,
        ).reshape(PIECES + (dim,))
    else:
        w2 = lax.all_gather(jnp.concatenate(mats, axis=1), "fsdp", axis=0, tiled=True)

        def packed(w):
            w = lax.all_gather(w, "fsdp", axis=0, tiled=True).reshape(4, 3, 64, 8, 256)
            return w.transpose(0, 3, 2, 1, 4).reshape(4, 8, 64, dim)

        w_down = lax.all_gather(down_out, "fsdp", axis=0, tiled=True).reshape(4, 8, 64, dim)
        w3 = jnp.stack([packed(gate_in), packed(up_in), w_down], axis=2)
    x_far, enc_sent = lax.optimization_barrier((x_far, enc_own))
    enc_far = from_ctx(enc_sent)

    n1, q, k, v = qkv_forward(order_here, x_own, x_far, gain_self, w1, block)
    spot = jnp.arange(128, dtype=jnp.int32)[None, :] % HEAD
    minus = jnp.where((spot >= PART0) & (spot < PART0 + 3), -1.0, 0.0)
    seg_q = jnp.where(spot == segs[:, None], 1.0, 0.0).astype(BF)
    seg_k = jnp.where((spot < SEGS) & (spot != segs[:, None]), -BIG, minus).astype(BF)
    o1, lse1 = self_forward(counts, slots, q, k, v, seg_q, seg_k, block)
    pieces = [o1] + [
        lax.ppermute(o1[i * rows : (i + 1) * rows], "ctx", turned(n_ctx, i)) for i in range(1, n_ctx)
    ]
    turn = (place - jnp.arange(n_ctx, dtype=jnp.int32)) % n_ctx
    wo = w2 if padded == dim else jnp.pad(w2[:, :dim], ((0, padded - dim), (0, 0)))
    kv2 = enc_forward(enc_own, enc_far, w2)
    pieces[1], kv2 = lax.optimization_barrier((pieces[1], kv2))
    h1, n2, q2, stat1 = after_self(turn, x_own, pieces, wo, gain_cross, w2)

    where_key = (ring[:, None] * enc_rows + jnp.arange(enc_rows, dtype=jnp.int32)).reshape(-1, 1)
    len_q = jnp.where(spot == 0, jnp.ones((rows, 1), F32), 0.0).astype(BF)
    len_k = jnp.where((spot == 0) & (where_key >= prompt_len[0]), -BIG, minus).astype(BF)
    o2, inv2, p2 = cross_forward(q2, kv2, len_q, len_k)

    layer_out, dh2, dc, do2, stat2, g_ff = feed_forward(o2, h1, w2, gain_mlp, cotangent[0], w3)
    if fast:
        part_ff = lax.psum_scatter(
            g_ff.reshape(-1, dim), AROUND, scatter_dimension=0, tiled=True
        ).reshape(2, 3, 64, dim)

    dq2, dk2, dv2 = cross_backward(q2, kv2, do2, o2, inv2, p2)
    dh1, da, stat3, *do1 = before_self(turn, dq2, w2, h1, dh2, gain_cross, wo, width)
    do_far = [lax.ppermute(do1[i], "ctx", turned(n_ctx, -i)) for i in range(1, n_ctx)]
    do_far = do_far[0] if n_ctx == 2 else jnp.concatenate(do_far, axis=0)
    do_own = do1[0]
    core = jnp.reshape(part % 2, (1,)).astype(jnp.int32)
    g_mid, d_far = mid_grads(
        turn, pieces, da, n2, dq2, enc_own, enc_far, dk2, dv2, o2, dc, w2
    )

    entries = float(n_parts * n_ctx * n_fsdp * rows * dim)

    if fast:
        net = Plane(part, place, z, n_parts, n_fsdp)
        do_own, do_far, d_far, g_mid, part_ff = lax.optimization_barrier(
            (do_own, do_far, d_far, g_mid, part_ff)
        )
        part_mid = lax.psum_scatter(g_mid, AROUND, scatter_dimension=0, tiled=True)
        sum_ff = net.over_ctx(part_ff)
    enc_got = [
        lax.ppermute(d_far[(i - 1) * enc_rows : i * enc_rows], "ctx", turned(n_ctx, i))
        for i in range(1, n_ctx)
    ]
    ds = self_backward(counts, slots, q, k, v, do_own, do_far, o1, lse1, seg_q, seg_k, block)
    if fast:
        ds, sum_ff, enc_got = lax.optimization_barrier((ds, sum_ff, enc_got))
    g_qkv = qkv_grads(core, ds, n1, w1, gain_self, (stat1, stat2, stat3), fast)
    ds, g_qkv = lax.optimization_barrier((ds, g_qkv))
    dn_far = qkv_back(order_here, per_dev, ds, w1, total - rows, BF, block)
    dn_got = [
        lax.ppermute(dn_far[(i - 1) * rows : i * rows], "ctx", turned(n_ctx, i))
        for i in range(1, n_ctx)
    ]
    dn_own = qkv_back(order_here, 0, ds, w1, rows, F32, block)
    enc_grad = enc_finish(dk2, dv2, w2, enc_got)
    if fast:
        send, keep = net.over_core(*g_qkv)
        send, keep, dn_far = lax.optimization_barrier((send, keep, dn_far))
        g_qkv, enc_grad, sum_ff, dn_own = lax.optimization_barrier(
            (net.over_x(send, keep), enc_grad, sum_ff, dn_own)
        )
        sum_ff = net.widen_x(sum_ff)
        shares = net.from_fsdp(g_qkv)
        shares[1], part_mid = lax.optimization_barrier((shares[1], part_mid))
        got_mid = lax.ppermute(part_mid, "ctx", turned(2, 1))
        g_qkv = functools.reduce(jnp.add, [share.astype(F32) for share in shares]).astype(BF)
        g_qkv, dn_got, got_mid = lax.optimization_barrier((net.widen_ctx(g_qkv), dn_got, got_mid))
        part_mid = (part_mid.astype(F32) + got_mid.astype(F32)).astype(BF)
    decoder_grad = finish(x_own, dh1, gain_self, dn_own, dn_got)

    if fast:
        me = jnp.stack([net.core, net.x, place]).astype(jnp.int32)
        square = (shard, dim)
        ff = settle(
            unpack_kernel, me, sum_ff, net.from_core(sum_ff),
            [(shard, hidden), (shard, hidden), (hidden // n_fsdp, dim)],
        )
        g_qkv, ff, decoder_grad = lax.optimization_barrier((net.widen_x(g_qkv), ff, decoder_grad))
        grad_gate, grad_up, grad_down = ff
        sum_mid = net.widen_x(part_mid)
        *grads_qkv, grad_gself, grad_gmlp, grad_gcross, rms_values = settle(
            settle_qkv_kernel, me, g_qkv, net.from_core(g_qkv),
            [square] * 3 + [(1, shard)] * 3 + [(1, 4)],
            [pltpu.VMEM((shard, 128), F32)], entries=entries,
        )
        mids = settle(settle_mid_kernel, me, sum_mid, net.from_core(sum_mid), [square] * 5)
    else:

        def total_of(g):
            g = lax.psum_scatter(g, "fsdp", scatter_dimension=0, tiled=True).astype(F32)
            return lax.psum(g, ("parts", "ctx"))

        (g_qkv,) = g_qkv
        sum_mid = total_of(g_mid)
        flat = [
            g_ff[:, :, i].reshape(4, 8, 64, 3, 256).transpose(0, 3, 2, 1, 4).reshape(dim, hidden)
            for i in range(2)
        ]
        grad_gate, grad_up = total_of(flat[0]), total_of(flat[1])
        grad_down = total_of(g_ff[:, :, 2].reshape(hidden, dim))
        sum_qkv = lax.psum_scatter(g_qkv, "fsdp", scatter_dimension=0, tiled=True).astype(F32)
        every = lax.all_gather(lax.psum(sum_qkv, "parts"), "ctx", axis=0)
        grads_qkv = [
            jnp.concatenate(
                [every[c, :, i * width : (i + 1) * width] for c in range(n_ctx)], axis=1
            )[:, :dim]
            for i in range(3)
        ]
        tail = jnp.sum(every[:, :, 3 * width :], axis=0)
        mids = [sum_mid[:, i * dim : (i + 1) * dim] for i in range(5)]
        grad_gself, grad_gmlp, grad_gcross = tail[:, 0], tail[:, 1], tail[:, 2]
        rms_values = jnp.sqrt(tail[0, 3:7] / entries)
    return (
        layer_out[None],
        decoder_grad[None],
        enc_grad[None],
        *grads_qkv,
        *mids,
        grad_gate,
        grad_up,
        grad_down,
        grad_gself.reshape(shard),
        grad_gcross.reshape(shard),
        grad_gmlp.reshape(shard),
        rms_values.reshape(4),
    )


def solution(mesh):
    rows3 = P(("parts", "fsdp"), "ctx", None)
    group = P(("parts", "fsdp"), None)
    matrix, vector = P("fsdp", None), P("fsdp")
    shape = tuple(mesh.shape[a] for a in ("parts", "ctx", "fsdp"))
    return jax.shard_map(
        functools.partial(local, shape),
        mesh=mesh,
        in_specs=(rows3, rows3, group, group, P(("parts", "fsdp")))
        + (matrix,) * 11
        + (vector,) * 3
        + (rows3,),
        out_specs=(rows3,) * 3 + (matrix,) * 11 + (vector,) * 3 + (P(),),
        check_vma=False,
    )
```
